32 devices in a mesh: clip: 2 (over x), seq: 16 (over z, y, core).
Axes of the slice: x: 2, y: 2, z: 4, core: 2. Of those that a mesh axis runs over, the one named last changes fastest.
Arguments:
- hidden: bfloat16 [2, 1792, 1536], P(None, ('clip', 'seq')), parts along dimension 1, may hold values from -6 to 6
- latent: float32 [1792, 100], P(('clip', 'seq')), parts along dimension 0, may hold values from -6 to 6
- lengths: int32 [2], P('clip'), parts along dimension 0, may hold values from 448 to 896
- step_index: int32 [1], replicated, may hold values from 0 to 31
- guidance: float32 [1], replicated, may hold values from 1.5 to 2.5
- modulation: float32 [5, 1536], replicated, may hold values from -2.5 to 2.5
- conv_kernel: float32 [31, 1536], replicated, may hold values from -1 to 1
- w_qkv: bfloat16 [1536, 3072], replicated, may hold values from -1 to 1
- w_out: bfloat16 [1024, 1536], replicated, may hold values from -0.1875 to 0.1875
- w_mel: bfloat16 [1536, 100], replicated, may hold values from -0.15625 to 0.15625
Outputs:
- velocity: float32 [1792, 100], P(('clip', 'seq')), parts along dimension 0
- estimate: float32 [1792, 100], P(('clip', 'seq')), parts along dimension 0
The draws below stay inside these ranges and needn't reach their ends.
There are 2 independent parts, one for each index of `clip`. The reference program is written for one: setup_inputs(seed, part) draws one part's arguments, and reference() takes and returns one part's arrays. A program takes and returns all parts, laid end to end along the dimension named above; an argument that names none is the same for every part. Nothing has to cross between parts.
All inputs are finite; a program needn't handle non-finite values.
Results may differ from the reference program's by a relative error of at most 0.0061.
Values may be sent and summed in bfloat16 or wider, within the bound.
No kernel may reach another device: no remote copies, remote signals or barrier semaphores. Data moves between devices by JAX's collectives and lax.ppermute only.
A program may use at most 192 MiB of HBM per device.

```python
import math
import jax
import jax.numpy as jnp
from jax import lax

D = 1536
HEADS = 16
HEAD_DIM = 64
MEL = 100
KERNEL = 31
STEPS = 32
HW = 1024
FRAMES = 896


def draw_w_qkv(key, part):
    attn_width = HEADS * HEAD_DIM
    columns = 3 * attn_width
    column_index = jnp.arange(columns)
    sharpen = jnp.where(column_index < 2 * attn_width, 2.0, 1.0)
    entries = jax.random.truncated_normal(jax.random.fold_in(key, 13), -4.0, 4.0, (D, columns), jnp.float32) * D ** (-0.5)
    entries = jnp.clip(entries * sharpen[None, :], -1.0, 1.0)
    return entries.astype(jnp.bfloat16)


def level_of(own_key, shape, shards, least, top_value):
    gain, own = 1.0, jax.random.fold_in(own_key, 6)
    for axis_at, shards_of in shards:
        steps = jnp.exp(jax.random.uniform(jax.random.fold_in(own, axis_at), (shards_of,), jnp.float32, least / len(shards), top_value / len(shards)))
        gain = gain * jnp.repeat(steps, shape[axis_at] // shards_of).reshape([-1 if axis == axis_at else 1 for axis in range(len(shape))])
    return gain


def normal_values(key, shape, deviation, most, split=(), kind=jnp.bfloat16):
    result = jax.random.normal(key, shape, jnp.float32) * deviation
    if len(split) > 0:
        result = level_of(key, shape, split, -0.22, 0.18) * result
    return jnp.clip(result, min=-most, max=most).astype(kind)


def setup_inputs(seed: int = 0, part: int = 0) -> dict:
    arg_keys = jax.random.split(jax.random.key(seed), 11)
    part_keys = jax.random.split(jax.random.fold_in(arg_keys[10], part), 11)
    return {
        "hidden": normal_values(part_keys[0], (2, FRAMES, D), 1.0, 6.0, ((1, 16),)),
        "latent": normal_values(part_keys[1], (FRAMES, MEL), 1.0, 6.0, ((0, 16),), jnp.float32),
        "lengths": jax.random.randint(part_keys[2], (1,), FRAMES // 2, FRAMES + 1).astype(jnp.int32),
        "step_index": jax.random.randint(arg_keys[3], (1,), 0, STEPS).astype(jnp.int32),
        "guidance": jnp.clip(jax.random.uniform(arg_keys[4], (1,), jnp.float32, 1.5, 2.5), 1.5, 2.5),
        "modulation": normal_values(arg_keys[5], (5, D), 0.5, 2.5, (), jnp.float32),
        "conv_kernel": normal_values(arg_keys[6], (KERNEL, D), KERNEL ** -0.5, 1.0, (), jnp.float32),
        "w_qkv": draw_w_qkv(jax.random.fold_in(arg_keys[10], 71), part),
        "w_out": normal_values(arg_keys[8], (HW, D), HW ** -0.5, 0.1875),
        "w_mel": normal_values(arg_keys[9], (D, MEL), D ** -0.5, 0.15625),
    }


EPSILON = 1e-06
NEGATIVE = -1e+30

def layer_norm(values, shift_row, scale_row):
    mean_value = lax.optimization_barrier(jnp.mean(values, axis=-1, keepdims=True))
    centered = values - mean_value
    variance = lax.optimization_barrier(jnp.mean(centered * centered, axis=-1, keepdims=True))
    return centered * lax.rsqrt(variance + EPSILON) * (1.0 + scale_row) + shift_row

def mish(values):
    return values * jnp.tanh(jax.nn.softplus(values))

def rotate(values, positions):
    half_dim = values.shape[-1] // 2
    inverse = 10000.0 ** (-jnp.arange(half_dim, dtype=jnp.float32) / half_dim)
    angles = positions.astype(jnp.float32)[:, None] * inverse[None, :]
    cosine = jnp.cos(angles)[:, None, :]
    sine_table = jnp.sin(angles)[:, None, :]
    lower_half = values[..., :half_dim]
    upper_half = values[..., half_dim:]
    return jnp.concatenate([lower_half * cosine - upper_half * sine_table, upper_half * cosine + lower_half * sine_table], axis=-1)

def reference(hidden, latent, lengths, step_index, guidance, modulation, conv_kernel, w_qkv, w_out, w_mel):
    positions = jnp.arange(FRAMES, dtype=jnp.int32)
    is_live = positions < lengths[0]
    masked = hidden * is_live[None, :, None].astype(jnp.bfloat16)
    half_width = KERNEL // 2
    padded = jnp.pad(masked, ((0, 0), (half_width, half_width), (0, 0)))
    convolved = jnp.zeros(hidden.shape, jnp.float32)
    for tap_index in range(KERNEL):
        convolved = convolved + conv_kernel[tap_index] * padded[:, tap_index:tap_index + FRAMES, :].astype(jnp.float32)
    residual = hidden.astype(jnp.float32) + mish(convolved)
    normed = layer_norm(residual, modulation[0], modulation[1]).astype(jnp.bfloat16)
    projected = jnp.dot(normed.reshape(-1, D), w_qkv, preferred_element_type=jnp.float32)
    projected = projected.reshape(2, FRAMES, 3, HEADS, HEAD_DIM)
    queries = rotate(projected[:, :, 0], positions).astype(jnp.bfloat16)
    keys_all = rotate(projected[:, :, 1], positions).astype(jnp.bfloat16).astype(jnp.float32)
    values_all = projected[:, :, 2].astype(jnp.bfloat16).astype(jnp.float32)
    block_rows = math.gcd(FRAMES, 512)
    query_blocks = queries.reshape(2, FRAMES // block_rows, block_rows, HEADS, HEAD_DIM).transpose(1, 0, 2, 3, 4)
    scale_factor = HEAD_DIM ** (-0.5)

    def attend_block(query_block):
        scores = jnp.einsum('cqhd,ckhd->chqk', query_block.astype(jnp.float32), keys_all) * scale_factor
        key_live = is_live[None, None, None, :]
        scores = jnp.where(key_live, scores, NEGATIVE)
        row_peak = lax.optimization_barrier(jnp.max(scores, axis=-1, keepdims=True))
        weights = jnp.where(key_live, jnp.exp(scores - row_peak), 0.0)
        weight_sum = lax.optimization_barrier(jnp.sum(weights, axis=-1))
        rounded = lax.optimization_barrier(weights.astype(jnp.bfloat16))
        weighted = jnp.einsum('chqk,ckhd->chqd', rounded.astype(jnp.float32), values_all)
        return (weighted / weight_sum[..., None]).transpose(0, 2, 1, 3).astype(jnp.bfloat16)
    attended = lax.map(attend_block, query_blocks)
    attended = attended.transpose(1, 0, 2, 3, 4).reshape(2 * FRAMES, HW)
    branch = jnp.dot(attended, w_out, preferred_element_type=jnp.float32).reshape(2, FRAMES, D)
    after = residual + modulation[2] * branch
    final_norm = layer_norm(after, modulation[3], modulation[4]).astype(jnp.bfloat16)
    speed = jnp.dot(final_norm.reshape(-1, D), w_mel, preferred_element_type=jnp.float32).reshape(2, FRAMES, MEL)
    guided = speed[0] + guidance[0] * (speed[0] - speed[1])
    velocity = jnp.where(is_live[:, None], guided, 0.0)
    progress = step_index[0].astype(jnp.float32) / STEPS
    time_now = 1.0 - jnp.cos(0.5 * jnp.pi * progress)
    estimate = latent + (1.0 - time_now) * velocity
    return (velocity, estimate)
```

```python
import functools

import jax
import jax.numpy as jnp
from jax import lax
from jax.experimental import pallas as pl
from jax.experimental.pallas import tpu as pltpu
from jax.sharding import PartitionSpec as P

HEADS = 16
HEAD_DIM = 64
KERNEL = 31
STEPS = 32
LANES = 128


EPSILON = 1e-06
NEGATIVE = -1e30
VMEM = pltpu.VMEM
SMEM = pltpu.SMEM


def vmem_spec():
    return pl.BlockSpec(memory_space=VMEM)


def smem_spec():
    return pl.BlockSpec(memory_space=SMEM)


def hbm_spec():
    return pl.BlockSpec(memory_space=pl.ANY)


def rotary_tables(positions):
    half_dim = HEAD_DIM // 2
    inverse = 10000.0 ** (-jnp.arange(half_dim, dtype=jnp.float32) / half_dim)
    angles = positions.astype(jnp.float32)[:, None] * inverse[None, :]
    cosine = jnp.cos(angles)
    sine = jnp.sin(angles)
    return (
        jnp.concatenate([cosine, cosine, cosine, cosine], axis=1),
        jnp.concatenate([-sine, sine, -sine, sine], axis=1),
    )


def row_norm(load, store, tiles, width, mod_ref, row, total, rows_shape):
    mean = jnp.sum(total, axis=-1, keepdims=True) * (1.0 / width)

    def square(tile, acc):
        centered = load(tile) - mean
        return acc + centered * centered

    squares = lax.fori_loop(0, tiles, square, jnp.zeros(rows_shape, jnp.float32), unroll=2)
    variance = jnp.sum(squares, axis=-1, keepdims=True) * (1.0 / width)
    factor = lax.rsqrt(variance + EPSILON)

    def write(tile, carry):
        lanes = pl.ds(pl.multiple_of(tile * LANES, LANES), LANES)
        scale = 1.0 + mod_ref[row + 1 : row + 2, lanes]
        shift = mod_ref[row : row + 1, lanes]
        store(lanes, (load(tile) - mean) * factor * scale + shift)
        return carry

    lax.fori_loop(0, tiles, write, 0, unroll=2)


def front_kernel(
    info_ref, hidden_ref, left_ref, right_ref, taps_ref, mod_ref, cos_ref, sin_ref, weight_hbm,
    residual_ref, sent_ref, padded, normed, weight, sems,
):
    copies, rows, width = hidden_ref.shape
    halo = left_ref.shape[1]
    tiles = width // LANES
    depth = width // 8
    loads = [
        pltpu.make_async_copy(
            weight_hbm.at[pl.ds(i * depth, depth)], weight.at[pl.ds(i * depth, depth)], sems.at[i]
        )
        for i in range(8)
    ]
    for load in loads:
        load.start()
    length = info_ref[0]
    offset = info_ref[1]
    span = rows + 2 * halo
    frame = offset - halo + lax.broadcasted_iota(jnp.int32, (1, span, LANES), 1)
    live = (frame < length).astype(jnp.float32)
    first = halo - KERNEL // 2

    def convolve(tile, total):
        lanes = pl.ds(pl.multiple_of(tile * LANES, LANES), LANES)
        own = hidden_ref[:, :, lanes].astype(jnp.float32)
        padded[:, 0:halo] = left_ref[:, :, lanes].astype(jnp.float32) * live[:, 0:halo]
        padded[:, halo : halo + rows] = own * live[:, halo : halo + rows]
        padded[:, halo + rows : span] = (
            right_ref[:, :, lanes].astype(jnp.float32) * live[:, halo + rows : span]
        )
        acc = jnp.zeros((copies, rows, LANES), jnp.float32)
        for tap in range(KERNEL):
            acc = acc + taps_ref[tap : tap + 1, lanes][None] * padded[
                :, first + tap : first + tap + rows, :
            ]
        grown = jnp.exp(jnp.minimum(acc, 20.0))
        product = grown * (grown + 2.0)
        value = own + acc * (product / (product + 2.0))
        residual_ref[:, :, lanes] = value
        return total + value

    total = lax.fori_loop(0, tiles, convolve, jnp.zeros((copies, rows, LANES), jnp.float32))

    def load_tile(tile):
        return residual_ref[:, :, pl.ds(pl.multiple_of(tile * LANES, LANES), LANES)]

    def store_tile(lanes, value):
        normed[:, lanes] = value.reshape(copies * rows, LANES).astype(jnp.bfloat16)

    row_norm(
        load_tile, store_tile, tiles, width, mod_ref, 0, total,
        (copies, rows, LANES),
    )
    for load in loads:
        load.wait()
    blocks = sent_ref.shape[0] // copies
    wide = 2 * LANES
    cosine = jnp.concatenate([cos_ref[...]] * copies, axis=0)
    sine = jnp.concatenate([sin_ref[...]] * copies, axis=0)
    lane = lax.broadcasted_iota(jnp.int32, (copies * rows, LANES), 1)
    lower = lane % HEAD_DIM < HEAD_DIM // 2
    half = HEAD_DIM // 2
    for part in range(3):

        def project(block, carry):
            lanes = pl.ds(pl.multiple_of((part * blocks // 2 + block) * wide, wide), wide)
            both = jnp.dot(normed[...], weight[:, lanes], preferred_element_type=jnp.float32)
            for side in range(2):
                value = both[:, side * LANES : (side + 1) * LANES]
                if part < 2:
                    swapped = jnp.where(
                        lower, pltpu.roll(value, LANES - half, 1), pltpu.roll(value, half, 1)
                    )
                    value = value * cosine + swapped * sine
                value = value.astype(jnp.bfloat16)
                if part == 0:
                    value = value * jnp.bfloat16(HEAD_DIM**-0.5)
                value = value.astype(jnp.float32).reshape(copies, rows, LANES)
                for copy in range(copies):
                    sent_ref[copy * blocks + 2 * block + side, part] = value[copy].astype(
                        jnp.bfloat16
                    )
            return carry

        lax.fori_loop(0, blocks // 2, project, 0)


def attend_kernel(info_ref, got_ref, out_ref, keys, values_t, queries):
    groups, _, rows, _ = got_ref.shape
    key_total = groups * rows
    step = queries.shape[0] // 4
    length = info_ref[0]
    lane_low = lax.broadcasted_iota(jnp.int32, (rows, LANES), 1) < HEAD_DIM
    keys[...] = got_ref[:, 1].astype(jnp.float32).reshape(key_total, LANES).astype(jnp.bfloat16)
    values = got_ref[:, 2].astype(jnp.float32).reshape(key_total, LANES)
    values_t[...] = values.T.astype(jnp.bfloat16)
    queries[...] = jnp.zeros(queries.shape, jnp.bfloat16)
    live = lax.broadcasted_iota(jnp.int32, (key_total, 4 * step), 0) < length

    def one_pair(pair, carry):
        for at in range(2):
            query = got_ref[2 * pair + at, 0].astype(jnp.float32)
            queries[(2 * at) * step : (2 * at) * step + rows, :] = jnp.where(
                lane_low, query, 0.0
            ).astype(jnp.bfloat16)
            queries[(2 * at + 1) * step : (2 * at + 1) * step + rows, :] = jnp.where(
                lane_low, 0.0, query
            ).astype(jnp.bfloat16)
        scores = lax.dot_general(
            keys[...], queries[...], (((1,), (1,)), ((), ())), preferred_element_type=jnp.float32
        )
        scores = jnp.where(live, scores, NEGATIVE)
        peak = jnp.max(scores, axis=0, keepdims=True)
        weights = jnp.exp(scores - peak)
        weight_sum = jnp.sum(weights, axis=0, keepdims=True)
        mixed = jnp.dot(
            values_t[...], weights.astype(jnp.bfloat16), preferred_element_type=jnp.float32
        )
        mixed = (mixed / weight_sum).T
        for at in range(2):
            base = 2 * at * step
            out_ref[2 * pair + at] = jnp.where(
                lane_low, mixed[base : base + rows], mixed[base + step : base + step + rows]
            ).astype(jnp.bfloat16)
        return carry

    lax.fori_loop(0, groups // 2, one_pair, 0)


def back_kernel(
    info_ref, real_ref, got_ref, residual_ref, mod_ref, latent_ref, w_out_ref, w_mel_ref,
    velocity_ref, estimate_ref, attended, after,
):
    copies, rows, width = residual_ref.shape
    blocks = got_ref.shape[0] // copies
    tiles = width // LANES
    for block in range(blocks):
        pieces = [got_ref[copy * blocks + block].astype(jnp.float32) for copy in range(copies)]
        attended[:, block * LANES : (block + 1) * LANES] = jnp.concatenate(pieces, axis=0).astype(
            jnp.bfloat16
        )
    wide = 2 * LANES

    def project(block, total):
        lanes = pl.ds(pl.multiple_of(block * wide, wide), wide)
        branch = jnp.dot(attended[...], w_out_ref[:, lanes], preferred_element_type=jnp.float32)
        value = residual_ref[:, :, lanes].reshape(copies * rows, wide) + mod_ref[2:3, lanes] * branch
        after[:, lanes] = value
        return total + value[:, :LANES] + value[:, LANES:]

    total = lax.fori_loop(
        0, width // wide, project, jnp.zeros((copies * rows, LANES), jnp.float32)
    )
    final = after

    def load_tile(tile):
        return after[:, pl.ds(pl.multiple_of(tile * LANES, LANES), LANES)]

    def store_tile(lanes, value):
        final[:, lanes] = value

    row_norm(
        load_tile, store_tile, tiles, width, mod_ref, 3, total,
        (copies * rows, LANES),
    )
    speed = jnp.dot(
        final[...].astype(jnp.bfloat16), w_mel_ref[...], preferred_element_type=jnp.float32
    )
    first, second = speed[:rows], speed[rows : 2 * rows]
    guided = first + real_ref[0] * (first - second)
    frame = info_ref[1] + lax.broadcasted_iota(jnp.int32, guided.shape, 0)
    velocity = jnp.where(frame < info_ref[0], guided, 0.0)
    velocity_ref[...] = velocity
    estimate_ref[...] = latent_ref[...] + real_ref[1] * velocity


def to_groups(values, subs):
    copies, rows, _ = values.shape
    grouped = values.reshape(copies, subs, rows // subs, HEADS, HEAD_DIM).transpose(0, 3, 1, 2, 4)
    return grouped.reshape(copies * HEADS * subs, rows // subs, HEAD_DIM)


def from_groups(grouped, copies, rows, subs):
    split = grouped.reshape(copies, HEADS, subs, rows // subs, HEAD_DIM).transpose(0, 2, 3, 1, 4)
    return split.reshape(copies, rows, HEADS * HEAD_DIM)


def exchange(values):
    return lax.all_to_all(values, "seq", split_axis=0, concat_axis=1, tiled=True)


def attend_blocks(queries, keys, values, live):
    groups, total, _ = queries.shape
    block = max(size for size in range(1, min(total, 1024) + 1) if total % size == 0)
    blocks = queries.reshape(groups, total // block, block, HEAD_DIM).transpose(1, 0, 2, 3)
    live = live[None, None, :]

    def one_block(query):
        scores = jnp.einsum("gqd,gkd->gqk", query, keys, preferred_element_type=jnp.float32)
        scores = jnp.where(live, scores, NEGATIVE)
        weights = jnp.exp(scores - jnp.max(scores, axis=-1, keepdims=True))
        weights = jnp.where(live, weights, 0.0)
        mixed = jnp.einsum(
            "gqk,gkd->gqd",
            weights.astype(jnp.bfloat16),
            values,
            preferred_element_type=jnp.float32,
        )
        return (mixed / jnp.sum(weights, axis=-1)[..., None]).astype(jnp.bfloat16)

    return lax.map(one_block, blocks).transpose(1, 0, 2, 3).reshape(groups, total, HEAD_DIM)


def attend_any(sent, copies, length):
    groups, _, rows, _ = sent.shape
    count = lax.axis_size("seq")
    pairs = copies * HEADS
    subs = max(1, count // pairs)
    sub_index = lax.axis_index("seq") % subs
    part_rows = rows // subs

    def frames_first(part):
        split = sent[:, part].reshape(copies, groups // copies, rows, LANES)
        return split.transpose(0, 2, 1, 3).reshape(copies, rows, HEADS * HEAD_DIM)

    queries, keys, values = (exchange(to_groups(frames_first(part), subs)) for part in range(3))

    def frames_of(sub):
        start = jnp.arange(count, dtype=jnp.int32)[:, None] * rows + sub * part_rows
        return (start + jnp.arange(part_rows, dtype=jnp.int32)[None, :]).reshape(-1)

    frames = [frames_of(sub_index)]
    parts = [(keys, values)]
    for apart in range(1, subs):
        perm = [(i, i - i % subs + (i + apart) % subs) for i in range(count)]
        parts.append(tuple(lax.ppermute(part, "seq", perm) for part in (keys, values)))
        frames.append(frames_of((sub_index - apart) % subs))
    keys = jnp.concatenate([part[0] for part in parts], axis=1)
    values = jnp.concatenate([part[1] for part in parts], axis=1)
    attended = attend_blocks(queries, keys, values, jnp.concatenate(frames) < length)
    back = lax.all_to_all(attended, "seq", split_axis=1, concat_axis=0, tiled=True)
    joined = from_groups(back, copies, rows, subs)
    split = joined.reshape(copies, rows, groups // copies, LANES).transpose(0, 2, 1, 3)
    return split.reshape(groups, rows, LANES)


def attend_pairs(sent, info):
    count, _, rows, _ = sent.shape
    got = lax.all_to_all(sent, "seq", split_axis=0, concat_axis=0, tiled=True)
    attended = pl.pallas_call(
        attend_kernel,
        name="attend",
        out_shape=jax.ShapeDtypeStruct((count, rows, LANES), jnp.bfloat16),
        in_specs=[smem_spec(), vmem_spec()],
        out_specs=vmem_spec(),
        scratch_shapes=[
            VMEM((count * rows, LANES), jnp.bfloat16),
            VMEM((LANES, count * rows), jnp.bfloat16),
            VMEM((4 * (-(-rows // 16) * 16), LANES), jnp.bfloat16),
        ],
    )(info, got)
    return lax.all_to_all(attended, "seq", split_axis=0, concat_axis=0, tiled=True)


def per_device(
    hidden, latent, lengths, step_index, guidance, modulation, conv_kernel, w_qkv, w_out, w_mel
):
    copies, rows, width = hidden.shape
    count = lax.axis_size("seq")
    offset = lax.axis_index("seq") * rows
    positions = offset + jnp.arange(rows, dtype=jnp.int32)
    info = jnp.stack([lengths[0], offset.astype(jnp.int32)])
    halo = 16
    left = lax.ppermute(hidden[:, rows - halo :], "seq", [(i, i + 1) for i in range(count - 1)])
    right = lax.ppermute(hidden[:, :halo], "seq", [(i + 1, i) for i in range(count - 1)])
    cosine, sine = rotary_tables(positions)
    blocks = HEADS * HEAD_DIM // LANES
    residual, sent = pl.pallas_call(
        front_kernel,
        name="front",
        out_shape=(
            jax.ShapeDtypeStruct((copies, rows, width), jnp.float32),
            jax.ShapeDtypeStruct((copies * blocks, 3, rows, LANES), jnp.bfloat16),
        ),
        in_specs=[smem_spec()] + [vmem_spec()] * 7 + [hbm_spec()],
        out_specs=(vmem_spec(), vmem_spec()),
        scratch_shapes=[
            VMEM((copies, rows + 2 * halo, LANES), jnp.float32),
            VMEM((copies * rows, width), jnp.bfloat16),
            VMEM(w_qkv.shape, jnp.bfloat16),
            pltpu.SemaphoreType.DMA((8,)),
        ],
    )(info, hidden, left, right, conv_kernel, modulation, cosine, sine, w_qkv)
    if count == copies * blocks:
        back = attend_pairs(sent, info)
    else:
        back = attend_any(sent, copies, lengths[0])
    progress = step_index[0].astype(jnp.float32) / STEPS
    time_now = 1.0 - jnp.cos(0.5 * jnp.pi * progress)
    real = jnp.stack([guidance[0], 1.0 - time_now])
    return pl.pallas_call(
        back_kernel,
        name="back",
        out_shape=(
            jax.ShapeDtypeStruct(latent.shape, jnp.float32),
            jax.ShapeDtypeStruct(latent.shape, jnp.float32),
        ),
        in_specs=[smem_spec(), smem_spec()] + [vmem_spec()] * 6,
        out_specs=(vmem_spec(), vmem_spec()),
        scratch_shapes=[
            VMEM((copies * rows, HEADS * HEAD_DIM), jnp.bfloat16),
            VMEM((copies * rows, width), jnp.float32),
        ],
    )(info, real, back, residual, modulation, latent, w_out, w_mel)


def solution(mesh):
    return jax.shard_map(
        per_device,
        mesh=mesh,
        in_specs=(
            P(None, ("clip", "seq"), None),
            P(("clip", "seq"), None),
            P("clip"),
            P(),
            P(),
            P(),
            P(),
            P(),
            P(),
            P(),
        ),
        out_specs=(P(("clip", "seq"), None), P(("clip", "seq"), None)),
        check_vma=False,
    )
```

```python
import functools

import jax
import jax.numpy as jnp
from jax import lax
from jax.experimental import pallas as pl
from jax.experimental.pallas import tpu as pltpu
from jax.sharding import PartitionSpec as P

HEADS = 16
HEAD_DIM = 64
KERNEL = 31
STEPS = 32
LANES = 128
HALO = 16


EPSILON = 1e-06
NEGATIVE = -1e30
LENGTH, CORE, CHIP = 0, 1, 2
VMEM = pltpu.VMEM
SMEM = pltpu.SMEM
MIB = 1 << 20


def vmem_spec():
    return pl.BlockSpec(memory_space=VMEM)


def smem_spec():
    return pl.BlockSpec(memory_space=SMEM)


def rotary_tables(positions):
    half_dim = HEAD_DIM // 2
    lane = jnp.arange(LANES, dtype=jnp.int32)
    inverse = 10000.0 ** (-(lane % half_dim).astype(jnp.float32) / half_dim)
    angles = positions.astype(jnp.float32)[:, None] * inverse[None, :]
    sign = jnp.where(lane % HEAD_DIM < half_dim, -1.0, 1.0)
    return jnp.cos(angles), jnp.sin(angles) * sign[None, :]


def hbm_spec():
    return pl.BlockSpec(memory_space=pltpu.HBM)


def tile_lanes(tile):
    return pl.ds(pl.multiple_of(tile * LANES, LANES), LANES)


def row_norm(load, store, tiles, mod_ref, row, total):
    width = tiles * LANES
    mean = jnp.sum(total, axis=-1, keepdims=True) * (1.0 / width)

    def square(tile, acc):
        centered = load(tile) - mean
        return acc + centered * centered

    squares = lax.fori_loop(0, tiles, square, jnp.zeros(total.shape, jnp.float32), unroll=6)
    variance = jnp.sum(squares, axis=-1, keepdims=True) * (1.0 / width)
    factor = lax.rsqrt(variance + EPSILON)

    def write(tile, carry):
        lanes = tile_lanes(tile)
        scale = 1.0 + mod_ref[row + 1 : row + 2, lanes]
        shift = mod_ref[row : row + 1, lanes]
        store(lanes, (load(tile) - mean) * factor * scale + shift)
        return carry

    lax.fori_loop(0, tiles, write, 0, unroll=6)


def edge_kernel(
    info_ref, hidden_hbm, taps_hbm, mod_hbm, near_ref, far_ref, own_ref, taps_ref, mod_ref, sems
):
    rows = own_ref.shape[0]
    core = info_ref[CORE]
    edge = pl.ds(pl.multiple_of(core * (rows - HALO), 8), HALO)
    copies = [
        pltpu.make_async_copy(hidden_hbm.at[1 - core, edge], near_ref, sems.at[0]),
        pltpu.make_async_copy(hidden_hbm.at[core, edge], far_ref, sems.at[1]),
        pltpu.make_async_copy(hidden_hbm.at[core], own_ref, sems.at[2]),
        pltpu.make_async_copy(taps_hbm, taps_ref, sems.at[3]),
        pltpu.make_async_copy(mod_hbm, mod_ref, sems.at[4]),
    ]
    for copy in copies:
        copy.start()
    for copy in copies:
        copy.wait()


def front_kernel(
    info_ref, own_ref, partner_ref, near_ref, far_ref, taps_ref, mod_ref, weight_hbm,
    residual_ref, normed_ref, weight_ref, padded, sems,
):
    rows, width = own_ref.shape
    halo = near_ref.shape[0]
    total_rows = 2 * rows
    tiles = width // LANES
    parts = 8
    depth = width // parts
    loads = []
    for part in range(parts):
        here = pl.ds(part * depth, depth)
        loads.append(
            pltpu.make_async_copy(weight_hbm.at[here], weight_ref.at[here], sems.at[part])
        )
    for load in loads:
        load.start()
    length, core = info_ref[LENGTH], info_ref[CORE]
    offset = info_ref[CHIP] * total_rows
    span = total_rows + 2 * halo
    frame = offset - halo + lax.broadcasted_iota(jnp.int32, (span, LANES), 0)
    live = (frame < length).astype(jnp.float32)
    first = halo - KERNEL // 2
    own_at = pl.ds(pl.multiple_of(halo + core * rows, 8), rows)
    partner_at = pl.ds(pl.multiple_of(halo + (1 - core) * rows, 8), rows)
    near_at = pl.ds(pl.multiple_of(core * (halo + total_rows), 8), halo)
    far_at = pl.ds(pl.multiple_of((1 - core) * (halo + total_rows), 8), halo)

    def convolve(tile, total):
        lanes = tile_lanes(tile)
        padded[near_at] = near_ref[:, lanes].astype(jnp.float32)
        padded[far_at] = far_ref[:, lanes].astype(jnp.float32)
        padded[own_at] = own_ref[:, lanes].astype(jnp.float32)
        padded[partner_at] = partner_ref[core, :, lanes].astype(jnp.float32)
        own = padded[halo : halo + total_rows]
        padded[...] = padded[...] * live
        acc = jnp.zeros((total_rows, LANES), jnp.float32)
        for tap in range(KERNEL):
            acc = acc + taps_ref[tap : tap + 1, lanes] * padded[
                first + tap : first + tap + total_rows
            ]
        grown = jnp.exp(jnp.minimum(acc, 20.0))
        product = grown * (grown + 2.0)
        value = own + acc * (product / (product + 2.0))
        residual_ref[:, lanes] = value
        return total + value

    total = lax.fori_loop(
        0, tiles, convolve, jnp.zeros((total_rows, LANES), jnp.float32), unroll=3
    )

    def store(lanes, value):
        normed_ref[:, lanes] = value.astype(jnp.bfloat16)

    row_norm(lambda tile: residual_ref[:, tile_lanes(tile)], store, tiles, mod_ref, 0, total)
    for load in loads:
        load.wait()


def project_kernel(firsts, origin, info_ref, normed_ref, weight_ref, cos_ref, sin_ref, *out_refs):
    rows = normed_ref.shape[0]
    attn = weight_ref.shape[1] // 3
    wide = 2 * LANES
    half = HEAD_DIM // 2
    cosine, sine = cos_ref[...], sin_ref[...]
    lower = lax.broadcasted_iota(jnp.int32, (rows, LANES), 1) % HEAD_DIM < half
    chip = info_ref[CHIP] if origin is None else origin
    swap = jnp.full((rows, LANES), chip & 1, jnp.int32) > 0
    for at, apart in enumerate(firsts):
        pair = (chip ^ apart) >> 1
        for part in range(3):
            start = part * attn + pair * wide
            both = jnp.dot(
                normed_ref[...],
                weight_ref[:, pl.ds(pl.multiple_of(start, wide), wide)],
                preferred_element_type=jnp.float32,
            )
            sides = []
            for side in range(2):
                value = both[:, side * LANES : (side + 1) * LANES]
                if part < 2:
                    swapped = jnp.where(
                        lower, pltpu.roll(value, LANES - half, 1), pltpu.roll(value, half, 1)
                    )
                    value = value * cosine + swapped * sine
                if part == 0:
                    value = value * HEAD_DIM**-0.5
                sides.append(value)
            out_refs[2 * at][part] = jnp.where(swap, sides[1], sides[0]).astype(jnp.bfloat16)
            out_refs[2 * at + 1][part] = jnp.where(swap, sides[0], sides[1]).astype(jnp.bfloat16)


def attend_kernel(info_ref, *refs):
    chips = len(refs) - 4
    got_refs, out_ref = refs[:chips], refs[chips]
    keys, values, queries = refs[chips + 1 :]
    _, rows, _ = got_refs[0].shape
    total = chips * rows
    length, chip = info_ref[LENGTH], info_ref[CHIP]
    low = lax.broadcasted_iota(jnp.int32, (rows, LANES), 1) < HEAD_DIM
    lane = lax.broadcasted_iota(jnp.int32, (rows, LANES), 1)
    row = lax.broadcasted_iota(jnp.int32, (rows, LANES), 0)
    zero = jnp.zeros((rows, LANES), jnp.bfloat16)
    queries[:, LANES:] = jnp.where(
        lax.broadcasted_iota(jnp.int32, (2 * total, LANES), 1) == 0, 1.0, 0.0
    ).astype(jnp.bfloat16)
    for apart, got_ref in enumerate(got_refs):
        here = slice(apart * rows, (apart + 1) * rows)
        keys[here, :LANES] = got_ref[1]
        dead = (lane == 0) & (row + (chip ^ apart) * rows >= length)
        keys[here, LANES:] = jnp.where(dead, NEGATIVE, 0.0).astype(jnp.bfloat16)
        values[here, :] = got_ref[2]
        query = got_ref[0]
        at = 2 * apart * rows
        queries[at : at + rows, :LANES] = jnp.where(low, query, zero)
        queries[at + rows : at + 2 * rows, :LANES] = jnp.where(low, zero, query)
    for first in range(0, chips, 2):
        at = 2 * first * rows
        scores = lax.dot_general(
            queries[at : at + 4 * rows, :], keys[...], (((1,), (1,)), ((), ())),
            preferred_element_type=jnp.float32,
        )
        weights = jnp.exp(scores - jnp.max(scores, axis=1, keepdims=True))
        weight_sum = jnp.sum(weights, axis=1, keepdims=True)
        mixed = jnp.dot(
            weights.astype(jnp.bfloat16), values[...], preferred_element_type=jnp.float32
        )
        mixed = mixed / weight_sum
        for side in range(2):
            base = 2 * side * rows
            out_ref[chip ^ (first + side)] = jnp.where(
                low, mixed[base : base + rows], mixed[base + rows : base + 2 * rows]
            ).astype(jnp.bfloat16)


def back_kernel(
    info_ref, got_ref, residual_ref, mod_ref, w_out_ref, w_mel_ref, keep_ref, send_ref, attended,
    after, speed,
):
    rows, width = residual_ref.shape
    tiles = width // LANES
    core = info_ref[CORE]
    for block in range(got_ref.shape[0]):
        attended[:, block * LANES : (block + 1) * LANES] = got_ref[block]
    wide = 2 * LANES
    total = jnp.zeros((rows, LANES), jnp.float32)
    for block in range(width // wide):
        lanes = slice(block * wide, (block + 1) * wide)
        branch = jnp.dot(attended[...], w_out_ref[:, lanes], preferred_element_type=jnp.float32)
        value = residual_ref[:, lanes] + mod_ref[2:3, lanes] * branch
        after[:, lanes] = value
        total = total + value[:, :LANES] + value[:, LANES:]

    def store(lanes, value):
        after[:, lanes] = value

    row_norm(lambda tile: after[:, tile_lanes(tile)], store, tiles, mod_ref, 3, total)
    speed[...] = lax.dot_general(
        after[...].astype(jnp.bfloat16), w_mel_ref[...], (((1,), (1,)), ((), ())),
        preferred_element_type=jnp.float32,
    )
    half = rows // 2
    keep_ref[...] = speed[pl.ds(pl.multiple_of(core * half, 8), half), :]
    send_ref[...] = speed[pl.ds(pl.multiple_of((1 - core) * half, 8), half), :]


def call(kernel, name, out_shape, inputs, scratch, limit, hbm=()):
    single = not isinstance(out_shape, tuple)
    specs = [hbm_spec() if at in hbm else vmem_spec() for at in range(1, len(inputs))]
    inputs = [
        pltpu.with_memory_space_constraint(value, pltpu.HBM) if at in hbm else value
        for at, value in enumerate(inputs)
    ]
    return pl.pallas_call(
        kernel,
        name=name,
        out_shape=out_shape,
        in_specs=[smem_spec()] + specs,
        out_specs=vmem_spec() if single else tuple(vmem_spec() for _ in out_shape),
        scratch_shapes=scratch,
        compiler_params=pltpu.CompilerParams(vmem_limit_bytes=limit * MIB),
    )(*inputs)


def array(shape, dtype=jnp.float32):
    return jax.ShapeDtypeStruct(shape, dtype)


def project(normed, w_qkv, tables, info, firsts, origin=None):
    shape = array((3, normed.shape[0], LANES), jnp.bfloat16)
    return call(
        functools.partial(project_kernel, tuple(firsts), origin),
        "project",
        (shape,) * (2 * len(firsts)),
        (info, normed, w_qkv) + tables,
        [],
        8,
    )


def same_core(count):
    return [list(range(core, count, 2)) for core in range(2)]


def across(value, apart, count):
    return lax.ppermute(value, "seq", [(i, i ^ apart) for i in range(count)])


def to_groups(values, subs):
    rows, _ = values.shape
    grouped = values.reshape(subs, rows // subs, HEADS, HEAD_DIM).transpose(2, 0, 1, 3)
    return grouped.reshape(HEADS * subs, rows // subs, HEAD_DIM)


def from_groups(grouped, rows, subs):
    split = grouped.reshape(HEADS, subs, rows // subs, HEAD_DIM).transpose(1, 2, 0, 3)
    return split.reshape(rows, HEADS * HEAD_DIM)


def attend_blocks(queries, keys, values, live):
    groups, total, _ = queries.shape
    block = max(size for size in range(1, min(total, 1024) + 1) if total % size == 0)
    blocks = queries.reshape(groups, total // block, block, HEAD_DIM).transpose(1, 0, 2, 3)
    live = live[None, None, :]

    def one_block(query):
        scores = jnp.einsum("gqd,gkd->gqk", query, keys, preferred_element_type=jnp.float32)
        scores = jnp.where(live, scores, NEGATIVE)
        weights = jnp.exp(scores - jnp.max(scores, axis=-1, keepdims=True))
        weights = jnp.where(live, weights, 0.0)
        mixed = jnp.einsum(
            "gqk,gkd->gqd",
            weights.astype(jnp.bfloat16),
            values,
            preferred_element_type=jnp.float32,
        )
        return (mixed / jnp.sum(weights, axis=-1)[..., None]).astype(jnp.bfloat16)

    return lax.map(one_block, blocks).transpose(1, 0, 2, 3).reshape(groups, total, HEAD_DIM)


def attend_any(normed, w_qkv, tables, info, length, count):
    rows = normed.shape[0]
    chips = count // 2
    groups = HEADS * HEAD_DIM // LANES
    sent = project(normed, w_qkv, tables, info, range(0, groups, 2), 0)
    subs = max(1, chips // HEADS)
    chip = lax.axis_index("seq") >> 1
    part_rows = rows // subs

    def exchange(part):
        whole = jnp.concatenate([group[part] for group in sent], axis=1)
        return lax.all_to_all(
            to_groups(whole, subs), "seq", split_axis=0, concat_axis=1, tiled=True,
            axis_index_groups=same_core(count),
        )

    queries, keys, values = (exchange(part) for part in range(3))

    def frames_of(sub):
        start = jnp.arange(chips, dtype=jnp.int32)[:, None] * rows + sub * part_rows
        return (start + jnp.arange(part_rows, dtype=jnp.int32)[None, :]).reshape(-1)

    frames = [frames_of(chip % subs)]
    parts = [(keys, values)]
    for apart in range(1, subs):
        perm = []
        for i in range(count):
            at = i // 2
            target = at - at % subs + (at + apart) % subs
            perm.append((i, 2 * target + i % 2))
        parts.append(tuple(lax.ppermute(part, "seq", perm) for part in (keys, values)))
        frames.append(frames_of((chip - apart) % subs))
    keys = jnp.concatenate([part[0] for part in parts], axis=1)
    values = jnp.concatenate([part[1] for part in parts], axis=1)
    attended = attend_blocks(queries, keys, values, jnp.concatenate(frames) < length)
    back = lax.all_to_all(
        attended, "seq", split_axis=1, concat_axis=0, tiled=True,
        axis_index_groups=same_core(count),
    )
    return from_groups(back, rows, subs).reshape(rows, groups, LANES).transpose(1, 0, 2)


def attend_chips(normed, w_qkv, tables, info, count):
    rows = normed.shape[0]
    chips = count // 2
    order = list(range(chips // 2, chips, 2)) + list(range(2, chips // 2, 2)) + [0]
    held = {}
    for first in order:
        made = project(normed, w_qkv, tables, info, [first])
        for side in range(2):
            apart = first + side
            held[apart] = across(made[side], 2 * apart, count) if apart else made[side]
    total = chips * rows
    attended = call(
        attend_kernel,
        "attend",
        array((chips, rows, LANES), jnp.bfloat16),
        (info,) + tuple(held[apart] for apart in range(chips)),
        [
            VMEM((total, 2 * LANES), jnp.bfloat16),
            VMEM((total, LANES), jnp.bfloat16),
            VMEM((2 * total, 2 * LANES), jnp.bfloat16),
        ],
        24,
    )
    return lax.all_to_all(
        attended, "seq", split_axis=0, concat_axis=0, tiled=True,
        axis_index_groups=same_core(count),
    )


def per_device(
    hidden, latent, lengths, step_index, guidance, modulation, conv_kernel, w_qkv, w_out, w_mel
):
    copies, rows, width = hidden.shape
    count = lax.axis_size("seq")
    chips = count // 2
    index = lax.axis_index("seq").astype(jnp.int32)
    chip, core = index >> 1, index & 1
    chip_rows = 2 * rows
    info = jnp.stack([lengths[0], core, chip])

    partner = across(hidden, 1, count)
    near, far, own, taps, mods = call(
        edge_kernel,
        "edge",
        (
            array((HALO, width), jnp.bfloat16),
            array((HALO, width), jnp.bfloat16),
            array((rows, width), jnp.bfloat16),
            array(conv_kernel.shape),
            array(modulation.shape),
        ),
        (info, hidden, conv_kernel, modulation),
        [pltpu.SemaphoreType.DMA((5,))],
        4,
        hbm=(1, 2, 3),
    )
    steps = range(chips - 1)
    near = lax.ppermute(
        near, "seq",
        [(2 * m + 1, 2 * m + 2) for m in steps] + [(2 * m + 2, 2 * m + 1) for m in steps],
    )
    far = lax.ppermute(
        far, "seq",
        [(2 * m + 1, 2 * m + 3) for m in steps] + [(2 * m + 2, 2 * m) for m in steps],
    )
    tables = rotary_tables(chip * chip_rows + jnp.arange(chip_rows, dtype=jnp.int32))
    residual, normed, weight = call(
        front_kernel,
        "front",
        (
            array((chip_rows, width)),
            array((chip_rows, width), jnp.bfloat16),
            array(w_qkv.shape, jnp.bfloat16),
        ),
        (info, own, partner, near, far, taps, mods, w_qkv),
        [VMEM((chip_rows + 2 * HALO, LANES), jnp.float32), pltpu.SemaphoreType.DMA((8,))],
        8,
        hbm=(7,),
    )
    groups = HEADS * HEAD_DIM // LANES
    if chips == groups and chips & (chips - 1) == 0 and chips >= 4:
        back = attend_chips(normed, weight, tables, info, count)
    else:
        back = attend_any(normed, weight, tables, info, lengths[0], count)
    mels = w_mel.shape[1]
    keep, send = call(
        back_kernel,
        "back",
        (array((rows, mels)),) * 2,
        (info, back, residual, mods, w_out, w_mel.T),
        [
            VMEM((chip_rows, HEADS * HEAD_DIM), jnp.bfloat16),
            VMEM((chip_rows, width), jnp.float32),
            VMEM((chip_rows, mels), jnp.float32),
        ],
        12,
    )
    other = across(send, 1, count)
    first = jnp.where(core == 0, keep, other)
    second = jnp.where(core == 0, other, keep)
    guided = first + guidance[0] * (first - second)
    live = index * rows + jnp.arange(rows, dtype=jnp.int32) < lengths[0]
    velocity = jnp.where(live[:, None], guided, 0.0)
    progress = step_index[0].astype(jnp.float32) / STEPS
    time_now = 1.0 - jnp.cos(0.5 * jnp.pi * progress)
    return (velocity, latent + (1.0 - time_now) * velocity)


def solution(mesh):
    return jax.shard_map(
        per_device,
        mesh=mesh,
        in_specs=(
            P(None, ("clip", "seq"), None),
            P(("clip", "seq"), None),
            P("clip"),
            P(),
            P(),
            P(),
            P(),
            P(),
            P(),
            P(),
        ),
        out_specs=(P(("clip", "seq"), None), P(("clip", "seq"), None)),
        check_vma=False,
    )
```

```python
import functools

import jax
import jax.numpy as jnp
from jax import lax
from jax.experimental import pallas as pl
from jax.experimental.pallas import tpu as pltpu
from jax.sharding import PartitionSpec as P


HEADS = 16
HEAD_DIM = 64
KERNEL = 31
STEPS = 32
LANES = 128
HALO = 16


EPSILON = 1e-06
NEGATIVE = -1e30
CORE, CHIP, LENGTH = 0, 1, 2
VMEM = pltpu.VMEM
SMEM = pltpu.SMEM
MIB = 1 << 20


def vmem_spec():
    return pl.BlockSpec(memory_space=VMEM)


def smem_spec():
    return pl.BlockSpec(memory_space=SMEM)


def rotary_tables(positions):
    half_dim = HEAD_DIM // 2
    lane = jnp.arange(LANES, dtype=jnp.int32)
    inverse = 10000.0 ** (-(lane % half_dim).astype(jnp.float32) / half_dim)
    angles = positions.astype(jnp.float32)[:, None] * inverse[None, :]
    sign = jnp.where(lane % HEAD_DIM < half_dim, -1.0, 1.0)
    return jnp.cos(angles), jnp.sin(angles) * sign[None, :]


def hbm_spec():
    return pl.BlockSpec(memory_space=pltpu.HBM)


def tile_lanes(tile):
    return pl.ds(pl.multiple_of(tile * LANES, LANES), LANES)


def row_norm(load, store, tiles, mod_ref, row, total):
    width = tiles * LANES
    mean = jnp.sum(total, axis=-1, keepdims=True) * (1.0 / width)

    def square(tile, acc):
        centered = load(tile) - mean
        return acc + centered * centered

    squares = lax.fori_loop(0, tiles, square, jnp.zeros(total.shape, jnp.float32), unroll=6)
    variance = jnp.sum(squares, axis=-1, keepdims=True) * (1.0 / width)
    factor = lax.rsqrt(variance + EPSILON)

    def write(tile, carry):
        lanes = tile_lanes(tile)
        scale = 1.0 + mod_ref[row + 1 : row + 2, lanes]
        shift = mod_ref[row : row + 1, lanes]
        store(lanes, (load(tile) - mean) * factor * scale + shift)
        return carry

    lax.fori_loop(0, tiles, write, 0, unroll=6)


def run_copies(pairs, sems):
    copies = [
        pltpu.make_async_copy(source, target, sems.at[at])
        for at, (source, target) in enumerate(pairs)
    ]
    for copy in copies:
        copy.start()
    for copy in copies:
        copy.wait()


def edge_kernel(info_ref, hidden_hbm, near_ref, far_ref, sems):
    core = info_ref[CORE]
    edge = pl.ds(pl.multiple_of(core * (hidden_hbm.shape[1] - HALO), 8), HALO)
    run_copies(
        [(hidden_hbm.at[1 - core, edge], near_ref), (hidden_hbm.at[core, edge], far_ref)], sems
    )


def stage_kernel(info_ref, hidden_hbm, taps_hbm, mod_hbm, own_ref, taps_ref, mod_ref, sems):
    run_copies(
        [
            (hidden_hbm.at[info_ref[CORE]], own_ref),
            (taps_hbm, taps_ref),
            (mod_hbm, mod_ref),
        ],
        sems,
    )


def fetch_kernel(info_ref, residual_hbm, w_mel_hbm, residual_ref, w_mel_ref, sems):
    del info_ref
    run_copies([(residual_hbm, residual_ref), (w_mel_hbm, w_mel_ref)], sems)


def front_kernel(
    info_ref, own_ref, partner_ref, near_ref, far_ref, taps_ref, mod_ref, weight_hbm,
    residual_ref, normed_ref, weight_ref, padded, sems,
):
    rows, width = own_ref.shape
    halo = near_ref.shape[0]
    total_rows = 2 * rows
    tiles = width // LANES
    parts = 8
    depth = width // parts
    loads = []
    for part in range(parts):
        here = pl.ds(part * depth, depth)
        loads.append(
            pltpu.make_async_copy(weight_hbm.at[here], weight_ref.at[here], sems.at[part])
        )
    for load in loads:
        load.start()
    length, core = info_ref[LENGTH], info_ref[CORE]
    offset = info_ref[CHIP] * total_rows
    span = total_rows + 2 * halo
    frame = offset - halo + lax.broadcasted_iota(jnp.int32, (span, LANES), 0)
    live = (frame < length).astype(jnp.float32)
    first = halo - KERNEL // 2
    own_at = pl.ds(pl.multiple_of(halo + core * rows, 8), rows)
    partner_at = pl.ds(pl.multiple_of(halo + (1 - core) * rows, 8), rows)
    near_at = pl.ds(pl.multiple_of(core * (halo + total_rows), 8), halo)
    far_at = pl.ds(pl.multiple_of((1 - core) * (halo + total_rows), 8), halo)

    def convolve(tile, total):
        lanes = tile_lanes(tile)
        padded[near_at] = near_ref[:, lanes].astype(jnp.float32)
        padded[far_at] = far_ref[:, lanes].astype(jnp.float32)
        padded[own_at] = own_ref[:, lanes].astype(jnp.float32)
        padded[partner_at] = partner_ref[core, :, lanes].astype(jnp.float32)
        own = padded[halo : halo + total_rows]
        padded[...] = padded[...] * live
        acc = jnp.zeros((total_rows, LANES), jnp.float32)
        for tap in range(KERNEL):
            acc = acc + taps_ref[tap : tap + 1, lanes] * padded[
                first + tap : first + tap + total_rows
            ]
        grown = jnp.exp(jnp.minimum(acc, 20.0))
        product = grown * (grown + 2.0)
        value = own + acc * (product / (product + 2.0))
        residual_ref[:, lanes] = value
        return total + value

    total = lax.fori_loop(
        0, tiles, convolve, jnp.zeros((total_rows, LANES), jnp.float32), unroll=3
    )

    def store(lanes, value):
        normed_ref[:, lanes] = value.astype(jnp.bfloat16)

    row_norm(lambda tile: residual_ref[:, tile_lanes(tile)], store, tiles, mod_ref, 0, total)
    for load in loads:
        load.wait()


def project_kernel(firsts, origin, info_ref, normed_ref, weight_ref, cos_ref, sin_ref, *out_refs):
    rows = normed_ref.shape[0]
    attn = weight_ref.shape[1] // 3
    wide = 2 * LANES
    half = HEAD_DIM // 2
    cosine, sine = cos_ref[...], sin_ref[...]
    lower = lax.broadcasted_iota(jnp.int32, (rows, LANES), 1) % HEAD_DIM < half
    chip = info_ref[CHIP] if origin is None else origin
    swap = jnp.full((rows, LANES), chip & 1, jnp.int32) > 0
    for at, apart in enumerate(firsts):
        pair = (chip ^ apart) >> 1
        for part in range(3):
            start = part * attn + pair * wide
            both = jnp.dot(
                normed_ref[...],
                weight_ref[:, pl.ds(pl.multiple_of(start, wide), wide)],
                preferred_element_type=jnp.float32,
            )
            sides = []
            for side in range(2):
                value = both[:, side * LANES : (side + 1) * LANES]
                if part < 2:
                    swapped = jnp.where(
                        lower, pltpu.roll(value, LANES - half, 1), pltpu.roll(value, half, 1)
                    )
                    value = value * cosine + swapped * sine
                if part == 0:
                    value = value * HEAD_DIM**-0.5
                sides.append(value)
            out_refs[2 * at][part] = jnp.where(swap, sides[1], sides[0]).astype(jnp.bfloat16)
            out_refs[2 * at + 1][part] = jnp.where(swap, sides[0], sides[1]).astype(jnp.bfloat16)


def attend_kernel(info_ref, *refs):
    chips = len(refs) - 4
    got_refs, out_ref = refs[:chips], refs[chips]
    keys, values, queries = refs[chips + 1 :]
    _, rows, _ = got_refs[0].shape
    total = chips * rows
    length, chip = info_ref[LENGTH], info_ref[CHIP]
    low = lax.broadcasted_iota(jnp.int32, (rows, LANES), 1) < HEAD_DIM
    lane = lax.broadcasted_iota(jnp.int32, (rows, LANES), 1)
    row = lax.broadcasted_iota(jnp.int32, (rows, LANES), 0)
    zero = jnp.zeros((rows, LANES), jnp.bfloat16)
    queries[:, LANES:] = jnp.where(
        lax.broadcasted_iota(jnp.int32, (2 * total, LANES), 1) == 0, 1.0, 0.0
    ).astype(jnp.bfloat16)
    for apart, got_ref in enumerate(got_refs):
        here = slice(apart * rows, (apart + 1) * rows)
        keys[here, :LANES] = got_ref[1]
        dead = (lane == 0) & (row + (chip ^ apart) * rows >= length)
        keys[here, LANES:] = jnp.where(dead, NEGATIVE, 0.0).astype(jnp.bfloat16)
        values[here, :] = got_ref[2]
        query = got_ref[0]
        at = 2 * apart * rows
        queries[at : at + rows, :LANES] = jnp.where(low, query, zero)
        queries[at + rows : at + 2 * rows, :LANES] = jnp.where(low, zero, query)
    for first in range(0, chips, 2):
        at = 2 * first * rows
        scores = lax.dot_general(
            queries[at : at + 4 * rows, :], keys[...], (((1,), (1,)), ((), ())),
            preferred_element_type=jnp.float32,
        )
        weights = jnp.exp(scores - jnp.max(scores, axis=1, keepdims=True))
        weight_sum = jnp.sum(weights, axis=1, keepdims=True)
        mixed = jnp.dot(
            weights.astype(jnp.bfloat16), values[...], preferred_element_type=jnp.float32
        )
        mixed = mixed / weight_sum
        for side in range(2):
            base = 2 * side * rows
            out_ref[chip ^ (first + side)] = jnp.where(
                low, mixed[base : base + rows], mixed[base + rows : base + 2 * rows]
            ).astype(jnp.bfloat16)


def back_kernel(
    info_ref, got_ref, residual_ref, mod_ref, w_out_ref, w_mel_ref, keep_ref, send_ref, attended,
    after, speed,
):
    rows, width = residual_ref.shape
    tiles = width // LANES
    core = info_ref[CORE]
    for block in range(got_ref.shape[0]):
        attended[:, block * LANES : (block + 1) * LANES] = got_ref[block]
    wide = 2 * LANES
    total = jnp.zeros((rows, LANES), jnp.float32)
    for block in range(width // wide):
        lanes = slice(block * wide, (block + 1) * wide)
        branch = jnp.dot(attended[...], w_out_ref[:, lanes], preferred_element_type=jnp.float32)
        value = residual_ref[:, lanes] + mod_ref[2:3, lanes] * branch
        after[:, lanes] = value
        total = total + value[:, :LANES] + value[:, LANES:]

    def store(lanes, value):
        after[:, lanes] = value

    row_norm(lambda tile: after[:, tile_lanes(tile)], store, tiles, mod_ref, 3, total)
    speed[...] = lax.dot_general(
        after[...].astype(jnp.bfloat16), w_mel_ref[...], (((1,), (1,)), ((), ())),
        preferred_element_type=jnp.float32,
    )
    half = rows // 2
    keep_ref[...] = speed[pl.ds(pl.multiple_of(core * half, 8), half), :]
    send_ref[...] = speed[pl.ds(pl.multiple_of((1 - core) * half, 8), half), :]


def call(kernel, out_shape, inputs, scratch, limit, hbm=()):
    single = not isinstance(out_shape, tuple)
    specs = [hbm_spec() if at in hbm else vmem_spec() for at in range(1, len(inputs))]
    inputs = [
        pltpu.with_memory_space_constraint(value, pltpu.HBM) if at in hbm else value
        for at, value in enumerate(inputs)
    ]
    return pl.pallas_call(
        kernel,
        out_shape=out_shape,
        in_specs=[smem_spec()] + specs,
        out_specs=vmem_spec() if single else tuple(vmem_spec() for _ in out_shape),
        scratch_shapes=scratch,
        compiler_params=pltpu.CompilerParams(vmem_limit_bytes=limit * MIB),
    )(*inputs)


def array(shape, dtype=jnp.float32):
    return jax.ShapeDtypeStruct(shape, dtype)


def project(normed, w_qkv, tables, info, firsts, origin=None):
    shape = array((3, normed.shape[0], LANES), jnp.bfloat16)
    return call(
        functools.partial(project_kernel, tuple(firsts), origin),
        (shape,) * (2 * len(firsts)),
        (info, normed, w_qkv) + tables,
        [],
        8,
    )


def same_core(count):
    return [list(range(core, count, 2)) for core in range(2)]


def across(value, apart, count):
    return lax.ppermute(value, "seq", [(i, i ^ apart) for i in range(count)])


def to_groups(values, subs):
    rows, _ = values.shape
    grouped = values.reshape(subs, rows // subs, HEADS, HEAD_DIM).transpose(2, 0, 1, 3)
    return grouped.reshape(HEADS * subs, rows // subs, HEAD_DIM)


def from_groups(grouped, rows, subs):
    split = grouped.reshape(HEADS, subs, rows // subs, HEAD_DIM).transpose(1, 2, 0, 3)
    return split.reshape(rows, HEADS * HEAD_DIM)


def attend_blocks(queries, keys, values, live):
    groups, total, _ = queries.shape
    block = max(size for size in range(1, min(total, 1024) + 1) if total % size == 0)
    blocks = queries.reshape(groups, total // block, block, HEAD_DIM).transpose(1, 0, 2, 3)
    live = live[None, None, :]

    def one_block(query):
        scores = jnp.einsum("gqd,gkd->gqk", query, keys, preferred_element_type=jnp.float32)
        scores = jnp.where(live, scores, NEGATIVE)
        weights = jnp.exp(scores - jnp.max(scores, axis=-1, keepdims=True))
        weights = jnp.where(live, weights, 0.0)
        mixed = jnp.einsum(
            "gqk,gkd->gqd",
            weights.astype(jnp.bfloat16),
            values,
            preferred_element_type=jnp.float32,
        )
        return (mixed / jnp.sum(weights, axis=-1)[..., None]).astype(jnp.bfloat16)

    return lax.map(one_block, blocks).transpose(1, 0, 2, 3).reshape(groups, total, HEAD_DIM)


def attend_any(normed, w_qkv, tables, info, length, count):
    rows = normed.shape[0]
    chips = count // 2
    groups = HEADS * HEAD_DIM // LANES
    sent = project(normed, w_qkv, tables, info, range(0, groups, 2), 0)
    subs = max(1, chips // HEADS)
    chip = lax.axis_index("seq") >> 1
    part_rows = rows // subs

    def exchange(part):
        whole = jnp.concatenate([group[part] for group in sent], axis=1)
        return lax.all_to_all(
            to_groups(whole, subs), "seq", split_axis=0, concat_axis=1, tiled=True,
            axis_index_groups=same_core(count),
        )

    queries, keys, values = (exchange(part) for part in range(3))

    def frames_of(sub):
        start = jnp.arange(chips, dtype=jnp.int32)[:, None] * rows + sub * part_rows
        return (start + jnp.arange(part_rows, dtype=jnp.int32)[None, :]).reshape(-1)

    frames = [frames_of(chip % subs)]
    parts = [(keys, values)]
    for apart in range(1, subs):
        perm = []
        for i in range(count):
            at = i // 2
            target = at - at % subs + (at + apart) % subs
            perm.append((i, 2 * target + i % 2))
        parts.append(tuple(lax.ppermute(part, "seq", perm) for part in (keys, values)))
        frames.append(frames_of((chip - apart) % subs))
    keys = jnp.concatenate([part[0] for part in parts], axis=1)
    values = jnp.concatenate([part[1] for part in parts], axis=1)
    attended = attend_blocks(queries, keys, values, jnp.concatenate(frames) < length)
    back = lax.all_to_all(
        attended, "seq", split_axis=1, concat_axis=0, tiled=True,
        axis_index_groups=same_core(count),
    )
    return from_groups(back, rows, subs).reshape(rows, groups, LANES).transpose(1, 0, 2)


def chips_hold_groups(count):
    chips = count // 2
    return chips == HEADS * HEAD_DIM // LANES and chips >= 4 and chips & (chips - 1) == 0


def send_order(chips):
    return list(range(chips // 2, chips, 2)) + list(range(2, chips // 2, 2)) + [0]


def attend_chips(normed, w_qkv, tables, info, count):
    rows = normed.shape[0]
    chips = count // 2
    held = {}
    for first in send_order(chips):
        made = project(normed, w_qkv, tables, info, [first])
        for side in range(2):
            apart = first + side
            held[apart] = across(made[side], 2 * apart, count) if apart else made[side]
    total = chips * rows
    attended = call(
        attend_kernel,
        array((chips, rows, LANES), jnp.bfloat16),
        (info,) + tuple(held[apart] for apart in range(chips)),
        [
            VMEM((total, 2 * LANES), jnp.bfloat16),
            VMEM((total, LANES), jnp.bfloat16),
            VMEM((2 * total, 2 * LANES), jnp.bfloat16),
        ],
        24,
    )
    return lax.all_to_all(
        attended, "seq", split_axis=0, concat_axis=0, tiled=True,
        axis_index_groups=same_core(count),
    )


def per_device(
    hidden, latent, lengths, step_index, guidance, modulation, conv_kernel, w_qkv, w_out, w_mel
):
    _, rows, width = hidden.shape
    count = lax.axis_size("seq")
    chips = count // 2
    index = lax.axis_index("seq").astype(jnp.int32)
    chip, core = index >> 1, index & 1
    chip_rows = 2 * rows
    place = jnp.stack([core, chip])

    partner = across(hidden, 1, count)
    near, far = call(
        edge_kernel,
        (array((HALO, width), jnp.bfloat16),) * 2,
        (place, hidden),
        [pltpu.SemaphoreType.DMA((2,))],
        4,
        hbm=(1,),
    )
    steps = range(chips - 1)
    near = lax.ppermute(
        near, "seq",
        [(2 * m + 1, 2 * m + 2) for m in steps] + [(2 * m + 2, 2 * m + 1) for m in steps],
    )
    far = lax.ppermute(
        far, "seq",
        [(2 * m + 1, 2 * m + 3) for m in steps] + [(2 * m + 2, 2 * m) for m in steps],
    )
    own, taps, mods = call(
        stage_kernel,
        (
            array((rows, width), jnp.bfloat16),
            array(conv_kernel.shape),
            array(modulation.shape),
        ),
        (place, hidden, conv_kernel, modulation),
        [pltpu.SemaphoreType.DMA((3,))],
        4,
        hbm=(1, 2, 3),
    )
    info = jnp.stack([core, chip, lengths[0]])
    tables = rotary_tables(chip * chip_rows + jnp.arange(chip_rows, dtype=jnp.int32))
    residual, normed, weight = call(
        front_kernel,
        (
            array((chip_rows, width)),
            array((chip_rows, width), jnp.bfloat16),
            array(w_qkv.shape, jnp.bfloat16),
        ),
        (info, own, partner, near, far, taps, mods, w_qkv),
        [VMEM((chip_rows + 2 * HALO, LANES), jnp.float32), pltpu.SemaphoreType.DMA((8,))],
        8,
        hbm=(7,),
    )
    if chips_hold_groups(count):
        back = attend_chips(normed, weight, tables, info, count)
    else:
        back = attend_any(normed, weight, tables, info, lengths[0], count)
    mels = w_mel.shape[1]
    residual, w_mel = call(
        fetch_kernel,
        (array(residual.shape), array((mels, width), jnp.bfloat16)),
        (place, residual, w_mel.T),
        [pltpu.SemaphoreType.DMA((2,))],
        4,
        hbm=(1, 2),
    )
    keep, send = call(
        back_kernel,
        (array((rows, mels)),) * 2,
        (info, back, residual, mods, w_out, w_mel),
        [
            VMEM((chip_rows, HEADS * HEAD_DIM), jnp.bfloat16),
            VMEM((chip_rows, width), jnp.float32),
            VMEM((chip_rows, mels), jnp.float32),
        ],
        12,
    )
    other = across(send, 1, count)
    first = jnp.where(core == 0, keep, other)
    second = jnp.where(core == 0, other, keep)
    guided = first + guidance[0] * (first - second)
    live = index * rows + jnp.arange(rows, dtype=jnp.int32) < lengths[0]
    velocity = jnp.where(live[:, None], guided, 0.0)
    progress = step_index[0].astype(jnp.float32) / STEPS
    time_now = 1.0 - jnp.cos(0.5 * jnp.pi * progress)
    return (velocity, latent + (1.0 - time_now) * velocity)


def solution(mesh):
    return jax.shard_map(
        per_device,
        mesh=mesh,
        in_specs=(
            P(None, ("clip", "seq"), None),
            P(("clip", "seq"), None),
            P("clip"),
            P(),
            P(),
            P(),
            P(),
            P(),
            P(),
            P(),
        ),
        out_specs=(P(("clip", "seq"), None), P(("clip", "seq"), None)),
        check_vma=False,
    )
```

```python
import functools

import jax
import jax.numpy as jnp
from jax import lax
from jax.experimental import pallas as pl
from jax.experimental.pallas import tpu as pltpu
from jax.sharding import PartitionSpec as P


HEADS = 16
HEAD_DIM = 64
KERNEL = 31
STEPS = 32
LANES = 128
HALO = 16


EPSILON = 1e-06
NEGATIVE = -1e30
CORE, CHIP, LENGTH = 0, 1, 2
VMEM = pltpu.VMEM
SMEM = pltpu.SMEM
MIB = 1 << 20


def vmem_spec():
    return pl.BlockSpec(memory_space=VMEM)


def smem_spec():
    return pl.BlockSpec(memory_space=SMEM)


def rotary_tables(positions):
    half_dim = HEAD_DIM // 2
    lane = jnp.arange(LANES, dtype=jnp.int32)
    inverse = 10000.0 ** (-(lane % half_dim).astype(jnp.float32) / half_dim)
    angles = positions.astype(jnp.float32)[:, None] * inverse[None, :]
    sign = jnp.where(lane % HEAD_DIM < half_dim, -1.0, 1.0)
    return jnp.cos(angles), jnp.sin(angles) * sign[None, :]


def hbm_spec():
    return pl.BlockSpec(memory_space=pltpu.HBM)


def tile_lanes(tile):
    return pl.ds(pl.multiple_of(tile * LANES, LANES), LANES)


def row_norm(load, store, tiles, mod_ref, row, total):
    width = tiles * LANES
    mean = jnp.sum(total, axis=-1, keepdims=True) * (1.0 / width)

    def square(tile, acc):
        centered = load(tile) - mean
        return acc + centered * centered

    squares = lax.fori_loop(0, tiles, square, jnp.zeros(total.shape, jnp.float32), unroll=6)
    variance = jnp.sum(squares, axis=-1, keepdims=True) * (1.0 / width)
    factor = lax.rsqrt(variance + EPSILON)

    def write(tile, carry):
        lanes = tile_lanes(tile)
        scale = 1.0 + mod_ref[row + 1 : row + 2, lanes]
        shift = mod_ref[row : row + 1, lanes]
        store(lanes, (load(tile) - mean) * factor * scale + shift)
        return carry

    lax.fori_loop(0, tiles, write, 0, unroll=6)


def run_copies(pairs, sems):
    copies = [
        pltpu.make_async_copy(source, target, sems.at[at])
        for at, (source, target) in enumerate(pairs)
    ]
    for copy in copies:
        copy.start()
    for copy in copies:
        copy.wait()


def stage_kernel(info_ref, hidden_hbm, taps_hbm, mod_hbm, own_ref, taps_ref, mod_ref, sems):
    run_copies(
        [
            (hidden_hbm.at[info_ref[CORE]], own_ref),
            (taps_hbm, taps_ref),
            (mod_hbm, mod_ref),
        ],
        sems,
    )


def front_kernel(
    info_ref, own_ref, partner_ref, near_ref, far_ref, taps_ref, mod_ref, weight_hbm,
    residual_ref, normed_ref, weight_ref, padded, sems,
):
    rows, width = own_ref.shape
    halo = near_ref.shape[0]
    total_rows = 2 * rows
    tiles = width // LANES
    parts = 8
    depth = width // parts
    loads = []
    for part in range(parts):
        here = pl.ds(part * depth, depth)
        loads.append(
            pltpu.make_async_copy(weight_hbm.at[here], weight_ref.at[here], sems.at[part])
        )
    for load in loads:
        load.start()
    length, core = info_ref[LENGTH], info_ref[CORE]
    offset = info_ref[CHIP] * total_rows
    span = total_rows + 2 * halo
    frame = offset - halo + lax.broadcasted_iota(jnp.int32, (span, LANES), 0)
    live = (frame < length).astype(jnp.float32)
    first = halo - KERNEL // 2
    own_at = pl.ds(pl.multiple_of(halo + core * rows, 8), rows)
    partner_at = pl.ds(pl.multiple_of(halo + (1 - core) * rows, 8), rows)
    near_at = pl.ds(pl.multiple_of(core * (halo + total_rows), 8), halo)
    far_at = pl.ds(pl.multiple_of((1 - core) * (halo + total_rows), 8), halo)

    def convolve(tile, total):
        lanes = tile_lanes(tile)
        padded[near_at] = near_ref[:, lanes].astype(jnp.float32)
        padded[far_at] = far_ref[:, lanes].astype(jnp.float32)
        padded[own_at] = own_ref[:, lanes].astype(jnp.float32)
        padded[partner_at] = partner_ref[core, :, lanes].astype(jnp.float32)
        own = padded[halo : halo + total_rows]
        padded[...] = padded[...] * live
        acc = jnp.zeros((total_rows, LANES), jnp.float32)
        for tap in range(KERNEL):
            acc = acc + taps_ref[tap : tap + 1, lanes] * padded[
                first + tap : first + tap + total_rows
            ]
        grown = jnp.exp(jnp.minimum(acc, 20.0))
        product = grown * (grown + 2.0)
        value = own + acc * (product / (product + 2.0))
        residual_ref[:, lanes] = value
        return total + value

    total = lax.fori_loop(
        0, tiles, convolve, jnp.zeros((total_rows, LANES), jnp.float32), unroll=3
    )

    def store(lanes, value):
        normed_ref[:, lanes] = value.astype(jnp.bfloat16)

    row_norm(lambda tile: residual_ref[:, tile_lanes(tile)], store, tiles, mod_ref, 0, total)
    for load in loads:
        load.wait()


def project_kernel(firsts, origin, info_ref, normed_ref, weight_ref, cos_ref, sin_ref, *out_refs):
    rows = normed_ref.shape[0]
    attn = weight_ref.shape[1] // 3
    wide = 2 * LANES
    half = HEAD_DIM // 2
    cosine, sine = cos_ref[...], sin_ref[...]
    lower = lax.broadcasted_iota(jnp.int32, (rows, LANES), 1) % HEAD_DIM < half
    chip = info_ref[CHIP] if origin is None else origin
    swap = jnp.full((rows, LANES), chip & 1, jnp.int32) > 0
    for at, apart in enumerate(firsts):
        pair = (chip ^ apart) >> 1
        for part in range(3):
            start = part * attn + pair * wide
            both = jnp.dot(
                normed_ref[...],
                weight_ref[:, pl.ds(pl.multiple_of(start, wide), wide)],
                preferred_element_type=jnp.float32,
            )
            sides = []
            for side in range(2):
                value = both[:, side * LANES : (side + 1) * LANES]
                if part < 2:
                    swapped = jnp.where(
                        lower, pltpu.roll(value, LANES - half, 1), pltpu.roll(value, half, 1)
                    )
                    value = value * cosine + swapped * sine
                if part == 0:
                    value = value * HEAD_DIM**-0.5
                sides.append(value)
            out_refs[2 * at][part] = jnp.where(swap, sides[1], sides[0]).astype(jnp.bfloat16)
            out_refs[2 * at + 1][part] = jnp.where(swap, sides[0], sides[1]).astype(jnp.bfloat16)


def gather_keys(info_ref, got_refs, keys, values):
    _, rows, _ = got_refs[0].shape
    length, chip = info_ref[LENGTH], info_ref[CHIP]
    lane = lax.broadcasted_iota(jnp.int32, (rows, LANES), 1)
    row = lax.broadcasted_iota(jnp.int32, (rows, LANES), 0)
    for apart, got_ref in enumerate(got_refs):
        here = slice(apart * rows, (apart + 1) * rows)
        keys[here, :LANES] = got_ref[1]
        dead = (lane == 0) & (row + (chip ^ apart) * rows >= length)
        keys[here, LANES:] = jnp.where(dead, NEGATIVE, 0.0).astype(jnp.bfloat16)
        values[here, :] = got_ref[2]


def attend_rows(query_refs, keys, values, out_ref, queries):
    _, rows, _ = query_refs[0].shape
    low = lax.broadcasted_iota(jnp.int32, (rows, LANES), 1) < HEAD_DIM
    zero = jnp.zeros((rows, LANES), jnp.bfloat16)
    queries[:, LANES:] = jnp.where(
        lax.broadcasted_iota(jnp.int32, (queries.shape[0], LANES), 1) == 0, 1.0, 0.0
    ).astype(jnp.bfloat16)
    for at, query_ref in enumerate(query_refs):
        query = query_ref[0]
        base = 2 * at * rows
        queries[base : base + rows, :LANES] = jnp.where(low, query, zero)
        queries[base + rows : base + 2 * rows, :LANES] = jnp.where(low, zero, query)
    for first in range(0, len(query_refs), 2):
        base = 2 * first * rows
        scores = lax.dot_general(
            queries[base : base + 4 * rows, :], keys[...], (((1,), (1,)), ((), ())),
            preferred_element_type=jnp.float32,
        )
        weights = jnp.exp(scores - jnp.max(scores, axis=1, keepdims=True))
        weight_sum = jnp.sum(weights, axis=1, keepdims=True)
        mixed = jnp.dot(
            weights.astype(jnp.bfloat16), values[...], preferred_element_type=jnp.float32
        )
        mixed = mixed / weight_sum
        for side in range(2):
            base = 2 * side * rows
            out_ref[first + side] = jnp.where(
                low, mixed[base : base + rows], mixed[base + rows : base + 2 * rows]
            ).astype(jnp.bfloat16)


def attend_first_kernel(info_ref, *refs):
    chips = len(refs) - 4
    got_refs = refs[:chips]
    out_ref, keys, values, queries = refs[chips:]
    gather_keys(info_ref, got_refs, keys, values)
    attend_rows(got_refs[1::2], keys, values, out_ref, queries)


def attend_second_kernel(info_ref, keys, values, *refs):
    del info_ref
    attend_rows(refs[:-2], keys, values, refs[-2], refs[-1])


def merge_kernel(info_ref, own_ref, got_ref, *out_refs):
    del info_ref
    for at, out_ref in enumerate(out_refs):
        out_ref[0] = own_ref[at + 1]
        out_ref[1] = got_ref[at + 1]


def back_kernel(blocks, info_ref, residual_hbm, w_mel_hbm, mod_ref, w_out_ref, *refs):
    count = 1 + max(at for at, _, _ in blocks)
    got_refs = refs[:count]
    keep_ref, send_ref, attended, after, speed, residual, w_mel, sems = refs[count:]
    rows, width = residual.shape
    tiles = width // LANES
    core, chip = info_ref[CORE], info_ref[CHIP]
    loads = [
        pltpu.make_async_copy(residual_hbm, residual, sems.at[0]),
        pltpu.make_async_copy(w_mel_hbm, w_mel, sems.at[1]),
    ]
    for load in loads:
        load.start()
    for at, place, apart in blocks:
        group = place if apart is None else chip ^ apart
        attended[:, tile_lanes(group)] = got_refs[at][place]
    wide = 2 * LANES
    for block in range(width // wide):
        lanes = slice(block * wide, (block + 1) * wide)
        branch = jnp.dot(attended[...], w_out_ref[:, lanes], preferred_element_type=jnp.float32)
        after[:, lanes] = mod_ref[2:3, lanes] * branch
    loads[0].wait()

    def join(tile, total):
        lanes = tile_lanes(tile)
        value = residual[:, lanes] + after[:, lanes]
        after[:, lanes] = value
        return total + value

    total = lax.fori_loop(0, tiles, join, jnp.zeros((rows, LANES), jnp.float32), unroll=6)

    def store(lanes, value):
        after[:, lanes] = value

    row_norm(lambda tile: after[:, tile_lanes(tile)], store, tiles, mod_ref, 3, total)
    loads[1].wait()
    speed[...] = lax.dot_general(
        after[...].astype(jnp.bfloat16), w_mel[...], (((1,), (1,)), ((), ())),
        preferred_element_type=jnp.float32,
    )
    half = rows // 2
    keep_ref[...] = speed[pl.ds(pl.multiple_of(core * half, 8), half), :]
    send_ref[...] = speed[pl.ds(pl.multiple_of((1 - core) * half, 8), half), :]


def call(kernel, out_shape, inputs, scratch, limit, hbm=()):
    single = not isinstance(out_shape, tuple)
    specs = [hbm_spec() if at in hbm else vmem_spec() for at in range(1, len(inputs))]
    inputs = list(inputs)
    for at in hbm:
        inputs[at] = pltpu.with_memory_space_constraint(inputs[at], pltpu.HBM)
    return pl.pallas_call(
        kernel,
        out_shape=out_shape,
        in_specs=[smem_spec()] + specs,
        out_specs=vmem_spec() if single else tuple(vmem_spec() for _ in out_shape),
        scratch_shapes=scratch,
        compiler_params=pltpu.CompilerParams(vmem_limit_bytes=limit * MIB),
    )(*inputs)


def array(shape, dtype=jnp.float32):
    return jax.ShapeDtypeStruct(shape, dtype)


def project(normed, w_qkv, tables, info, firsts, origin=None):
    shape = array((3, normed.shape[0], LANES), jnp.bfloat16)
    return call(
        functools.partial(project_kernel, tuple(firsts), origin),
        (shape,) * (2 * len(firsts)),
        (info, normed, w_qkv) + tables,
        [],
        8,
    )


def same_core(count):
    return [list(range(core, count, 2)) for core in range(2)]


def across(value, apart, count):
    return lax.ppermute(value, "seq", [(i, i ^ apart) for i in range(count)])


def to_groups(values, subs):
    rows, _ = values.shape
    grouped = values.reshape(subs, rows // subs, HEADS, HEAD_DIM).transpose(2, 0, 1, 3)
    return grouped.reshape(HEADS * subs, rows // subs, HEAD_DIM)


def from_groups(grouped, rows, subs):
    split = grouped.reshape(HEADS, subs, rows // subs, HEAD_DIM).transpose(1, 2, 0, 3)
    return split.reshape(rows, HEADS * HEAD_DIM)


def attend_blocks(queries, keys, values, live):
    groups, total, _ = queries.shape
    block = max(size for size in range(1, min(total, 1024) + 1) if total % size == 0)
    blocks = queries.reshape(groups, total // block, block, HEAD_DIM).transpose(1, 0, 2, 3)
    live = live[None, None, :]

    def one_block(query):
        scores = jnp.einsum("gqd,gkd->gqk", query, keys, preferred_element_type=jnp.float32)
        scores = jnp.where(live, scores, NEGATIVE)
        weights = jnp.exp(scores - jnp.max(scores, axis=-1, keepdims=True))
        weights = jnp.where(live, weights, 0.0)
        mixed = jnp.einsum(
            "gqk,gkd->gqd",
            weights.astype(jnp.bfloat16),
            values,
            preferred_element_type=jnp.float32,
        )
        return (mixed / jnp.sum(weights, axis=-1)[..., None]).astype(jnp.bfloat16)

    return lax.map(one_block, blocks).transpose(1, 0, 2, 3).reshape(groups, total, HEAD_DIM)


def attend_any(normed, w_qkv, tables, info, length, count):
    rows = normed.shape[0]
    chips = count // 2
    groups = HEADS * HEAD_DIM // LANES
    sent = project(normed, w_qkv, tables, info, range(0, groups, 2), 0)
    subs = max(1, chips // HEADS)
    chip = lax.axis_index("seq") >> 1
    part_rows = rows // subs

    def exchange(part):
        whole = jnp.concatenate([group[part] for group in sent], axis=1)
        return lax.all_to_all(
            to_groups(whole, subs), "seq", split_axis=0, concat_axis=1, tiled=True,
            axis_index_groups=same_core(count),
        )

    queries, keys, values = (exchange(part) for part in range(3))

    def frames_of(sub):
        start = jnp.arange(chips, dtype=jnp.int32)[:, None] * rows + sub * part_rows
        return (start + jnp.arange(part_rows, dtype=jnp.int32)[None, :]).reshape(-1)

    frames = [frames_of(chip % subs)]
    parts = [(keys, values)]
    for apart in range(1, subs):
        perm = []
        for i in range(count):
            at = i // 2
            target = at - at % subs + (at + apart) % subs
            perm.append((i, 2 * target + i % 2))
        parts.append(tuple(lax.ppermute(part, "seq", perm) for part in (keys, values)))
        frames.append(frames_of((chip - apart) % subs))
    keys = jnp.concatenate([part[0] for part in parts], axis=1)
    values = jnp.concatenate([part[1] for part in parts], axis=1)
    attended = attend_blocks(queries, keys, values, jnp.concatenate(frames) < length)
    back = lax.all_to_all(
        attended, "seq", split_axis=1, concat_axis=0, tiled=True,
        axis_index_groups=same_core(count),
    )
    return from_groups(back, rows, subs).reshape(rows, groups, LANES).transpose(1, 0, 2)


def chips_hold_groups(count):
    chips = count // 2
    return chips == HEADS * HEAD_DIM // LANES and chips >= 4 and chips & (chips - 1) == 0


def send_order(chips):
    return list(range(chips // 2, chips, 2)) + list(range(2, chips // 2, 2)) + [0]


def attend_chips(normed, w_qkv, tables, info, count):
    rows = normed.shape[0]
    chips = count // 2
    held = {}
    for first in send_order(chips):
        made = project(normed, w_qkv, tables, info, [first])
        for side in range(2):
            apart = first + side
            held[apart] = across(made[side], 2 * apart, count) if apart else made[side]
    total, half = chips * rows, chips // 2
    queries = VMEM((total, 2 * LANES), jnp.bfloat16)
    crossing, keys, values = call(
        attend_first_kernel,
        (
            array((half, rows, LANES), jnp.bfloat16),
            array((total, 2 * LANES), jnp.bfloat16),
            array((total, LANES), jnp.bfloat16),
        ),
        (info,) + tuple(held[apart] for apart in range(chips)),
        [queries],
        16,
    )
    crossed = across(crossing, 2, count)
    staying = call(
        attend_second_kernel,
        array((half, rows, LANES), jnp.bfloat16),
        (info, keys, values) + tuple(held[apart] for apart in range(0, chips, 2)),
        [queries],
        16,
    )
    joined = call(
        merge_kernel,
        (array((2, rows, LANES), jnp.bfloat16),) * (half - 1),
        (info, staying, crossed),
        [],
        4,
    )
    back, blocks = [staying, crossed], [(0, 0, 0), (1, 0, 1)]
    apart_first = sorted(range(1, half), reverse=True)
    got = {apart: across(joined[apart - 1], 4 * apart, count) for apart in apart_first}
    for apart in range(1, half):
        blocks += [(len(back), side, 2 * apart + side) for side in range(2)]
        back.append(got[apart])
    return back, blocks


def per_device(
    hidden, latent, lengths, step_index, guidance, modulation, conv_kernel, w_qkv, w_out, w_mel
):
    _, rows, width = hidden.shape
    count = lax.axis_size("seq")
    chips = count // 2
    index = lax.axis_index("seq").astype(jnp.int32)
    chip, core = index >> 1, index & 1
    chip_rows = 2 * rows
    place = jnp.stack([core, chip])

    partner = across(hidden, 1, count)
    edge = core * (rows - HALO)
    near = lax.dynamic_slice(hidden, (1 - core, edge, 0), (1, HALO, width))[0]
    far = lax.dynamic_slice(hidden, (core, edge, 0), (1, HALO, width))[0]
    steps = range(chips - 1)
    near = lax.ppermute(
        near, "seq",
        [(2 * m + 1, 2 * m + 2) for m in steps] + [(2 * m + 2, 2 * m + 1) for m in steps],
    )
    far = lax.ppermute(
        far, "seq",
        [(2 * m + 1, 2 * m + 3) for m in steps] + [(2 * m + 2, 2 * m) for m in steps],
    )
    own, taps, mods = call(
        stage_kernel,
        (
            array((rows, width), jnp.bfloat16),
            array(conv_kernel.shape),
            array(modulation.shape),
        ),
        (place, hidden, conv_kernel, modulation),
        [pltpu.SemaphoreType.DMA((3,))],
        4,
        hbm=(1, 2, 3),
    )
    info = jnp.stack([core, chip, lengths[0]])
    tables = rotary_tables(chip * chip_rows + jnp.arange(chip_rows, dtype=jnp.int32))
    residual, normed, weight = call(
        front_kernel,
        (
            array((chip_rows, width)),
            array((chip_rows, width), jnp.bfloat16),
            array(w_qkv.shape, jnp.bfloat16),
        ),
        (info, own, partner, near, far, taps, mods, w_qkv),
        [VMEM((chip_rows + 2 * HALO, LANES), jnp.float32), pltpu.SemaphoreType.DMA((8,))],
        8,
        hbm=(7,),
    )
    if chips_hold_groups(count):
        back, blocks = attend_chips(normed, weight, tables, info, count)
    else:
        back = [attend_any(normed, weight, tables, info, lengths[0], count)]
        blocks = [(0, group, None) for group in range(back[0].shape[0])]
    mels = w_mel.shape[1]
    keep, send = call(
        functools.partial(back_kernel, tuple(blocks)),
        (array((rows, mels)),) * 2,
        (info, residual, w_mel.T, mods, w_out) + tuple(back),
        [
            VMEM((chip_rows, HEADS * HEAD_DIM), jnp.bfloat16),
            VMEM((chip_rows, width), jnp.float32),
            VMEM((chip_rows, mels), jnp.float32),
            VMEM((chip_rows, width), jnp.float32),
            VMEM((mels, width), jnp.bfloat16),
            pltpu.SemaphoreType.DMA((2,)),
        ],
        12,
        hbm=(1, 2),
    )
    other = across(send, 1, count)
    first = jnp.where(core == 0, keep, other)
    second = jnp.where(core == 0, other, keep)
    guided = first + guidance[0] * (first - second)
    live = index * rows + jnp.arange(rows, dtype=jnp.int32) < lengths[0]
    velocity = jnp.where(live[:, None], guided, 0.0)
    progress = step_index[0].astype(jnp.float32) / STEPS
    time_now = 1.0 - jnp.cos(0.5 * jnp.pi * progress)
    return (velocity, latent + (1.0 - time_now) * velocity)


def solution(mesh):
    return jax.shard_map(
        per_device,
        mesh=mesh,
        in_specs=(
            P(None, ("clip", "seq"), None),
            P(("clip", "seq"), None),
            P("clip"),
            P(),
            P(),
            P(),
            P(),
            P(),
            P(),
            P(),
        ),
        out_specs=(P(("clip", "seq"), None), P(("clip", "seq"), None)),
        check_vma=False,
    )
```

```python
import functools

import jax
import jax.numpy as jnp
from jax import lax
from jax.experimental import pallas as pl
from jax.experimental.pallas import tpu as pltpu
from jax.sharding import PartitionSpec as P


HEADS = 16
HEAD_DIM = 64
KERNEL = 31
STEPS = 32
LANES = 128
HALO = 16


EPSILON = 1e-06
NEGATIVE = -1e30
CORE, CHIP, LENGTH = 0, 1, 2
VMEM = pltpu.VMEM
SMEM = pltpu.SMEM
MIB = 1 << 20


def vmem_spec():
    return pl.BlockSpec(memory_space=VMEM)


def smem_spec():
    return pl.BlockSpec(memory_space=SMEM)


def rotary_tables(positions):
    half_dim = HEAD_DIM // 2
    lane = jnp.arange(LANES, dtype=jnp.int32)
    inverse = 10000.0 ** (-(lane % half_dim).astype(jnp.float32) / half_dim)
    angles = positions.astype(jnp.float32)[:, None] * inverse[None, :]
    sign = jnp.where(lane % HEAD_DIM < half_dim, -1.0, 1.0)
    return jnp.cos(angles), jnp.sin(angles) * sign[None, :]


def hbm_spec():
    return pl.BlockSpec(memory_space=pltpu.HBM)


def tile_lanes(tile):
    return pl.ds(pl.multiple_of(tile * LANES, LANES), LANES)


def row_norm(load, store, tiles, mod_ref, row, total):
    width = tiles * LANES
    mean = jnp.sum(total, axis=-1, keepdims=True) * (1.0 / width)

    def square(tile, acc):
        centered = load(tile) - mean
        return acc + centered * centered

    squares = lax.fori_loop(0, tiles, square, jnp.zeros(total.shape, jnp.float32), unroll=6)
    variance = jnp.sum(squares, axis=-1, keepdims=True) * (1.0 / width)
    factor = lax.rsqrt(variance + EPSILON)

    def write(tile, carry):
        lanes = tile_lanes(tile)
        scale = 1.0 + mod_ref[row + 1 : row + 2, lanes]
        shift = mod_ref[row : row + 1, lanes]
        store(lanes, (load(tile) - mean) * factor * scale + shift)
        return carry

    lax.fori_loop(0, tiles, write, 0, unroll=6)


def run_copies(pairs, sems):
    copies = [
        pltpu.make_async_copy(source, target, sems.at[at])
        for at, (source, target) in enumerate(pairs)
    ]
    for copy in copies:
        copy.start()
    for copy in copies:
        copy.wait()


def stage_kernel(info_ref, hidden_hbm, taps_hbm, mod_hbm, own_ref, taps_ref, mod_ref, sems):
    run_copies(
        [
            (hidden_hbm.at[info_ref[CORE]], own_ref),
            (taps_hbm, taps_ref),
            (mod_hbm, mod_ref),
        ],
        sems,
    )


def front_kernel(
    info_ref, own_ref, partner_ref, near_ref, far_ref, taps_ref, mod_ref, weight_hbm,
    residual_ref, normed_ref, weight_ref, padded, sems,
):
    rows, width = own_ref.shape
    halo = near_ref.shape[0]
    total_rows = 2 * rows
    tiles = width // LANES
    parts = 8
    depth = width // parts
    loads = []
    for part in range(parts):
        here = pl.ds(part * depth, depth)
        loads.append(
            pltpu.make_async_copy(weight_hbm.at[here], weight_ref.at[here], sems.at[part])
        )
    for load in loads:
        load.start()
    length, core = info_ref[LENGTH], info_ref[CORE]
    offset = info_ref[CHIP] * total_rows
    span = total_rows + 2 * halo
    frame = offset - halo + lax.broadcasted_iota(jnp.int32, (span, LANES), 0)
    live = (frame < length).astype(jnp.float32)
    first = halo - KERNEL // 2
    own_at = pl.ds(pl.multiple_of(halo + core * rows, 8), rows)
    partner_at = pl.ds(pl.multiple_of(halo + (1 - core) * rows, 8), rows)
    near_at = pl.ds(pl.multiple_of(core * (halo + total_rows), 8), halo)
    far_at = pl.ds(pl.multiple_of((1 - core) * (halo + total_rows), 8), halo)

    def convolve(tile, total):
        lanes = tile_lanes(tile)
        padded[near_at] = near_ref[:, lanes].astype(jnp.float32)
        padded[far_at] = far_ref[:, lanes].astype(jnp.float32)
        padded[own_at] = own_ref[:, lanes].astype(jnp.float32)
        padded[partner_at] = partner_ref[core, :, lanes].astype(jnp.float32)
        own = padded[halo : halo + total_rows]
        padded[...] = padded[...] * live
        acc = jnp.zeros((total_rows, LANES), jnp.float32)
        for tap in range(KERNEL):
            acc = acc + taps_ref[tap : tap + 1, lanes] * padded[
                first + tap : first + tap + total_rows
            ]
        grown = jnp.exp(jnp.minimum(acc, 20.0))
        product = grown * (grown + 2.0)
        value = own + acc * (product / (product + 2.0))
        residual_ref[:, lanes] = value
        return total + value

    total = lax.fori_loop(
        0, tiles, convolve, jnp.zeros((total_rows, LANES), jnp.float32), unroll=3
    )

    def store(lanes, value):
        normed_ref[:, lanes] = value.astype(jnp.bfloat16)

    row_norm(lambda tile: residual_ref[:, tile_lanes(tile)], store, tiles, mod_ref, 0, total)
    for load in loads:
        load.wait()


def project_kernel(firsts, origin, info_ref, normed_ref, weight_ref, cos_ref, sin_ref, *out_refs):
    rows = normed_ref.shape[0]
    attn = weight_ref.shape[1] // 3
    wide = 2 * LANES
    half = HEAD_DIM // 2
    cosine, sine = cos_ref[...], sin_ref[...]
    lower = lax.broadcasted_iota(jnp.int32, (rows, LANES), 1) % HEAD_DIM < half
    chip = info_ref[CHIP] if origin is None else origin
    swap = jnp.full((rows, LANES), chip & 1, jnp.int32) > 0
    for at, apart in enumerate(firsts):
        pair = (chip ^ apart) >> 1
        for part in range(3):
            start = part * attn + pair * wide
            both = jnp.dot(
                normed_ref[...],
                weight_ref[:, pl.ds(pl.multiple_of(start, wide), wide)],
                preferred_element_type=jnp.float32,
            )
            sides = []
            for side in range(2):
                value = both[:, side * LANES : (side + 1) * LANES]
                if part < 2:
                    swapped = jnp.where(
                        lower, pltpu.roll(value, LANES - half, 1), pltpu.roll(value, half, 1)
                    )
                    value = value * cosine + swapped * sine
                if part == 0:
                    value = value * HEAD_DIM**-0.5
                sides.append(value)
            out_refs[2 * at][part] = jnp.where(swap, sides[1], sides[0]).astype(jnp.bfloat16)
            out_refs[2 * at + 1][part] = jnp.where(swap, sides[0], sides[1]).astype(jnp.bfloat16)


def gather_keys(info_ref, got_refs, keys, values):
    _, rows, _ = got_refs[0].shape
    length, chip = info_ref[LENGTH], info_ref[CHIP]
    lane = lax.broadcasted_iota(jnp.int32, (rows, LANES), 1)
    row = lax.broadcasted_iota(jnp.int32, (rows, LANES), 0)
    for apart, got_ref in enumerate(got_refs):
        here = slice(apart * rows, (apart + 1) * rows)
        keys[here, :LANES] = got_ref[1]
        dead = (lane == 0) & (row + (chip ^ apart) * rows >= length)
        keys[here, LANES:] = jnp.where(dead, NEGATIVE, 0.0).astype(jnp.bfloat16)
        values[here, :] = got_ref[2]


def attend_rows(query_refs, keys, values, out_ref, queries, chip):
    _, rows, _ = query_refs[0].shape
    low = lax.broadcasted_iota(jnp.int32, (rows, LANES), 1) < HEAD_DIM
    zero = jnp.zeros((rows, LANES), jnp.bfloat16)
    queries[:, LANES:] = jnp.where(
        lax.broadcasted_iota(jnp.int32, (queries.shape[0], LANES), 1) == 0, 1.0, 0.0
    ).astype(jnp.bfloat16)
    for at, query_ref in enumerate(query_refs):
        query = query_ref[0]
        base = 2 * at * rows
        queries[base : base + rows, :LANES] = jnp.where(low, query, zero)
        queries[base + rows : base + 2 * rows, :LANES] = jnp.where(low, zero, query)
    for first in range(0, len(query_refs), 2):
        base = 2 * first * rows
        scores = lax.dot_general(
            queries[base : base + 4 * rows, :], keys[...], (((1,), (1,)), ((), ())),
            preferred_element_type=jnp.float32,
        )
        weights = jnp.exp(scores - jnp.max(scores, axis=1, keepdims=True))
        weight_sum = jnp.sum(weights, axis=1, keepdims=True)
        mixed = jnp.dot(
            weights.astype(jnp.bfloat16), values[...], preferred_element_type=jnp.float32
        )
        mixed = mixed / weight_sum
        for side in range(2):
            base = 2 * side * rows
            out_ref[chip ^ (first + side)] = jnp.where(
                low, mixed[base : base + rows], mixed[base + rows : base + 2 * rows]
            ).astype(jnp.bfloat16)


def attend_kernel(info_ref, *refs):
    chips = len(refs) - 4
    got_refs = refs[:chips]
    out_ref, keys, values, queries = refs[chips:]
    gather_keys(info_ref, got_refs, keys, values)
    attend_rows(got_refs, keys, values, out_ref, queries, info_ref[CHIP])


def back_kernel(
    info_ref, residual_hbm, w_mel_hbm, mod_ref, w_out_ref, got_ref, keep_ref, send_ref, attended,
    after, speed, residual, w_mel, sems,
):
    rows, width = residual.shape
    tiles = width // LANES
    core = info_ref[CORE]
    loads = [
        pltpu.make_async_copy(residual_hbm, residual, sems.at[0]),
        pltpu.make_async_copy(w_mel_hbm, w_mel, sems.at[1]),
    ]
    for load in loads:
        load.start()
    for group in range(got_ref.shape[0]):
        attended[:, group * LANES : (group + 1) * LANES] = got_ref[group]
    wide = 2 * LANES
    for block in range(width // wide):
        lanes = slice(block * wide, (block + 1) * wide)
        branch = jnp.dot(attended[...], w_out_ref[:, lanes], preferred_element_type=jnp.float32)
        after[:, lanes] = mod_ref[2:3, lanes] * branch
    loads[0].wait()

    def join(tile, total):
        lanes = tile_lanes(tile)
        value = residual[:, lanes] + after[:, lanes]
        after[:, lanes] = value
        return total + value

    total = lax.fori_loop(0, tiles, join, jnp.zeros((rows, LANES), jnp.float32), unroll=6)

    def store(lanes, value):
        after[:, lanes] = value

    row_norm(lambda tile: after[:, tile_lanes(tile)], store, tiles, mod_ref, 3, total)
    loads[1].wait()
    speed[...] = lax.dot_general(
        after[...].astype(jnp.bfloat16), w_mel[...], (((1,), (1,)), ((), ())),
        preferred_element_type=jnp.float32,
    )
    half = rows // 2
    keep_ref[...] = speed[pl.ds(pl.multiple_of(core * half, 8), half), :]
    send_ref[...] = speed[pl.ds(pl.multiple_of((1 - core) * half, 8), half), :]


def call(kernel, out_shape, inputs, scratch, limit, hbm=()):
    single = not isinstance(out_shape, tuple)
    specs = [hbm_spec() if at in hbm else vmem_spec() for at in range(1, len(inputs))]
    inputs = list(inputs)
    for at in hbm:
        inputs[at] = pltpu.with_memory_space_constraint(inputs[at], pltpu.HBM)
    return pl.pallas_call(
        kernel,
        out_shape=out_shape,
        in_specs=[smem_spec()] + specs,
        out_specs=vmem_spec() if single else tuple(vmem_spec() for _ in out_shape),
        scratch_shapes=scratch,
        compiler_params=pltpu.CompilerParams(vmem_limit_bytes=limit * MIB),
    )(*inputs)


def array(shape, dtype=jnp.float32):
    return jax.ShapeDtypeStruct(shape, dtype)


def project(normed, w_qkv, tables, info, firsts, origin=None):
    shape = array((3, normed.shape[0], LANES), jnp.bfloat16)
    return call(
        functools.partial(project_kernel, tuple(firsts), origin),
        (shape,) * (2 * len(firsts)),
        (info, normed, w_qkv) + tables,
        [],
        8,
    )


def same_core(count):
    return [list(range(core, count, 2)) for core in range(2)]


def across(value, apart, count):
    return lax.ppermute(value, "seq", [(i, i ^ apart) for i in range(count)])


def to_groups(values, subs):
    rows, _ = values.shape
    grouped = values.reshape(subs, rows // subs, HEADS, HEAD_DIM).transpose(2, 0, 1, 3)
    return grouped.reshape(HEADS * subs, rows // subs, HEAD_DIM)


def from_groups(grouped, rows, subs):
    split = grouped.reshape(HEADS, subs, rows // subs, HEAD_DIM).transpose(1, 2, 0, 3)
    return split.reshape(rows, HEADS * HEAD_DIM)


def attend_blocks(queries, keys, values, live):
    groups, total, _ = queries.shape
    block = max(size for size in range(1, min(total, 1024) + 1) if total % size == 0)
    blocks = queries.reshape(groups, total // block, block, HEAD_DIM).transpose(1, 0, 2, 3)
    live = live[None, None, :]

    def one_block(query):
        scores = jnp.einsum("gqd,gkd->gqk", query, keys, preferred_element_type=jnp.float32)
        scores = jnp.where(live, scores, NEGATIVE)
        weights = jnp.exp(scores - jnp.max(scores, axis=-1, keepdims=True))
        weights = jnp.where(live, weights, 0.0)
        mixed = jnp.einsum(
            "gqk,gkd->gqd",
            weights.astype(jnp.bfloat16),
            values,
            preferred_element_type=jnp.float32,
        )
        return (mixed / jnp.sum(weights, axis=-1)[..., None]).astype(jnp.bfloat16)

    return lax.map(one_block, blocks).transpose(1, 0, 2, 3).reshape(groups, total, HEAD_DIM)


def attend_any(normed, w_qkv, tables, info, length, count):
    rows = normed.shape[0]
    chips = count // 2
    groups = HEADS * HEAD_DIM // LANES
    sent = project(normed, w_qkv, tables, info, range(0, groups, 2), 0)
    subs = max(1, chips // HEADS)
    chip = lax.axis_index("seq") >> 1
    part_rows = rows // subs

    def exchange(part):
        whole = jnp.concatenate([group[part] for group in sent], axis=1)
        return lax.all_to_all(
            to_groups(whole, subs), "seq", split_axis=0, concat_axis=1, tiled=True,
            axis_index_groups=same_core(count),
        )

    queries, keys, values = (exchange(part) for part in range(3))

    def frames_of(sub):
        start = jnp.arange(chips, dtype=jnp.int32)[:, None] * rows + sub * part_rows
        return (start + jnp.arange(part_rows, dtype=jnp.int32)[None, :]).reshape(-1)

    frames = [frames_of(chip % subs)]
    parts = [(keys, values)]
    for apart in range(1, subs):
        perm = []
        for i in range(count):
            at = i // 2
            target = at - at % subs + (at + apart) % subs
            perm.append((i, 2 * target + i % 2))
        parts.append(tuple(lax.ppermute(part, "seq", perm) for part in (keys, values)))
        frames.append(frames_of((chip - apart) % subs))
    keys = jnp.concatenate([part[0] for part in parts], axis=1)
    values = jnp.concatenate([part[1] for part in parts], axis=1)
    attended = attend_blocks(queries, keys, values, jnp.concatenate(frames) < length)
    back = lax.all_to_all(
        attended, "seq", split_axis=1, concat_axis=0, tiled=True,
        axis_index_groups=same_core(count),
    )
    return from_groups(back, rows, subs).reshape(rows, groups, LANES).transpose(1, 0, 2)


def chips_hold_groups(count):
    chips = count // 2
    return chips == HEADS * HEAD_DIM // LANES and chips >= 4 and chips & (chips - 1) == 0


def send_order(chips):
    return list(range(chips // 2, chips, 2)) + list(range(2, chips // 2, 2)) + [0]


def attend_chips(normed, w_qkv, tables, info, count):
    rows = normed.shape[0]
    chips = count // 2
    held = {}
    for first in send_order(chips):
        made = project(normed, w_qkv, tables, info, [first])
        for side in range(2):
            apart = first + side
            held[apart] = across(made[side], 2 * apart, count) if apart else made[side]
    total = chips * rows
    attended = call(
        attend_kernel,
        array((chips, rows, LANES), jnp.bfloat16),
        (info,) + tuple(held[apart] for apart in range(chips)),
        [
            VMEM((total, 2 * LANES), jnp.bfloat16),
            VMEM((total, LANES), jnp.bfloat16),
            VMEM((2 * total, 2 * LANES), jnp.bfloat16),
        ],
        24,
    )
    return lax.all_to_all(
        attended, "seq", split_axis=0, concat_axis=0, tiled=True,
        axis_index_groups=same_core(count),
    )


def per_device(
    hidden, latent, lengths, step_index, guidance, modulation, conv_kernel, w_qkv, w_out, w_mel
):
    _, rows, width = hidden.shape
    count = lax.axis_size("seq")
    chips = count // 2
    index = lax.axis_index("seq").astype(jnp.int32)
    chip, core = index >> 1, index & 1
    chip_rows = 2 * rows
    place = jnp.stack([core, chip])

    partner = across(hidden, 1, count)
    edge = core * (rows - HALO)
    near = lax.dynamic_slice(hidden, (1 - core, edge, 0), (1, HALO, width))[0]
    far = lax.dynamic_slice(hidden, (core, edge, 0), (1, HALO, width))[0]
    steps = range(chips - 1)
    near = lax.ppermute(
        near, "seq",
        [(2 * m + 1, 2 * m + 2) for m in steps] + [(2 * m + 2, 2 * m + 1) for m in steps],
    )
    far = lax.ppermute(
        far, "seq",
        [(2 * m + 1, 2 * m + 3) for m in steps] + [(2 * m + 2, 2 * m) for m in steps],
    )
    own, taps, mods = call(
        stage_kernel,
        (
            array((rows, width), jnp.bfloat16),
            array(conv_kernel.shape),
            array(modulation.shape),
        ),
        (place, hidden, conv_kernel, modulation),
        [pltpu.SemaphoreType.DMA((3,))],
        4,
        hbm=(1, 2, 3),
    )
    info = jnp.stack([core, chip, lengths[0]])
    tables = rotary_tables(chip * chip_rows + jnp.arange(chip_rows, dtype=jnp.int32))
    residual, normed, weight = call(
        front_kernel,
        (
            array((chip_rows, width)),
            array((chip_rows, width), jnp.bfloat16),
            array(w_qkv.shape, jnp.bfloat16),
        ),
        (info, own, partner, near, far, taps, mods, w_qkv),
        [VMEM((chip_rows + 2 * HALO, LANES), jnp.float32), pltpu.SemaphoreType.DMA((8,))],
        8,
        hbm=(7,),
    )
    if chips_hold_groups(count):
        back = attend_chips(normed, weight, tables, info, count)
    else:
        back = attend_any(normed, weight, tables, info, lengths[0], count)
    mels = w_mel.shape[1]
    keep, send = call(
        back_kernel,
        (array((rows, mels)),) * 2,
        (info, residual, w_mel.T, mods, w_out, back),
        [
            VMEM((chip_rows, HEADS * HEAD_DIM), jnp.bfloat16),
            VMEM((chip_rows, width), jnp.float32),
            VMEM((chip_rows, mels), jnp.float32),
            VMEM((chip_rows, width), jnp.float32),
            VMEM((mels, width), jnp.bfloat16),
            pltpu.SemaphoreType.DMA((2,)),
        ],
        12,
        hbm=(1, 2),
    )
    other = across(send, 1, count)
    first = jnp.where(core == 0, keep, other)
    second = jnp.where(core == 0, other, keep)
    guided = first + guidance[0] * (first - second)
    live = index * rows + jnp.arange(rows, dtype=jnp.int32) < lengths[0]
    velocity = jnp.where(live[:, None], guided, 0.0)
    progress = step_index[0].astype(jnp.float32) / STEPS
    time_now = 1.0 - jnp.cos(0.5 * jnp.pi * progress)
    return (velocity, latent + (1.0 - time_now) * velocity)


def solution(mesh):
    return jax.shard_map(
        per_device,
        mesh=mesh,
        in_specs=(
            P(None, ("clip", "seq"), None),
            P(("clip", "seq"), None),
            P("clip"),
            P(),
            P(),
            P(),
            P(),
            P(),
            P(),
            P(),
        ),
        out_specs=(P(("clip", "seq"), None), P(("clip", "seq"), None)),
        check_vma=False,
    )
```

```python
import functools

import jax
import jax.numpy as jnp
from jax import lax
from jax.experimental import pallas as pl
from jax.experimental.pallas import tpu as pltpu
from jax.sharding import PartitionSpec as P


HEADS = 16
HEAD_DIM = 64
KERNEL = 31
STEPS = 32
LANES = 128
HALO = 16


EPSILON = 1e-06
NEGATIVE = -1e30
CORE, CHIP, LENGTH = 0, 1, 2
VMEM = pltpu.VMEM
SMEM = pltpu.SMEM
MIB = 1 << 20


def vmem_spec():
    return pl.BlockSpec(memory_space=VMEM)


def smem_spec():
    return pl.BlockSpec(memory_space=SMEM)


def rotary_tables(positions):
    half_dim = HEAD_DIM // 2
    lane = jnp.arange(LANES, dtype=jnp.int32)
    inverse = 10000.0 ** (-(lane % half_dim).astype(jnp.float32) / half_dim)
    angles = positions.astype(jnp.float32)[:, None] * inverse[None, :]
    sign = jnp.where(lane % HEAD_DIM < half_dim, -1.0, 1.0)
    return jnp.cos(angles), jnp.sin(angles) * sign[None, :]


def hbm_spec():
    return pl.BlockSpec(memory_space=pltpu.HBM)


def tile_lanes(tile):
    return pl.ds(pl.multiple_of(tile * LANES, LANES), LANES)


def row_norm(load, store, tiles, mod_ref, row, total):
    width = tiles * LANES
    mean = jnp.sum(total, axis=-1, keepdims=True) * (1.0 / width)

    def square(tile, acc):
        centered = load(tile) - mean
        return acc + centered * centered

    squares = lax.fori_loop(0, tiles, square, jnp.zeros(total.shape, jnp.float32), unroll=6)
    variance = jnp.sum(squares, axis=-1, keepdims=True) * (1.0 / width)
    factor = lax.rsqrt(variance + EPSILON)

    def write(tile, carry):
        lanes = tile_lanes(tile)
        scale = 1.0 + mod_ref[row + 1 : row + 2, lanes]
        shift = mod_ref[row : row + 1, lanes]
        store(lanes, (load(tile) - mean) * factor * scale + shift)
        return carry

    lax.fori_loop(0, tiles, write, 0, unroll=6)


def run_copies(pairs, sems):
    copies = [
        pltpu.make_async_copy(source, target, sems.at[at])
        for at, (source, target) in enumerate(pairs)
    ]
    for copy in copies:
        copy.start()
    for copy in copies:
        copy.wait()


def stage_kernel(info_ref, hidden_hbm, taps_hbm, mod_hbm, own_ref, taps_ref, mod_ref, sems):
    run_copies(
        [
            (hidden_hbm.at[info_ref[CORE]], own_ref),
            (taps_hbm, taps_ref),
            (mod_hbm, mod_ref),
        ],
        sems,
    )


def front_kernel(
    info_ref, own_ref, partner_ref, near_ref, far_ref, taps_ref, mod_ref, weight_hbm,
    residual_ref, normed_ref, weight_ref, padded, sems,
):
    rows, width = own_ref.shape
    halo = near_ref.shape[0]
    total_rows = 2 * rows
    tiles = width // LANES
    parts = 8
    depth = width // parts
    loads = []
    for part in range(parts):
        here = pl.ds(part * depth, depth)
        loads.append(
            pltpu.make_async_copy(weight_hbm.at[here], weight_ref.at[here], sems.at[part])
        )
    for load in loads:
        load.start()
    length, core = info_ref[LENGTH], info_ref[CORE]
    offset = info_ref[CHIP] * total_rows
    span = total_rows + 2 * halo
    frame = offset - halo + lax.broadcasted_iota(jnp.int32, (span, LANES), 0)
    live = (frame < length).astype(jnp.float32)
    first = halo - KERNEL // 2
    own_at = pl.ds(pl.multiple_of(halo + core * rows, 8), rows)
    partner_at = pl.ds(pl.multiple_of(halo + (1 - core) * rows, 8), rows)
    near_at = pl.ds(pl.multiple_of(core * (halo + total_rows), 8), halo)
    far_at = pl.ds(pl.multiple_of((1 - core) * (halo + total_rows), 8), halo)

    def convolve(tile, total):
        lanes = tile_lanes(tile)
        padded[near_at] = near_ref[:, lanes].astype(jnp.float32)
        padded[far_at] = far_ref[:, lanes].astype(jnp.float32)
        padded[own_at] = own_ref[:, lanes].astype(jnp.float32)
        padded[partner_at] = partner_ref[:, lanes].astype(jnp.float32)
        own = padded[halo : halo + total_rows]
        padded[...] = padded[...] * live
        acc = jnp.zeros((total_rows, LANES), jnp.float32)
        for tap in range(KERNEL):
            acc = acc + taps_ref[tap : tap + 1, lanes] * padded[
                first + tap : first + tap + total_rows
            ]
        grown = jnp.exp(jnp.minimum(acc, 20.0))
        product = grown * (grown + 2.0)
        value = own + acc * (product / (product + 2.0))
        residual_ref[:, lanes] = value
        return total + value

    total = lax.fori_loop(
        0, tiles, convolve, jnp.zeros((total_rows, LANES), jnp.float32), unroll=3
    )

    def store(lanes, value):
        normed_ref[:, lanes] = value.astype(jnp.bfloat16)

    row_norm(lambda tile: residual_ref[:, tile_lanes(tile)], store, tiles, mod_ref, 0, total)
    for load in loads:
        load.wait()


def project_kernel(firsts, origin, info_ref, normed_ref, weight_ref, cos_ref, sin_ref, *out_refs):
    rows = normed_ref.shape[0]
    attn = weight_ref.shape[1] // 3
    wide = 2 * LANES
    half = HEAD_DIM // 2
    cosine, sine = cos_ref[...], sin_ref[...]
    lower = lax.broadcasted_iota(jnp.int32, (rows, LANES), 1) % HEAD_DIM < half
    chip = info_ref[CHIP] if origin is None else origin
    swap = jnp.full((rows, LANES), chip & 1, jnp.int32) > 0
    for at, apart in enumerate(firsts):
        pair = (chip ^ apart) >> 1
        for part in range(3):
            start = part * attn + pair * wide
            both = jnp.dot(
                normed_ref[...],
                weight_ref[:, pl.ds(pl.multiple_of(start, wide), wide)],
                preferred_element_type=jnp.float32,
            )
            sides = []
            for side in range(2):
                value = both[:, side * LANES : (side + 1) * LANES]
                if part < 2:
                    swapped = jnp.where(
                        lower, pltpu.roll(value, LANES - half, 1), pltpu.roll(value, half, 1)
                    )
                    value = value * cosine + swapped * sine
                if part == 0:
                    value = value * HEAD_DIM**-0.5
                sides.append(value)
            out_refs[2 * at][part] = jnp.where(swap, sides[1], sides[0]).astype(jnp.bfloat16)
            out_refs[2 * at + 1][part] = jnp.where(swap, sides[0], sides[1]).astype(jnp.bfloat16)


def gather_keys(info_ref, got_refs, keys, values):
    _, rows, _ = got_refs[0].shape
    length, chip = info_ref[LENGTH], info_ref[CHIP]
    lane = lax.broadcasted_iota(jnp.int32, (rows, LANES), 1)
    row = lax.broadcasted_iota(jnp.int32, (rows, LANES), 0)
    for apart, got_ref in enumerate(got_refs):
        here = slice(apart * rows, (apart + 1) * rows)
        keys[here, :LANES] = got_ref[1]
        dead = (lane == 0) & (row + (chip ^ apart) * rows >= length)
        keys[here, LANES:] = jnp.where(dead, NEGATIVE, 0.0).astype(jnp.bfloat16)
        values[here, :] = got_ref[2]


def attend_rows(query_refs, keys, values, out_ref, queries, chip):
    _, rows, _ = query_refs[0].shape
    low = lax.broadcasted_iota(jnp.int32, (rows, LANES), 1) < HEAD_DIM
    zero = jnp.zeros((rows, LANES), jnp.bfloat16)
    queries[:, LANES:] = jnp.where(
        lax.broadcasted_iota(jnp.int32, (queries.shape[0], LANES), 1) == 0, 1.0, 0.0
    ).astype(jnp.bfloat16)
    for at, query_ref in enumerate(query_refs):
        query = query_ref[0]
        base = 2 * at * rows
        queries[base : base + rows, :LANES] = jnp.where(low, query, zero)
        queries[base + rows : base + 2 * rows, :LANES] = jnp.where(low, zero, query)
    for first in range(0, len(query_refs), 2):
        base = 2 * first * rows
        scores = lax.dot_general(
            queries[base : base + 4 * rows, :], keys[...], (((1,), (1,)), ((), ())),
            preferred_element_type=jnp.float32,
        )
        weights = jnp.exp(scores - jnp.max(scores, axis=1, keepdims=True))
        weight_sum = jnp.sum(weights, axis=1, keepdims=True)
        mixed = jnp.dot(
            weights.astype(jnp.bfloat16), values[...], preferred_element_type=jnp.float32
        )
        mixed = mixed / weight_sum
        for side in range(2):
            base = 2 * side * rows
            out_ref[chip ^ (first + side)] = jnp.where(
                low, mixed[base : base + rows], mixed[base + rows : base + 2 * rows]
            ).astype(jnp.bfloat16)


def attend_kernel(info_ref, *refs):
    chips = len(refs) - 4
    got_refs = refs[:chips]
    out_ref, keys, values, queries = refs[chips:]
    gather_keys(info_ref, got_refs, keys, values)
    attend_rows(got_refs, keys, values, out_ref, queries, info_ref[CHIP])


def back_kernel(
    info_ref, residual_hbm, w_mel_hbm, mod_ref, w_out_ref, got_ref, keep_ref, send_ref, attended,
    after, speed, residual, w_mel, sems,
):
    rows, width = residual.shape
    tiles = width // LANES
    core = info_ref[CORE]
    loads = [
        pltpu.make_async_copy(residual_hbm, residual, sems.at[0]),
        pltpu.make_async_copy(w_mel_hbm, w_mel, sems.at[1]),
    ]
    for load in loads:
        load.start()
    for group in range(got_ref.shape[0]):
        attended[:, group * LANES : (group + 1) * LANES] = got_ref[group]
    wide = 2 * LANES
    for block in range(width // wide):
        lanes = slice(block * wide, (block + 1) * wide)
        branch = jnp.dot(attended[...], w_out_ref[:, lanes], preferred_element_type=jnp.float32)
        after[:, lanes] = mod_ref[2:3, lanes] * branch
    loads[0].wait()

    def join(tile, total):
        lanes = tile_lanes(tile)
        value = residual[:, lanes] + after[:, lanes]
        after[:, lanes] = value
        return total + value

    total = lax.fori_loop(0, tiles, join, jnp.zeros((rows, LANES), jnp.float32), unroll=6)

    def store(lanes, value):
        after[:, lanes] = value

    row_norm(lambda tile: after[:, tile_lanes(tile)], store, tiles, mod_ref, 3, total)
    loads[1].wait()
    speed[...] = lax.dot_general(
        after[...].astype(jnp.bfloat16), w_mel[...], (((1,), (1,)), ((), ())),
        preferred_element_type=jnp.float32,
    )
    half = rows // 2
    keep_ref[...] = speed[pl.ds(pl.multiple_of(core * half, 8), half), :]
    send_ref[...] = speed[pl.ds(pl.multiple_of((1 - core) * half, 8), half), :]


def call(kernel, out_shape, inputs, scratch, limit, hbm=()):
    single = not isinstance(out_shape, tuple)
    specs = [hbm_spec() if at in hbm else vmem_spec() for at in range(1, len(inputs))]
    inputs = list(inputs)
    for at in hbm:
        inputs[at] = pltpu.with_memory_space_constraint(inputs[at], pltpu.HBM)
    return pl.pallas_call(
        kernel,
        out_shape=out_shape,
        in_specs=[smem_spec()] + specs,
        out_specs=vmem_spec() if single else tuple(vmem_spec() for _ in out_shape),
        scratch_shapes=scratch,
        compiler_params=pltpu.CompilerParams(vmem_limit_bytes=limit * MIB),
    )(*inputs)


def array(shape, dtype=jnp.float32):
    return jax.ShapeDtypeStruct(shape, dtype)


def project(normed, w_qkv, tables, info, firsts, origin=None):
    shape = array((3, normed.shape[0], LANES), jnp.bfloat16)
    return call(
        functools.partial(project_kernel, tuple(firsts), origin),
        (shape,) * (2 * len(firsts)),
        (info, normed, w_qkv) + tables,
        [],
        8,
    )


def same_core(count):
    return [list(range(core, count, 2)) for core in range(2)]


def across(value, apart, count):
    return lax.ppermute(value, "seq", [(i, i ^ apart) for i in range(count)])


def to_groups(values, subs):
    rows, _ = values.shape
    grouped = values.reshape(subs, rows // subs, HEADS, HEAD_DIM).transpose(2, 0, 1, 3)
    return grouped.reshape(HEADS * subs, rows // subs, HEAD_DIM)


def from_groups(grouped, rows, subs):
    split = grouped.reshape(HEADS, subs, rows // subs, HEAD_DIM).transpose(1, 2, 0, 3)
    return split.reshape(rows, HEADS * HEAD_DIM)


def attend_blocks(queries, keys, values, live):
    groups, total, _ = queries.shape
    block = max(size for size in range(1, min(total, 1024) + 1) if total % size == 0)
    blocks = queries.reshape(groups, total // block, block, HEAD_DIM).transpose(1, 0, 2, 3)
    live = live[None, None, :]

    def one_block(query):
        scores = jnp.einsum("gqd,gkd->gqk", query, keys, preferred_element_type=jnp.float32)
        scores = jnp.where(live, scores, NEGATIVE)
        weights = jnp.exp(scores - jnp.max(scores, axis=-1, keepdims=True))
        weights = jnp.where(live, weights, 0.0)
        mixed = jnp.einsum(
            "gqk,gkd->gqd",
            weights.astype(jnp.bfloat16),
            values,
            preferred_element_type=jnp.float32,
        )
        return (mixed / jnp.sum(weights, axis=-1)[..., None]).astype(jnp.bfloat16)

    return lax.map(one_block, blocks).transpose(1, 0, 2, 3).reshape(groups, total, HEAD_DIM)


def attend_any(normed, w_qkv, tables, info, length, count):
    rows = normed.shape[0]
    chips = count // 2
    groups = HEADS * HEAD_DIM // LANES
    sent = project(normed, w_qkv, tables, info, range(0, groups, 2), 0)
    subs = max(1, chips // HEADS)
    chip = lax.axis_index("seq") >> 1
    part_rows = rows // subs

    def exchange(part):
        whole = jnp.concatenate([group[part] for group in sent], axis=1)
        return lax.all_to_all(
            to_groups(whole, subs), "seq", split_axis=0, concat_axis=1, tiled=True,
            axis_index_groups=same_core(count),
        )

    queries, keys, values = (exchange(part) for part in range(3))

    def frames_of(sub):
        start = jnp.arange(chips, dtype=jnp.int32)[:, None] * rows + sub * part_rows
        return (start + jnp.arange(part_rows, dtype=jnp.int32)[None, :]).reshape(-1)

    frames = [frames_of(chip % subs)]
    parts = [(keys, values)]
    for apart in range(1, subs):
        perm = []
        for i in range(count):
            at = i // 2
            target = at - at % subs + (at + apart) % subs
            perm.append((i, 2 * target + i % 2))
        parts.append(tuple(lax.ppermute(part, "seq", perm) for part in (keys, values)))
        frames.append(frames_of((chip - apart) % subs))
    keys = jnp.concatenate([part[0] for part in parts], axis=1)
    values = jnp.concatenate([part[1] for part in parts], axis=1)
    attended = attend_blocks(queries, keys, values, jnp.concatenate(frames) < length)
    back = lax.all_to_all(
        attended, "seq", split_axis=1, concat_axis=0, tiled=True,
        axis_index_groups=same_core(count),
    )
    return from_groups(back, rows, subs).reshape(rows, groups, LANES).transpose(1, 0, 2)


def chips_hold_groups(count):
    chips = count // 2
    return chips == HEADS * HEAD_DIM // LANES and chips >= 4 and chips & (chips - 1) == 0


def send_order(chips):
    far = list(range(chips // 2, chips, 2))
    return far[:1] + [0] + far[1:] + list(range(2, chips // 2, 2))


def attend_chips(normed, w_qkv, tables, info, count):
    rows = normed.shape[0]
    chips = count // 2
    held = {}
    for first in send_order(chips):
        made = project(normed, w_qkv, tables, info, [first])
        for side in range(2):
            apart = first + side
            held[apart] = across(made[side], 2 * apart, count) if apart else made[side]
    total = chips * rows
    attended = call(
        attend_kernel,
        array((chips, rows, LANES), jnp.bfloat16),
        (info,) + tuple(held[apart] for apart in range(chips)),
        [
            VMEM((total, 2 * LANES), jnp.bfloat16),
            VMEM((total, LANES), jnp.bfloat16),
            VMEM((2 * total, 2 * LANES), jnp.bfloat16),
        ],
        24,
    )
    return lax.all_to_all(
        attended, "seq", split_axis=0, concat_axis=0, tiled=True,
        axis_index_groups=same_core(count),
    )


def per_device(
    hidden, latent, lengths, step_index, guidance, modulation, conv_kernel, w_qkv, w_out, w_mel
):
    _, rows, width = hidden.shape
    count = lax.axis_size("seq")
    chips = count // 2
    index = lax.axis_index("seq").astype(jnp.int32)
    chip, core = index >> 1, index & 1
    chip_rows = 2 * rows
    place = jnp.stack([core, chip])

    edge = core * (rows - HALO)
    near = lax.dynamic_slice(hidden, (1 - core, edge, 0), (1, HALO, width))[0]
    far = lax.dynamic_slice(hidden, (core, edge, 0), (1, HALO, width))[0]
    partner = lax.dynamic_slice(hidden, (1 - core, 0, 0), (1, rows, width))[0]
    steps = range(chips - 1)
    near = lax.ppermute(
        near, "seq",
        [(2 * m + 1, 2 * m + 2) for m in steps] + [(2 * m + 2, 2 * m + 1) for m in steps],
    )
    far = lax.ppermute(
        far, "seq",
        [(2 * m + 1, 2 * m + 3) for m in steps] + [(2 * m + 2, 2 * m) for m in steps],
    )
    partner = across(partner, 1, count)
    own, taps, mods = call(
        stage_kernel,
        (
            array((rows, width), jnp.bfloat16),
            array(conv_kernel.shape),
            array(modulation.shape),
        ),
        (place, hidden, conv_kernel, modulation),
        [pltpu.SemaphoreType.DMA((3,))],
        4,
        hbm=(1, 2, 3),
    )
    info = jnp.stack([core, chip, lengths[0]])
    tables = rotary_tables(chip * chip_rows + jnp.arange(chip_rows, dtype=jnp.int32))
    residual, normed, weight = call(
        front_kernel,
        (
            array((chip_rows, width)),
            array((chip_rows, width), jnp.bfloat16),
            array(w_qkv.shape, jnp.bfloat16),
        ),
        (info, own, partner, near, far, taps, mods, w_qkv),
        [VMEM((chip_rows + 2 * HALO, LANES), jnp.float32), pltpu.SemaphoreType.DMA((8,))],
        8,
        hbm=(7,),
    )
    if chips_hold_groups(count):
        back = attend_chips(normed, weight, tables, info, count)
    else:
        back = attend_any(normed, weight, tables, info, lengths[0], count)
    mels = w_mel.shape[1]
    keep, send = call(
        back_kernel,
        (array((rows, mels)),) * 2,
        (info, residual, w_mel.T, mods, w_out, back),
        [
            VMEM((chip_rows, HEADS * HEAD_DIM), jnp.bfloat16),
            VMEM((chip_rows, width), jnp.float32),
            VMEM((chip_rows, mels), jnp.float32),
            VMEM((chip_rows, width), jnp.float32),
            VMEM((mels, width), jnp.bfloat16),
            pltpu.SemaphoreType.DMA((2,)),
        ],
        12,
        hbm=(1, 2),
    )
    other = across(send, 1, count)
    first = jnp.where(core == 0, keep, other)
    second = jnp.where(core == 0, other, keep)
    guided = first + guidance[0] * (first - second)
    live = index * rows + jnp.arange(rows, dtype=jnp.int32) < lengths[0]
    velocity = jnp.where(live[:, None], guided, 0.0)
    progress = step_index[0].astype(jnp.float32) / STEPS
    time_now = 1.0 - jnp.cos(0.5 * jnp.pi * progress)
    return (velocity, latent + (1.0 - time_now) * velocity)


def solution(mesh):
    return jax.shard_map(
        per_device,
        mesh=mesh,
        in_specs=(
            P(None, ("clip", "seq"), None),
            P(("clip", "seq"), None),
            P("clip"),
            P(),
            P(),
            P(),
            P(),
            P(),
            P(),
            P(),
        ),
        out_specs=(P(("clip", "seq"), None), P(("clip", "seq"), None)),
        check_vma=False,
    )
```

```python
import functools

import jax
import jax.numpy as jnp
from jax import lax
from jax.experimental import pallas as pl
from jax.experimental.pallas import tpu as pltpu
from jax.sharding import PartitionSpec as P


HEADS = 16
HEAD_DIM = 64
KERNEL = 31
STEPS = 32
LANES = 128
HALO = 16


EPSILON = 1e-06
NEGATIVE = -1e30
CORE, CHIP, LENGTH = 0, 1, 2
VMEM = pltpu.VMEM
SMEM = pltpu.SMEM
MIB = 1 << 20


def vmem_spec():
    return pl.BlockSpec(memory_space=VMEM)


def smem_spec():
    return pl.BlockSpec(memory_space=SMEM)


def rotary_tables(positions):
    half_dim = HEAD_DIM // 2
    lane = jnp.arange(LANES, dtype=jnp.int32)
    inverse = 10000.0 ** (-(lane % half_dim).astype(jnp.float32) / half_dim)
    angles = positions.astype(jnp.float32)[:, None] * inverse[None, :]
    sign = jnp.where(lane % HEAD_DIM < half_dim, -1.0, 1.0)
    return jnp.cos(angles), jnp.sin(angles) * sign[None, :]


def hbm_spec():
    return pl.BlockSpec(memory_space=pltpu.HBM)


def tile_lanes(tile):
    return pl.ds(pl.multiple_of(tile * LANES, LANES), LANES)


def row_norm(load, store, tiles, mod_ref, row, total):
    width = tiles * LANES
    mean = jnp.sum(total, axis=-1, keepdims=True) * (1.0 / width)

    def square(tile, acc):
        centered = load(tile) - mean
        return acc + centered * centered

    squares = lax.fori_loop(0, tiles, square, jnp.zeros(total.shape, jnp.float32), unroll=6)
    variance = jnp.sum(squares, axis=-1, keepdims=True) * (1.0 / width)
    factor = lax.rsqrt(variance + EPSILON)

    def write(tile, carry):
        lanes = tile_lanes(tile)
        scale = 1.0 + mod_ref[row + 1 : row + 2, lanes]
        shift = mod_ref[row : row + 1, lanes]
        store(lanes, (load(tile) - mean) * factor * scale + shift)
        return carry

    lax.fori_loop(0, tiles, write, 0, unroll=6)


def run_copies(pairs, sems):
    copies = [
        pltpu.make_async_copy(source, target, sems.at[at])
        for at, (source, target) in enumerate(pairs)
    ]
    for copy in copies:
        copy.start()
    for copy in copies:
        copy.wait()


def stage_kernel(info_ref, hidden_hbm, taps_hbm, mod_hbm, own_ref, taps_ref, mod_ref, sems):
    run_copies(
        [
            (hidden_hbm.at[info_ref[CORE]], own_ref),
            (taps_hbm, taps_ref),
            (mod_hbm, mod_ref),
        ],
        sems,
    )


def front_kernel(
    info_ref, own_ref, partner_ref, near_ref, far_ref, taps_ref, mod_ref, weight_hbm,
    residual_ref, normed_ref, weight_ref, padded, sems,
):
    rows, width = own_ref.shape
    halo = near_ref.shape[1]
    total_rows = 2 * rows
    tiles = width // LANES
    parts = 8
    depth = width // parts
    loads = []
    for part in range(parts):
        here = pl.ds(part * depth, depth)
        loads.append(
            pltpu.make_async_copy(weight_hbm.at[here], weight_ref.at[here], sems.at[part])
        )
    for load in loads:
        load.start()
    length, core = info_ref[LENGTH], info_ref[CORE]
    offset = info_ref[CHIP] * total_rows
    span = total_rows + 2 * halo
    frame = offset - halo + lax.broadcasted_iota(jnp.int32, (span, LANES), 0)
    live = ((frame >= 0) & (frame < length)).astype(jnp.float32)
    first = halo - KERNEL // 2
    own_at = pl.ds(pl.multiple_of(halo + core * rows, 8), rows)
    partner_at = pl.ds(pl.multiple_of(halo + (1 - core) * rows, 8), rows)
    near_at = pl.ds(pl.multiple_of(core * (halo + total_rows), 8), halo)
    far_at = pl.ds(pl.multiple_of((1 - core) * (halo + total_rows), 8), halo)

    def convolve(tile, total):
        lanes = tile_lanes(tile)
        padded[near_at] = near_ref[core, :, lanes].astype(jnp.float32)
        padded[far_at] = far_ref[core, :, lanes].astype(jnp.float32)
        padded[own_at] = own_ref[:, lanes].astype(jnp.float32)
        padded[partner_at] = partner_ref[:, lanes].astype(jnp.float32)
        own = padded[halo : halo + total_rows]
        padded[...] = padded[...] * live
        acc = jnp.zeros((total_rows, LANES), jnp.float32)
        for tap in range(KERNEL):
            acc = acc + taps_ref[tap : tap + 1, lanes] * padded[
                first + tap : first + tap + total_rows
            ]
        grown = jnp.exp(jnp.minimum(acc, 20.0))
        product = grown * (grown + 2.0)
        value = own + acc * (product / (product + 2.0))
        residual_ref[:, lanes] = value
        return total + value

    total = lax.fori_loop(
        0, tiles, convolve, jnp.zeros((total_rows, LANES), jnp.float32), unroll=3
    )

    def store(lanes, value):
        normed_ref[:, lanes] = value.astype(jnp.bfloat16)

    row_norm(lambda tile: residual_ref[:, tile_lanes(tile)], store, tiles, mod_ref, 0, total)
    for load in loads:
        load.wait()


def project_kernel(firsts, origin, info_ref, normed_ref, weight_ref, cos_ref, sin_ref, *out_refs):
    rows = normed_ref.shape[0]
    attn = weight_ref.shape[1] // 3
    wide = 2 * LANES
    half = HEAD_DIM // 2
    cosine, sine = cos_ref[...], sin_ref[...]
    lower = lax.broadcasted_iota(jnp.int32, (rows, LANES), 1) % HEAD_DIM < half
    chip = info_ref[CHIP] if origin is None else origin
    swap = jnp.full((rows, LANES), chip & 1, jnp.int32) > 0
    for at, apart in enumerate(firsts):
        pair = (chip ^ apart) >> 1
        for part in range(3):
            start = part * attn + pair * wide
            both = jnp.dot(
                normed_ref[...],
                weight_ref[:, pl.ds(pl.multiple_of(start, wide), wide)],
                preferred_element_type=jnp.float32,
            )
            sides = []
            for side in range(2):
                value = both[:, side * LANES : (side + 1) * LANES]
                if part < 2:
                    swapped = jnp.where(
                        lower, pltpu.roll(value, LANES - half, 1), pltpu.roll(value, half, 1)
                    )
                    value = value * cosine + swapped * sine
                if part == 0:
                    value = value * HEAD_DIM**-0.5
                sides.append(value)
            out_refs[2 * at][part] = jnp.where(swap, sides[1], sides[0]).astype(jnp.bfloat16)
            out_refs[2 * at + 1][part] = jnp.where(swap, sides[0], sides[1]).astype(jnp.bfloat16)


def gather_keys(info_ref, got_refs, keys, values):
    _, rows, _ = got_refs[0].shape
    length, chip = info_ref[LENGTH], info_ref[CHIP]
    lane = lax.broadcasted_iota(jnp.int32, (rows, LANES), 1)
    row = lax.broadcasted_iota(jnp.int32, (rows, LANES), 0)
    for apart, got_ref in enumerate(got_refs):
        here = slice(apart * rows, (apart + 1) * rows)
        keys[here, :LANES] = got_ref[1]
        dead = (lane == 0) & (row + (chip ^ apart) * rows >= length)
        keys[here, LANES:] = jnp.where(dead, NEGATIVE, 0.0).astype(jnp.bfloat16)
        values[here, :] = got_ref[2]


def attend_rows(query_refs, keys, values, out_ref, queries, chip):
    _, rows, _ = query_refs[0].shape
    low = lax.broadcasted_iota(jnp.int32, (rows, LANES), 1) < HEAD_DIM
    zero = jnp.zeros((rows, LANES), jnp.bfloat16)
    queries[:, LANES:] = jnp.where(
        lax.broadcasted_iota(jnp.int32, (queries.shape[0], LANES), 1) == 0, 1.0, 0.0
    ).astype(jnp.bfloat16)
    for at, query_ref in enumerate(query_refs):
        query = query_ref[0]
        base = 2 * at * rows
        queries[base : base + rows, :LANES] = jnp.where(low, query, zero)
        queries[base + rows : base + 2 * rows, :LANES] = jnp.where(low, zero, query)
    for first in range(0, len(query_refs), 2):
        base = 2 * first * rows
        scores = lax.dot_general(
            queries[base : base + 4 * rows, :], keys[...], (((1,), (1,)), ((), ())),
            preferred_element_type=jnp.float32,
        )
        weights = jnp.exp(scores - jnp.max(scores, axis=1, keepdims=True))
        weight_sum = jnp.sum(weights, axis=1, keepdims=True)
        mixed = jnp.dot(
            weights.astype(jnp.bfloat16), values[...], preferred_element_type=jnp.float32
        )
        mixed = mixed / weight_sum
        for side in range(2):
            base = 2 * side * rows
            out_ref[chip ^ (first + side)] = jnp.where(
                low, mixed[base : base + rows], mixed[base + rows : base + 2 * rows]
            ).astype(jnp.bfloat16)


def attend_kernel(info_ref, *refs):
    chips = len(refs) - 4
    got_refs = refs[:chips]
    out_ref, keys, values, queries = refs[chips:]
    gather_keys(info_ref, got_refs, keys, values)
    attend_rows(got_refs, keys, values, out_ref, queries, info_ref[CHIP])


def back_kernel(
    info_ref, residual_hbm, w_mel_hbm, mod_ref, w_out_ref, got_ref, keep_ref, send_ref, attended,
    after, speed, residual, w_mel, sems,
):
    rows, width = residual.shape
    tiles = width // LANES
    core = info_ref[CORE]
    loads = [
        pltpu.make_async_copy(residual_hbm, residual, sems.at[0]),
        pltpu.make_async_copy(w_mel_hbm, w_mel, sems.at[1]),
    ]
    for load in loads:
        load.start()
    for group in range(got_ref.shape[0]):
        attended[:, group * LANES : (group + 1) * LANES] = got_ref[group]
    wide = 2 * LANES
    for block in range(width // wide):
        lanes = slice(block * wide, (block + 1) * wide)
        branch = jnp.dot(attended[...], w_out_ref[:, lanes], preferred_element_type=jnp.float32)
        after[:, lanes] = mod_ref[2:3, lanes] * branch
    loads[0].wait()

    def join(tile, total):
        lanes = tile_lanes(tile)
        value = residual[:, lanes] + after[:, lanes]
        after[:, lanes] = value
        return total + value

    total = lax.fori_loop(0, tiles, join, jnp.zeros((rows, LANES), jnp.float32), unroll=6)

    def store(lanes, value):
        after[:, lanes] = value

    row_norm(lambda tile: after[:, tile_lanes(tile)], store, tiles, mod_ref, 3, total)
    loads[1].wait()
    speed[...] = lax.dot_general(
        after[...].astype(jnp.bfloat16), w_mel[...], (((1,), (1,)), ((), ())),
        preferred_element_type=jnp.float32,
    )
    half = rows // 2
    keep_ref[...] = speed[pl.ds(pl.multiple_of(core * half, 8), half), :]
    send_ref[...] = speed[pl.ds(pl.multiple_of((1 - core) * half, 8), half), :]


def call(kernel, out_shape, inputs, scratch, limit, hbm=()):
    single = not isinstance(out_shape, tuple)
    specs = [hbm_spec() if at in hbm else vmem_spec() for at in range(1, len(inputs))]
    inputs = list(inputs)
    for at in hbm:
        inputs[at] = pltpu.with_memory_space_constraint(inputs[at], pltpu.HBM)
    return pl.pallas_call(
        kernel,
        out_shape=out_shape,
        in_specs=[smem_spec()] + specs,
        out_specs=vmem_spec() if single else tuple(vmem_spec() for _ in out_shape),
        scratch_shapes=scratch,
        compiler_params=pltpu.CompilerParams(vmem_limit_bytes=limit * MIB),
    )(*inputs)


def array(shape, dtype=jnp.float32):
    return jax.ShapeDtypeStruct(shape, dtype)


def project(normed, w_qkv, tables, info, firsts, origin=None):
    shape = array((3, normed.shape[0], LANES), jnp.bfloat16)
    return call(
        functools.partial(project_kernel, tuple(firsts), origin),
        (shape,) * (2 * len(firsts)),
        (info, normed, w_qkv) + tables,
        [],
        8,
    )


def same_core(count):
    return [list(range(core, count, 2)) for core in range(2)]


def facing_pairs(clips, count):
    pairs = []
    for clip in range(clips):
        base = clip * count
        for at in range(1, count - 1, 2):
            pairs += [(base + at, base + at + 1), (base + at + 1, base + at)]
        if clip ^ 1 < clips:
            pairs += [(base + end, (clip ^ 1) * count + end) for end in (0, count - 1)]
    return pairs


def across(value, apart, count):
    return lax.ppermute(value, "seq", [(i, i ^ apart) for i in range(count)])


def to_groups(values, subs):
    rows, _ = values.shape
    grouped = values.reshape(subs, rows // subs, HEADS, HEAD_DIM).transpose(2, 0, 1, 3)
    return grouped.reshape(HEADS * subs, rows // subs, HEAD_DIM)


def from_groups(grouped, rows, subs):
    split = grouped.reshape(HEADS, subs, rows // subs, HEAD_DIM).transpose(1, 2, 0, 3)
    return split.reshape(rows, HEADS * HEAD_DIM)


def attend_blocks(queries, keys, values, live):
    groups, total, _ = queries.shape
    block = max(size for size in range(1, min(total, 1024) + 1) if total % size == 0)
    blocks = queries.reshape(groups, total // block, block, HEAD_DIM).transpose(1, 0, 2, 3)
    live = live[None, None, :]

    def one_block(query):
        scores = jnp.einsum("gqd,gkd->gqk", query, keys, preferred_element_type=jnp.float32)
        scores = jnp.where(live, scores, NEGATIVE)
        weights = jnp.exp(scores - jnp.max(scores, axis=-1, keepdims=True))
        weights = jnp.where(live, weights, 0.0)
        mixed = jnp.einsum(
            "gqk,gkd->gqd",
            weights.astype(jnp.bfloat16),
            values,
            preferred_element_type=jnp.float32,
        )
        return (mixed / jnp.sum(weights, axis=-1)[..., None]).astype(jnp.bfloat16)

    return lax.map(one_block, blocks).transpose(1, 0, 2, 3).reshape(groups, total, HEAD_DIM)


def attend_any(normed, w_qkv, tables, info, length, count):
    rows = normed.shape[0]
    chips = count // 2
    groups = HEADS * HEAD_DIM // LANES
    sent = project(normed, w_qkv, tables, info, range(0, groups, 2), 0)
    subs = max(1, chips // HEADS)
    chip = lax.axis_index("seq") >> 1
    part_rows = rows // subs

    def exchange(part):
        whole = jnp.concatenate([group[part] for group in sent], axis=1)
        return lax.all_to_all(
            to_groups(whole, subs), "seq", split_axis=0, concat_axis=1, tiled=True,
            axis_index_groups=same_core(count),
        )

    queries, keys, values = (exchange(part) for part in range(3))

    def frames_of(sub):
        start = jnp.arange(chips, dtype=jnp.int32)[:, None] * rows + sub * part_rows
        return (start + jnp.arange(part_rows, dtype=jnp.int32)[None, :]).reshape(-1)

    frames = [frames_of(chip % subs)]
    parts = [(keys, values)]
    for apart in range(1, subs):
        perm = []
        for i in range(count):
            at = i // 2
            target = at - at % subs + (at + apart) % subs
            perm.append((i, 2 * target + i % 2))
        parts.append(tuple(lax.ppermute(part, "seq", perm) for part in (keys, values)))
        frames.append(frames_of((chip - apart) % subs))
    keys = jnp.concatenate([part[0] for part in parts], axis=1)
    values = jnp.concatenate([part[1] for part in parts], axis=1)
    attended = attend_blocks(queries, keys, values, jnp.concatenate(frames) < length)
    back = lax.all_to_all(
        attended, "seq", split_axis=1, concat_axis=0, tiled=True,
        axis_index_groups=same_core(count),
    )
    return from_groups(back, rows, subs).reshape(rows, groups, LANES).transpose(1, 0, 2)


def chips_hold_groups(count):
    chips = count // 2
    return chips == HEADS * HEAD_DIM // LANES and chips >= 4 and chips & (chips - 1) == 0


def send_order(chips):
    far = list(range(chips // 2, chips, 2))
    return far[:1] + [0] + far[1:] + list(range(2, chips // 2, 2))


def attend_chips(normed, w_qkv, tables, info, count):
    rows = normed.shape[0]
    chips = count // 2
    held = {}
    for first in send_order(chips):
        made = project(normed, w_qkv, tables, info, [first])
        for side in range(2):
            apart = first + side
            held[apart] = across(made[side], 2 * apart, count) if apart else made[side]
    total = chips * rows
    attended = call(
        attend_kernel,
        array((chips, rows, LANES), jnp.bfloat16),
        (info,) + tuple(held[apart] for apart in range(chips)),
        [
            VMEM((total, 2 * LANES), jnp.bfloat16),
            VMEM((total, LANES), jnp.bfloat16),
            VMEM((2 * total, 2 * LANES), jnp.bfloat16),
        ],
        24,
    )
    return lax.all_to_all(
        attended, "seq", split_axis=0, concat_axis=0, tiled=True,
        axis_index_groups=same_core(count),
    )


def per_device(
    hidden, latent, lengths, step_index, guidance, modulation, conv_kernel, w_qkv, w_out, w_mel
):
    copies, rows, width = hidden.shape
    count = lax.axis_size("seq")
    index = lax.axis_index("seq").astype(jnp.int32)
    chip, core = index >> 1, index & 1
    chip_rows = 2 * rows
    place = jnp.stack([core, chip])

    edges = lax.dynamic_slice(hidden, (0, core * (rows - HALO), 0), (copies, HALO, width))
    partner = lax.dynamic_slice(hidden, (1 - core, 0, 0), (1, rows, width))[0]
    near = lax.ppermute(edges, ("clip", "seq"), facing_pairs(lax.axis_size("clip"), count))
    far = across(near, 1, count)
    partner = across(partner, 1, count)
    own, taps, mods = call(
        stage_kernel,
        (
            array((rows, width), jnp.bfloat16),
            array(conv_kernel.shape),
            array(modulation.shape),
        ),
        (place, hidden, conv_kernel, modulation),
        [pltpu.SemaphoreType.DMA((3,))],
        4,
        hbm=(1, 2, 3),
    )
    info = jnp.stack([core, chip, lengths[0]])
    tables = rotary_tables(chip * chip_rows + jnp.arange(chip_rows, dtype=jnp.int32))
    residual, normed, weight = call(
        front_kernel,
        (
            array((chip_rows, width)),
            array((chip_rows, width), jnp.bfloat16),
            array(w_qkv.shape, jnp.bfloat16),
        ),
        (info, own, partner, near, far, taps, mods, w_qkv),
        [VMEM((chip_rows + 2 * HALO, LANES), jnp.float32), pltpu.SemaphoreType.DMA((8,))],
        8,
        hbm=(7,),
    )
    if chips_hold_groups(count):
        back = attend_chips(normed, weight, tables, info, count)
    else:
        back = attend_any(normed, weight, tables, info, lengths[0], count)
    mels = w_mel.shape[1]
    keep, send = call(
        back_kernel,
        (array((rows, mels)),) * 2,
        (info, residual, w_mel.T, mods, w_out, back),
        [
            VMEM((chip_rows, HEADS * HEAD_DIM), jnp.bfloat16),
            VMEM((chip_rows, width), jnp.float32),
            VMEM((chip_rows, mels), jnp.float32),
            VMEM((chip_rows, width), jnp.float32),
            VMEM((mels, width), jnp.bfloat16),
            pltpu.SemaphoreType.DMA((2,)),
        ],
        12,
        hbm=(1, 2),
    )
    other = across(send, 1, count)
    first = jnp.where(core == 0, keep, other)
    second = jnp.where(core == 0, other, keep)
    guided = first + guidance[0] * (first - second)
    live = index * rows + jnp.arange(rows, dtype=jnp.int32) < lengths[0]
    velocity = jnp.where(live[:, None], guided, 0.0)
    progress = step_index[0].astype(jnp.float32) / STEPS
    time_now = 1.0 - jnp.cos(0.5 * jnp.pi * progress)
    return (velocity, latent + (1.0 - time_now) * velocity)


def solution(mesh):
    return jax.shard_map(
        per_device,
        mesh=mesh,
        in_specs=(
            P(None, ("clip", "seq"), None),
            P(("clip", "seq"), None),
            P("clip"),
            P(),
            P(),
            P(),
            P(),
            P(),
            P(),
            P(),
        ),
        out_specs=(P(("clip", "seq"), None), P(("clip", "seq"), None)),
        check_vma=False,
    )
```

```python
import functools

import jax
import jax.numpy as jnp
from jax import lax
from jax.experimental import pallas as pl
from jax.experimental.pallas import tpu as pltpu
from jax.sharding import PartitionSpec as P


HEADS = 16
HEAD_DIM = 64
KERNEL = 31
STEPS = 32
LANES = 128
HALO = 16


EPSILON = 1e-06
NEGATIVE = -1e30
CORE, CHIP, LENGTH = 0, 1, 2
VMEM = pltpu.VMEM
SMEM = pltpu.SMEM
GRANT = 12 << 20


def vmem_spec():
    return pl.BlockSpec(memory_space=VMEM)


def smem_spec():
    return pl.BlockSpec(memory_space=SMEM)


def rotary_tables(positions):
    half_dim = HEAD_DIM // 2
    lane = jnp.arange(LANES, dtype=jnp.int32)
    inverse = 10000.0 ** (-(lane % half_dim).astype(jnp.float32) / half_dim)
    angles = positions.astype(jnp.float32)[:, None] * inverse[None, :]
    sign = jnp.where(lane % HEAD_DIM < half_dim, -1.0, 1.0)
    return jnp.cos(angles), jnp.sin(angles) * sign[None, :]


def hbm_spec():
    return pl.BlockSpec(memory_space=pltpu.HBM)


def tile_lanes(tile):
    return pl.ds(pl.multiple_of(tile * LANES, LANES), LANES)


def row_norm(load, store, tiles, mod_ref, row, total):
    width = tiles * LANES
    mean = jnp.sum(total, axis=-1, keepdims=True) * (1.0 / width)

    def square(tile, acc):
        centered = load(tile) - mean
        return acc + centered * centered

    squares = lax.fori_loop(0, tiles, square, jnp.zeros(total.shape, jnp.float32), unroll=6)
    variance = jnp.sum(squares, axis=-1, keepdims=True) * (1.0 / width)
    factor = lax.rsqrt(variance + EPSILON)

    def write(tile, carry):
        lanes = tile_lanes(tile)
        scale = 1.0 + mod_ref[row + 1 : row + 2, lanes]
        shift = mod_ref[row : row + 1, lanes]
        store(lanes, (load(tile) - mean) * factor * scale + shift)
        return carry

    lax.fori_loop(0, tiles, write, 0, unroll=6)


def run_copies(pairs, sems):
    copies = [
        pltpu.make_async_copy(source, target, sems.at[at])
        for at, (source, target) in enumerate(pairs)
    ]
    for copy in copies:
        copy.start()
    for copy in copies:
        copy.wait()


def stage_kernel(
    info_ref, hidden_hbm, taps_hbm, mod_hbm, own_ref, taps_ref, mod_ref, first_ref, live_ref, sems
):
    rows = own_ref.shape[0]
    core = info_ref[CORE]
    first_ref[...] = jnp.zeros(first_ref.shape, jnp.float32) + (1 - core).astype(jnp.float32)
    row = lax.broadcasted_iota(jnp.int32, live_ref.shape, 0)
    frame = row + (2 * info_ref[CHIP] + core) * rows
    live_ref[...] = (frame < info_ref[LENGTH]).astype(jnp.float32)
    run_copies(
        [(hidden_hbm.at[core], own_ref), (taps_hbm, taps_ref), (mod_hbm, mod_ref)], sems
    )


def front_kernel(
    info_ref, own_ref, partner_ref, near_ref, far_ref, taps_ref, mod_ref, weight_hbm,
    residual_ref, normed_ref, weight_ref, padded, sems,
):
    rows, width = own_ref.shape
    halo = near_ref.shape[1]
    total_rows = 2 * rows
    tiles = width // LANES
    parts = 8
    depth = width // parts
    loads = []
    for part in range(parts):
        here = pl.ds(part * depth, depth)
        loads.append(
            pltpu.make_async_copy(weight_hbm.at[here], weight_ref.at[here], sems.at[part])
        )
    for load in loads:
        load.start()
    length, core = info_ref[LENGTH], info_ref[CORE]
    offset = info_ref[CHIP] * total_rows
    span = total_rows + 2 * halo
    frame = offset - halo + lax.broadcasted_iota(jnp.int32, (span, LANES), 0)
    live = ((frame >= 0) & (frame < length)).astype(jnp.float32)
    first = halo - KERNEL // 2
    own_at = pl.ds(pl.multiple_of(halo + core * rows, 8), rows)
    partner_at = pl.ds(pl.multiple_of(halo + (1 - core) * rows, 8), rows)
    near_at = pl.ds(pl.multiple_of(core * (halo + total_rows), 8), halo)
    far_at = pl.ds(pl.multiple_of((1 - core) * (halo + total_rows), 8), halo)

    def convolve(tile, total):
        lanes = tile_lanes(tile)
        padded[near_at] = near_ref[core, :, lanes].astype(jnp.float32)
        padded[far_at] = far_ref[core, :, lanes].astype(jnp.float32)
        padded[own_at] = own_ref[:, lanes].astype(jnp.float32)
        padded[partner_at] = partner_ref[:, lanes].astype(jnp.float32)
        own = padded[halo : halo + total_rows]
        padded[...] = padded[...] * live
        acc = jnp.zeros((total_rows, LANES), jnp.float32)
        for tap in range(KERNEL):
            acc = acc + taps_ref[tap : tap + 1, lanes] * padded[
                first + tap : first + tap + total_rows
            ]
        grown = jnp.exp(jnp.minimum(acc, 20.0))
        product = grown * (grown + 2.0)
        value = own + acc * (product / (product + 2.0))
        residual_ref[:, lanes] = value
        return total + value

    total = lax.fori_loop(
        0, tiles, convolve, jnp.zeros((total_rows, LANES), jnp.float32), unroll=3
    )

    def store(lanes, value):
        normed_ref[:, lanes] = value.astype(jnp.bfloat16)

    row_norm(lambda tile: residual_ref[:, tile_lanes(tile)], store, tiles, mod_ref, 0, total)
    for load in loads:
        load.wait()


def project_kernel(firsts, origin, info_ref, normed_ref, weight_ref, cos_ref, sin_ref, *out_refs):
    rows = normed_ref.shape[0]
    attn = weight_ref.shape[1] // 3
    wide = 2 * LANES
    half = HEAD_DIM // 2
    cosine, sine = cos_ref[...], sin_ref[...]
    lower = lax.broadcasted_iota(jnp.int32, (rows, LANES), 1) % HEAD_DIM < half
    chip = info_ref[CHIP] if origin is None else origin
    swap = jnp.full((rows, LANES), chip & 1, jnp.int32) > 0
    for at, apart in enumerate(firsts):
        pair = (chip ^ apart) >> 1
        for part in range(3):
            start = part * attn + pair * wide
            both = jnp.dot(
                normed_ref[...],
                weight_ref[:, pl.ds(pl.multiple_of(start, wide), wide)],
                preferred_element_type=jnp.float32,
            )
            sides = []
            for side in range(2):
                value = both[:, side * LANES : (side + 1) * LANES]
                if part < 2:
                    swapped = jnp.where(
                        lower, pltpu.roll(value, LANES - half, 1), pltpu.roll(value, half, 1)
                    )
                    value = value * cosine + swapped * sine
                if part == 0:
                    value = value * HEAD_DIM**-0.5
                sides.append(value)
            out_refs[2 * at][part] = jnp.where(swap, sides[1], sides[0]).astype(jnp.bfloat16)
            out_refs[2 * at + 1][part] = jnp.where(swap, sides[0], sides[1]).astype(jnp.bfloat16)


def gather_keys(info_ref, got_refs, keys, values):
    _, rows, _ = got_refs[0].shape
    length, chip = info_ref[LENGTH], info_ref[CHIP]
    lane = lax.broadcasted_iota(jnp.int32, (rows, LANES), 1)
    row = lax.broadcasted_iota(jnp.int32, (rows, LANES), 0)
    for apart, got_ref in enumerate(got_refs):
        here = slice(apart * rows, (apart + 1) * rows)
        keys[here, :LANES] = got_ref[1]
        dead = (lane == 0) & (row + (chip ^ apart) * rows >= length)
        keys[here, LANES:] = jnp.where(dead, NEGATIVE, 0.0).astype(jnp.bfloat16)
        values[here, :] = got_ref[2]


def attend_rows(query_refs, keys, values, out_ref, queries):
    _, rows, _ = query_refs[0].shape
    low = lax.broadcasted_iota(jnp.int32, (rows, LANES), 1) < HEAD_DIM
    zero = jnp.zeros((rows, LANES), jnp.bfloat16)
    queries[:, LANES:] = jnp.where(
        lax.broadcasted_iota(jnp.int32, (queries.shape[0], LANES), 1) == 0, 1.0, 0.0
    ).astype(jnp.bfloat16)
    for at, query_ref in enumerate(query_refs):
        query = query_ref[0]
        base = 2 * at * rows
        queries[base : base + rows, :LANES] = jnp.where(low, query, zero)
        queries[base + rows : base + 2 * rows, :LANES] = jnp.where(low, zero, query)
    for first in range(0, len(query_refs), 2):
        base = 2 * first * rows
        scores = lax.dot_general(
            queries[base : base + 4 * rows, :], keys[...], (((1,), (1,)), ((), ())),
            preferred_element_type=jnp.float32,
        )
        weights = jnp.exp(scores - jnp.max(scores, axis=1, keepdims=True))
        weight_sum = jnp.sum(weights, axis=1, keepdims=True)
        mixed = jnp.dot(
            weights.astype(jnp.bfloat16), values[...], preferred_element_type=jnp.float32
        )
        mixed = mixed / weight_sum
        for side in range(2):
            base = 2 * side * rows
            out_ref[first + side] = jnp.where(
                low, mixed[base : base + rows], mixed[base + rows : base + 2 * rows]
            ).astype(jnp.bfloat16)


def attend_first_kernel(info_ref, *refs):
    chips = len(refs) - 4
    got_refs = refs[:chips]
    out_ref, keys, values, queries = refs[chips:]
    gather_keys(info_ref, got_refs, keys, values)
    attend_rows(got_refs[1::2], keys, values, out_ref, queries)


def attend_second_kernel(info_ref, keys, values, *refs):
    del info_ref
    attend_rows(refs[:-2], keys, values, refs[-2], refs[-1])


def merge_kernel(info_ref, own_ref, got_ref, *out_refs):
    del info_ref
    for at, out_ref in enumerate(out_refs):
        out_ref[0] = own_ref[at + 1]
        out_ref[1] = got_ref[at + 1]


def back_kernel(blocks, info_ref, residual, w_mel, mod_ref, w_out_ref, *refs):
    count = 1 + max(at for at, _, _ in blocks)
    got_refs = refs[:count]
    keep_ref, send_ref, attended, after, speed = refs[count:]
    rows, width = residual.shape
    tiles = width // LANES
    core, chip = info_ref[CORE], info_ref[CHIP]
    for at, place, apart in blocks:
        group = place if apart is None else chip ^ apart
        attended[:, tile_lanes(group)] = got_refs[at][place]
    wide = 2 * LANES
    total = jnp.zeros((rows, LANES), jnp.float32)
    for block in range(width // wide):
        lanes = slice(block * wide, (block + 1) * wide)
        branch = jnp.dot(attended[...], w_out_ref[:, lanes], preferred_element_type=jnp.float32)
        value = residual[:, lanes] + mod_ref[2:3, lanes] * branch
        after[:, lanes] = value
        total = total + value[:, :LANES] + value[:, LANES:]

    def store(lanes, value):
        after[:, lanes] = value

    row_norm(lambda tile: after[:, tile_lanes(tile)], store, tiles, mod_ref, 3, total)
    speed[...] = lax.dot_general(
        after[...].astype(jnp.bfloat16), w_mel[...], (((1,), (1,)), ((), ())),
        preferred_element_type=jnp.float32,
    )
    half = rows // 2
    keep_ref[...] = speed[pl.ds(pl.multiple_of(core * half, 8), half), :]
    send_ref[...] = speed[pl.ds(pl.multiple_of((1 - core) * half, 8), half), :]


def call(kernel, out_shape, inputs, scratch, hbm=()):
    single = not isinstance(out_shape, tuple)
    specs = [hbm_spec() if at in hbm else vmem_spec() for at in range(1, len(inputs))]
    inputs = list(inputs)
    for at in hbm:
        inputs[at] = pltpu.with_memory_space_constraint(inputs[at], pltpu.HBM)
    return pl.pallas_call(
        kernel,
        out_shape=out_shape,
        in_specs=[smem_spec()] + specs,
        out_specs=vmem_spec() if single else tuple(vmem_spec() for _ in out_shape),
        scratch_shapes=scratch,
        compiler_params=pltpu.CompilerParams(vmem_limit_bytes=GRANT),
    )(*inputs)


def array(shape, dtype=jnp.float32):
    return jax.ShapeDtypeStruct(shape, dtype)


def project(normed, w_qkv, tables, info, firsts, origin=None):
    shape = array((3, normed.shape[0], LANES), jnp.bfloat16)
    return call(
        functools.partial(project_kernel, tuple(firsts), origin),
        (shape,) * (2 * len(firsts)),
        (info, normed, w_qkv) + tables,
        [],
    )


def same_core(count):
    return [list(range(core, count, 2)) for core in range(2)]


def facing_pairs(clips, count):
    pairs = []
    for clip in range(clips):
        base = clip * count
        for at in range(1, count - 1, 2):
            pairs += [(base + at, base + at + 1), (base + at + 1, base + at)]
        if clip ^ 1 < clips:
            pairs += [(base + end, (clip ^ 1) * count + end) for end in (0, count - 1)]
    return pairs


def across(value, apart, count):
    return lax.ppermute(value, "seq", [(i, i ^ apart) for i in range(count)])


def to_groups(values, subs):
    rows, _ = values.shape
    grouped = values.reshape(subs, rows // subs, HEADS, HEAD_DIM).transpose(2, 0, 1, 3)
    return grouped.reshape(HEADS * subs, rows // subs, HEAD_DIM)


def from_groups(grouped, rows, subs):
    split = grouped.reshape(HEADS, subs, rows // subs, HEAD_DIM).transpose(1, 2, 0, 3)
    return split.reshape(rows, HEADS * HEAD_DIM)


def attend_blocks(queries, keys, values, live):
    groups, total, _ = queries.shape
    block = max(size for size in range(1, min(total, 1024) + 1) if total % size == 0)
    blocks = queries.reshape(groups, total // block, block, HEAD_DIM).transpose(1, 0, 2, 3)
    live = live[None, None, :]

    def one_block(query):
        scores = jnp.einsum("gqd,gkd->gqk", query, keys, preferred_element_type=jnp.float32)
        scores = jnp.where(live, scores, NEGATIVE)
        weights = jnp.exp(scores - jnp.max(scores, axis=-1, keepdims=True))
        weights = jnp.where(live, weights, 0.0)
        mixed = jnp.einsum(
            "gqk,gkd->gqd",
            weights.astype(jnp.bfloat16),
            values,
            preferred_element_type=jnp.float32,
        )
        return (mixed / jnp.sum(weights, axis=-1)[..., None]).astype(jnp.bfloat16)

    return lax.map(one_block, blocks).transpose(1, 0, 2, 3).reshape(groups, total, HEAD_DIM)


def attend_any(normed, w_qkv, tables, info, length, count):
    rows = normed.shape[0]
    chips = count // 2
    groups = HEADS * HEAD_DIM // LANES
    sent = project(normed, w_qkv, tables, info, range(0, groups, 2), 0)
    subs = max(1, chips // HEADS)
    chip = lax.axis_index("seq") >> 1
    part_rows = rows // subs

    def exchange(part):
        whole = jnp.concatenate([group[part] for group in sent], axis=1)
        return lax.all_to_all(
            to_groups(whole, subs), "seq", split_axis=0, concat_axis=1, tiled=True,
            axis_index_groups=same_core(count),
        )

    queries, keys, values = (exchange(part) for part in range(3))

    def frames_of(sub):
        start = jnp.arange(chips, dtype=jnp.int32)[:, None] * rows + sub * part_rows
        return (start + jnp.arange(part_rows, dtype=jnp.int32)[None, :]).reshape(-1)

    frames = [frames_of(chip % subs)]
    parts = [(keys, values)]
    for apart in range(1, subs):
        perm = []
        for i in range(count):
            at = i // 2
            target = at - at % subs + (at + apart) % subs
            perm.append((i, 2 * target + i % 2))
        parts.append(tuple(lax.ppermute(part, "seq", perm) for part in (keys, values)))
        frames.append(frames_of((chip - apart) % subs))
    keys = jnp.concatenate([part[0] for part in parts], axis=1)
    values = jnp.concatenate([part[1] for part in parts], axis=1)
    attended = attend_blocks(queries, keys, values, jnp.concatenate(frames) < length)
    back = lax.all_to_all(
        attended, "seq", split_axis=1, concat_axis=0, tiled=True,
        axis_index_groups=same_core(count),
    )
    return from_groups(back, rows, subs).reshape(rows, groups, LANES).transpose(1, 0, 2)


def chips_hold_groups(count):
    chips = count // 2
    return chips == HEADS * HEAD_DIM // LANES and chips >= 4 and chips & (chips - 1) == 0


def send_order(chips):
    far = list(range(chips // 2, chips, 2))
    return far[:1] + list(range(2, chips // 2, 2)) + far[1:] + [0]


def attend_chips(normed, w_qkv, tables, info, count):
    rows = normed.shape[0]
    chips = count // 2
    held = {}
    for first in send_order(chips):
        made = project(normed, w_qkv, tables, info, [first])
        for side in range(2):
            apart = first + side
            held[apart] = across(made[side], 2 * apart, count) if apart else made[side]
    total, half = chips * rows, chips // 2
    queries = VMEM((total, 2 * LANES), jnp.bfloat16)
    crossing, keys, values = call(
        attend_first_kernel,
        (
            array((half, rows, LANES), jnp.bfloat16),
            array((total, 2 * LANES), jnp.bfloat16),
            array((total, LANES), jnp.bfloat16),
        ),
        (info,) + tuple(held[apart] for apart in range(chips)),
        [queries],
    )
    crossed = across(crossing, 2, count)
    staying = call(
        attend_second_kernel,
        array((half, rows, LANES), jnp.bfloat16),
        (info, keys, values) + tuple(held[apart] for apart in range(0, chips, 2)),
        [queries],
    )
    joined = call(
        merge_kernel,
        (array((2, rows, LANES), jnp.bfloat16),) * (half - 1),
        (info, staying, crossed),
        [],
    )
    back, blocks = [staying, crossed], [(0, 0, 0), (1, 0, 1)]
    apart_first = sorted(range(1, half), reverse=True)
    got = {apart: across(joined[apart - 1], 4 * apart, count) for apart in apart_first}
    for apart in range(1, half):
        blocks += [(len(back), side, 2 * apart + side) for side in range(2)]
        back.append(got[apart])
    return back, blocks


def per_device(
    hidden, latent, lengths, step_index, guidance, modulation, conv_kernel, w_qkv, w_out, w_mel
):
    copies, rows, width = hidden.shape
    count = lax.axis_size("seq")
    index = lax.axis_index("seq").astype(jnp.int32)
    chip, core = index >> 1, index & 1
    chip_rows = 2 * rows
    info = jnp.stack([core, chip, lengths[0]])

    edges = lax.dynamic_slice(hidden, (0, core * (rows - HALO), 0), (copies, HALO, width))
    partner = lax.dynamic_slice(hidden, (1 - core, 0, 0), (1, rows, width))[0]
    near = lax.ppermute(edges, ("clip", "seq"), facing_pairs(lax.axis_size("clip"), count))
    far = across(near, 1, count)
    partner = across(partner, 1, count)
    own, taps, mods, is_first, live = call(
        stage_kernel,
        (
            array((rows, width), jnp.bfloat16),
            array(conv_kernel.shape),
            array(modulation.shape),
            array(latent.shape),
            array(latent.shape),
        ),
        (info, hidden, conv_kernel, modulation),
        [pltpu.SemaphoreType.DMA((3,))],
        hbm=(1, 2, 3),
    )
    tables = rotary_tables(chip * chip_rows + jnp.arange(chip_rows, dtype=jnp.int32))
    residual, normed, weight = call(
        front_kernel,
        (
            array((chip_rows, width)),
            array((chip_rows, width), jnp.bfloat16),
            array(w_qkv.shape, jnp.bfloat16),
        ),
        (info, own, partner, near, far, taps, mods, w_qkv),
        [VMEM((chip_rows + 2 * HALO, LANES), jnp.float32), pltpu.SemaphoreType.DMA((8,))],
        hbm=(7,),
    )
    if chips_hold_groups(count):
        back, blocks = attend_chips(normed, weight, tables, info, count)
    else:
        back = [attend_any(normed, weight, tables, info, lengths[0], count)]
        blocks = [(0, group, None) for group in range(back[0].shape[0])]
    mels = w_mel.shape[1]
    keep, send = call(
        functools.partial(back_kernel, tuple(blocks)),
        (array((rows, mels)),) * 2,
        (info, residual, w_mel.T, mods, w_out) + tuple(back),
        [
            VMEM((chip_rows, HEADS * HEAD_DIM), jnp.bfloat16),
            VMEM((chip_rows, width), jnp.float32),
            VMEM((chip_rows, mels), jnp.float32),
        ],
    )
    other = across(send, 1, count)
    first = jnp.where(is_first > 0.5, keep, other)
    second = jnp.where(is_first > 0.5, other, keep)
    guided = first + guidance[0] * (first - second)
    velocity = jnp.where(live > 0.5, guided, 0.0)
    progress = step_index[0].astype(jnp.float32) / STEPS
    time_now = 1.0 - jnp.cos(0.5 * jnp.pi * progress)
    return (velocity, latent + (1.0 - time_now) * velocity)


def solution(mesh):
    return jax.shard_map(
        per_device,
        mesh=mesh,
        in_specs=(
            P(None, ("clip", "seq"), None),
            P(("clip", "seq"), None),
            P("clip"),
            P(),
            P(),
            P(),
            P(),
            P(),
            P(),
            P(),
        ),
        out_specs=(P(("clip", "seq"), None), P(("clip", "seq"), None)),
        check_vma=False,
    )
```

```python
import functools

import jax
import jax.numpy as jnp
from jax import lax
from jax.experimental import pallas as pl
from jax.experimental.pallas import tpu as pltpu
from jax.sharding import PartitionSpec as P


HEADS = 16
HEAD_DIM = 64
KERNEL = 31
STEPS = 32
LANES = 128
HALO = 16


EPSILON = 1e-06
NEGATIVE = -1e30
CORE, CHIP, LENGTH = 0, 1, 2
VMEM = pltpu.VMEM
SMEM = pltpu.SMEM
GRANT = 12 << 20


def vmem_spec():
    return pl.BlockSpec(memory_space=VMEM)


def smem_spec():
    return pl.BlockSpec(memory_space=SMEM)


def rotary_tables(positions):
    half_dim = HEAD_DIM // 2
    lane = jnp.arange(LANES, dtype=jnp.int32)
    inverse = 10000.0 ** (-(lane % half_dim).astype(jnp.float32) / half_dim)
    angles = positions.astype(jnp.float32)[:, None] * inverse[None, :]
    sign = jnp.where(lane % HEAD_DIM < half_dim, -1.0, 1.0)
    return jnp.cos(angles), jnp.sin(angles) * sign[None, :]


def hbm_spec():
    return pl.BlockSpec(memory_space=pltpu.HBM)


def tile_lanes(tile):
    return pl.ds(pl.multiple_of(tile * LANES, LANES), LANES)


def row_norm(load, store, tiles, mod_ref, row, total):
    width = tiles * LANES
    mean = jnp.sum(total, axis=-1, keepdims=True) * (1.0 / width)

    def square(tile, acc):
        centered = load(tile) - mean
        return acc + centered * centered

    squares = lax.fori_loop(0, tiles, square, jnp.zeros(total.shape, jnp.float32), unroll=6)
    variance = jnp.sum(squares, axis=-1, keepdims=True) * (1.0 / width)
    factor = lax.rsqrt(variance + EPSILON)

    def write(tile, carry):
        lanes = tile_lanes(tile)
        scale = 1.0 + mod_ref[row + 1 : row + 2, lanes]
        shift = mod_ref[row : row + 1, lanes]
        store(lanes, (load(tile) - mean) * factor * scale + shift)
        return carry

    lax.fori_loop(0, tiles, write, 0, unroll=6)


def run_copies(pairs, sems):
    copies = [
        pltpu.make_async_copy(source, target, sems.at[at])
        for at, (source, target) in enumerate(pairs)
    ]
    for copy in copies:
        copy.start()
    for copy in copies:
        copy.wait()


def stage_kernel(
    info_ref, hidden_hbm, taps_hbm, mod_hbm, own_ref, taps_ref, mod_ref, first_ref, live_ref, sems
):
    rows = own_ref.shape[0]
    core = info_ref[CORE]
    first_ref[...] = jnp.zeros(first_ref.shape, jnp.float32) + (1 - core).astype(jnp.float32)
    row = lax.broadcasted_iota(jnp.int32, live_ref.shape, 0)
    frame = row + (2 * info_ref[CHIP] + core) * rows
    live_ref[...] = (frame < info_ref[LENGTH]).astype(jnp.float32)
    run_copies(
        [(hidden_hbm.at[core], own_ref), (taps_hbm, taps_ref), (mod_hbm, mod_ref)], sems
    )


def front_kernel(
    info_ref, own_ref, partner_ref, near_ref, far_ref, taps_ref, mod_ref, weight_hbm,
    residual_ref, normed_ref, weight_ref, padded, sems,
):
    rows, width = own_ref.shape
    halo = near_ref.shape[1]
    total_rows = 2 * rows
    tiles = width // LANES
    parts = 8
    depth = width // parts
    loads = []
    for part in range(parts):
        here = pl.ds(part * depth, depth)
        loads.append(
            pltpu.make_async_copy(weight_hbm.at[here], weight_ref.at[here], sems.at[part])
        )
    for load in loads:
        load.start()
    length, core = info_ref[LENGTH], info_ref[CORE]
    offset = info_ref[CHIP] * total_rows
    span = total_rows + 2 * halo
    frame = offset - halo + lax.broadcasted_iota(jnp.int32, (span, LANES), 0)
    live = ((frame >= 0) & (frame < length)).astype(jnp.float32)
    first = halo - KERNEL // 2
    own_at = pl.ds(pl.multiple_of(halo + core * rows, 8), rows)
    partner_at = pl.ds(pl.multiple_of(halo + (1 - core) * rows, 8), rows)
    near_at = pl.ds(pl.multiple_of(core * (halo + total_rows), 8), halo)
    far_at = pl.ds(pl.multiple_of((1 - core) * (halo + total_rows), 8), halo)

    def convolve(tile, total):
        lanes = tile_lanes(tile)
        padded[near_at] = near_ref[core, :, lanes].astype(jnp.float32)
        padded[far_at] = far_ref[core, :, lanes].astype(jnp.float32)
        padded[own_at] = own_ref[:, lanes].astype(jnp.float32)
        padded[partner_at] = partner_ref[:, lanes].astype(jnp.float32)
        own = padded[halo : halo + total_rows]
        padded[...] = padded[...] * live
        acc = jnp.zeros((total_rows, LANES), jnp.float32)
        for tap in range(KERNEL):
            acc = acc + taps_ref[tap : tap + 1, lanes] * padded[
                first + tap : first + tap + total_rows
            ]
        grown = jnp.exp(jnp.minimum(acc, 20.0))
        product = grown * (grown + 2.0)
        value = own + acc * (product / (product + 2.0))
        residual_ref[:, lanes] = value
        return total + value

    total = lax.fori_loop(
        0, tiles, convolve, jnp.zeros((total_rows, LANES), jnp.float32), unroll=3
    )

    def store(lanes, value):
        normed_ref[:, lanes] = value.astype(jnp.bfloat16)

    row_norm(lambda tile: residual_ref[:, tile_lanes(tile)], store, tiles, mod_ref, 0, total)
    for load in loads:
        load.wait()


def project_kernel(firsts, origin, info_ref, normed_ref, weight_ref, cos_ref, sin_ref, *out_refs):
    rows = normed_ref.shape[0]
    attn = weight_ref.shape[1] // 3
    wide = 2 * LANES
    half = HEAD_DIM // 2
    cosine, sine = cos_ref[...], sin_ref[...]
    lower = lax.broadcasted_iota(jnp.int32, (rows, LANES), 1) % HEAD_DIM < half
    chip = info_ref[CHIP] if origin is None else origin
    swap = jnp.full((rows, LANES), chip & 1, jnp.int32) > 0
    for at, apart in enumerate(firsts):
        pair = (chip ^ apart) >> 1
        for part in range(3):
            start = part * attn + pair * wide
            both = jnp.dot(
                normed_ref[...],
                weight_ref[:, pl.ds(pl.multiple_of(start, wide), wide)],
                preferred_element_type=jnp.float32,
            )
            sides = []
            for side in range(2):
                value = both[:, side * LANES : (side + 1) * LANES]
                if part < 2:
                    swapped = jnp.where(
                        lower, pltpu.roll(value, LANES - half, 1), pltpu.roll(value, half, 1)
                    )
                    value = value * cosine + swapped * sine
                if part == 0:
                    value = value * HEAD_DIM**-0.5
                sides.append(value)
            out_refs[2 * at][part] = jnp.where(swap, sides[1], sides[0]).astype(jnp.bfloat16)
            out_refs[2 * at + 1][part] = jnp.where(swap, sides[0], sides[1]).astype(jnp.bfloat16)


def place_keys(info_ref, apart, got_ref, keys, values, first):
    _, rows, _ = got_ref.shape
    chip = info_ref[CHIP] ^ apart
    lane = lax.broadcasted_iota(jnp.int32, (rows, LANES), 1)
    row = lax.broadcasted_iota(jnp.int32, (rows, LANES), 0)
    here = slice(first, first + rows)
    keys[here, :LANES] = got_ref[1]
    dead = (lane == 0) & (row + chip * rows >= info_ref[LENGTH])
    keys[here, LANES:] = jnp.where(dead, NEGATIVE, 0.0).astype(jnp.bfloat16)
    values[here, :] = got_ref[2]


def place_queries(query_refs, queries):
    _, rows, _ = query_refs[0].shape
    low = lax.broadcasted_iota(jnp.int32, (rows, LANES), 1) < HEAD_DIM
    zero = jnp.zeros((rows, LANES), jnp.bfloat16)
    queries[:, LANES:] = jnp.where(
        lax.broadcasted_iota(jnp.int32, (queries.shape[0], LANES), 1) == 0, 1.0, 0.0
    ).astype(jnp.bfloat16)
    for at, query_ref in enumerate(query_refs):
        query = query_ref[0]
        base = 2 * at * rows
        queries[base : base + rows, :LANES] = jnp.where(low, query, zero)
        queries[base + rows : base + 2 * rows, :LANES] = jnp.where(low, zero, query)


def score(queries, keys):
    return lax.dot_general(
        queries, keys, (((1,), (1,)), ((), ())), preferred_element_type=jnp.float32
    )


def mix(weights, values):
    return jnp.dot(weights.astype(jnp.bfloat16), values, preferred_element_type=jnp.float32)


def store_heads(mixed, out_ref, first):
    _, rows, _ = out_ref.shape
    low = lax.broadcasted_iota(jnp.int32, (rows, LANES), 1) < HEAD_DIM
    for at in range(mixed.shape[0] // (2 * rows)):
        base = 2 * at * rows
        out_ref[first + at] = jnp.where(
            low, mixed[base : base + rows], mixed[base + rows : base + 2 * rows]
        ).astype(jnp.bfloat16)


def attend_rows(keys, values, queries, out_ref, first):
    _, rows, _ = out_ref.shape
    total = queries.shape[0]
    for base in range(0, total, 4 * rows):
        block = slice(base, min(base + 4 * rows, total))
        scores = score(queries[block, :], keys[...])
        weights = jnp.exp(scores - jnp.max(scores, axis=1, keepdims=True))
        weight_sum = jnp.sum(weights, axis=1, keepdims=True)
        store_heads(mix(weights, values[...]) / weight_sum, out_ref, first + base // (2 * rows))


def attend_early_kernel(info_ref, *refs):
    chips = len(refs) - 6
    got_refs = refs[:chips]
    keys, values, queries, mixed_ref, peak_ref, sum_ref = refs[chips:]
    _, rows, _ = got_refs[0].shape
    for apart, got_ref in enumerate(got_refs):
        place_keys(info_ref, apart, got_ref, keys, values, apart * rows)
    place_queries(got_refs[1::2], queries)
    scores = score(queries[...], keys[...])
    peak = jnp.max(scores, axis=1, keepdims=True)
    weights = jnp.exp(scores - peak)
    peak_ref[...] = jnp.broadcast_to(peak, peak_ref.shape)
    sum_ref[...] = jnp.broadcast_to(jnp.sum(weights, axis=1, keepdims=True), sum_ref.shape)
    mixed_ref[...] = mix(weights, values[...])


def attend_last_kernel(
    info_ref, early_keys, early_values, early_queries, mixed_ref, peak_ref, sum_ref, last_ref,
    out_ref, keys, values, queries,
):
    held, _ = early_values.shape
    _, rows, _ = last_ref.shape
    keys[:held, :] = early_keys[...]
    values[:held, :] = early_values[...]
    place_keys(info_ref, held // rows, last_ref, keys, values, held)
    place_queries([last_ref], queries)
    attend_rows(keys, values, queries, out_ref, out_ref.shape[0] - 1)
    scores = score(early_queries[...], keys[held:, :])
    peak = peak_ref[...]
    joined = jnp.maximum(peak, jnp.max(scores, axis=1, keepdims=True))
    scale = jnp.exp(peak - joined)
    weights = jnp.exp(scores - joined[:, : scores.shape[1]])
    weight_sum = sum_ref[...] * scale + jnp.sum(weights, axis=1, keepdims=True)
    mixed = mixed_ref[...] * scale + mix(weights, values[held:, :])
    store_heads(mixed / weight_sum, out_ref, 0)


def attend_second_kernel(info_ref, keys, values, *refs):
    del info_ref
    out_ref, queries = refs[-2:]
    place_queries(refs[:-2], queries)
    attend_rows(keys, values, queries, out_ref, 0)


def merge_kernel(info_ref, own_ref, got_ref, *out_refs):
    del info_ref
    for at, out_ref in enumerate(out_refs):
        out_ref[0] = own_ref[at + 1]
        out_ref[1] = got_ref[at + 1]


def back_kernel(blocks, info_ref, residual, w_mel, mod_ref, w_out_ref, *refs):
    count = 1 + max(at for at, _, _ in blocks)
    got_refs = refs[:count]
    keep_ref, send_ref, attended, after, speed = refs[count:]
    rows, width = residual.shape
    tiles = width // LANES
    core, chip = info_ref[CORE], info_ref[CHIP]
    for at, place, apart in blocks:
        group = place if apart is None else chip ^ apart
        attended[:, tile_lanes(group)] = got_refs[at][place]
    wide = 2 * LANES
    total = jnp.zeros((rows, LANES), jnp.float32)
    for block in range(width // wide):
        lanes = slice(block * wide, (block + 1) * wide)
        branch = jnp.dot(attended[...], w_out_ref[:, lanes], preferred_element_type=jnp.float32)
        value = residual[:, lanes] + mod_ref[2:3, lanes] * branch
        after[:, lanes] = value
        total = total + value[:, :LANES] + value[:, LANES:]

    def store(lanes, value):
        after[:, lanes] = value

    row_norm(lambda tile: after[:, tile_lanes(tile)], store, tiles, mod_ref, 3, total)
    speed[...] = lax.dot_general(
        after[...].astype(jnp.bfloat16), w_mel[...], (((1,), (1,)), ((), ())),
        preferred_element_type=jnp.float32,
    )
    half = rows // 2
    keep_ref[...] = speed[pl.ds(pl.multiple_of(core * half, 8), half), :]
    send_ref[...] = speed[pl.ds(pl.multiple_of((1 - core) * half, 8), half), :]


def call(kernel, out_shape, inputs, scratch, hbm=()):
    single = not isinstance(out_shape, tuple)
    specs = [hbm_spec() if at in hbm else vmem_spec() for at in range(1, len(inputs))]
    inputs = list(inputs)
    for at in hbm:
        inputs[at] = pltpu.with_memory_space_constraint(inputs[at], pltpu.HBM)
    return pl.pallas_call(
        kernel,
        out_shape=out_shape,
        in_specs=[smem_spec()] + specs,
        out_specs=vmem_spec() if single else tuple(vmem_spec() for _ in out_shape),
        scratch_shapes=scratch,
        compiler_params=pltpu.CompilerParams(vmem_limit_bytes=GRANT),
    )(*inputs)


def array(shape, dtype=jnp.float32):
    return jax.ShapeDtypeStruct(shape, dtype)


def project(normed, w_qkv, tables, info, firsts, origin=None):
    shape = array((3, normed.shape[0], LANES), jnp.bfloat16)
    return call(
        functools.partial(project_kernel, tuple(firsts), origin),
        (shape,) * (2 * len(firsts)),
        (info, normed, w_qkv) + tables,
        [],
    )


def same_core(count):
    return [list(range(core, count, 2)) for core in range(2)]


def facing_pairs(clips, count):
    pairs = []
    for clip in range(clips):
        base = clip * count
        for at in range(1, count - 1, 2):
            pairs += [(base + at, base + at + 1), (base + at + 1, base + at)]
        if clip ^ 1 < clips:
            pairs += [(base + end, (clip ^ 1) * count + end) for end in (0, count - 1)]
    return pairs


def across(value, apart, count):
    return lax.ppermute(value, "seq", [(i, i ^ apart) for i in range(count)])


def to_groups(values, subs):
    rows, _ = values.shape
    grouped = values.reshape(subs, rows // subs, HEADS, HEAD_DIM).transpose(2, 0, 1, 3)
    return grouped.reshape(HEADS * subs, rows // subs, HEAD_DIM)


def from_groups(grouped, rows, subs):
    split = grouped.reshape(HEADS, subs, rows // subs, HEAD_DIM).transpose(1, 2, 0, 3)
    return split.reshape(rows, HEADS * HEAD_DIM)


def attend_blocks(queries, keys, values, live):
    groups, total, _ = queries.shape
    block = max(size for size in range(1, min(total, 1024) + 1) if total % size == 0)
    blocks = queries.reshape(groups, total // block, block, HEAD_DIM).transpose(1, 0, 2, 3)
    live = live[None, None, :]

    def one_block(query):
        scores = jnp.einsum("gqd,gkd->gqk", query, keys, preferred_element_type=jnp.float32)
        scores = jnp.where(live, scores, NEGATIVE)
        weights = jnp.exp(scores - jnp.max(scores, axis=-1, keepdims=True))
        weights = jnp.where(live, weights, 0.0)
        mixed = jnp.einsum(
            "gqk,gkd->gqd",
            weights.astype(jnp.bfloat16),
            values,
            preferred_element_type=jnp.float32,
        )
        return (mixed / jnp.sum(weights, axis=-1)[..., None]).astype(jnp.bfloat16)

    return lax.map(one_block, blocks).transpose(1, 0, 2, 3).reshape(groups, total, HEAD_DIM)


def attend_any(normed, w_qkv, tables, info, length, count):
    rows = normed.shape[0]
    chips = count // 2
    groups = HEADS * HEAD_DIM // LANES
    sent = project(normed, w_qkv, tables, info, range(0, groups, 2), 0)
    subs = max(1, chips // HEADS)
    chip = lax.axis_index("seq") >> 1
    part_rows = rows // subs

    def exchange(part):
        whole = jnp.concatenate([group[part] for group in sent], axis=1)
        return lax.all_to_all(
            to_groups(whole, subs), "seq", split_axis=0, concat_axis=1, tiled=True,
            axis_index_groups=same_core(count),
        )

    queries, keys, values = (exchange(part) for part in range(3))

    def frames_of(sub):
        start = jnp.arange(chips, dtype=jnp.int32)[:, None] * rows + sub * part_rows
        return (start + jnp.arange(part_rows, dtype=jnp.int32)[None, :]).reshape(-1)

    frames = [frames_of(chip % subs)]
    parts = [(keys, values)]
    for apart in range(1, subs):
        perm = []
        for i in range(count):
            at = i // 2
            target = at - at % subs + (at + apart) % subs
            perm.append((i, 2 * target + i % 2))
        parts.append(tuple(lax.ppermute(part, "seq", perm) for part in (keys, values)))
        frames.append(frames_of((chip - apart) % subs))
    keys = jnp.concatenate([part[0] for part in parts], axis=1)
    values = jnp.concatenate([part[1] for part in parts], axis=1)
    attended = attend_blocks(queries, keys, values, jnp.concatenate(frames) < length)
    back = lax.all_to_all(
        attended, "seq", split_axis=1, concat_axis=0, tiled=True,
        axis_index_groups=same_core(count),
    )
    return from_groups(back, rows, subs).reshape(rows, groups, LANES).transpose(1, 0, 2)


def chips_hold_groups(count):
    chips = count // 2
    return chips == HEADS * HEAD_DIM // LANES and chips >= 4 and chips & (chips - 1) == 0


def send_order(chips):
    far = list(range(chips // 2, chips, 2))
    return far[:1] + list(range(2, chips // 2, 2)) + far[1:] + [0]


def attend_chips(normed, w_qkv, tables, info, count):
    rows = normed.shape[0]
    chips = count // 2
    held = {}
    for first in send_order(chips):
        made = project(normed, w_qkv, tables, info, [first])
        for side in range(2):
            apart = first + side
            held[apart] = across(made[side], 2 * apart, count) if apart else made[side]
    total, half = chips * rows, chips // 2
    early, early_rows = total - rows, 2 * (half - 1) * rows
    parts = call(
        attend_early_kernel,
        (
            array((early, 2 * LANES), jnp.bfloat16),
            array((early, LANES), jnp.bfloat16),
            array((early_rows, 2 * LANES), jnp.bfloat16),
        )
        + (array((early_rows, LANES)),) * 3,
        (info,) + tuple(held[apart] for apart in range(chips - 1)),
        [],
    )
    crossing, keys, values = call(
        attend_last_kernel,
        (
            array((half, rows, LANES), jnp.bfloat16),
            array((total, 2 * LANES), jnp.bfloat16),
            array((total, LANES), jnp.bfloat16),
        ),
        (info,) + tuple(parts) + (held[chips - 1],),
        [VMEM((2 * rows, 2 * LANES), jnp.bfloat16)],
    )
    crossed = across(crossing, 2, count)
    staying = call(
        attend_second_kernel,
        array((half, rows, LANES), jnp.bfloat16),
        (info, keys, values) + tuple(held[apart] for apart in range(0, chips, 2)),
        [VMEM((total, 2 * LANES), jnp.bfloat16)],
    )
    joined = call(
        merge_kernel,
        (array((2, rows, LANES), jnp.bfloat16),) * (half - 1),
        (info, staying, crossed),
        [],
    )
    back, blocks = [staying, crossed], [(0, 0, 0), (1, 0, 1)]
    apart_first = sorted(range(1, half), reverse=True)
    got = {apart: across(joined[apart - 1], 4 * apart, count) for apart in apart_first}
    for apart in range(1, half):
        blocks += [(len(back), side, 2 * apart + side) for side in range(2)]
        back.append(got[apart])
    return back, blocks


def per_device(
    hidden, latent, lengths, step_index, guidance, modulation, conv_kernel, w_qkv, w_out, w_mel
):
    copies, rows, width = hidden.shape
    count = lax.axis_size("seq")
    index = lax.axis_index("seq").astype(jnp.int32)
    chip, core = index >> 1, index & 1
    chip_rows = 2 * rows
    info = jnp.stack([core, chip, lengths[0]])

    edges = lax.dynamic_slice(hidden, (0, core * (rows - HALO), 0), (copies, HALO, width))
    partner = lax.dynamic_slice(hidden, (1 - core, 0, 0), (1, rows, width))[0]
    near = lax.ppermute(edges, ("clip", "seq"), facing_pairs(lax.axis_size("clip"), count))
    far = across(near, 1, count)
    partner = across(partner, 1, count)
    own, taps, mods, is_first, live = call(
        stage_kernel,
        (
            array((rows, width), jnp.bfloat16),
            array(conv_kernel.shape),
            array(modulation.shape),
            array(latent.shape),
            array(latent.shape),
        ),
        (info, hidden, conv_kernel, modulation),
        [pltpu.SemaphoreType.DMA((3,))],
        hbm=(1, 2, 3),
    )
    tables = rotary_tables(chip * chip_rows + jnp.arange(chip_rows, dtype=jnp.int32))
    residual, normed, weight = call(
        front_kernel,
        (
            array((chip_rows, width)),
            array((chip_rows, width), jnp.bfloat16),
            array(w_qkv.shape, jnp.bfloat16),
        ),
        (info, own, partner, near, far, taps, mods, w_qkv),
        [VMEM((chip_rows + 2 * HALO, LANES), jnp.float32), pltpu.SemaphoreType.DMA((8,))],
        hbm=(7,),
    )
    if chips_hold_groups(count):
        back, blocks = attend_chips(normed, weight, tables, info, count)
    else:
        back = [attend_any(normed, weight, tables, info, lengths[0], count)]
        blocks = [(0, group, None) for group in range(back[0].shape[0])]
    mels = w_mel.shape[1]
    keep, send = call(
        functools.partial(back_kernel, tuple(blocks)),
        (array((rows, mels)),) * 2,
        (info, residual, w_mel.T, mods, w_out) + tuple(back),
        [
            VMEM((chip_rows, HEADS * HEAD_DIM), jnp.bfloat16),
            VMEM((chip_rows, width), jnp.float32),
            VMEM((chip_rows, mels), jnp.float32),
        ],
    )
    other = across(send, 1, count)
    first = jnp.where(is_first > 0.5, keep, other)
    second = jnp.where(is_first > 0.5, other, keep)
    guided = first + guidance[0] * (first - second)
    velocity = jnp.where(live > 0.5, guided, 0.0)
    progress = step_index[0].astype(jnp.float32) / STEPS
    time_now = 1.0 - jnp.cos(0.5 * jnp.pi * progress)
    return (velocity, latent + (1.0 - time_now) * velocity)


def solution(mesh):
    return jax.shard_map(
        per_device,
        mesh=mesh,
        in_specs=(
            P(None, ("clip", "seq"), None),
            P(("clip", "seq"), None),
            P("clip"),
            P(),
            P(),
            P(),
            P(),
            P(),
            P(),
            P(),
        ),
        out_specs=(P(("clip", "seq"), None), P(("clip", "seq"), None)),
        check_vma=False,
    )
```

```python
import functools

import jax
import jax.numpy as jnp
from jax import lax
from jax.experimental import pallas as pl
from jax.experimental.pallas import tpu as pltpu
from jax.sharding import PartitionSpec as P


HEADS = 16
HEAD_DIM = 64
KERNEL = 31
STEPS = 32
LANES = 128
HALO = 16


EPSILON = 1e-06
NEGATIVE = -1e30
CORE, CHIP, LENGTH = 0, 1, 2
VMEM = pltpu.VMEM
SMEM = pltpu.SMEM
GRANT = 12 << 20


def vmem_spec():
    return pl.BlockSpec(memory_space=VMEM)


def smem_spec():
    return pl.BlockSpec(memory_space=SMEM)


def rotary_rates():
    half_dim = HEAD_DIM // 2
    lane = jnp.arange(LANES, dtype=jnp.int32)
    inverse = 10000.0 ** (-(lane % half_dim).astype(jnp.float32) / half_dim)
    sign = jnp.where(lane % HEAD_DIM < half_dim, -1.0, 1.0)
    return jnp.stack([inverse, sign])


def hbm_spec():
    return pl.BlockSpec(memory_space=pltpu.HBM)


def tile_lanes(tile):
    return pl.ds(pl.multiple_of(tile * LANES, LANES), LANES)


def row_norm(load, store, tiles, mod_ref, row, total):
    width = tiles * LANES
    mean = jnp.sum(total, axis=-1, keepdims=True) * (1.0 / width)

    def square(tile, acc):
        centered = load(tile) - mean
        return acc + centered * centered

    squares = lax.fori_loop(0, tiles, square, jnp.zeros(total.shape, jnp.float32), unroll=6)
    variance = jnp.sum(squares, axis=-1, keepdims=True) * (1.0 / width)
    factor = lax.rsqrt(variance + EPSILON)

    def write(tile, carry):
        lanes = tile_lanes(tile)
        scale = 1.0 + mod_ref[row + 1 : row + 2, lanes]
        shift = mod_ref[row : row + 1, lanes]
        store(lanes, (load(tile) - mean) * factor * scale + shift)
        return carry

    lax.fori_loop(0, tiles, write, 0, unroll=6)


def run_copies(pairs, sems):
    copies = [
        pltpu.make_async_copy(source, target, sems.at[at])
        for at, (source, target) in enumerate(pairs)
    ]
    for copy in copies:
        copy.start()
    for copy in copies:
        copy.wait()


def start_loads(source, first, target, sems):
    parts = sems.shape[0]
    depth = target.shape[0] // parts
    loads = [
        pltpu.make_async_copy(
            source.at[pl.ds(first + part * depth, depth)],
            target.at[pl.ds(part * depth, depth)],
            sems.at[part],
        )
        for part in range(parts)
    ]
    for load in loads:
        load.start()
    return loads


def stage_kernel(
    info_ref, hidden_hbm, taps_hbm, mod_hbm, own_ref, taps_ref, mod_ref, first_ref, live_ref, sems
):
    rows = own_ref.shape[0]
    core = info_ref[CORE]
    first_ref[...] = jnp.zeros(first_ref.shape, jnp.float32) + (1 - core).astype(jnp.float32)
    row = lax.broadcasted_iota(jnp.int32, live_ref.shape, 0)
    frame = row + (2 * info_ref[CHIP] + core) * rows
    live_ref[...] = (frame < info_ref[LENGTH]).astype(jnp.float32)
    run_copies(
        [(hidden_hbm.at[core], own_ref), (taps_hbm, taps_ref), (mod_hbm, mod_ref)], sems
    )


def load_kernel(info_ref, rates_ref, weight_hbm, weight_ref, cos_ref, sin_ref, sems):
    rows = cos_ref.shape[0]
    loads = start_loads(weight_hbm, 0, weight_ref, sems)
    frame = info_ref[CHIP] * rows + lax.broadcasted_iota(jnp.int32, (rows, LANES), 0)
    angles = frame.astype(jnp.float32) * rates_ref[0:1, :]
    cos_ref[...] = jnp.cos(angles)
    sin_ref[...] = jnp.sin(angles) * rates_ref[1:2, :]
    for load in loads:
        load.wait()


def front_kernel(
    info_ref, own_ref, partner_ref, near_ref, far_ref, taps_ref, mod_ref, weight_hbm,
    residual_ref, normed_ref, weight_ref, padded, sems,
):
    rows, width = own_ref.shape
    halo = near_ref.shape[1]
    total_rows = 2 * rows
    tiles = width // LANES
    loads = start_loads(weight_hbm, width - weight_ref.shape[0], weight_ref, sems)
    length, core = info_ref[LENGTH], info_ref[CORE]
    offset = info_ref[CHIP] * total_rows
    span = total_rows + 2 * halo
    frame = offset - halo + lax.broadcasted_iota(jnp.int32, (span, LANES), 0)
    live = ((frame >= 0) & (frame < length)).astype(jnp.float32)
    first = halo - KERNEL // 2
    own_at = pl.ds(pl.multiple_of(halo + core * rows, 8), rows)
    partner_at = pl.ds(pl.multiple_of(halo + (1 - core) * rows, 8), rows)
    near_at = pl.ds(pl.multiple_of(core * (halo + total_rows), 8), halo)
    far_at = pl.ds(pl.multiple_of((1 - core) * (halo + total_rows), 8), halo)

    def convolve(tile, total):
        lanes = tile_lanes(tile)
        padded[near_at] = near_ref[core, :, lanes].astype(jnp.float32)
        padded[far_at] = far_ref[core, :, lanes].astype(jnp.float32)
        padded[own_at] = own_ref[:, lanes].astype(jnp.float32)
        padded[partner_at] = partner_ref[:, lanes].astype(jnp.float32)
        own = padded[halo : halo + total_rows]
        padded[...] = padded[...] * live
        acc = jnp.zeros((total_rows, LANES), jnp.float32)
        for tap in range(KERNEL):
            acc = acc + taps_ref[tap : tap + 1, lanes] * padded[
                first + tap : first + tap + total_rows
            ]
        grown = jnp.exp(jnp.minimum(acc, 20.0))
        product = grown * (grown + 2.0)
        value = own + acc * (product / (product + 2.0))
        residual_ref[:, lanes] = value
        return total + value

    total = lax.fori_loop(
        0, tiles, convolve, jnp.zeros((total_rows, LANES), jnp.float32), unroll=3
    )

    def store(lanes, value):
        normed_ref[:, lanes] = value.astype(jnp.bfloat16)

    row_norm(lambda tile: residual_ref[:, tile_lanes(tile)], store, tiles, mod_ref, 0, total)
    for load in loads:
        load.wait()


def project_kernel(
    firsts, origin, info_ref, normed_ref, top_ref, rest_ref, cos_ref, sin_ref, *out_refs
):
    rows = normed_ref.shape[0]
    attn = rest_ref.shape[1] // 3
    top = top_ref.shape[0]
    wide = 2 * LANES
    half = HEAD_DIM // 2
    cosine, sine = cos_ref[...], sin_ref[...]
    lower = lax.broadcasted_iota(jnp.int32, (rows, LANES), 1) % HEAD_DIM < half
    chip = info_ref[CHIP] if origin is None else origin
    swap = jnp.full((rows, LANES), chip & 1, jnp.int32) > 0
    for at, apart in enumerate(firsts):
        pair = (chip ^ apart) >> 1
        for part in range(3):
            start = part * attn + pair * wide
            lanes = pl.ds(pl.multiple_of(start, wide), wide)
            both = jnp.dot(
                normed_ref[:, :top], top_ref[:, lanes], preferred_element_type=jnp.float32
            ) + jnp.dot(
                normed_ref[:, top:], rest_ref[:, lanes], preferred_element_type=jnp.float32
            )
            sides = []
            for side in range(2):
                value = both[:, side * LANES : (side + 1) * LANES]
                if part < 2:
                    swapped = jnp.where(
                        lower, pltpu.roll(value, LANES - half, 1), pltpu.roll(value, half, 1)
                    )
                    value = value * cosine + swapped * sine
                if part == 0:
                    value = value * HEAD_DIM**-0.5
                sides.append(value)
            out_refs[2 * at][part] = jnp.where(swap, sides[1], sides[0]).astype(jnp.bfloat16)
            out_refs[2 * at + 1][part] = jnp.where(swap, sides[0], sides[1]).astype(jnp.bfloat16)


def place_keys(info_ref, apart, got_ref, keys, values, first):
    _, rows, _ = got_ref.shape
    chip = info_ref[CHIP] ^ apart
    lane = lax.broadcasted_iota(jnp.int32, (rows, LANES), 1)
    row = lax.broadcasted_iota(jnp.int32, (rows, LANES), 0)
    here = slice(first, first + rows)
    keys[here, :LANES] = got_ref[1]
    dead = (lane == 0) & (row + chip * rows >= info_ref[LENGTH])
    keys[here, LANES:] = jnp.where(dead, NEGATIVE, 0.0).astype(jnp.bfloat16)
    values[here, :] = got_ref[2]


def place_queries(query_refs, queries):
    _, rows, _ = query_refs[0].shape
    low = lax.broadcasted_iota(jnp.int32, (rows, LANES), 1) < HEAD_DIM
    zero = jnp.zeros((rows, LANES), jnp.bfloat16)
    queries[:, LANES:] = jnp.where(
        lax.broadcasted_iota(jnp.int32, (queries.shape[0], LANES), 1) == 0, 1.0, 0.0
    ).astype(jnp.bfloat16)
    for at, query_ref in enumerate(query_refs):
        query = query_ref[0]
        base = 2 * at * rows
        queries[base : base + rows, :LANES] = jnp.where(low, query, zero)
        queries[base + rows : base + 2 * rows, :LANES] = jnp.where(low, zero, query)


def score(queries, keys):
    return lax.dot_general(
        queries, keys, (((1,), (1,)), ((), ())), preferred_element_type=jnp.float32
    )


def mix(weights, values):
    return jnp.dot(weights.astype(jnp.bfloat16), values, preferred_element_type=jnp.float32)


def store_heads(mixed, out_ref, places):
    _, rows, _ = out_ref.shape
    low = lax.broadcasted_iota(jnp.int32, (rows, LANES), 1) < HEAD_DIM
    for at in range(mixed.shape[0] // (2 * rows)):
        base = 2 * at * rows
        out_ref[places[at]] = jnp.where(
            low, mixed[base : base + rows], mixed[base + rows : base + 2 * rows]
        ).astype(jnp.bfloat16)


def attend_rows(keys, values, queries, out_ref, places):
    _, rows, _ = out_ref.shape
    total = queries.shape[0]
    for base in range(0, total, 4 * rows):
        block = slice(base, min(base + 4 * rows, total))
        scores = score(queries[block, :], keys[...])
        weights = jnp.exp(scores - jnp.max(scores, axis=1, keepdims=True))
        weight_sum = jnp.sum(weights, axis=1, keepdims=True)
        mixed = mix(weights, values[...]) / weight_sum
        store_heads(mixed, out_ref, places[base // (2 * rows) :])


def attend_early_kernel(aparts, info_ref, *refs):
    got_refs = refs[: len(aparts)]
    keys, values, queries, mixed_ref, peak_ref, sum_ref = refs[len(aparts) :]
    _, rows, _ = got_refs[0].shape
    for at, apart in enumerate(aparts):
        place_keys(info_ref, apart, got_refs[at], keys, values, at * rows)
    place_queries([ref for apart, ref in zip(aparts, got_refs) if apart % 2], queries)
    scores = score(queries[...], keys[...])
    peak = jnp.max(scores, axis=1, keepdims=True)
    weights = jnp.exp(scores - peak)
    peak_ref[...] = jnp.broadcast_to(peak, peak_ref.shape)
    sum_ref[...] = jnp.broadcast_to(jnp.sum(weights, axis=1, keepdims=True), sum_ref.shape)
    mixed_ref[...] = mix(weights, values[...])


def attend_last_kernel(
    aparts, places, info_ref, early_keys, early_values, early_queries, mixed_ref, peak_ref, sum_ref,
    *refs,
):
    got_refs = refs[: len(aparts)]
    out_ref, keys, values, queries = refs[len(aparts) :]
    early_places, last_places = places
    held, _ = early_values.shape
    _, rows, _ = got_refs[0].shape
    keys[:held, :] = early_keys[...]
    values[:held, :] = early_values[...]
    for at, apart in enumerate(aparts):
        place_keys(info_ref, apart, got_refs[at], keys, values, held + at * rows)
    place_queries([ref for apart, ref in zip(aparts, got_refs) if apart % 2], queries)
    attend_rows(keys, values, queries, out_ref, last_places)
    scores = score(early_queries[...], keys[held:, :])
    peak = peak_ref[:, :1]
    joined = jnp.maximum(peak, jnp.max(scores, axis=1, keepdims=True))
    scale = jnp.exp(peak - joined)
    weights = jnp.exp(scores - joined)
    weight_sum = sum_ref[:, :1] * scale + jnp.sum(weights, axis=1, keepdims=True)
    mixed = mixed_ref[...] * scale + mix(weights, values[held:, :])
    store_heads(mixed / weight_sum, out_ref, early_places)


def attend_second_kernel(info_ref, keys, values, *refs):
    del info_ref
    out_ref, queries = refs[-2:]
    place_queries(refs[:-2], queries)
    attend_rows(keys, values, queries, out_ref, list(range(out_ref.shape[0])))


def merge_kernel(info_ref, own_ref, got_ref, *out_refs):
    del info_ref
    for at, out_ref in enumerate(out_refs):
        out_ref[0] = own_ref[at + 1]
        out_ref[1] = got_ref[at + 1]


def back_kernel(blocks, info_ref, residual, w_mel, mod_ref, w_out_ref, *refs):
    count = 1 + max(at for at, _, _ in blocks)
    got_refs = refs[:count]
    keep_ref, send_ref, attended, after, speed = refs[count:]
    rows, width = residual.shape
    tiles = width // LANES
    core, chip = info_ref[CORE], info_ref[CHIP]
    for at, place, apart in blocks:
        group = place if apart is None else chip ^ apart
        attended[:, tile_lanes(group)] = got_refs[at][place]
    wide = 2 * LANES
    total = jnp.zeros((rows, LANES), jnp.float32)
    for block in range(width // wide):
        lanes = slice(block * wide, (block + 1) * wide)
        branch = jnp.dot(attended[...], w_out_ref[:, lanes], preferred_element_type=jnp.float32)
        value = residual[:, lanes] + mod_ref[2:3, lanes] * branch
        after[:, lanes] = value
        total = total + value[:, :LANES] + value[:, LANES:]

    def store(lanes, value):
        after[:, lanes] = value

    row_norm(lambda tile: after[:, tile_lanes(tile)], store, tiles, mod_ref, 3, total)
    speed[...] = lax.dot_general(
        after[...].astype(jnp.bfloat16), w_mel[...], (((1,), (1,)), ((), ())),
        preferred_element_type=jnp.float32,
    )
    half = rows // 2
    keep_ref[...] = speed[pl.ds(pl.multiple_of(core * half, 8), half), :]
    send_ref[...] = speed[pl.ds(pl.multiple_of((1 - core) * half, 8), half), :]


def call(kernel, out_shape, inputs, scratch, hbm=()):
    single = not isinstance(out_shape, tuple)
    specs = [hbm_spec() if at in hbm else vmem_spec() for at in range(1, len(inputs))]
    inputs = list(inputs)
    for at in hbm:
        inputs[at] = pltpu.with_memory_space_constraint(inputs[at], pltpu.HBM)
    return pl.pallas_call(
        kernel,
        out_shape=out_shape,
        in_specs=[smem_spec()] + specs,
        out_specs=vmem_spec() if single else tuple(vmem_spec() for _ in out_shape),
        scratch_shapes=scratch,
        compiler_params=pltpu.CompilerParams(vmem_limit_bytes=GRANT),
    )(*inputs)


def array(shape, dtype=jnp.float32):
    return jax.ShapeDtypeStruct(shape, dtype)


def project(normed, w_qkv, tables, info, firsts, origin=None):
    shape = array((3, normed.shape[0], LANES), jnp.bfloat16)
    return call(
        functools.partial(project_kernel, tuple(firsts), origin),
        (shape,) * (2 * len(firsts)),
        (info, normed) + w_qkv + tables,
        [],
    )


def same_core(count):
    return [list(range(core, count, 2)) for core in range(2)]


def facing_pairs(clips, count):
    pairs = []
    for clip in range(clips):
        base = clip * count
        for at in range(1, count - 1, 2):
            pairs += [(base + at, base + at + 1), (base + at + 1, base + at)]
        if clip ^ 1 < clips:
            pairs += [(base + end, (clip ^ 1) * count + end) for end in (0, count - 1)]
    return pairs


def across(value, apart, count):
    return lax.ppermute(value, "seq", [(i, i ^ apart) for i in range(count)])


def to_groups(values, subs):
    rows, _ = values.shape
    grouped = values.reshape(subs, rows // subs, HEADS, HEAD_DIM).transpose(2, 0, 1, 3)
    return grouped.reshape(HEADS * subs, rows // subs, HEAD_DIM)


def from_groups(grouped, rows, subs):
    split = grouped.reshape(HEADS, subs, rows // subs, HEAD_DIM).transpose(1, 2, 0, 3)
    return split.reshape(rows, HEADS * HEAD_DIM)


def attend_blocks(queries, keys, values, live):
    groups, total, _ = queries.shape
    block = max(size for size in range(1, min(total, 1024) + 1) if total % size == 0)
    blocks = queries.reshape(groups, total // block, block, HEAD_DIM).transpose(1, 0, 2, 3)
    live = live[None, None, :]

    def one_block(query):
        scores = jnp.einsum("gqd,gkd->gqk", query, keys, preferred_element_type=jnp.float32)
        scores = jnp.where(live, scores, NEGATIVE)
        weights = jnp.exp(scores - jnp.max(scores, axis=-1, keepdims=True))
        weights = jnp.where(live, weights, 0.0)
        mixed = jnp.einsum(
            "gqk,gkd->gqd",
            weights.astype(jnp.bfloat16),
            values,
            preferred_element_type=jnp.float32,
        )
        return (mixed / jnp.sum(weights, axis=-1)[..., None]).astype(jnp.bfloat16)

    return lax.map(one_block, blocks).transpose(1, 0, 2, 3).reshape(groups, total, HEAD_DIM)


def attend_any(normed, w_qkv, tables, info, length, count):
    rows = normed.shape[0]
    chips = count // 2
    groups = HEADS * HEAD_DIM // LANES
    sent = project(normed, w_qkv, tables, info, range(0, groups, 2), 0)
    subs = max(1, chips // HEADS)
    chip = lax.axis_index("seq") >> 1
    part_rows = rows // subs

    def exchange(part):
        whole = jnp.concatenate([group[part] for group in sent], axis=1)
        return lax.all_to_all(
            to_groups(whole, subs), "seq", split_axis=0, concat_axis=1, tiled=True,
            axis_index_groups=same_core(count),
        )

    queries, keys, values = (exchange(part) for part in range(3))

    def frames_of(sub):
        start = jnp.arange(chips, dtype=jnp.int32)[:, None] * rows + sub * part_rows
        return (start + jnp.arange(part_rows, dtype=jnp.int32)[None, :]).reshape(-1)

    frames = [frames_of(chip % subs)]
    parts = [(keys, values)]
    for apart in range(1, subs):
        perm = []
        for i in range(count):
            at = i // 2
            target = at - at % subs + (at + apart) % subs
            perm.append((i, 2 * target + i % 2))
        parts.append(tuple(lax.ppermute(part, "seq", perm) for part in (keys, values)))
        frames.append(frames_of((chip - apart) % subs))
    keys = jnp.concatenate([part[0] for part in parts], axis=1)
    values = jnp.concatenate([part[1] for part in parts], axis=1)
    attended = attend_blocks(queries, keys, values, jnp.concatenate(frames) < length)
    back = lax.all_to_all(
        attended, "seq", split_axis=1, concat_axis=0, tiled=True,
        axis_index_groups=same_core(count),
    )
    return from_groups(back, rows, subs).reshape(rows, groups, LANES).transpose(1, 0, 2)


def chips_hold_groups(count):
    chips = count // 2
    return chips == HEADS * HEAD_DIM // LANES and chips >= 4 and chips & (chips - 1) == 0


def send_order(chips):
    far = list(range(chips // 2, chips, 2))
    return far[:1] + [0] + far[1:] + list(range(2, chips // 2, 2))


def late_sends(chips):
    return list(range(2, chips // 2)) + [chips - 1]


def attend_chips(normed, w_qkv, tables, info, count):
    rows = normed.shape[0]
    chips = count // 2
    held = {}
    for first in send_order(chips):
        made = project(normed, w_qkv, tables, info, [first])
        for side in range(2):
            apart = first + side
            held[apart] = across(made[side], 2 * apart, count) if apart else made[side]
    total, half = chips * rows, chips // 2
    late = late_sends(chips)
    soon = [apart for apart in range(chips) if apart not in late]
    odd_soon = [apart for apart in soon if apart % 2]
    odd_late = [apart for apart in late if apart % 2]
    early, early_rows = len(soon) * rows, 2 * len(odd_soon) * rows
    parts = call(
        functools.partial(attend_early_kernel, tuple(soon)),
        (
            array((early, 2 * LANES), jnp.bfloat16),
            array((early, LANES), jnp.bfloat16),
            array((early_rows, 2 * LANES), jnp.bfloat16),
        )
        + (array((early_rows, LANES)),) * 3,
        (info,) + tuple(held[apart] for apart in soon),
        [],
    )
    places = tuple(tuple(apart // 2 for apart in odds) for odds in (odd_soon, odd_late))
    crossing, keys, values = call(
        functools.partial(attend_last_kernel, tuple(late), places),
        (
            array((half, rows, LANES), jnp.bfloat16),
            array((total, 2 * LANES), jnp.bfloat16),
            array((total, LANES), jnp.bfloat16),
        ),
        (info,) + tuple(parts) + tuple(held[apart] for apart in late),
        [VMEM((2 * len(odd_late) * rows, 2 * LANES), jnp.bfloat16)],
    )
    crossed = across(crossing, 2, count)
    staying = call(
        attend_second_kernel,
        array((half, rows, LANES), jnp.bfloat16),
        (info, keys, values) + tuple(held[apart] for apart in range(0, chips, 2)),
        [VMEM((total, 2 * LANES), jnp.bfloat16)],
    )
    joined = call(
        merge_kernel,
        (array((2, rows, LANES), jnp.bfloat16),) * (half - 1),
        (info, staying, crossed),
        [],
    )
    back, blocks = [staying, crossed], [(0, 0, 0), (1, 0, 1)]
    apart_first = sorted(range(1, half), reverse=True)
    got = {apart: across(joined[apart - 1], 4 * apart, count) for apart in apart_first}
    for apart in range(1, half):
        blocks += [(len(back), side, 2 * apart + side) for side in range(2)]
        back.append(got[apart])
    return back, blocks


def per_device(
    hidden, latent, lengths, step_index, guidance, modulation, conv_kernel, w_qkv, w_out, w_mel
):
    copies, rows, width = hidden.shape
    count = lax.axis_size("seq")
    index = lax.axis_index("seq").astype(jnp.int32)
    chip, core = index >> 1, index & 1
    chip_rows = 2 * rows
    info = jnp.stack([core, chip, lengths[0]])

    edges = lax.dynamic_slice(hidden, (0, core * (rows - HALO), 0), (copies, HALO, width))
    partner = lax.dynamic_slice(hidden, (1 - core, 0, 0), (1, rows, width))[0]
    near = lax.ppermute(edges, ("clip", "seq"), facing_pairs(lax.axis_size("clip"), count))
    far = across(near, 1, count)
    partner = across(partner, 1, count)
    own, taps, mods, is_first, live = call(
        stage_kernel,
        (
            array((rows, width), jnp.bfloat16),
            array(conv_kernel.shape),
            array(modulation.shape),
            array(latent.shape),
            array(latent.shape),
        ),
        (info, hidden, conv_kernel, modulation),
        [pltpu.SemaphoreType.DMA((3,))],
        hbm=(1, 2, 3),
    )
    top = min(2 * LANES, width // 2)
    weight_top, *tables = call(
        load_kernel,
        (
            array((top, w_qkv.shape[1]), jnp.bfloat16),
            array((chip_rows, LANES)),
            array((chip_rows, LANES)),
        ),
        (info, rotary_rates(), w_qkv),
        [pltpu.SemaphoreType.DMA((2,))],
        hbm=(2,),
    )
    tables = tuple(tables)
    residual, normed, weight = call(
        front_kernel,
        (
            array((chip_rows, width)),
            array((chip_rows, width), jnp.bfloat16),
            array((width - top, w_qkv.shape[1]), jnp.bfloat16),
        ),
        (info, own, partner, near, far, taps, mods, w_qkv),
        [VMEM((chip_rows + 2 * HALO, LANES), jnp.float32), pltpu.SemaphoreType.DMA((8,))],
        hbm=(7,),
    )
    weight = (weight_top, weight)
    if chips_hold_groups(count):
        back, blocks = attend_chips(normed, weight, tables, info, count)
    else:
        back = [attend_any(normed, weight, tables, info, lengths[0], count)]
        blocks = [(0, group, None) for group in range(back[0].shape[0])]
    mels = w_mel.shape[1]
    keep, send = call(
        functools.partial(back_kernel, tuple(blocks)),
        (array((rows, mels)),) * 2,
        (info, residual, w_mel.T, mods, w_out) + tuple(back),
        [
            VMEM((chip_rows, HEADS * HEAD_DIM), jnp.bfloat16),
            VMEM((chip_rows, width), jnp.float32),
            VMEM((chip_rows, mels), jnp.float32),
        ],
    )
    other = across(send, 1, count)
    first = jnp.where(is_first > 0.5, keep, other)
    second = jnp.where(is_first > 0.5, other, keep)
    guided = first + guidance[0] * (first - second)
    velocity = jnp.where(live > 0.5, guided, 0.0)
    progress = step_index[0].astype(jnp.float32) / STEPS
    time_now = 1.0 - jnp.cos(0.5 * jnp.pi * progress)
    return (velocity, latent + (1.0 - time_now) * velocity)


def solution(mesh):
    return jax.shard_map(
        per_device,
        mesh=mesh,
        in_specs=(
            P(None, ("clip", "seq"), None),
            P(("clip", "seq"), None),
            P("clip"),
            P(),
            P(),
            P(),
            P(),
            P(),
            P(),
            P(),
        ),
        out_specs=(P(("clip", "seq"), None), P(("clip", "seq"), None)),
        check_vma=False,
    )
```

```python
import functools

import jax
import jax.numpy as jnp
from jax import lax
from jax.experimental import pallas as pl
from jax.experimental.pallas import tpu as pltpu
from jax.sharding import PartitionSpec as P


HEADS = 16
HEAD_DIM = 64
KERNEL = 31
STEPS = 32
LANES = 128
HALO = 16


EPSILON = 1e-06
NEGATIVE = -1e30
CORE, CHIP, LENGTH = 0, 1, 2
VMEM = pltpu.VMEM
SMEM = pltpu.SMEM
GRANT = 12 << 20


def vmem_spec():
    return pl.BlockSpec(memory_space=VMEM)


def smem_spec():
    return pl.BlockSpec(memory_space=SMEM)


def rotary_tables(positions):
    half_dim = HEAD_DIM // 2
    lane = jnp.arange(LANES, dtype=jnp.int32)
    inverse = 10000.0 ** (-(lane % half_dim).astype(jnp.float32) / half_dim)
    angles = positions.astype(jnp.float32)[:, None] * inverse[None, :]
    sign = jnp.where(lane % HEAD_DIM < half_dim, -1.0, 1.0)
    return jnp.cos(angles), jnp.sin(angles) * sign[None, :]


def hbm_spec():
    return pl.BlockSpec(memory_space=pltpu.HBM)


def tile_lanes(tile):
    return pl.ds(pl.multiple_of(tile * LANES, LANES), LANES)


def row_norm(load, store, tiles, mod_ref, row, total):
    width = tiles * LANES
    mean = jnp.sum(total, axis=-1, keepdims=True) * (1.0 / width)

    def square(tile, acc):
        centered = load(tile) - mean
        return acc + centered * centered

    squares = lax.fori_loop(0, tiles, square, jnp.zeros(total.shape, jnp.float32), unroll=6)
    variance = jnp.sum(squares, axis=-1, keepdims=True) * (1.0 / width)
    factor = lax.rsqrt(variance + EPSILON)

    def write(tile, carry):
        lanes = tile_lanes(tile)
        scale = 1.0 + mod_ref[row + 1 : row + 2, lanes]
        shift = mod_ref[row : row + 1, lanes]
        store(lanes, (load(tile) - mean) * factor * scale + shift)
        return carry

    lax.fori_loop(0, tiles, write, 0, unroll=6)


def run_copies(pairs, sems):
    copies = [
        pltpu.make_async_copy(source, target, sems.at[at])
        for at, (source, target) in enumerate(pairs)
    ]
    for copy in copies:
        copy.start()
    for copy in copies:
        copy.wait()


def stage_kernel(
    info_ref, hidden_hbm, taps_hbm, mod_hbm, own_ref, taps_ref, mod_ref, first_ref, live_ref, sems
):
    rows = own_ref.shape[0]
    core = info_ref[CORE]
    first_ref[...] = jnp.zeros(first_ref.shape, jnp.float32) + (1 - core).astype(jnp.float32)
    row = lax.broadcasted_iota(jnp.int32, live_ref.shape, 0)
    frame = row + (2 * info_ref[CHIP] + core) * rows
    live_ref[...] = (frame < info_ref[LENGTH]).astype(jnp.float32)
    run_copies(
        [(hidden_hbm.at[core], own_ref), (taps_hbm, taps_ref), (mod_hbm, mod_ref)], sems
    )


def front_kernel(
    firsts, info_ref, own_ref, partner_ref, near_ref, far_ref, taps_ref, mod_ref, cos_ref, sin_ref,
    weight_hbm, residual_ref, normed_ref, weight_ref, *refs,
):
    *out_refs, padded, sems = refs
    rows, width = own_ref.shape
    halo = near_ref.shape[1]
    total_rows = 2 * rows
    tiles = width // LANES
    parts = 8
    depth = width // parts
    loads = []
    for part in range(parts):
        here = pl.ds(part * depth, depth)
        loads.append(
            pltpu.make_async_copy(weight_hbm.at[here], weight_ref.at[here], sems.at[part])
        )
    for load in loads:
        load.start()
    length, core = info_ref[LENGTH], info_ref[CORE]
    offset = info_ref[CHIP] * total_rows
    span = total_rows + 2 * halo
    frame = offset - halo + lax.broadcasted_iota(jnp.int32, (span, LANES), 0)
    live = ((frame >= 0) & (frame < length)).astype(jnp.float32)
    first = halo - KERNEL // 2
    own_at = pl.ds(pl.multiple_of(halo + core * rows, 8), rows)
    partner_at = pl.ds(pl.multiple_of(halo + (1 - core) * rows, 8), rows)
    near_at = pl.ds(pl.multiple_of(core * (halo + total_rows), 8), halo)
    far_at = pl.ds(pl.multiple_of((1 - core) * (halo + total_rows), 8), halo)

    def convolve(tile, total):
        lanes = tile_lanes(tile)
        padded[near_at] = near_ref[core, :, lanes].astype(jnp.float32)
        padded[far_at] = far_ref[core, :, lanes].astype(jnp.float32)
        padded[own_at] = own_ref[:, lanes].astype(jnp.float32)
        padded[partner_at] = partner_ref[:, lanes].astype(jnp.float32)
        own = padded[halo : halo + total_rows]
        padded[...] = padded[...] * live
        acc = jnp.zeros((total_rows, LANES), jnp.float32)
        for tap in range(KERNEL):
            acc = acc + taps_ref[tap : tap + 1, lanes] * padded[
                first + tap : first + tap + total_rows
            ]
        grown = jnp.exp(jnp.minimum(acc, 20.0))
        product = grown * (grown + 2.0)
        value = own + acc * (product / (product + 2.0))
        residual_ref[:, lanes] = value
        return total + value

    total = lax.fori_loop(
        0, tiles, convolve, jnp.zeros((total_rows, LANES), jnp.float32), unroll=3
    )

    def store(lanes, value):
        normed_ref[:, lanes] = value.astype(jnp.bfloat16)

    row_norm(lambda tile: residual_ref[:, tile_lanes(tile)], store, tiles, mod_ref, 0, total)
    for load in loads:
        load.wait()
    chip = info_ref[CHIP]
    project_pairs(firsts, chip, normed_ref, weight_ref, cos_ref, sin_ref, out_refs)


def project_pairs(firsts, chip, normed_ref, weight_ref, cos_ref, sin_ref, out_refs):
    rows = normed_ref.shape[0]
    attn = weight_ref.shape[1] // 3
    wide = 2 * LANES
    half = HEAD_DIM // 2
    cosine, sine = cos_ref[...], sin_ref[...]
    lower = lax.broadcasted_iota(jnp.int32, (rows, LANES), 1) % HEAD_DIM < half
    swap = jnp.full((rows, LANES), chip & 1, jnp.int32) > 0
    for at, apart in enumerate(firsts):
        pair = (chip ^ apart) >> 1
        for part in range(3):
            start = part * attn + pair * wide
            both = jnp.dot(
                normed_ref[...],
                weight_ref[:, pl.ds(pl.multiple_of(start, wide), wide)],
                preferred_element_type=jnp.float32,
            )
            sides = []
            for side in range(2):
                value = both[:, side * LANES : (side + 1) * LANES]
                if part < 2:
                    swapped = jnp.where(
                        lower, pltpu.roll(value, LANES - half, 1), pltpu.roll(value, half, 1)
                    )
                    value = value * cosine + swapped * sine
                if part == 0:
                    value = value * HEAD_DIM**-0.5
                sides.append(value)
            out_refs[2 * at][part] = jnp.where(swap, sides[1], sides[0]).astype(jnp.bfloat16)
            out_refs[2 * at + 1][part] = jnp.where(swap, sides[0], sides[1]).astype(jnp.bfloat16)


def project_kernel(firsts, origin, info_ref, normed_ref, weight_ref, cos_ref, sin_ref, *out_refs):
    chip = info_ref[CHIP] if origin is None else origin
    project_pairs(firsts, chip, normed_ref, weight_ref, cos_ref, sin_ref, out_refs)


def place_keys(info_ref, apart, got_ref, keys, values, first):
    _, rows, _ = got_ref.shape
    chip = info_ref[CHIP] ^ apart
    lane = lax.broadcasted_iota(jnp.int32, (rows, LANES), 1)
    row = lax.broadcasted_iota(jnp.int32, (rows, LANES), 0)
    here = slice(first, first + rows)
    keys[here, :LANES] = got_ref[1]
    dead = (lane == 0) & (row + chip * rows >= info_ref[LENGTH])
    keys[here, LANES:] = jnp.where(dead, NEGATIVE, 0.0).astype(jnp.bfloat16)
    values[here, :] = got_ref[2]


def place_queries(query_refs, queries):
    _, rows, _ = query_refs[0].shape
    low = lax.broadcasted_iota(jnp.int32, (rows, LANES), 1) < HEAD_DIM
    zero = jnp.zeros((rows, LANES), jnp.bfloat16)
    queries[:, LANES:] = jnp.where(
        lax.broadcasted_iota(jnp.int32, (queries.shape[0], LANES), 1) == 0, 1.0, 0.0
    ).astype(jnp.bfloat16)
    for at, query_ref in enumerate(query_refs):
        query = query_ref[0]
        base = 2 * at * rows
        queries[base : base + rows, :LANES] = jnp.where(low, query, zero)
        queries[base + rows : base + 2 * rows, :LANES] = jnp.where(low, zero, query)


def score(queries, keys):
    return lax.dot_general(
        queries, keys, (((1,), (1,)), ((), ())), preferred_element_type=jnp.float32
    )


def mix(weights, values):
    return jnp.dot(weights.astype(jnp.bfloat16), values, preferred_element_type=jnp.float32)


def store_heads(mixed, out_ref, first):
    _, rows, _ = out_ref.shape
    low = lax.broadcasted_iota(jnp.int32, (rows, LANES), 1) < HEAD_DIM
    for at in range(mixed.shape[0] // (2 * rows)):
        base = 2 * at * rows
        out_ref[first + at] = jnp.where(
            low, mixed[base : base + rows], mixed[base + rows : base + 2 * rows]
        ).astype(jnp.bfloat16)


def attend_rows(keys, values, queries, out_ref, first):
    _, rows, _ = out_ref.shape
    total = queries.shape[0]
    for base in range(0, total, 4 * rows):
        block = slice(base, min(base + 4 * rows, total))
        scores = score(queries[block, :], keys[...])
        weights = jnp.exp(scores - jnp.max(scores, axis=1, keepdims=True))
        weight_sum = jnp.sum(weights, axis=1, keepdims=True)
        store_heads(mix(weights, values[...]) / weight_sum, out_ref, first + base // (2 * rows))


def attend_early_kernel(info_ref, *refs):
    chips = len(refs) - 6
    got_refs = refs[:chips]
    keys, values, queries, mixed_ref, peak_ref, sum_ref = refs[chips:]
    _, rows, _ = got_refs[0].shape
    for apart, got_ref in enumerate(got_refs):
        place_keys(info_ref, apart, got_ref, keys, values, apart * rows)
    place_queries(got_refs[1::2], queries)
    scores = score(queries[...], keys[...])
    peak = jnp.max(scores, axis=1, keepdims=True)
    weights = jnp.exp(scores - peak)
    peak_ref[...] = jnp.broadcast_to(peak, peak_ref.shape)
    sum_ref[...] = jnp.broadcast_to(jnp.sum(weights, axis=1, keepdims=True), sum_ref.shape)
    mixed_ref[...] = mix(weights, values[...])


def attend_last_kernel(
    info_ref, early_keys, early_values, early_queries, mixed_ref, peak_ref, sum_ref, last_ref,
    out_ref, keys, values, queries,
):
    held, _ = early_values.shape
    _, rows, _ = last_ref.shape
    keys[:held, :] = early_keys[...]
    values[:held, :] = early_values[...]
    place_keys(info_ref, held // rows, last_ref, keys, values, held)
    place_queries([last_ref], queries)
    attend_rows(keys, values, queries, out_ref, out_ref.shape[0] - 1)
    scores = score(early_queries[...], keys[held:, :])
    peak = peak_ref[...]
    joined = jnp.maximum(peak, jnp.max(scores, axis=1, keepdims=True))
    scale = jnp.exp(peak - joined)
    weights = jnp.exp(scores - joined[:, : scores.shape[1]])
    weight_sum = sum_ref[...] * scale + jnp.sum(weights, axis=1, keepdims=True)
    mixed = mixed_ref[...] * scale + mix(weights, values[held:, :])
    store_heads(mixed / weight_sum, out_ref, 0)


def attend_second_kernel(info_ref, keys, values, *refs):
    del info_ref
    out_ref, queries = refs[-2:]
    place_queries(refs[:-2], queries)
    attend_rows(keys, values, queries, out_ref, 0)


def merge_kernel(info_ref, own_ref, got_ref, *out_refs):
    del info_ref
    for at, out_ref in enumerate(out_refs):
        out_ref[0] = own_ref[at + 1]
        out_ref[1] = got_ref[at + 1]


def back_kernel(blocks, info_ref, residual, w_mel, mod_ref, w_out_ref, *refs):
    count = 1 + max(at for at, _, _ in blocks)
    got_refs = refs[:count]
    keep_ref, send_ref, attended, after, speed = refs[count:]
    rows, width = residual.shape
    tiles = width // LANES
    core, chip = info_ref[CORE], info_ref[CHIP]
    for at, place, apart in blocks:
        group = place if apart is None else chip ^ apart
        attended[:, tile_lanes(group)] = got_refs[at][place]
    wide = 2 * LANES
    total = jnp.zeros((rows, LANES), jnp.float32)
    for block in range(width // wide):
        lanes = slice(block * wide, (block + 1) * wide)
        branch = jnp.dot(attended[...], w_out_ref[:, lanes], preferred_element_type=jnp.float32)
        value = residual[:, lanes] + mod_ref[2:3, lanes] * branch
        after[:, lanes] = value
        total = total + value[:, :LANES] + value[:, LANES:]

    def store(lanes, value):
        after[:, lanes] = value

    row_norm(lambda tile: after[:, tile_lanes(tile)], store, tiles, mod_ref, 3, total)
    speed[...] = lax.dot_general(
        after[...].astype(jnp.bfloat16), w_mel[...], (((1,), (1,)), ((), ())),
        preferred_element_type=jnp.float32,
    )
    half = rows // 2
    keep_ref[...] = speed[pl.ds(pl.multiple_of(core * half, 8), half), :]
    send_ref[...] = speed[pl.ds(pl.multiple_of((1 - core) * half, 8), half), :]


def call(kernel, out_shape, inputs, scratch, hbm=()):
    single = not isinstance(out_shape, tuple)
    specs = [hbm_spec() if at in hbm else vmem_spec() for at in range(1, len(inputs))]
    inputs = list(inputs)
    for at in hbm:
        inputs[at] = pltpu.with_memory_space_constraint(inputs[at], pltpu.HBM)
    return pl.pallas_call(
        kernel,
        out_shape=out_shape,
        in_specs=[smem_spec()] + specs,
        out_specs=vmem_spec() if single else tuple(vmem_spec() for _ in out_shape),
        scratch_shapes=scratch,
        compiler_params=pltpu.CompilerParams(vmem_limit_bytes=GRANT),
    )(*inputs)


def array(shape, dtype=jnp.float32):
    return jax.ShapeDtypeStruct(shape, dtype)


def project(normed, w_qkv, tables, info, firsts, origin=None):
    shape = array((3, normed.shape[0], LANES), jnp.bfloat16)
    return call(
        functools.partial(project_kernel, tuple(firsts), origin),
        (shape,) * (2 * len(firsts)),
        (info, normed, w_qkv) + tables,
        [],
    )


def same_core(count):
    return [list(range(core, count, 2)) for core in range(2)]


def facing_pairs(clips, count):
    pairs = []
    for clip in range(clips):
        base = clip * count
        for at in range(1, count - 1, 2):
            pairs += [(base + at, base + at + 1), (base + at + 1, base + at)]
        if clip ^ 1 < clips:
            pairs += [(base + end, (clip ^ 1) * count + end) for end in (0, count - 1)]
    return pairs


def across(value, apart, count):
    return lax.ppermute(value, "seq", [(i, i ^ apart) for i in range(count)])


def to_groups(values, subs):
    rows, _ = values.shape
    grouped = values.reshape(subs, rows // subs, HEADS, HEAD_DIM).transpose(2, 0, 1, 3)
    return grouped.reshape(HEADS * subs, rows // subs, HEAD_DIM)


def from_groups(grouped, rows, subs):
    split = grouped.reshape(HEADS, subs, rows // subs, HEAD_DIM).transpose(1, 2, 0, 3)
    return split.reshape(rows, HEADS * HEAD_DIM)


def attend_blocks(queries, keys, values, live):
    groups, total, _ = queries.shape
    block = max(size for size in range(1, min(total, 1024) + 1) if total % size == 0)
    blocks = queries.reshape(groups, total // block, block, HEAD_DIM).transpose(1, 0, 2, 3)
    live = live[None, None, :]

    def one_block(query):
        scores = jnp.einsum("gqd,gkd->gqk", query, keys, preferred_element_type=jnp.float32)
        scores = jnp.where(live, scores, NEGATIVE)
        weights = jnp.exp(scores - jnp.max(scores, axis=-1, keepdims=True))
        weights = jnp.where(live, weights, 0.0)
        mixed = jnp.einsum(
            "gqk,gkd->gqd",
            weights.astype(jnp.bfloat16),
            values,
            preferred_element_type=jnp.float32,
        )
        return (mixed / jnp.sum(weights, axis=-1)[..., None]).astype(jnp.bfloat16)

    return lax.map(one_block, blocks).transpose(1, 0, 2, 3).reshape(groups, total, HEAD_DIM)


def attend_any(normed, w_qkv, tables, info, length, count):
    rows = normed.shape[0]
    chips = count // 2
    groups = HEADS * HEAD_DIM // LANES
    sent = project(normed, w_qkv, tables, info, range(0, groups, 2), 0)
    subs = max(1, chips // HEADS)
    chip = lax.axis_index("seq") >> 1
    part_rows = rows // subs

    def exchange(part):
        whole = jnp.concatenate([group[part] for group in sent], axis=1)
        return lax.all_to_all(
            to_groups(whole, subs), "seq", split_axis=0, concat_axis=1, tiled=True,
            axis_index_groups=same_core(count),
        )

    queries, keys, values = (exchange(part) for part in range(3))

    def frames_of(sub):
        start = jnp.arange(chips, dtype=jnp.int32)[:, None] * rows + sub * part_rows
        return (start + jnp.arange(part_rows, dtype=jnp.int32)[None, :]).reshape(-1)

    frames = [frames_of(chip % subs)]
    parts = [(keys, values)]
    for apart in range(1, subs):
        perm = []
        for i in range(count):
            at = i // 2
            target = at - at % subs + (at + apart) % subs
            perm.append((i, 2 * target + i % 2))
        parts.append(tuple(lax.ppermute(part, "seq", perm) for part in (keys, values)))
        frames.append(frames_of((chip - apart) % subs))
    keys = jnp.concatenate([part[0] for part in parts], axis=1)
    values = jnp.concatenate([part[1] for part in parts], axis=1)
    attended = attend_blocks(queries, keys, values, jnp.concatenate(frames) < length)
    back = lax.all_to_all(
        attended, "seq", split_axis=1, concat_axis=0, tiled=True,
        axis_index_groups=same_core(count),
    )
    return from_groups(back, rows, subs).reshape(rows, groups, LANES).transpose(1, 0, 2)


def chips_hold_groups(count):
    chips = count // 2
    return chips == HEADS * HEAD_DIM // LANES and chips >= 4 and chips & (chips - 1) == 0


def send_order(chips):
    far = list(range(chips // 2, chips, 2))
    return far[:1] + list(range(2, chips // 2, 2)) + far[1:] + [0]


def attend_chips(made, normed, w_qkv, tables, info, count):
    rows = normed.shape[0]
    chips = count // 2
    held = {}
    for first in send_order(chips):
        if held:
            made = project(normed, w_qkv, tables, info, [first])
        for side in range(2):
            apart = first + side
            held[apart] = across(made[side], 2 * apart, count) if apart else made[side]
    total, half = chips * rows, chips // 2
    early, early_rows = total - rows, 2 * (half - 1) * rows
    parts = call(
        attend_early_kernel,
        (
            array((early, 2 * LANES), jnp.bfloat16),
            array((early, LANES), jnp.bfloat16),
            array((early_rows, 2 * LANES), jnp.bfloat16),
        )
        + (array((early_rows, LANES)),) * 3,
        (info,) + tuple(held[apart] for apart in range(chips - 1)),
        [],
    )
    crossing, keys, values = call(
        attend_last_kernel,
        (
            array((half, rows, LANES), jnp.bfloat16),
            array((total, 2 * LANES), jnp.bfloat16),
            array((total, LANES), jnp.bfloat16),
        ),
        (info,) + tuple(parts) + (held[chips - 1],),
        [VMEM((2 * rows, 2 * LANES), jnp.bfloat16)],
    )
    crossed = across(crossing, 2, count)
    staying = call(
        attend_second_kernel,
        array((half, rows, LANES), jnp.bfloat16),
        (info, keys, values) + tuple(held[apart] for apart in range(0, chips, 2)),
        [VMEM((total, 2 * LANES), jnp.bfloat16)],
    )
    joined = call(
        merge_kernel,
        (array((2, rows, LANES), jnp.bfloat16),) * (half - 1),
        (info, staying, crossed),
        [],
    )
    back, blocks = [staying, crossed], [(0, 0, 0), (1, 0, 1)]
    apart_first = sorted(range(1, half), reverse=True)
    got = {apart: across(joined[apart - 1], 4 * apart, count) for apart in apart_first}
    for apart in range(1, half):
        blocks += [(len(back), side, 2 * apart + side) for side in range(2)]
        back.append(got[apart])
    return back, blocks


def per_device(
    hidden, latent, lengths, step_index, guidance, modulation, conv_kernel, w_qkv, w_out, w_mel
):
    copies, rows, width = hidden.shape
    count = lax.axis_size("seq")
    chips = count // 2
    index = lax.axis_index("seq").astype(jnp.int32)
    chip, core = index >> 1, index & 1
    chip_rows = 2 * rows
    info = jnp.stack([core, chip, lengths[0]])

    edges = lax.dynamic_slice(hidden, (0, core * (rows - HALO), 0), (copies, HALO, width))
    partner = lax.dynamic_slice(hidden, (1 - core, 0, 0), (1, rows, width))[0]
    near = lax.ppermute(edges, ("clip", "seq"), facing_pairs(lax.axis_size("clip"), count))
    far = across(near, 1, count)
    partner = across(partner, 1, count)
    own, taps, mods, is_first, live = call(
        stage_kernel,
        (
            array((rows, width), jnp.bfloat16),
            array(conv_kernel.shape),
            array(modulation.shape),
            array(latent.shape),
            array(latent.shape),
        ),
        (info, hidden, conv_kernel, modulation),
        [pltpu.SemaphoreType.DMA((3,))],
        hbm=(1, 2, 3),
    )
    tables = rotary_tables(chip * chip_rows + jnp.arange(chip_rows, dtype=jnp.int32))
    firsts = tuple(send_order(chips)[:1]) if chips_hold_groups(count) else ()
    group = array((3, chip_rows, LANES), jnp.bfloat16)
    residual, normed, weight, *made = call(
        functools.partial(front_kernel, firsts),
        (
            array((chip_rows, width)),
            array((chip_rows, width), jnp.bfloat16),
            array(w_qkv.shape, jnp.bfloat16),
        )
        + (group,) * (2 * len(firsts)),
        (info, own, partner, near, far, taps, mods) + tables + (w_qkv,),
        [VMEM((chip_rows + 2 * HALO, LANES), jnp.float32), pltpu.SemaphoreType.DMA((8,))],
        hbm=(9,),
    )
    if chips_hold_groups(count):
        back, blocks = attend_chips(made, normed, weight, tables, info, count)
    else:
        back = [attend_any(normed, weight, tables, info, lengths[0], count)]
        blocks = [(0, group, None) for group in range(back[0].shape[0])]
    mels = w_mel.shape[1]
    keep, send = call(
        functools.partial(back_kernel, tuple(blocks)),
        (array((rows, mels)),) * 2,
        (info, residual, w_mel.T, mods, w_out) + tuple(back),
        [
            VMEM((chip_rows, HEADS * HEAD_DIM), jnp.bfloat16),
            VMEM((chip_rows, width), jnp.float32),
            VMEM((chip_rows, mels), jnp.float32),
        ],
    )
    other = across(send, 1, count)
    first = jnp.where(is_first > 0.5, keep, other)
    second = jnp.where(is_first > 0.5, other, keep)
    guided = first + guidance[0] * (first - second)
    velocity = jnp.where(live > 0.5, guided, 0.0)
    progress = step_index[0].astype(jnp.float32) / STEPS
    time_now = 1.0 - jnp.cos(0.5 * jnp.pi * progress)
    return (velocity, latent + (1.0 - time_now) * velocity)


def solution(mesh):
    return jax.shard_map(
        per_device,
        mesh=mesh,
        in_specs=(
            P(None, ("clip", "seq"), None),
            P(("clip", "seq"), None),
            P("clip"),
            P(),
            P(),
            P(),
            P(),
            P(),
            P(),
            P(),
        ),
        out_specs=(P(("clip", "seq"), None), P(("clip", "seq"), None)),
        check_vma=False,
    )
```

```python
import functools

import jax
import jax.numpy as jnp
from jax import lax
from jax.experimental import pallas as pl
from jax.experimental.pallas import tpu as pltpu
from jax.sharding import PartitionSpec as P


HEADS = 16
HEAD_DIM = 64
KERNEL = 31
STEPS = 32
LANES = 128
HALO = 16


EPSILON = 1e-06
NEGATIVE = -1e30
CORE, CHIP, LENGTH = 0, 1, 2
VMEM = pltpu.VMEM
SMEM = pltpu.SMEM
GRANT = 12 << 20


def vmem_spec():
    return pl.BlockSpec(memory_space=VMEM)


def smem_spec():
    return pl.BlockSpec(memory_space=SMEM)


def rotary_tables(positions):
    half_dim = HEAD_DIM // 2
    lane = jnp.arange(LANES, dtype=jnp.int32)
    inverse = 10000.0 ** (-(lane % half_dim).astype(jnp.float32) / half_dim)
    angles = positions.astype(jnp.float32)[:, None] * inverse[None, :]
    sign = jnp.where(lane % HEAD_DIM < half_dim, -1.0, 1.0)
    return jnp.cos(angles), jnp.sin(angles) * sign[None, :]


def hbm_spec():
    return pl.BlockSpec(memory_space=pltpu.HBM)


def tile_lanes(tile):
    return pl.ds(pl.multiple_of(tile * LANES, LANES), LANES)


def row_norm(load, store, tiles, mod_ref, row, total):
    width = tiles * LANES
    mean = jnp.sum(total, axis=-1, keepdims=True) * (1.0 / width)

    def square(tile, acc):
        centered = load(tile) - mean
        return acc + centered * centered

    squares = lax.fori_loop(0, tiles, square, jnp.zeros(total.shape, jnp.float32), unroll=6)
    variance = jnp.sum(squares, axis=-1, keepdims=True) * (1.0 / width)
    factor = lax.rsqrt(variance + EPSILON)

    def write(tile, carry):
        lanes = tile_lanes(tile)
        scale = 1.0 + mod_ref[row + 1 : row + 2, lanes]
        shift = mod_ref[row : row + 1, lanes]
        store(lanes, (load(tile) - mean) * factor * scale + shift)
        return carry

    lax.fori_loop(0, tiles, write, 0, unroll=6)


def run_copies(pairs, sems):
    copies = [
        pltpu.make_async_copy(source, target, sems.at[at])
        for at, (source, target) in enumerate(pairs)
    ]
    for copy in copies:
        copy.start()
    for copy in copies:
        copy.wait()


def stage_kernel(
    info_ref, hidden_hbm, taps_hbm, mod_hbm, own_ref, taps_ref, mod_ref, first_ref, live_ref, sems
):
    rows = own_ref.shape[0]
    core = info_ref[CORE]
    first_ref[...] = jnp.zeros(first_ref.shape, jnp.float32) + (1 - core).astype(jnp.float32)
    row = lax.broadcasted_iota(jnp.int32, live_ref.shape, 0)
    frame = row + (2 * info_ref[CHIP] + core) * rows
    live_ref[...] = (frame < info_ref[LENGTH]).astype(jnp.float32)
    run_copies(
        [(hidden_hbm.at[core], own_ref), (taps_hbm, taps_ref), (mod_hbm, mod_ref)], sems
    )


def front_kernel(
    first_pair, info_ref, own_ref, partner_ref, near_ref, far_ref, taps_ref, mod_ref, cos_ref, sin_ref,
    weight_hbm, residual_ref, normed_ref, weight_ref, *refs,
):
    *out_refs, padded, sems = refs
    rows, width = own_ref.shape
    halo = near_ref.shape[1]
    total_rows = 2 * rows
    tiles = width // LANES
    parts = sems.shape[0]
    depth = width // parts
    loads = []
    for part in range(parts):
        here = pl.ds(part * depth, depth)
        loads.append(
            pltpu.make_async_copy(weight_hbm.at[here], weight_ref.at[here], sems.at[part])
        )
    for load in loads:
        load.start()
    length, core = info_ref[LENGTH], info_ref[CORE]
    offset = info_ref[CHIP] * total_rows
    span = total_rows + 2 * halo
    frame = offset - halo + lax.broadcasted_iota(jnp.int32, (span, LANES), 0)
    live = ((frame >= 0) & (frame < length)).astype(jnp.float32)
    first = halo - KERNEL // 2
    own_at = pl.ds(pl.multiple_of(halo + core * rows, 8), rows)
    partner_at = pl.ds(pl.multiple_of(halo + (1 - core) * rows, 8), rows)
    near_at = pl.ds(pl.multiple_of(core * (halo + total_rows), 8), halo)
    far_at = pl.ds(pl.multiple_of((1 - core) * (halo + total_rows), 8), halo)

    def convolve(tile, total):
        lanes = tile_lanes(tile)
        padded[near_at] = near_ref[core, :, lanes].astype(jnp.float32)
        padded[far_at] = far_ref[core, :, lanes].astype(jnp.float32)
        padded[own_at] = own_ref[:, lanes].astype(jnp.float32)
        padded[partner_at] = partner_ref[:, lanes].astype(jnp.float32)
        own = padded[halo : halo + total_rows]
        padded[...] = padded[...] * live
        acc = jnp.zeros((total_rows, LANES), jnp.float32)
        for tap in range(KERNEL):
            acc = acc + taps_ref[tap : tap + 1, lanes] * padded[
                first + tap : first + tap + total_rows
            ]
        grown = jnp.exp(jnp.minimum(acc, 20.0))
        product = grown * (grown + 2.0)
        value = own + acc * (product / (product + 2.0))
        residual_ref[:, lanes] = value
        return total + value

    total = lax.fori_loop(
        0, tiles, convolve, jnp.zeros((total_rows, LANES), jnp.float32), unroll=3
    )

    def store(lanes, value):
        normed_ref[:, lanes] = value.astype(jnp.bfloat16)

    row_norm(lambda tile: residual_ref[:, tile_lanes(tile)], store, tiles, mod_ref, 0, total)
    if first_pair is None:
        for load in loads:
            load.wait()
    else:
        project_landing(
            first_pair, info_ref[CHIP], loads, normed_ref, weight_ref, cos_ref, sin_ref, out_refs
        )


def pair_lanes(chip, apart, part, attn):
    wide = 2 * LANES
    start = part * attn + ((chip ^ apart) >> 1) * wide
    return pl.ds(pl.multiple_of(start, wide), wide)


def store_pair(products, chip, cos_ref, sin_ref, out_refs):
    rows = cos_ref.shape[0]
    half = HEAD_DIM // 2
    cosine, sine = cos_ref[...], sin_ref[...]
    lower = lax.broadcasted_iota(jnp.int32, (rows, LANES), 1) % HEAD_DIM < half
    swap = jnp.full((rows, LANES), chip & 1, jnp.int32) > 0
    for part, both in enumerate(products):
        sides = []
        for side in range(2):
            value = both[:, side * LANES : (side + 1) * LANES]
            if part < 2:
                swapped = jnp.where(
                    lower, pltpu.roll(value, LANES - half, 1), pltpu.roll(value, half, 1)
                )
                value = value * cosine + swapped * sine
            if part == 0:
                value = value * HEAD_DIM**-0.5
            sides.append(value)
        out_refs[0][part] = jnp.where(swap, sides[1], sides[0]).astype(jnp.bfloat16)
        out_refs[1][part] = jnp.where(swap, sides[0], sides[1]).astype(jnp.bfloat16)


def project_landing(apart, chip, loads, normed_ref, weight_ref, cos_ref, sin_ref, out_refs):
    depth = weight_ref.shape[0] // len(loads)
    attn = weight_ref.shape[1] // 3
    products = [jnp.zeros((normed_ref.shape[0], 2 * LANES), jnp.float32)] * 3
    for at, load in enumerate(loads):
        load.wait()
        here = slice(at * depth, (at + 1) * depth)
        for part in range(3):
            products[part] = products[part] + jnp.dot(
                normed_ref[:, here],
                weight_ref[here, pair_lanes(chip, apart, part, attn)],
                preferred_element_type=jnp.float32,
            )
    store_pair(products, chip, cos_ref, sin_ref, out_refs)


def project_kernel(firsts, origin, info_ref, normed_ref, weight_ref, cos_ref, sin_ref, *out_refs):
    chip = info_ref[CHIP] if origin is None else origin
    attn = weight_ref.shape[1] // 3
    for at, apart in enumerate(firsts):
        products = [
            jnp.dot(
                normed_ref[...],
                weight_ref[:, pair_lanes(chip, apart, part, attn)],
                preferred_element_type=jnp.float32,
            )
            for part in range(3)
        ]
        store_pair(products, chip, cos_ref, sin_ref, out_refs[2 * at : 2 * at + 2])


def place_keys(info_ref, apart, got_ref, keys, values, first):
    _, rows, _ = got_ref.shape
    chip = info_ref[CHIP] ^ apart
    lane = lax.broadcasted_iota(jnp.int32, (rows, LANES), 1)
    row = lax.broadcasted_iota(jnp.int32, (rows, LANES), 0)
    here = slice(first, first + rows)
    keys[here, :LANES] = got_ref[1]
    dead = (lane == 0) & (row + chip * rows >= info_ref[LENGTH])
    keys[here, LANES:] = jnp.where(dead, NEGATIVE, 0.0).astype(jnp.bfloat16)
    values[here, :] = got_ref[2]


def place_queries(query_refs, queries):
    _, rows, _ = query_refs[0].shape
    low = lax.broadcasted_iota(jnp.int32, (rows, LANES), 1) < HEAD_DIM
    zero = jnp.zeros((rows, LANES), jnp.bfloat16)
    queries[:, LANES:] = jnp.where(
        lax.broadcasted_iota(jnp.int32, (queries.shape[0], LANES), 1) == 0, 1.0, 0.0
    ).astype(jnp.bfloat16)
    for at, query_ref in enumerate(query_refs):
        query = query_ref[0]
        base = 2 * at * rows
        queries[base : base + rows, :LANES] = jnp.where(low, query, zero)
        queries[base + rows : base + 2 * rows, :LANES] = jnp.where(low, zero, query)


def score(queries, keys):
    return lax.dot_general(
        queries, keys, (((1,), (1,)), ((), ())), preferred_element_type=jnp.float32
    )


def mix(weights, values):
    return jnp.dot(weights.astype(jnp.bfloat16), values, preferred_element_type=jnp.float32)


def store_heads(mixed, out_ref, first):
    _, rows, _ = out_ref.shape
    low = lax.broadcasted_iota(jnp.int32, (rows, LANES), 1) < HEAD_DIM
    for at in range(mixed.shape[0] // (2 * rows)):
        base = 2 * at * rows
        out_ref[first + at] = jnp.where(
            low, mixed[base : base + rows], mixed[base + rows : base + 2 * rows]
        ).astype(jnp.bfloat16)


def attend_rows(keys, values, queries, out_ref, first):
    _, rows, _ = out_ref.shape
    total = queries.shape[0]
    for base in range(0, total, 4 * rows):
        block = slice(base, min(base + 4 * rows, total))
        scores = score(queries[block, :], keys[...])
        weights = jnp.exp(scores - jnp.max(scores, axis=1, keepdims=True))
        weight_sum = jnp.sum(weights, axis=1, keepdims=True)
        store_heads(mix(weights, values[...]) / weight_sum, out_ref, first + base // (2 * rows))


def attend_early_kernel(info_ref, *refs):
    chips = len(refs) - 6
    got_refs = refs[:chips]
    keys, values, queries, mixed_ref, peak_ref, sum_ref = refs[chips:]
    _, rows, _ = got_refs[0].shape
    for apart, got_ref in enumerate(got_refs):
        place_keys(info_ref, apart, got_ref, keys, values, apart * rows)
    place_queries(got_refs[1::2], queries)
    scores = score(queries[...], keys[...])
    peak = jnp.max(scores, axis=1, keepdims=True)
    weights = jnp.exp(scores - peak)
    peak_ref[...] = jnp.broadcast_to(peak, peak_ref.shape)
    sum_ref[...] = jnp.broadcast_to(jnp.sum(weights, axis=1, keepdims=True), sum_ref.shape)
    mixed_ref[...] = mix(weights, values[...])


def attend_last_kernel(
    info_ref, early_keys, early_values, early_queries, mixed_ref, peak_ref, sum_ref, last_ref,
    out_ref, keys, values, queries,
):
    held, _ = early_values.shape
    _, rows, _ = last_ref.shape
    keys[:held, :] = early_keys[...]
    values[:held, :] = early_values[...]
    place_keys(info_ref, held // rows, last_ref, keys, values, held)
    place_queries([last_ref], queries)
    attend_rows(keys, values, queries, out_ref, out_ref.shape[0] - 1)
    scores = score(early_queries[...], keys[held:, :])
    peak = peak_ref[...]
    joined = jnp.maximum(peak, jnp.max(scores, axis=1, keepdims=True))
    scale = jnp.exp(peak - joined)
    weights = jnp.exp(scores - joined[:, : scores.shape[1]])
    weight_sum = sum_ref[...] * scale + jnp.sum(weights, axis=1, keepdims=True)
    mixed = mixed_ref[...] * scale + mix(weights, values[held:, :])
    store_heads(mixed / weight_sum, out_ref, 0)


def attend_second_kernel(info_ref, keys, values, *refs):
    del info_ref
    out_ref, queries = refs[-2:]
    place_queries(refs[:-2], queries)
    attend_rows(keys, values, queries, out_ref, 0)


def merge_kernel(info_ref, own_ref, got_ref, *out_refs):
    del info_ref
    for at, out_ref in enumerate(out_refs):
        out_ref[0] = own_ref[at + 1]
        out_ref[1] = got_ref[at + 1]


def back_kernel(blocks, info_ref, residual, w_mel, mod_ref, w_out_ref, *refs):
    count = 1 + max(at for at, _, _ in blocks)
    got_refs = refs[:count]
    keep_ref, send_ref, attended, after, speed = refs[count:]
    rows, width = residual.shape
    tiles = width // LANES
    core, chip = info_ref[CORE], info_ref[CHIP]
    for at, place, apart in blocks:
        group = place if apart is None else chip ^ apart
        attended[:, tile_lanes(group)] = got_refs[at][place]
    wide = 2 * LANES
    total = jnp.zeros((rows, LANES), jnp.float32)
    for block in range(width // wide):
        lanes = slice(block * wide, (block + 1) * wide)
        branch = jnp.dot(attended[...], w_out_ref[:, lanes], preferred_element_type=jnp.float32)
        value = residual[:, lanes] + mod_ref[2:3, lanes] * branch
        after[:, lanes] = value
        total = total + value[:, :LANES] + value[:, LANES:]

    def store(lanes, value):
        after[:, lanes] = value

    row_norm(lambda tile: after[:, tile_lanes(tile)], store, tiles, mod_ref, 3, total)
    speed[...] = lax.dot_general(
        after[...].astype(jnp.bfloat16), w_mel[...], (((1,), (1,)), ((), ())),
        preferred_element_type=jnp.float32,
    )
    half = rows // 2
    keep_ref[...] = speed[pl.ds(pl.multiple_of(core * half, 8), half), :]
    send_ref[...] = speed[pl.ds(pl.multiple_of((1 - core) * half, 8), half), :]


def call(kernel, out_shape, inputs, scratch, hbm=()):
    single = not isinstance(out_shape, tuple)
    specs = [hbm_spec() if at in hbm else vmem_spec() for at in range(1, len(inputs))]
    inputs = list(inputs)
    for at in hbm:
        inputs[at] = pltpu.with_memory_space_constraint(inputs[at], pltpu.HBM)
    return pl.pallas_call(
        kernel,
        out_shape=out_shape,
        in_specs=[smem_spec()] + specs,
        out_specs=vmem_spec() if single else tuple(vmem_spec() for _ in out_shape),
        scratch_shapes=scratch,
        compiler_params=pltpu.CompilerParams(vmem_limit_bytes=GRANT),
    )(*inputs)


def array(shape, dtype=jnp.float32):
    return jax.ShapeDtypeStruct(shape, dtype)


def project(normed, w_qkv, tables, info, firsts, origin=None):
    shape = array((3, normed.shape[0], LANES), jnp.bfloat16)
    return call(
        functools.partial(project_kernel, tuple(firsts), origin),
        (shape,) * (2 * len(firsts)),
        (info, normed, w_qkv) + tables,
        [],
    )


def same_core(count):
    return [list(range(core, count, 2)) for core in range(2)]


def facing_pairs(clips, count):
    pairs = []
    for clip in range(clips):
        base = clip * count
        for at in range(1, count - 1, 2):
            pairs += [(base + at, base + at + 1), (base + at + 1, base + at)]
        if clip ^ 1 < clips:
            pairs += [(base + end, (clip ^ 1) * count + end) for end in (0, count - 1)]
    return pairs


def across(value, apart, count):
    return lax.ppermute(value, "seq", [(i, i ^ apart) for i in range(count)])


def to_groups(values, subs):
    rows, _ = values.shape
    grouped = values.reshape(subs, rows // subs, HEADS, HEAD_DIM).transpose(2, 0, 1, 3)
    return grouped.reshape(HEADS * subs, rows // subs, HEAD_DIM)


def from_groups(grouped, rows, subs):
    split = grouped.reshape(HEADS, subs, rows // subs, HEAD_DIM).transpose(1, 2, 0, 3)
    return split.reshape(rows, HEADS * HEAD_DIM)


def attend_blocks(queries, keys, values, live):
    groups, total, _ = queries.shape
    block = max(size for size in range(1, min(total, 1024) + 1) if total % size == 0)
    blocks = queries.reshape(groups, total // block, block, HEAD_DIM).transpose(1, 0, 2, 3)
    live = live[None, None, :]

    def one_block(query):
        scores = jnp.einsum("gqd,gkd->gqk", query, keys, preferred_element_type=jnp.float32)
        scores = jnp.where(live, scores, NEGATIVE)
        weights = jnp.exp(scores - jnp.max(scores, axis=-1, keepdims=True))
        weights = jnp.where(live, weights, 0.0)
        mixed = jnp.einsum(
            "gqk,gkd->gqd",
            weights.astype(jnp.bfloat16),
            values,
            preferred_element_type=jnp.float32,
        )
        return (mixed / jnp.sum(weights, axis=-1)[..., None]).astype(jnp.bfloat16)

    return lax.map(one_block, blocks).transpose(1, 0, 2, 3).reshape(groups, total, HEAD_DIM)


def attend_any(normed, w_qkv, tables, info, length, count):
    rows = normed.shape[0]
    chips = count // 2
    groups = HEADS * HEAD_DIM // LANES
    sent = project(normed, w_qkv, tables, info, range(0, groups, 2), 0)
    subs = max(1, chips // HEADS)
    chip = lax.axis_index("seq") >> 1
    part_rows = rows // subs

    def exchange(part):
        whole = jnp.concatenate([group[part] for group in sent], axis=1)
        return lax.all_to_all(
            to_groups(whole, subs), "seq", split_axis=0, concat_axis=1, tiled=True,
            axis_index_groups=same_core(count),
        )

    queries, keys, values = (exchange(part) for part in range(3))

    def frames_of(sub):
        start = jnp.arange(chips, dtype=jnp.int32)[:, None] * rows + sub * part_rows
        return (start + jnp.arange(part_rows, dtype=jnp.int32)[None, :]).reshape(-1)

    frames = [frames_of(chip % subs)]
    parts = [(keys, values)]
    for apart in range(1, subs):
        perm = []
        for i in range(count):
            at = i // 2
            target = at - at % subs + (at + apart) % subs
            perm.append((i, 2 * target + i % 2))
        parts.append(tuple(lax.ppermute(part, "seq", perm) for part in (keys, values)))
        frames.append(frames_of((chip - apart) % subs))
    keys = jnp.concatenate([part[0] for part in parts], axis=1)
    values = jnp.concatenate([part[1] for part in parts], axis=1)
    attended = attend_blocks(queries, keys, values, jnp.concatenate(frames) < length)
    back = lax.all_to_all(
        attended, "seq", split_axis=1, concat_axis=0, tiled=True,
        axis_index_groups=same_core(count),
    )
    return from_groups(back, rows, subs).reshape(rows, groups, LANES).transpose(1, 0, 2)


def chips_hold_groups(count):
    chips = count // 2
    return chips == HEADS * HEAD_DIM // LANES and chips >= 4 and chips & (chips - 1) == 0


def send_order(chips):
    far = list(range(chips // 2, chips, 2))
    return far[:1] + list(range(2, chips // 2, 2)) + far[1:] + [0]


def attend_chips(made, normed, w_qkv, tables, info, count):
    rows = normed.shape[0]
    chips = count // 2
    held = {}
    for first in send_order(chips):
        if held:
            made = project(normed, w_qkv, tables, info, [first])
        for side in range(2):
            apart = first + side
            held[apart] = across(made[side], 2 * apart, count) if apart else made[side]
    total, half = chips * rows, chips // 2
    early, early_rows = total - rows, 2 * (half - 1) * rows
    parts = call(
        attend_early_kernel,
        (
            array((early, 2 * LANES), jnp.bfloat16),
            array((early, LANES), jnp.bfloat16),
            array((early_rows, 2 * LANES), jnp.bfloat16),
        )
        + (array((early_rows, LANES)),) * 3,
        (info,) + tuple(held[apart] for apart in range(chips - 1)),
        [],
    )
    crossing, keys, values = call(
        attend_last_kernel,
        (
            array((half, rows, LANES), jnp.bfloat16),
            array((total, 2 * LANES), jnp.bfloat16),
            array((total, LANES), jnp.bfloat16),
        ),
        (info,) + tuple(parts) + (held[chips - 1],),
        [VMEM((2 * rows, 2 * LANES), jnp.bfloat16)],
    )
    crossed = across(crossing, 2, count)
    staying = call(
        attend_second_kernel,
        array((half, rows, LANES), jnp.bfloat16),
        (info, keys, values) + tuple(held[apart] for apart in range(0, chips, 2)),
        [VMEM((total, 2 * LANES), jnp.bfloat16)],
    )
    joined = call(
        merge_kernel,
        (array((2, rows, LANES), jnp.bfloat16),) * (half - 1),
        (info, staying, crossed),
        [],
    )
    back, blocks = [staying, crossed], [(0, 0, 0), (1, 0, 1)]
    apart_first = sorted(range(1, half), reverse=True)
    got = {apart: across(joined[apart - 1], 4 * apart, count) for apart in apart_first}
    for apart in range(1, half):
        blocks += [(len(back), side, 2 * apart + side) for side in range(2)]
        back.append(got[apart])
    return back, blocks


def per_device(
    hidden, latent, lengths, step_index, guidance, modulation, conv_kernel, w_qkv, w_out, w_mel
):
    copies, rows, width = hidden.shape
    count = lax.axis_size("seq")
    chips = count // 2
    index = lax.axis_index("seq").astype(jnp.int32)
    chip, core = index >> 1, index & 1
    chip_rows = 2 * rows
    info = jnp.stack([core, chip, lengths[0]])

    edges = lax.dynamic_slice(hidden, (0, core * (rows - HALO), 0), (copies, HALO, width))
    partner = lax.dynamic_slice(hidden, (1 - core, 0, 0), (1, rows, width))[0]
    near = lax.ppermute(edges, ("clip", "seq"), facing_pairs(lax.axis_size("clip"), count))
    far = across(near, 1, count)
    partner = across(partner, 1, count)
    own, taps, mods, is_first, live = call(
        stage_kernel,
        (
            array((rows, width), jnp.bfloat16),
            array(conv_kernel.shape),
            array(modulation.shape),
            array(latent.shape),
            array(latent.shape),
        ),
        (info, hidden, conv_kernel, modulation),
        [pltpu.SemaphoreType.DMA((3,))],
        hbm=(1, 2, 3),
    )
    tables = rotary_tables(chip * chip_rows + jnp.arange(chip_rows, dtype=jnp.int32))
    first_pair = send_order(chips)[0] if chips_hold_groups(count) else None
    group = array((3, chip_rows, LANES), jnp.bfloat16)
    residual, normed, weight, *made = call(
        functools.partial(front_kernel, first_pair),
        (
            array((chip_rows, width)),
            array((chip_rows, width), jnp.bfloat16),
            array(w_qkv.shape, jnp.bfloat16),
        )
        + (group,) * (0 if first_pair is None else 2),
        (info, own, partner, near, far, taps, mods) + tables + (w_qkv,),
        [
            VMEM((chip_rows + 2 * HALO, LANES), jnp.float32),
            pltpu.SemaphoreType.DMA((width // (2 * LANES),)),
        ],
        hbm=(9,),
    )
    if chips_hold_groups(count):
        back, blocks = attend_chips(made, normed, weight, tables, info, count)
    else:
        back = [attend_any(normed, weight, tables, info, lengths[0], count)]
        blocks = [(0, group, None) for group in range(back[0].shape[0])]
    mels = w_mel.shape[1]
    keep, send = call(
        functools.partial(back_kernel, tuple(blocks)),
        (array((rows, mels)),) * 2,
        (info, residual, w_mel.T, mods, w_out) + tuple(back),
        [
            VMEM((chip_rows, HEADS * HEAD_DIM), jnp.bfloat16),
            VMEM((chip_rows, width), jnp.float32),
            VMEM((chip_rows, mels), jnp.float32),
        ],
    )
    other = across(send, 1, count)
    first = jnp.where(is_first > 0.5, keep, other)
    second = jnp.where(is_first > 0.5, other, keep)
    guided = first + guidance[0] * (first - second)
    velocity = jnp.where(live > 0.5, guided, 0.0)
    progress = step_index[0].astype(jnp.float32) / STEPS
    time_now = 1.0 - jnp.cos(0.5 * jnp.pi * progress)
    return (velocity, latent + (1.0 - time_now) * velocity)


def solution(mesh):
    return jax.shard_map(
        per_device,
        mesh=mesh,
        in_specs=(
            P(None, ("clip", "seq"), None),
            P(("clip", "seq"), None),
            P("clip"),
            P(),
            P(),
            P(),
            P(),
            P(),
            P(),
            P(),
        ),
        out_specs=(P(("clip", "seq"), None), P(("clip", "seq"), None)),
        check_vma=False,
    )
```

```python
import functools

import jax
import jax.numpy as jnp
from jax import lax
from jax.experimental import pallas as pl
from jax.experimental.pallas import tpu as pltpu
from jax.sharding import PartitionSpec as P


HEADS = 16
HEAD_DIM = 64
KERNEL = 31
STEPS = 32
LANES = 128
HALO = 16


EPSILON = 1e-06
NEGATIVE = -1e30
CORE, CHIP, LENGTH = 0, 1, 2
VMEM = pltpu.VMEM
SMEM = pltpu.SMEM
GRANT = 12 << 20


def vmem_spec():
    return pl.BlockSpec(memory_space=VMEM)


def smem_spec():
    return pl.BlockSpec(memory_space=SMEM)


def rotary_tables(positions):
    half_dim = HEAD_DIM // 2
    lane = jnp.arange(LANES, dtype=jnp.int32)
    inverse = 10000.0 ** (-(lane % half_dim).astype(jnp.float32) / half_dim)
    angles = positions.astype(jnp.float32)[:, None] * inverse[None, :]
    sign = jnp.where(lane % HEAD_DIM < half_dim, -1.0, 1.0)
    return jnp.cos(angles), jnp.sin(angles) * sign[None, :]


def hbm_spec():
    return pl.BlockSpec(memory_space=pltpu.HBM)


def tile_lanes(tile):
    return pl.ds(pl.multiple_of(tile * LANES, LANES), LANES)


def row_norm(load, store, tiles, mod_ref, row, total):
    width = tiles * LANES
    mean = jnp.sum(total, axis=-1, keepdims=True) * (1.0 / width)

    def square(tile, acc):
        centered = load(tile) - mean
        return acc + centered * centered

    squares = lax.fori_loop(0, tiles, square, jnp.zeros(total.shape, jnp.float32), unroll=6)
    variance = jnp.sum(squares, axis=-1, keepdims=True) * (1.0 / width)
    factor = lax.rsqrt(variance + EPSILON)

    def write(tile, carry):
        lanes = tile_lanes(tile)
        scale = 1.0 + mod_ref[row + 1 : row + 2, lanes]
        shift = mod_ref[row : row + 1, lanes]
        store(lanes, (load(tile) - mean) * factor * scale + shift)
        return carry

    lax.fori_loop(0, tiles, write, 0, unroll=6)


def run_copies(pairs, sems):
    copies = [
        pltpu.make_async_copy(source, target, sems.at[at])
        for at, (source, target) in enumerate(pairs)
    ]
    for copy in copies:
        copy.start()
    for copy in copies:
        copy.wait()


def stage_kernel(
    info_ref, hidden_hbm, taps_hbm, mod_hbm, own_ref, taps_ref, mod_ref, first_ref, live_ref, sems
):
    rows = own_ref.shape[0]
    core = info_ref[CORE]
    first_ref[...] = jnp.zeros(first_ref.shape, jnp.float32) + (1 - core).astype(jnp.float32)
    row = lax.broadcasted_iota(jnp.int32, live_ref.shape, 0)
    frame = row + (2 * info_ref[CHIP] + core) * rows
    live_ref[...] = (frame < info_ref[LENGTH]).astype(jnp.float32)
    run_copies(
        [(hidden_hbm.at[core], own_ref), (taps_hbm, taps_ref), (mod_hbm, mod_ref)], sems
    )


def front_kernel(
    first_pair, info_ref, own_ref, partner_ref, near_ref, far_ref, taps_ref, mod_ref, cos_ref, sin_ref,
    weight_hbm, residual_ref, normed_ref, weight_ref, *refs,
):
    *out_refs, padded, sems = refs
    rows, width = own_ref.shape
    halo = near_ref.shape[1]
    total_rows = 2 * rows
    tiles = width // LANES
    parts = sems.shape[0]
    depth = width // parts
    loads = []
    for part in range(parts):
        here = pl.ds(part * depth, depth)
        loads.append(
            pltpu.make_async_copy(weight_hbm.at[here], weight_ref.at[here], sems.at[part])
        )
    for load in loads:
        load.start()
    length, core = info_ref[LENGTH], info_ref[CORE]
    offset = info_ref[CHIP] * total_rows
    span = total_rows + 2 * halo
    frame = offset - halo + lax.broadcasted_iota(jnp.int32, (span, LANES), 0)
    live = ((frame >= 0) & (frame < length)).astype(jnp.float32)
    first = halo - KERNEL // 2
    own_at = pl.ds(pl.multiple_of(halo + core * rows, 8), rows)
    partner_at = pl.ds(pl.multiple_of(halo + (1 - core) * rows, 8), rows)
    near_at = pl.ds(pl.multiple_of(core * (halo + total_rows), 8), halo)
    far_at = pl.ds(pl.multiple_of((1 - core) * (halo + total_rows), 8), halo)

    def convolve(tile, total):
        lanes = tile_lanes(tile)
        padded[near_at] = near_ref[core, :, lanes].astype(jnp.float32)
        padded[far_at] = far_ref[core, :, lanes].astype(jnp.float32)
        padded[own_at] = own_ref[:, lanes].astype(jnp.float32)
        padded[partner_at] = partner_ref[:, lanes].astype(jnp.float32)
        own = padded[halo : halo + total_rows]
        padded[...] = padded[...] * live
        acc = jnp.zeros((total_rows, LANES), jnp.float32)
        for tap in range(KERNEL):
            acc = acc + taps_ref[tap : tap + 1, lanes] * padded[
                first + tap : first + tap + total_rows
            ]
        grown = jnp.exp(jnp.minimum(acc, 20.0))
        product = grown * (grown + 2.0)
        value = own + acc * (product / (product + 2.0))
        residual_ref[:, lanes] = value
        return total + value

    total = lax.fori_loop(
        0, tiles, convolve, jnp.zeros((total_rows, LANES), jnp.float32), unroll=3
    )

    def store(lanes, value):
        normed_ref[:, lanes] = value.astype(jnp.bfloat16)

    row_norm(lambda tile: residual_ref[:, tile_lanes(tile)], store, tiles, mod_ref, 0, total)
    if first_pair is None:
        for load in loads:
            load.wait()
    else:
        project_landing(
            first_pair, info_ref[CHIP], loads, normed_ref, weight_ref, cos_ref, sin_ref, out_refs
        )


def pair_lanes(chip, apart, part, attn):
    wide = 2 * LANES
    start = part * attn + ((chip ^ apart) >> 1) * wide
    return pl.ds(pl.multiple_of(start, wide), wide)


def store_pair(products, chip, cos_ref, sin_ref, out_refs):
    rows = cos_ref.shape[0]
    half = HEAD_DIM // 2
    cosine, sine = cos_ref[...], sin_ref[...]
    lower = lax.broadcasted_iota(jnp.int32, (rows, LANES), 1) % HEAD_DIM < half
    swap = jnp.full((rows, LANES), chip & 1, jnp.int32) > 0
    for part, both in enumerate(products):
        sides = []
        for side in range(2):
            value = both[:, side * LANES : (side + 1) * LANES]
            if part < 2:
                swapped = jnp.where(
                    lower, pltpu.roll(value, LANES - half, 1), pltpu.roll(value, half, 1)
                )
                value = value * cosine + swapped * sine
            if part == 0:
                value = value * HEAD_DIM**-0.5
            sides.append(value)
        out_refs[0][part] = jnp.where(swap, sides[1], sides[0]).astype(jnp.bfloat16)
        out_refs[1][part] = jnp.where(swap, sides[0], sides[1]).astype(jnp.bfloat16)


def project_landing(apart, chip, loads, normed_ref, weight_ref, cos_ref, sin_ref, out_refs):
    depth = weight_ref.shape[0] // len(loads)
    attn = weight_ref.shape[1] // 3
    products = [jnp.zeros((normed_ref.shape[0], 2 * LANES), jnp.float32)] * 3
    for at, load in enumerate(loads):
        load.wait()
        here = slice(at * depth, (at + 1) * depth)
        for part in range(3):
            products[part] = products[part] + jnp.dot(
                normed_ref[:, here],
                weight_ref[here, pair_lanes(chip, apart, part, attn)],
                preferred_element_type=jnp.float32,
            )
    store_pair(products, chip, cos_ref, sin_ref, out_refs)


def project_kernel(firsts, origin, info_ref, normed_ref, weight_ref, cos_ref, sin_ref, *out_refs):
    chip = info_ref[CHIP] if origin is None else origin
    attn = weight_ref.shape[1] // 3
    for at, apart in enumerate(firsts):
        products = [
            jnp.dot(
                normed_ref[...],
                weight_ref[:, pair_lanes(chip, apart, part, attn)],
                preferred_element_type=jnp.float32,
            )
            for part in range(3)
        ]
        store_pair(products, chip, cos_ref, sin_ref, out_refs[2 * at : 2 * at + 2])


def place_keys(info_ref, apart, got_ref, keys, values, first):
    _, rows, _ = got_ref.shape
    chip = info_ref[CHIP] ^ apart
    lane = lax.broadcasted_iota(jnp.int32, (rows, LANES), 1)
    row = lax.broadcasted_iota(jnp.int32, (rows, LANES), 0)
    here = slice(first, first + rows)
    keys[here, :LANES] = got_ref[1]
    dead = (lane == 0) & (row + chip * rows >= info_ref[LENGTH])
    keys[here, LANES:] = jnp.where(dead, NEGATIVE, 0.0).astype(jnp.bfloat16)
    values[here, :] = got_ref[2]


def place_queries(query_refs, queries, first=0):
    _, rows, _ = query_refs[0].shape
    low = lax.broadcasted_iota(jnp.int32, (rows, LANES), 1) < HEAD_DIM
    zero = jnp.zeros((rows, LANES), jnp.bfloat16)
    one = jnp.where(
        lax.broadcasted_iota(jnp.int32, (2 * rows, LANES), 1) == 0, 1.0, 0.0
    ).astype(jnp.bfloat16)
    for at, query_ref in enumerate(query_refs):
        query = query_ref[0]
        base = 2 * (first + at) * rows
        queries[base : base + 2 * rows, LANES:] = one
        queries[base : base + rows, :LANES] = jnp.where(low, query, zero)
        queries[base + rows : base + 2 * rows, :LANES] = jnp.where(low, zero, query)


def score(queries, keys):
    return lax.dot_general(
        queries, keys, (((1,), (1,)), ((), ())), preferred_element_type=jnp.float32
    )


def mix(weights, values):
    return jnp.dot(weights.astype(jnp.bfloat16), values, preferred_element_type=jnp.float32)


def store_heads(mixed, out_ref, places):
    _, rows, _ = out_ref.shape
    low = lax.broadcasted_iota(jnp.int32, (rows, LANES), 1) < HEAD_DIM
    for at in range(mixed.shape[0] // (2 * rows)):
        base = 2 * at * rows
        out_ref[places[at]] = jnp.where(
            low, mixed[base : base + rows], mixed[base + rows : base + 2 * rows]
        ).astype(jnp.bfloat16)


def attend_rows(keys, values, queries, out_ref, places):
    _, rows, _ = out_ref.shape
    total = queries.shape[0]
    for base in range(0, total, 4 * rows):
        block = slice(base, min(base + 4 * rows, total))
        scores = score(queries[block, :], keys[...])
        weights = jnp.exp(scores - jnp.max(scores, axis=1, keepdims=True))
        weight_sum = jnp.sum(weights, axis=1, keepdims=True)
        mixed = mix(weights, values[...]) / weight_sum
        store_heads(mixed, out_ref, places[base // (2 * rows) :])


def place_chips(info_ref, aparts, first, got_refs, keys, values, queries, first_query):
    _, rows, _ = got_refs[0].shape
    for at, apart in enumerate(aparts):
        place_keys(info_ref, apart, got_refs[at], keys, values, (first + at) * rows)
    odd = [ref for apart, ref in zip(aparts, got_refs) if apart % 2]
    place_queries(odd, queries, first_query)


def prepare_kernel(aparts, info_ref, *refs):
    got_refs = refs[: len(aparts)]
    keys, values, queries = refs[len(aparts) :]
    place_chips(info_ref, aparts, 0, got_refs, keys, values, queries, 0)


def attend_early_kernel(aparts, first, first_query, info_ref, keys_in, values_in, queries_in, *refs):
    del keys_in, values_in, queries_in
    got_refs = refs[: len(aparts)]
    keys, values, queries, mixed_ref, peak_ref, sum_ref = refs[len(aparts) :]
    _, rows, _ = got_refs[0].shape
    place_chips(info_ref, aparts, first, got_refs, keys, values, queries, first_query)
    held = (first + len(aparts)) * rows
    scores = score(queries[...], keys[:held, :])
    peak = jnp.max(scores, axis=1, keepdims=True)
    weights = jnp.exp(scores - peak)
    peak_ref[...] = jnp.broadcast_to(peak, peak_ref.shape)
    sum_ref[...] = jnp.broadcast_to(jnp.sum(weights, axis=1, keepdims=True), sum_ref.shape)
    mixed_ref[...] = mix(weights, values[:held, :])


def attend_last_kernel(
    apart, places, info_ref, keys_in, values_in, early_queries, mixed_ref, peak_ref, sum_ref,
    last_ref, out_ref, keys, values, queries,
):
    del keys_in, values_in
    _, rows, _ = last_ref.shape
    held = keys.shape[0] - rows
    place_keys(info_ref, apart, last_ref, keys, values, held)
    place_queries([last_ref], queries)
    attend_rows(keys, values, queries, out_ref, (apart // 2,))
    scores = score(early_queries[...], keys[held:, :])
    peak = peak_ref[...]
    joined = jnp.maximum(peak, jnp.max(scores, axis=1, keepdims=True))
    scale = jnp.exp(peak - joined)
    weights = jnp.exp(scores - joined[:, : scores.shape[1]])
    weight_sum = sum_ref[...] * scale + jnp.sum(weights, axis=1, keepdims=True)
    mixed = mixed_ref[...] * scale + mix(weights, values[held:, :])
    store_heads(mixed / weight_sum, out_ref, places)


def attend_second_kernel(info_ref, keys, values, *refs):
    del info_ref
    out_ref, queries = refs[-2:]
    place_queries(refs[:-2], queries)
    attend_rows(keys, values, queries, out_ref, tuple(range(out_ref.shape[0])))


def merge_kernel(info_ref, own_ref, got_ref, *out_refs):
    del info_ref
    for at, out_ref in enumerate(out_refs):
        out_ref[0] = own_ref[at + 1]
        out_ref[1] = got_ref[at + 1]


def back_kernel(blocks, info_ref, residual, w_mel, mod_ref, w_out_ref, *refs):
    count = 1 + max(at for at, _, _ in blocks)
    got_refs = refs[:count]
    keep_ref, send_ref, attended, after, speed = refs[count:]
    rows, width = residual.shape
    tiles = width // LANES
    core, chip = info_ref[CORE], info_ref[CHIP]
    for at, place, apart in blocks:
        group = place if apart is None else chip ^ apart
        attended[:, tile_lanes(group)] = got_refs[at][place]
    wide = 2 * LANES
    total = jnp.zeros((rows, LANES), jnp.float32)
    for block in range(width // wide):
        lanes = slice(block * wide, (block + 1) * wide)
        branch = jnp.dot(attended[...], w_out_ref[:, lanes], preferred_element_type=jnp.float32)
        value = residual[:, lanes] + mod_ref[2:3, lanes] * branch
        after[:, lanes] = value
        total = total + value[:, :LANES] + value[:, LANES:]

    def store(lanes, value):
        after[:, lanes] = value

    row_norm(lambda tile: after[:, tile_lanes(tile)], store, tiles, mod_ref, 3, total)
    speed[...] = lax.dot_general(
        after[...].astype(jnp.bfloat16), w_mel[...], (((1,), (1,)), ((), ())),
        preferred_element_type=jnp.float32,
    )
    half = rows // 2
    keep_ref[...] = speed[pl.ds(pl.multiple_of(core * half, 8), half), :]
    send_ref[...] = speed[pl.ds(pl.multiple_of((1 - core) * half, 8), half), :]


def call(kernel, out_shape, inputs, scratch, hbm=(), aliases=None):
    single = not isinstance(out_shape, tuple)
    specs = [hbm_spec() if at in hbm else vmem_spec() for at in range(1, len(inputs))]
    inputs = list(inputs)
    for at in hbm:
        inputs[at] = pltpu.with_memory_space_constraint(inputs[at], pltpu.HBM)
    return pl.pallas_call(
        kernel,
        out_shape=out_shape,
        in_specs=[smem_spec()] + specs,
        out_specs=vmem_spec() if single else tuple(vmem_spec() for _ in out_shape),
        scratch_shapes=scratch,
        input_output_aliases=aliases or {},
        compiler_params=pltpu.CompilerParams(vmem_limit_bytes=GRANT),
    )(*inputs)


def array(shape, dtype=jnp.float32):
    return jax.ShapeDtypeStruct(shape, dtype)


def project(normed, w_qkv, tables, info, firsts, origin=None):
    shape = array((3, normed.shape[0], LANES), jnp.bfloat16)
    return call(
        functools.partial(project_kernel, tuple(firsts), origin),
        (shape,) * (2 * len(firsts)),
        (info, normed, w_qkv) + tables,
        [],
    )


def same_core(count):
    return [list(range(core, count, 2)) for core in range(2)]


def facing_pairs(clips, count):
    pairs = []
    for clip in range(clips):
        base = clip * count
        for at in range(1, count - 1, 2):
            pairs += [(base + at, base + at + 1), (base + at + 1, base + at)]
        if clip ^ 1 < clips:
            pairs += [(base + end, (clip ^ 1) * count + end) for end in (0, count - 1)]
    return pairs


def across(value, apart, count):
    return lax.ppermute(value, "seq", [(i, i ^ apart) for i in range(count)])


def to_groups(values, subs):
    rows, _ = values.shape
    grouped = values.reshape(subs, rows // subs, HEADS, HEAD_DIM).transpose(2, 0, 1, 3)
    return grouped.reshape(HEADS * subs, rows // subs, HEAD_DIM)


def from_groups(grouped, rows, subs):
    split = grouped.reshape(HEADS, subs, rows // subs, HEAD_DIM).transpose(1, 2, 0, 3)
    return split.reshape(rows, HEADS * HEAD_DIM)


def attend_blocks(queries, keys, values, live):
    groups, total, _ = queries.shape
    block = max(size for size in range(1, min(total, 1024) + 1) if total % size == 0)
    blocks = queries.reshape(groups, total // block, block, HEAD_DIM).transpose(1, 0, 2, 3)
    live = live[None, None, :]

    def one_block(query):
        scores = jnp.einsum("gqd,gkd->gqk", query, keys, preferred_element_type=jnp.float32)
        scores = jnp.where(live, scores, NEGATIVE)
        weights = jnp.exp(scores - jnp.max(scores, axis=-1, keepdims=True))
        weights = jnp.where(live, weights, 0.0)
        mixed = jnp.einsum(
            "gqk,gkd->gqd",
            weights.astype(jnp.bfloat16),
            values,
            preferred_element_type=jnp.float32,
        )
        return (mixed / jnp.sum(weights, axis=-1)[..., None]).astype(jnp.bfloat16)

    return lax.map(one_block, blocks).transpose(1, 0, 2, 3).reshape(groups, total, HEAD_DIM)


def attend_any(normed, w_qkv, tables, info, length, count):
    rows = normed.shape[0]
    chips = count // 2
    groups = HEADS * HEAD_DIM // LANES
    sent = project(normed, w_qkv, tables, info, range(0, groups, 2), 0)
    subs = max(1, chips // HEADS)
    chip = lax.axis_index("seq") >> 1
    part_rows = rows // subs

    def exchange(part):
        whole = jnp.concatenate([group[part] for group in sent], axis=1)
        return lax.all_to_all(
            to_groups(whole, subs), "seq", split_axis=0, concat_axis=1, tiled=True,
            axis_index_groups=same_core(count),
        )

    queries, keys, values = (exchange(part) for part in range(3))

    def frames_of(sub):
        start = jnp.arange(chips, dtype=jnp.int32)[:, None] * rows + sub * part_rows
        return (start + jnp.arange(part_rows, dtype=jnp.int32)[None, :]).reshape(-1)

    frames = [frames_of(chip % subs)]
    parts = [(keys, values)]
    for apart in range(1, subs):
        perm = []
        for i in range(count):
            at = i // 2
            target = at - at % subs + (at + apart) % subs
            perm.append((i, 2 * target + i % 2))
        parts.append(tuple(lax.ppermute(part, "seq", perm) for part in (keys, values)))
        frames.append(frames_of((chip - apart) % subs))
    keys = jnp.concatenate([part[0] for part in parts], axis=1)
    values = jnp.concatenate([part[1] for part in parts], axis=1)
    attended = attend_blocks(queries, keys, values, jnp.concatenate(frames) < length)
    back = lax.all_to_all(
        attended, "seq", split_axis=1, concat_axis=0, tiled=True,
        axis_index_groups=same_core(count),
    )
    return from_groups(back, rows, subs).reshape(rows, groups, LANES).transpose(1, 0, 2)


def chips_hold_groups(count):
    chips = count // 2
    return chips == HEADS * HEAD_DIM // LANES and chips >= 4 and chips & (chips - 1) == 0


def send_order(chips):
    far = list(range(chips // 2, chips, 2))
    return far[:1] + list(range(2, chips // 2, 2)) + far[1:] + [0]


def attend_chips(made, normed, w_qkv, tables, info, count):
    rows = normed.shape[0]
    chips = count // 2
    held = {}
    for first in send_order(chips):
        if held:
            made = project(normed, w_qkv, tables, info, [first])
        for side in range(2):
            apart = first + side
            held[apart] = across(made[side], 2 * apart, count) if apart else made[side]
    total, half = chips * rows, chips // 2
    last = chips - 1
    soon = (1, last - 1)
    ready = tuple(apart for apart in range(chips) if apart not in soon + (last,))
    query_order = tuple(apart for apart in ready + soon if apart % 2)
    query_rows = 2 * len(query_order) * rows
    buffers = (
        array((total, 2 * LANES), jnp.bfloat16),
        array((total, LANES), jnp.bfloat16),
        array((query_rows, 2 * LANES), jnp.bfloat16),
    )
    placed = call(
        functools.partial(prepare_kernel, ready),
        buffers,
        (info,) + tuple(held[apart] for apart in ready),
        [],
    )
    ready_odd = sum(apart % 2 for apart in ready)
    keys, values, early_queries, *parts = call(
        functools.partial(attend_early_kernel, soon, len(ready), ready_odd),
        buffers + (array((query_rows, LANES)),) * 3,
        (info,) + tuple(placed) + tuple(held[apart] for apart in soon),
        [],
        aliases={1: 0, 2: 1, 3: 2},
    )
    places = tuple(apart // 2 for apart in query_order)
    crossing, keys, values = call(
        functools.partial(attend_last_kernel, last, places),
        (array((half, rows, LANES), jnp.bfloat16),) + buffers[:2],
        (info, keys, values, early_queries) + tuple(parts) + (held[last],),
        [VMEM((2 * rows, 2 * LANES), jnp.bfloat16)],
        aliases={1: 1, 2: 2},
    )
    crossed = across(crossing, 2, count)
    staying = call(
        attend_second_kernel,
        array((half, rows, LANES), jnp.bfloat16),
        (info, keys, values) + tuple(held[apart] for apart in range(0, chips, 2)),
        [VMEM((total, 2 * LANES), jnp.bfloat16)],
    )
    joined = call(
        merge_kernel,
        (array((2, rows, LANES), jnp.bfloat16),) * (half - 1),
        (info, staying, crossed),
        [],
    )
    back, blocks = [staying, crossed], [(0, 0, 0), (1, 0, 1)]
    apart_first = sorted(range(1, half), reverse=True)
    got = {apart: across(joined[apart - 1], 4 * apart, count) for apart in apart_first}
    for apart in range(1, half):
        blocks += [(len(back), side, 2 * apart + side) for side in range(2)]
        back.append(got[apart])
    return back, blocks


def per_device(
    hidden, latent, lengths, step_index, guidance, modulation, conv_kernel, w_qkv, w_out, w_mel
):
    copies, rows, width = hidden.shape
    count = lax.axis_size("seq")
    chips = count // 2
    index = lax.axis_index("seq").astype(jnp.int32)
    chip, core = index >> 1, index & 1
    chip_rows = 2 * rows
    info = jnp.stack([core, chip, lengths[0]])

    edges = lax.dynamic_slice(hidden, (0, core * (rows - HALO), 0), (copies, HALO, width))
    partner = lax.dynamic_slice(hidden, (1 - core, 0, 0), (1, rows, width))[0]
    near = lax.ppermute(edges, ("clip", "seq"), facing_pairs(lax.axis_size("clip"), count))
    far = across(near, 1, count)
    partner = across(partner, 1, count)
    own, taps, mods, is_first, live = call(
        stage_kernel,
        (
            array((rows, width), jnp.bfloat16),
            array(conv_kernel.shape),
            array(modulation.shape),
            array(latent.shape),
            array(latent.shape),
        ),
        (info, hidden, conv_kernel, modulation),
        [pltpu.SemaphoreType.DMA((3,))],
        hbm=(1, 2, 3),
    )
    tables = rotary_tables(chip * chip_rows + jnp.arange(chip_rows, dtype=jnp.int32))
    first_pair = send_order(chips)[0] if chips_hold_groups(count) else None
    group = array((3, chip_rows, LANES), jnp.bfloat16)
    residual, normed, weight, *made = call(
        functools.partial(front_kernel, first_pair),
        (
            array((chip_rows, width)),
            array((chip_rows, width), jnp.bfloat16),
            array(w_qkv.shape, jnp.bfloat16),
        )
        + (group,) * (0 if first_pair is None else 2),
        (info, own, partner, near, far, taps, mods) + tables + (w_qkv,),
        [
            VMEM((chip_rows + 2 * HALO, LANES), jnp.float32),
            pltpu.SemaphoreType.DMA((width // (2 * LANES),)),
        ],
        hbm=(9,),
    )
    if chips_hold_groups(count):
        back, blocks = attend_chips(made, normed, weight, tables, info, count)
    else:
        back = [attend_any(normed, weight, tables, info, lengths[0], count)]
        blocks = [(0, group, None) for group in range(back[0].shape[0])]
    mels = w_mel.shape[1]
    keep, send = call(
        functools.partial(back_kernel, tuple(blocks)),
        (array((rows, mels)),) * 2,
        (info, residual, w_mel.T, mods, w_out) + tuple(back),
        [
            VMEM((chip_rows, HEADS * HEAD_DIM), jnp.bfloat16),
            VMEM((chip_rows, width), jnp.float32),
            VMEM((chip_rows, mels), jnp.float32),
        ],
    )
    other = across(send, 1, count)
    first = jnp.where(is_first > 0.5, keep, other)
    second = jnp.where(is_first > 0.5, other, keep)
    guided = first + guidance[0] * (first - second)
    velocity = jnp.where(live > 0.5, guided, 0.0)
    progress = step_index[0].astype(jnp.float32) / STEPS
    time_now = 1.0 - jnp.cos(0.5 * jnp.pi * progress)
    return (velocity, latent + (1.0 - time_now) * velocity)


def solution(mesh):
    return jax.shard_map(
        per_device,
        mesh=mesh,
        in_specs=(
            P(None, ("clip", "seq"), None),
            P(("clip", "seq"), None),
            P("clip"),
            P(),
            P(),
            P(),
            P(),
            P(),
            P(),
            P(),
        ),
        out_specs=(P(("clip", "seq"), None), P(("clip", "seq"), None)),
        check_vma=False,
    )
```

```python
import functools

import jax
import jax.numpy as jnp
from jax import lax
from jax.experimental import pallas as pl
from jax.experimental.pallas import tpu as pltpu
from jax.sharding import PartitionSpec as P


HEADS = 16
HEAD_DIM = 64
KERNEL = 31
STEPS = 32
LANES = 128
HALO = 16


EPSILON = 1e-06
NEGATIVE = -1e30
CORE, CHIP, LENGTH = 0, 1, 2
VMEM = pltpu.VMEM
SMEM = pltpu.SMEM
GRANT = 12 << 20


def vmem_spec():
    return pl.BlockSpec(memory_space=VMEM)


def smem_spec():
    return pl.BlockSpec(memory_space=SMEM)


def rotary_tables(positions):
    half_dim = HEAD_DIM // 2
    lane = jnp.arange(LANES, dtype=jnp.int32)
    inverse = 10000.0 ** (-(lane % half_dim).astype(jnp.float32) / half_dim)
    angles = positions.astype(jnp.float32)[:, None] * inverse[None, :]
    sign = jnp.where(lane % HEAD_DIM < half_dim, -1.0, 1.0)
    return jnp.cos(angles), jnp.sin(angles) * sign[None, :]


def hbm_spec():
    return pl.BlockSpec(memory_space=pltpu.HBM)


def tile_lanes(tile):
    return pl.ds(pl.multiple_of(tile * LANES, LANES), LANES)


def row_norm(load, store, tiles, mod_ref, row, total):
    width = tiles * LANES
    mean = jnp.sum(total, axis=-1, keepdims=True) * (1.0 / width)

    def square(tile, acc):
        centered = load(tile) - mean
        return acc + centered * centered

    squares = lax.fori_loop(0, tiles, square, jnp.zeros(total.shape, jnp.float32), unroll=6)
    variance = jnp.sum(squares, axis=-1, keepdims=True) * (1.0 / width)
    factor = lax.rsqrt(variance + EPSILON)

    def write(tile, carry):
        lanes = tile_lanes(tile)
        scale = 1.0 + mod_ref[row + 1 : row + 2, lanes]
        shift = mod_ref[row : row + 1, lanes]
        store(lanes, (load(tile) - mean) * factor * scale + shift)
        return carry

    lax.fori_loop(0, tiles, write, 0, unroll=6)


def run_copies(pairs, sems):
    copies = [
        pltpu.make_async_copy(source, target, sems.at[at])
        for at, (source, target) in enumerate(pairs)
    ]
    for copy in copies:
        copy.start()
    for copy in copies:
        copy.wait()


def stage_kernel(
    info_ref, hidden_hbm, taps_hbm, mod_hbm, own_ref, taps_ref, mod_ref, first_ref, live_ref, sems
):
    rows = own_ref.shape[0]
    core = info_ref[CORE]
    first_ref[...] = jnp.zeros(first_ref.shape, jnp.float32) + (1 - core).astype(jnp.float32)
    row = lax.broadcasted_iota(jnp.int32, live_ref.shape, 0)
    frame = row + (2 * info_ref[CHIP] + core) * rows
    live_ref[...] = (frame < info_ref[LENGTH]).astype(jnp.float32)
    run_copies(
        [(hidden_hbm.at[core], own_ref), (taps_hbm, taps_ref), (mod_hbm, mod_ref)], sems
    )


def front_kernel(
    first_pair, info_ref, own_ref, partner_ref, near_ref, far_ref, taps_ref, mod_ref, cos_ref, sin_ref,
    weight_hbm, residual_ref, normed_ref, weight_ref, *refs,
):
    *out_refs, padded, sems = refs
    rows, width = own_ref.shape
    halo = near_ref.shape[1]
    total_rows = 2 * rows
    tiles = width // LANES
    parts = sems.shape[0]
    depth = width // parts
    loads = []
    for part in range(parts):
        here = pl.ds(part * depth, depth)
        loads.append(
            pltpu.make_async_copy(weight_hbm.at[here], weight_ref.at[here], sems.at[part])
        )
    for load in loads:
        load.start()
    length, core = info_ref[LENGTH], info_ref[CORE]
    offset = info_ref[CHIP] * total_rows
    span = total_rows + 2 * halo
    frame = offset - halo + lax.broadcasted_iota(jnp.int32, (span, LANES), 0)
    live = ((frame >= 0) & (frame < length)).astype(jnp.float32)
    first = halo - KERNEL // 2
    own_at = pl.ds(pl.multiple_of(halo + core * rows, 8), rows)
    partner_at = pl.ds(pl.multiple_of(halo + (1 - core) * rows, 8), rows)
    near_at = pl.ds(pl.multiple_of(core * (halo + total_rows), 8), halo)
    far_at = pl.ds(pl.multiple_of((1 - core) * (halo + total_rows), 8), halo)

    def convolve(tile, total):
        lanes = tile_lanes(tile)
        padded[near_at] = near_ref[core, :, lanes].astype(jnp.float32)
        padded[far_at] = far_ref[core, :, lanes].astype(jnp.float32)
        padded[own_at] = own_ref[:, lanes].astype(jnp.float32)
        padded[partner_at] = partner_ref[:, lanes].astype(jnp.float32)
        own = padded[halo : halo + total_rows]
        padded[...] = padded[...] * live
        acc = jnp.zeros((total_rows, LANES), jnp.float32)
        for tap in range(KERNEL):
            acc = acc + taps_ref[tap : tap + 1, lanes] * padded[
                first + tap : first + tap + total_rows
            ]
        grown = jnp.exp(jnp.minimum(acc, 20.0))
        product = grown * (grown + 2.0)
        value = own + acc * (product / (product + 2.0))
        residual_ref[:, lanes] = value
        return total + value

    total = lax.fori_loop(
        0, tiles, convolve, jnp.zeros((total_rows, LANES), jnp.float32), unroll=3
    )

    def store(lanes, value):
        normed_ref[:, lanes] = value.astype(jnp.bfloat16)

    row_norm(lambda tile: residual_ref[:, tile_lanes(tile)], store, tiles, mod_ref, 0, total)
    if first_pair is None:
        for load in loads:
            load.wait()
    else:
        project_landing(
            first_pair, info_ref[CHIP], loads, normed_ref, weight_ref, cos_ref, sin_ref, out_refs
        )


def pair_lanes(chip, apart, part, attn):
    wide = 2 * LANES
    start = part * attn + ((chip ^ apart) >> 1) * wide
    return pl.ds(pl.multiple_of(start, wide), wide)


def store_pair(products, chip, cos_ref, sin_ref, out_refs):
    rows = cos_ref.shape[0]
    half = HEAD_DIM // 2
    cosine, sine = cos_ref[...], sin_ref[...]
    lower = lax.broadcasted_iota(jnp.int32, (rows, LANES), 1) % HEAD_DIM < half
    swap = jnp.full((rows, LANES), chip & 1, jnp.int32) > 0
    for part, both in enumerate(products):
        sides = []
        for side in range(2):
            value = both[:, side * LANES : (side + 1) * LANES]
            if part < 2:
                swapped = jnp.where(
                    lower, pltpu.roll(value, LANES - half, 1), pltpu.roll(value, half, 1)
                )
                value = value * cosine + swapped * sine
            if part == 0:
                value = value * HEAD_DIM**-0.5
            sides.append(value)
        out_refs[0][part] = jnp.where(swap, sides[1], sides[0]).astype(jnp.bfloat16)
        out_refs[1][part] = jnp.where(swap, sides[0], sides[1]).astype(jnp.bfloat16)


def project_landing(apart, chip, loads, normed_ref, weight_ref, cos_ref, sin_ref, out_refs):
    depth = weight_ref.shape[0] // len(loads)
    attn = weight_ref.shape[1] // 3
    products = [jnp.zeros((normed_ref.shape[0], 2 * LANES), jnp.float32)] * 3
    for at, load in enumerate(loads):
        load.wait()
        here = slice(at * depth, (at + 1) * depth)
        for part in range(3):
            products[part] = products[part] + jnp.dot(
                normed_ref[:, here],
                weight_ref[here, pair_lanes(chip, apart, part, attn)],
                preferred_element_type=jnp.float32,
            )
    store_pair(products, chip, cos_ref, sin_ref, out_refs)


def project_kernel(firsts, origin, info_ref, normed_ref, weight_ref, cos_ref, sin_ref, *out_refs):
    chip = info_ref[CHIP] if origin is None else origin
    attn = weight_ref.shape[1] // 3
    for at, apart in enumerate(firsts):
        products = [
            jnp.dot(
                normed_ref[...],
                weight_ref[:, pair_lanes(chip, apart, part, attn)],
                preferred_element_type=jnp.float32,
            )
            for part in range(3)
        ]
        store_pair(products, chip, cos_ref, sin_ref, out_refs[2 * at : 2 * at + 2])


def place_keys(info_ref, apart, got_ref, keys, values, first):
    _, rows, _ = got_ref.shape
    chip = info_ref[CHIP] ^ apart
    lane = lax.broadcasted_iota(jnp.int32, (rows, LANES), 1)
    row = lax.broadcasted_iota(jnp.int32, (rows, LANES), 0)
    here = slice(first, first + rows)
    keys[here, :LANES] = got_ref[1]
    dead = (lane == 0) & (row + chip * rows >= info_ref[LENGTH])
    keys[here, LANES:] = jnp.where(dead, NEGATIVE, 0.0).astype(jnp.bfloat16)
    values[here, :] = got_ref[2]


def place_queries(query_refs, queries):
    _, rows, _ = query_refs[0].shape
    low = lax.broadcasted_iota(jnp.int32, (rows, LANES), 1) < HEAD_DIM
    zero = jnp.zeros((rows, LANES), jnp.bfloat16)
    queries[:, LANES:] = jnp.where(
        lax.broadcasted_iota(jnp.int32, (queries.shape[0], LANES), 1) == 0, 1.0, 0.0
    ).astype(jnp.bfloat16)
    for at, query_ref in enumerate(query_refs):
        query = query_ref[0]
        base = 2 * at * rows
        queries[base : base + rows, :LANES] = jnp.where(low, query, zero)
        queries[base + rows : base + 2 * rows, :LANES] = jnp.where(low, zero, query)


def score(queries, keys):
    return lax.dot_general(
        queries, keys, (((1,), (1,)), ((), ())), preferred_element_type=jnp.float32
    )


def mix(weights, values):
    return jnp.dot(weights.astype(jnp.bfloat16), values, preferred_element_type=jnp.float32)


def store_heads(mixed, out_ref, first):
    _, rows, _ = out_ref.shape
    low = lax.broadcasted_iota(jnp.int32, (rows, LANES), 1) < HEAD_DIM
    for at in range(mixed.shape[0] // (2 * rows)):
        base = 2 * at * rows
        out_ref[first + at] = jnp.where(
            low, mixed[base : base + rows], mixed[base + rows : base + 2 * rows]
        ).astype(jnp.bfloat16)


def attend_rows(keys, values, queries, out_ref, first):
    _, rows, _ = out_ref.shape
    total = queries.shape[0]
    for base in range(0, total, 4 * rows):
        block = slice(base, min(base + 4 * rows, total))
        scores = score(queries[block, :], keys[...])
        weights = jnp.exp(scores - jnp.max(scores, axis=1, keepdims=True))
        weight_sum = jnp.sum(weights, axis=1, keepdims=True)
        store_heads(mix(weights, values[...]) / weight_sum, out_ref, first + base // (2 * rows))


def attend_early_kernel(first, info_ref, *refs):
    chips = len(refs) - 6
    got_refs = refs[:chips]
    keys, values, queries, mixed_ref, peak_ref, sum_ref = refs[chips:]
    _, rows, _ = got_refs[0].shape
    for apart, got_ref in enumerate(got_refs):
        place_keys(info_ref, apart, got_ref, keys, values, apart * rows)
    place_queries(got_refs[first : first + 2], queries)
    half = queries.shape[0] // 2
    for block in (slice(0, half), slice(half, 2 * half)):
        scores = score(queries[block, :], keys[...])
        peak = jnp.max(scores, axis=1, keepdims=True)
        weights = jnp.exp(scores - peak)
        peak_ref[block, :] = jnp.broadcast_to(peak, (half, LANES))
        weight_sum = jnp.sum(weights, axis=1, keepdims=True)
        sum_ref[block, :] = jnp.broadcast_to(weight_sum, (half, LANES))
        mixed_ref[block, :] = mix(weights, values[...])


def attend_last_kernel(
    info_ref, early_keys, early_values, early_queries, mixed_ref, peak_ref, sum_ref, last_ref,
    out_ref, keys, values,
):
    held, _ = early_values.shape
    _, rows, _ = last_ref.shape
    place_keys(info_ref, held // rows, last_ref, keys, values, held)
    scores = score(early_queries[...], keys[held:, :])
    peak = peak_ref[...]
    joined = jnp.maximum(peak, jnp.max(scores, axis=1, keepdims=True))
    scale = jnp.exp(peak - joined)
    weights = jnp.exp(scores - joined[:, : scores.shape[1]])
    weight_sum = sum_ref[...] * scale + jnp.sum(weights, axis=1, keepdims=True)
    mixed = mixed_ref[...] * scale + mix(weights, values[held:, :])
    store_heads(mixed / weight_sum, out_ref, 0)
    keys[:held, :] = early_keys[...]
    values[:held, :] = early_values[...]


def attend_second_kernel(info_ref, keys, values, *refs):
    del info_ref
    out_ref, queries = refs[-2:]
    place_queries(refs[:-2], queries)
    attend_rows(keys, values, queries, out_ref, 0)


def merge_kernel(info_ref, *refs):
    del info_ref
    for at, got_ref in enumerate(refs[:-1]):
        refs[-1][at] = got_ref[1]


def back_kernel(blocks, info_ref, residual, w_mel, mod_ref, w_out_ref, *refs):
    count = 1 + max(at for at, _, _ in blocks)
    got_refs = refs[:count]
    keep_ref, send_ref, attended, after, speed = refs[count:]
    rows, width = residual.shape
    tiles = width // LANES
    core, chip = info_ref[CORE], info_ref[CHIP]
    for at, place, apart in blocks:
        group = place if apart is None else chip ^ apart
        attended[:, tile_lanes(group)] = got_refs[at][place]
    wide = 2 * LANES
    total = jnp.zeros((rows, LANES), jnp.float32)
    for block in range(width // wide):
        lanes = slice(block * wide, (block + 1) * wide)
        branch = jnp.dot(attended[...], w_out_ref[:, lanes], preferred_element_type=jnp.float32)
        value = residual[:, lanes] + mod_ref[2:3, lanes] * branch
        after[:, lanes] = value
        total = total + value[:, :LANES] + value[:, LANES:]

    def store(lanes, value):
        after[:, lanes] = value

    row_norm(lambda tile: after[:, tile_lanes(tile)], store, tiles, mod_ref, 3, total)
    speed[...] = lax.dot_general(
        after[...].astype(jnp.bfloat16), w_mel[...], (((1,), (1,)), ((), ())),
        preferred_element_type=jnp.float32,
    )
    half = rows // 2
    keep_ref[...] = speed[pl.ds(pl.multiple_of(core * half, 8), half), :]
    send_ref[...] = speed[pl.ds(pl.multiple_of((1 - core) * half, 8), half), :]


def call(kernel, out_shape, inputs, scratch, hbm=()):
    single = not isinstance(out_shape, tuple)
    specs = [hbm_spec() if at in hbm else vmem_spec() for at in range(1, len(inputs))]
    inputs = list(inputs)
    for at in hbm:
        inputs[at] = pltpu.with_memory_space_constraint(inputs[at], pltpu.HBM)
    return pl.pallas_call(
        kernel,
        out_shape=out_shape,
        in_specs=[smem_spec()] + specs,
        out_specs=vmem_spec() if single else tuple(vmem_spec() for _ in out_shape),
        scratch_shapes=scratch,
        compiler_params=pltpu.CompilerParams(vmem_limit_bytes=GRANT),
    )(*inputs)


def array(shape, dtype=jnp.float32):
    return jax.ShapeDtypeStruct(shape, dtype)


def project(normed, w_qkv, tables, info, firsts, origin=None):
    shape = array((3, normed.shape[0], LANES), jnp.bfloat16)
    return call(
        functools.partial(project_kernel, tuple(firsts), origin),
        (shape,) * (2 * len(firsts)),
        (info, normed, w_qkv) + tables,
        [],
    )


def same_core(count):
    return [list(range(core, count, 2)) for core in range(2)]


def facing_pairs(clips, count):
    pairs = []
    for clip in range(clips):
        base = clip * count
        for at in range(1, count - 1, 2):
            pairs += [(base + at, base + at + 1), (base + at + 1, base + at)]
        if clip ^ 1 < clips:
            pairs += [(base + end, (clip ^ 1) * count + end) for end in (0, count - 1)]
    return pairs


def across(value, apart, count):
    return lax.ppermute(value, "seq", [(i, i ^ apart) for i in range(count)])


def to_groups(values, subs):
    rows, _ = values.shape
    grouped = values.reshape(subs, rows // subs, HEADS, HEAD_DIM).transpose(2, 0, 1, 3)
    return grouped.reshape(HEADS * subs, rows // subs, HEAD_DIM)


def from_groups(grouped, rows, subs):
    split = grouped.reshape(HEADS, subs, rows // subs, HEAD_DIM).transpose(1, 2, 0, 3)
    return split.reshape(rows, HEADS * HEAD_DIM)


def attend_blocks(queries, keys, values, live):
    groups, total, _ = queries.shape
    block = max(size for size in range(1, min(total, 1024) + 1) if total % size == 0)
    blocks = queries.reshape(groups, total // block, block, HEAD_DIM).transpose(1, 0, 2, 3)
    live = live[None, None, :]

    def one_block(query):
        scores = jnp.einsum("gqd,gkd->gqk", query, keys, preferred_element_type=jnp.float32)
        scores = jnp.where(live, scores, NEGATIVE)
        weights = jnp.exp(scores - jnp.max(scores, axis=-1, keepdims=True))
        weights = jnp.where(live, weights, 0.0)
        mixed = jnp.einsum(
            "gqk,gkd->gqd",
            weights.astype(jnp.bfloat16),
            values,
            preferred_element_type=jnp.float32,
        )
        return (mixed / jnp.sum(weights, axis=-1)[..., None]).astype(jnp.bfloat16)

    return lax.map(one_block, blocks).transpose(1, 0, 2, 3).reshape(groups, total, HEAD_DIM)


def attend_any(normed, w_qkv, tables, info, length, count):
    rows = normed.shape[0]
    chips = count // 2
    groups = HEADS * HEAD_DIM // LANES
    sent = project(normed, w_qkv, tables, info, range(0, groups, 2), 0)
    subs = max(1, chips // HEADS)
    chip = lax.axis_index("seq") >> 1
    part_rows = rows // subs

    def exchange(part):
        whole = jnp.concatenate([group[part] for group in sent], axis=1)
        return lax.all_to_all(
            to_groups(whole, subs), "seq", split_axis=0, concat_axis=1, tiled=True,
            axis_index_groups=same_core(count),
        )

    queries, keys, values = (exchange(part) for part in range(3))

    def frames_of(sub):
        start = jnp.arange(chips, dtype=jnp.int32)[:, None] * rows + sub * part_rows
        return (start + jnp.arange(part_rows, dtype=jnp.int32)[None, :]).reshape(-1)

    frames = [frames_of(chip % subs)]
    parts = [(keys, values)]
    for apart in range(1, subs):
        perm = []
        for i in range(count):
            at = i // 2
            target = at - at % subs + (at + apart) % subs
            perm.append((i, 2 * target + i % 2))
        parts.append(tuple(lax.ppermute(part, "seq", perm) for part in (keys, values)))
        frames.append(frames_of((chip - apart) % subs))
    keys = jnp.concatenate([part[0] for part in parts], axis=1)
    values = jnp.concatenate([part[1] for part in parts], axis=1)
    attended = attend_blocks(queries, keys, values, jnp.concatenate(frames) < length)
    back = lax.all_to_all(
        attended, "seq", split_axis=1, concat_axis=0, tiled=True,
        axis_index_groups=same_core(count),
    )
    return from_groups(back, rows, subs).reshape(rows, groups, LANES).transpose(1, 0, 2)


def chips_hold_groups(count):
    chips = count // 2
    return chips == HEADS * HEAD_DIM // LANES and chips >= 4 and chips & (chips - 1) == 0


def send_order(chips):
    far = list(range(chips // 2, chips, 2))
    return far[:1] + list(range(2, chips // 2, 2)) + far[1:] + [0]


def return_order(chips):
    return list(range(chips // 2, chips, 2)) + list(range(2, chips // 2, 2)) + [0]


def attend_chips(made, normed, w_qkv, tables, info, count):
    rows = normed.shape[0]
    chips = count // 2
    held = {}
    for first in send_order(chips):
        if held:
            made = project(normed, w_qkv, tables, info, [first])
        for side in range(2):
            apart = first + side
            held[apart] = across(made[side], 2 * apart, count) if apart else made[side]
    total, half = chips * rows, chips // 2
    order = return_order(chips)
    early, early_rows = total - rows, 4 * rows
    parts = call(
        functools.partial(attend_early_kernel, order[0]),
        (
            array((early, 2 * LANES), jnp.bfloat16),
            array((early, LANES), jnp.bfloat16),
            array((early_rows, 2 * LANES), jnp.bfloat16),
        )
        + (array((early_rows, LANES)),) * 3,
        (info,) + tuple(held[apart] for apart in range(chips - 1)),
        [],
    )
    pair = array((2, rows, LANES), jnp.bfloat16)
    got = {}
    for first in order:
        if first == order[0]:
            attended, keys, values = call(
                attend_last_kernel,
                (
                    pair,
                    array((total, 2 * LANES), jnp.bfloat16),
                    array((total, LANES), jnp.bfloat16),
                ),
                (info,) + tuple(parts) + (held[chips - 1],),
                [],
            )
        else:
            attended = call(
                attend_second_kernel,
                pair,
                (info, keys, values, held[first], held[first + 1]),
                [VMEM((4 * rows, 2 * LANES), jnp.bfloat16)],
            )
        got[first] = across(attended, 2 * first, count) if first else attended
    back = [got[2 * at] for at in range(half)]
    blocks = [(at, 0, 2 * at) for at in range(half)]
    merged = call(merge_kernel, array((half, rows, LANES), jnp.bfloat16), [info] + back, [])
    blocks += [(half, at, 2 * at + 1) for at in range(half)]
    back.append(across(merged, 2, count))
    return back, blocks


def per_device(
    hidden, latent, lengths, step_index, guidance, modulation, conv_kernel, w_qkv, w_out, w_mel
):
    copies, rows, width = hidden.shape
    count = lax.axis_size("seq")
    chips = count // 2
    index = lax.axis_index("seq").astype(jnp.int32)
    chip, core = index >> 1, index & 1
    chip_rows = 2 * rows
    info = jnp.stack([core, chip, lengths[0]])

    edges = lax.dynamic_slice(hidden, (0, core * (rows - HALO), 0), (copies, HALO, width))
    partner = lax.dynamic_slice(hidden, (1 - core, 0, 0), (1, rows, width))[0]
    near = lax.ppermute(edges, ("clip", "seq"), facing_pairs(lax.axis_size("clip"), count))
    far = across(near, 1, count)
    partner = across(partner, 1, count)
    own, taps, mods, is_first, live = call(
        stage_kernel,
        (
            array((rows, width), jnp.bfloat16),
            array(conv_kernel.shape),
            array(modulation.shape),
            array(latent.shape),
            array(latent.shape),
        ),
        (info, hidden, conv_kernel, modulation),
        [pltpu.SemaphoreType.DMA((3,))],
        hbm=(1, 2, 3),
    )
    tables = rotary_tables(chip * chip_rows + jnp.arange(chip_rows, dtype=jnp.int32))
    first_pair = send_order(chips)[0] if chips_hold_groups(count) else None
    group = array((3, chip_rows, LANES), jnp.bfloat16)
    residual, normed, weight, *made = call(
        functools.partial(front_kernel, first_pair),
        (
            array((chip_rows, width)),
            array((chip_rows, width), jnp.bfloat16),
            array(w_qkv.shape, jnp.bfloat16),
        )
        + (group,) * (0 if first_pair is None else 2),
        (info, own, partner, near, far, taps, mods) + tables + (w_qkv,),
        [
            VMEM((chip_rows + 2 * HALO, LANES), jnp.float32),
            pltpu.SemaphoreType.DMA((width // (2 * LANES),)),
        ],
        hbm=(9,),
    )
    if chips_hold_groups(count):
        back, blocks = attend_chips(made, normed, weight, tables, info, count)
    else:
        back = [attend_any(normed, weight, tables, info, lengths[0], count)]
        blocks = [(0, group, None) for group in range(back[0].shape[0])]
    mels = w_mel.shape[1]
    keep, send = call(
        functools.partial(back_kernel, tuple(blocks)),
        (array((rows, mels)),) * 2,
        (info, residual, w_mel.T, mods, w_out) + tuple(back),
        [
            VMEM((chip_rows, HEADS * HEAD_DIM), jnp.bfloat16),
            VMEM((chip_rows, width), jnp.float32),
            VMEM((chip_rows, mels), jnp.float32),
        ],
    )
    other = across(send, 1, count)
    first = jnp.where(is_first > 0.5, keep, other)
    second = jnp.where(is_first > 0.5, other, keep)
    guided = first + guidance[0] * (first - second)
    velocity = jnp.where(live > 0.5, guided, 0.0)
    progress = step_index[0].astype(jnp.float32) / STEPS
    time_now = 1.0 - jnp.cos(0.5 * jnp.pi * progress)
    return (velocity, latent + (1.0 - time_now) * velocity)


def solution(mesh):
    return jax.shard_map(
        per_device,
        mesh=mesh,
        in_specs=(
            P(None, ("clip", "seq"), None),
            P(("clip", "seq"), None),
            P("clip"),
            P(),
            P(),
            P(),
            P(),
            P(),
            P(),
            P(),
        ),
        out_specs=(P(("clip", "seq"), None), P(("clip", "seq"), None)),
        check_vma=False,
    )
```

```python
import functools

import jax
import jax.numpy as jnp
from jax import lax
from jax.experimental import pallas as pl
from jax.experimental.pallas import tpu as pltpu
from jax.sharding import PartitionSpec as P


HEADS = 16
HEAD_DIM = 64
KERNEL = 31
STEPS = 32
LANES = 128
HALO = 16


EPSILON = 1e-06
NEGATIVE = -1e30
CORE, CHIP, LENGTH = 0, 1, 2
VMEM = pltpu.VMEM
SMEM = pltpu.SMEM
GRANT = 12 << 20


def vmem_spec():
    return pl.BlockSpec(memory_space=VMEM)


def smem_spec():
    return pl.BlockSpec(memory_space=SMEM)


def rotary_tables(positions):
    half_dim = HEAD_DIM // 2
    lane = jnp.arange(LANES, dtype=jnp.int32)
    inverse = 10000.0 ** (-(lane % half_dim).astype(jnp.float32) / half_dim)
    angles = positions.astype(jnp.float32)[:, None] * inverse[None, :]
    sign = jnp.where(lane % HEAD_DIM < half_dim, -1.0, 1.0)
    return jnp.cos(angles), jnp.sin(angles) * sign[None, :]


def hbm_spec():
    return pl.BlockSpec(memory_space=pltpu.HBM)


def tile_lanes(tile):
    return pl.ds(pl.multiple_of(tile * LANES, LANES), LANES)


def row_norm(load, store, tiles, mod_ref, row, total):
    width = tiles * LANES
    mean = jnp.sum(total, axis=-1, keepdims=True) * (1.0 / width)

    def square(tile, acc):
        centered = load(tile) - mean
        return acc + centered * centered

    squares = lax.fori_loop(0, tiles, square, jnp.zeros(total.shape, jnp.float32), unroll=6)
    variance = jnp.sum(squares, axis=-1, keepdims=True) * (1.0 / width)
    factor = lax.rsqrt(variance + EPSILON)

    def write(tile, carry):
        lanes = tile_lanes(tile)
        scale = 1.0 + mod_ref[row + 1 : row + 2, lanes]
        shift = mod_ref[row : row + 1, lanes]
        store(lanes, (load(tile) - mean) * factor * scale + shift)
        return carry

    lax.fori_loop(0, tiles, write, 0, unroll=6)


def run_copies(pairs, sems):
    copies = [
        pltpu.make_async_copy(source, target, sems.at[at])
        for at, (source, target) in enumerate(pairs)
    ]
    for copy in copies:
        copy.start()
    for copy in copies:
        copy.wait()


def stage_kernel(
    info_ref, hidden_hbm, taps_hbm, mod_hbm, own_ref, taps_ref, mod_ref, first_ref, live_ref, sems
):
    rows = own_ref.shape[0]
    core = info_ref[CORE]
    first_ref[...] = jnp.zeros(first_ref.shape, jnp.float32) + (1 - core).astype(jnp.float32)
    row = lax.broadcasted_iota(jnp.int32, live_ref.shape, 0)
    frame = row + (2 * info_ref[CHIP] + core) * rows
    live_ref[...] = (frame < info_ref[LENGTH]).astype(jnp.float32)
    run_copies(
        [(hidden_hbm.at[core], own_ref), (taps_hbm, taps_ref), (mod_hbm, mod_ref)], sems
    )


def front_kernel(
    first_pair, info_ref, own_ref, partner_ref, near_ref, far_ref, taps_ref, mod_ref, cos_ref, sin_ref,
    weight_hbm, residual_ref, normed_ref, weight_ref, *refs,
):
    *out_refs, padded, sems = refs
    rows, width = own_ref.shape
    halo = near_ref.shape[1]
    total_rows = 2 * rows
    tiles = width // LANES
    parts = sems.shape[0]
    depth = width // parts
    loads = []
    for part in range(parts):
        here = pl.ds(part * depth, depth)
        loads.append(
            pltpu.make_async_copy(weight_hbm.at[here], weight_ref.at[here], sems.at[part])
        )
    for load in loads:
        load.start()
    length, core = info_ref[LENGTH], info_ref[CORE]
    offset = info_ref[CHIP] * total_rows
    span = total_rows + 2 * halo
    frame = offset - halo + lax.broadcasted_iota(jnp.int32, (span, LANES), 0)
    live = ((frame >= 0) & (frame < length)).astype(jnp.float32)
    first = halo - KERNEL // 2
    own_at = pl.ds(pl.multiple_of(halo + core * rows, 8), rows)
    partner_at = pl.ds(pl.multiple_of(halo + (1 - core) * rows, 8), rows)
    near_at = pl.ds(pl.multiple_of(core * (halo + total_rows), 8), halo)
    far_at = pl.ds(pl.multiple_of((1 - core) * (halo + total_rows), 8), halo)

    def convolve(tile, total):
        lanes = tile_lanes(tile)
        padded[near_at] = near_ref[core, :, lanes].astype(jnp.float32)
        padded[far_at] = far_ref[core, :, lanes].astype(jnp.float32)
        padded[own_at] = own_ref[:, lanes].astype(jnp.float32)
        padded[partner_at] = partner_ref[:, lanes].astype(jnp.float32)
        own = padded[halo : halo + total_rows]
        padded[...] = padded[...] * live
        acc = jnp.zeros((total_rows, LANES), jnp.float32)
        for tap in range(KERNEL):
            acc = acc + taps_ref[tap : tap + 1, lanes] * padded[
                first + tap : first + tap + total_rows
            ]
        grown = jnp.exp(jnp.minimum(acc, 20.0))
        product = grown * (grown + 2.0)
        value = own + acc * (product / (product + 2.0))
        residual_ref[:, lanes] = value
        return total + value

    total = lax.fori_loop(
        0, tiles, convolve, jnp.zeros((total_rows, LANES), jnp.float32), unroll=3
    )

    def store(lanes, value):
        normed_ref[:, lanes] = value.astype(jnp.bfloat16)

    row_norm(lambda tile: residual_ref[:, tile_lanes(tile)], store, tiles, mod_ref, 0, total)
    if first_pair is None:
        for load in loads:
            load.wait()
    else:
        project_landing(
            first_pair, info_ref[CHIP], loads, normed_ref, weight_ref, cos_ref, sin_ref, out_refs
        )


def pair_lanes(chip, apart, part, attn):
    wide = 2 * LANES
    start = part * attn + ((chip ^ apart) >> 1) * wide
    return pl.ds(pl.multiple_of(start, wide), wide)


def store_pair(products, chip, cos_ref, sin_ref, out_refs):
    rows = cos_ref.shape[0]
    half = HEAD_DIM // 2
    cosine, sine = cos_ref[...], sin_ref[...]
    lower = lax.broadcasted_iota(jnp.int32, (rows, LANES), 1) % HEAD_DIM < half
    swap = jnp.full((rows, LANES), chip & 1, jnp.int32) > 0
    for part, both in enumerate(products):
        sides = []
        for side in range(2):
            value = both[:, side * LANES : (side + 1) * LANES]
            if part < 2:
                swapped = jnp.where(
                    lower, pltpu.roll(value, LANES - half, 1), pltpu.roll(value, half, 1)
                )
                value = value * cosine + swapped * sine
            if part == 0:
                value = value * HEAD_DIM**-0.5
            sides.append(value)
        out_refs[0][part] = jnp.where(swap, sides[1], sides[0]).astype(jnp.bfloat16)
        out_refs[1][part] = jnp.where(swap, sides[0], sides[1]).astype(jnp.bfloat16)


def project_landing(apart, chip, loads, normed_ref, weight_ref, cos_ref, sin_ref, out_refs):
    depth = weight_ref.shape[0] // len(loads)
    attn = weight_ref.shape[1] // 3
    products = [jnp.zeros((normed_ref.shape[0], 2 * LANES), jnp.float32)] * 3
    for at, load in enumerate(loads):
        load.wait()
        here = slice(at * depth, (at + 1) * depth)
        for part in range(3):
            products[part] = products[part] + jnp.dot(
                normed_ref[:, here],
                weight_ref[here, pair_lanes(chip, apart, part, attn)],
                preferred_element_type=jnp.float32,
            )
    store_pair(products, chip, cos_ref, sin_ref, out_refs)


def project_kernel(firsts, origin, info_ref, normed_ref, weight_ref, cos_ref, sin_ref, *out_refs):
    chip = info_ref[CHIP] if origin is None else origin
    attn = weight_ref.shape[1] // 3
    for at, apart in enumerate(firsts):
        products = [
            jnp.dot(
                normed_ref[...],
                weight_ref[:, pair_lanes(chip, apart, part, attn)],
                preferred_element_type=jnp.float32,
            )
            for part in range(3)
        ]
        store_pair(products, chip, cos_ref, sin_ref, out_refs[2 * at : 2 * at + 2])


def place_keys(info_ref, apart, got_ref, keys, values, first):
    _, rows, _ = got_ref.shape
    chip = info_ref[CHIP] ^ apart
    lane = lax.broadcasted_iota(jnp.int32, (rows, LANES), 1)
    row = lax.broadcasted_iota(jnp.int32, (rows, LANES), 0)
    here = slice(first, first + rows)
    keys[here, :LANES] = got_ref[1]
    dead = (lane == 0) & (row + chip * rows >= info_ref[LENGTH])
    keys[here, LANES:] = jnp.where(dead, NEGATIVE, 0.0).astype(jnp.bfloat16)
    values[here, :] = got_ref[2]


def place_queries(query_refs, queries):
    _, rows, _ = query_refs[0].shape
    low = lax.broadcasted_iota(jnp.int32, (rows, LANES), 1) < HEAD_DIM
    zero = jnp.zeros((rows, LANES), jnp.bfloat16)
    queries[:, LANES:] = jnp.where(
        lax.broadcasted_iota(jnp.int32, (queries.shape[0], LANES), 1) == 0, 1.0, 0.0
    ).astype(jnp.bfloat16)
    for at, query_ref in enumerate(query_refs):
        query = query_ref[0]
        base = 2 * at * rows
        queries[base : base + rows, :LANES] = jnp.where(low, query, zero)
        queries[base + rows : base + 2 * rows, :LANES] = jnp.where(low, zero, query)


def score(queries, keys):
    return lax.dot_general(
        queries, keys, (((1,), (1,)), ((), ())), preferred_element_type=jnp.float32
    )


def mix(weights, values):
    return jnp.dot(weights.astype(jnp.bfloat16), values, preferred_element_type=jnp.float32)


def store_heads(mixed, out_ref, first):
    _, rows, _ = out_ref.shape
    low = lax.broadcasted_iota(jnp.int32, (rows, LANES), 1) < HEAD_DIM
    for at in range(mixed.shape[0] // (2 * rows)):
        base = 2 * at * rows
        out_ref[first + at] = jnp.where(
            low, mixed[base : base + rows], mixed[base + rows : base + 2 * rows]
        ).astype(jnp.bfloat16)


def attend_rows(keys, values, queries, out_ref, first):
    _, rows, _ = out_ref.shape
    total = queries.shape[0]
    for base in range(0, total, 4 * rows):
        block = slice(base, min(base + 4 * rows, total))
        scores = score(queries[block, :], keys[...])
        weights = jnp.exp(scores - jnp.max(scores, axis=1, keepdims=True))
        weight_sum = jnp.sum(weights, axis=1, keepdims=True)
        store_heads(mix(weights, values[...]) / weight_sum, out_ref, first + base // (2 * rows))


def attend_early_kernel(info_ref, *refs):
    chips = len(refs) - 6
    got_refs = refs[:chips]
    keys, values, queries, mixed_ref, peak_ref, sum_ref = refs[chips:]
    _, rows, _ = got_refs[0].shape
    for apart, got_ref in enumerate(got_refs):
        place_keys(info_ref, apart, got_ref, keys, values, apart * rows)
    place_queries(got_refs[1::2], queries)
    half = queries.shape[0] // 2
    for block in (slice(0, half), slice(half, 2 * half)):
        scores = score(queries[block, :], keys[...])
        peak = jnp.max(scores, axis=1, keepdims=True)
        weights = jnp.exp(scores - peak)
        peak_ref[block, :] = jnp.broadcast_to(peak, (half, LANES))
        weight_sum = jnp.sum(weights, axis=1, keepdims=True)
        sum_ref[block, :] = jnp.broadcast_to(weight_sum, (half, LANES))
        mixed_ref[block, :] = mix(weights, values[...])


def attend_last_kernel(
    info_ref, early_keys, early_values, early_queries, mixed_ref, peak_ref, sum_ref, last_ref,
    out_ref, keys, values, queries,
):
    held, _ = early_values.shape
    _, rows, _ = last_ref.shape
    keys[:held, :] = early_keys[...]
    values[:held, :] = early_values[...]
    place_keys(info_ref, held // rows, last_ref, keys, values, held)
    place_queries([last_ref], queries)
    attend_rows(keys, values, queries, out_ref, out_ref.shape[0] - 1)
    scores = score(early_queries[...], keys[held:, :])
    peak = peak_ref[...]
    joined = jnp.maximum(peak, jnp.max(scores, axis=1, keepdims=True))
    scale = jnp.exp(peak - joined)
    weights = jnp.exp(scores - joined[:, : scores.shape[1]])
    weight_sum = sum_ref[...] * scale + jnp.sum(weights, axis=1, keepdims=True)
    mixed = mixed_ref[...] * scale + mix(weights, values[held:, :])
    store_heads(mixed / weight_sum, out_ref, 0)


def attend_second_kernel(info_ref, keys, values, *refs):
    del info_ref
    out_ref, queries = refs[-2:]
    place_queries(refs[:-2], queries)
    attend_rows(keys, values, queries, out_ref, 0)


def merge_kernel(info_ref, own_ref, got_ref, *out_refs):
    del info_ref
    for at, out_ref in enumerate(out_refs):
        out_ref[0] = own_ref[at + 1]
        out_ref[1] = got_ref[at + 1]


def back_kernel(blocks, info_ref, residual, w_mel, mod_ref, w_out_ref, *refs):
    count = 1 + max(at for at, _, _ in blocks)
    got_refs = refs[:count]
    keep_ref, send_ref, attended, after, speed = refs[count:]
    rows, width = residual.shape
    tiles = width // LANES
    core, chip = info_ref[CORE], info_ref[CHIP]
    for at, place, apart in blocks:
        group = place if apart is None else chip ^ apart
        attended[:, tile_lanes(group)] = got_refs[at][place]
    wide = 2 * LANES
    total = jnp.zeros((rows, LANES), jnp.float32)
    for block in range(width // wide):
        lanes = slice(block * wide, (block + 1) * wide)
        branch = jnp.dot(attended[...], w_out_ref[:, lanes], preferred_element_type=jnp.float32)
        value = residual[:, lanes] + mod_ref[2:3, lanes] * branch
        after[:, lanes] = value
        total = total + value[:, :LANES] + value[:, LANES:]

    def store(lanes, value):
        after[:, lanes] = value

    row_norm(lambda tile: after[:, tile_lanes(tile)], store, tiles, mod_ref, 3, total)
    speed[...] = lax.dot_general(
        after[...].astype(jnp.bfloat16), w_mel[...], (((1,), (1,)), ((), ())),
        preferred_element_type=jnp.float32,
    )
    half = rows // 2
    keep_ref[...] = speed[pl.ds(pl.multiple_of(core * half, 8), half), :]
    send_ref[...] = speed[pl.ds(pl.multiple_of((1 - core) * half, 8), half), :]


def call(kernel, out_shape, inputs, scratch, hbm=()):
    single = not isinstance(out_shape, tuple)
    specs = [hbm_spec() if at in hbm else vmem_spec() for at in range(1, len(inputs))]
    inputs = list(inputs)
    for at in hbm:
        inputs[at] = pltpu.with_memory_space_constraint(inputs[at], pltpu.HBM)
    return pl.pallas_call(
        kernel,
        out_shape=out_shape,
        in_specs=[smem_spec()] + specs,
        out_specs=vmem_spec() if single else tuple(vmem_spec() for _ in out_shape),
        scratch_shapes=scratch,
        compiler_params=pltpu.CompilerParams(vmem_limit_bytes=GRANT),
    )(*inputs)


def array(shape, dtype=jnp.float32):
    return jax.ShapeDtypeStruct(shape, dtype)


def project(normed, w_qkv, tables, info, firsts, origin=None):
    shape = array((3, normed.shape[0], LANES), jnp.bfloat16)
    return call(
        functools.partial(project_kernel, tuple(firsts), origin),
        (shape,) * (2 * len(firsts)),
        (info, normed, w_qkv) + tables,
        [],
    )


def same_core(count):
    return [list(range(core, count, 2)) for core in range(2)]


def facing_pairs(clips, count):
    pairs = []
    for clip in range(clips):
        base = clip * count
        for at in range(1, count - 1, 2):
            pairs += [(base + at, base + at + 1), (base + at + 1, base + at)]
        if clip ^ 1 < clips:
            pairs += [(base + end, (clip ^ 1) * count + end) for end in (0, count - 1)]
    return pairs


def across(value, apart, count):
    return lax.ppermute(value, "seq", [(i, i ^ apart) for i in range(count)])


def to_groups(values, subs):
    rows, _ = values.shape
    grouped = values.reshape(subs, rows // subs, HEADS, HEAD_DIM).transpose(2, 0, 1, 3)
    return grouped.reshape(HEADS * subs, rows // subs, HEAD_DIM)


def from_groups(grouped, rows, subs):
    split = grouped.reshape(HEADS, subs, rows // subs, HEAD_DIM).transpose(1, 2, 0, 3)
    return split.reshape(rows, HEADS * HEAD_DIM)


def attend_blocks(queries, keys, values, live):
    groups, total, _ = queries.shape
    block = max(size for size in range(1, min(total, 1024) + 1) if total % size == 0)
    blocks = queries.reshape(groups, total // block, block, HEAD_DIM).transpose(1, 0, 2, 3)
    live = live[None, None, :]

    def one_block(query):
        scores = jnp.einsum("gqd,gkd->gqk", query, keys, preferred_element_type=jnp.float32)
        scores = jnp.where(live, scores, NEGATIVE)
        weights = jnp.exp(scores - jnp.max(scores, axis=-1, keepdims=True))
        weights = jnp.where(live, weights, 0.0)
        mixed = jnp.einsum(
            "gqk,gkd->gqd",
            weights.astype(jnp.bfloat16),
            values,
            preferred_element_type=jnp.float32,
        )
        return (mixed / jnp.sum(weights, axis=-1)[..., None]).astype(jnp.bfloat16)

    return lax.map(one_block, blocks).transpose(1, 0, 2, 3).reshape(groups, total, HEAD_DIM)


def attend_any(normed, w_qkv, tables, info, length, count):
    rows = normed.shape[0]
    chips = count // 2
    groups = HEADS * HEAD_DIM // LANES
    sent = project(normed, w_qkv, tables, info, range(0, groups, 2), 0)
    subs = max(1, chips // HEADS)
    chip = lax.axis_index("seq") >> 1
    part_rows = rows // subs

    def exchange(part):
        whole = jnp.concatenate([group[part] for group in sent], axis=1)
        return lax.all_to_all(
            to_groups(whole, subs), "seq", split_axis=0, concat_axis=1, tiled=True,
            axis_index_groups=same_core(count),
        )

    queries, keys, values = (exchange(part) for part in range(3))

    def frames_of(sub):
        start = jnp.arange(chips, dtype=jnp.int32)[:, None] * rows + sub * part_rows
        return (start + jnp.arange(part_rows, dtype=jnp.int32)[None, :]).reshape(-1)

    frames = [frames_of(chip % subs)]
    parts = [(keys, values)]
    for apart in range(1, subs):
        perm = []
        for i in range(count):
            at = i // 2
            target = at - at % subs + (at + apart) % subs
            perm.append((i, 2 * target + i % 2))
        parts.append(tuple(lax.ppermute(part, "seq", perm) for part in (keys, values)))
        frames.append(frames_of((chip - apart) % subs))
    keys = jnp.concatenate([part[0] for part in parts], axis=1)
    values = jnp.concatenate([part[1] for part in parts], axis=1)
    attended = attend_blocks(queries, keys, values, jnp.concatenate(frames) < length)
    back = lax.all_to_all(
        attended, "seq", split_axis=1, concat_axis=0, tiled=True,
        axis_index_groups=same_core(count),
    )
    return from_groups(back, rows, subs).reshape(rows, groups, LANES).transpose(1, 0, 2)


def chips_hold_groups(count):
    chips = count // 2
    return chips == HEADS * HEAD_DIM // LANES and chips >= 4 and chips & (chips - 1) == 0


def send_order(chips):
    far = list(range(chips // 2, chips, 2))
    return far[:1] + list(range(2, chips // 2, 2)) + far[1:] + [0]


def attend_chips(made, normed, w_qkv, tables, info, count):
    rows = normed.shape[0]
    chips = count // 2
    held = {}
    for first in send_order(chips):
        if held:
            made = project(normed, w_qkv, tables, info, [first])
        for side in range(2):
            apart = first + side
            held[apart] = across(made[side], 2 * apart, count) if apart else made[side]
    total, half = chips * rows, chips // 2
    early, early_rows = total - rows, 2 * (half - 1) * rows
    parts = call(
        attend_early_kernel,
        (
            array((early, 2 * LANES), jnp.bfloat16),
            array((early, LANES), jnp.bfloat16),
            array((early_rows, 2 * LANES), jnp.bfloat16),
        )
        + (array((early_rows, LANES)),) * 3,
        (info,) + tuple(held[apart] for apart in range(chips - 1)),
        [],
    )
    crossing, keys, values = call(
        attend_last_kernel,
        (
            array((half, rows, LANES), jnp.bfloat16),
            array((total, 2 * LANES), jnp.bfloat16),
            array((total, LANES), jnp.bfloat16),
        ),
        (info,) + tuple(parts) + (held[chips - 1],),
        [VMEM((2 * rows, 2 * LANES), jnp.bfloat16)],
    )
    crossed = across(crossing, 2, count)
    staying = call(
        attend_second_kernel,
        array((half, rows, LANES), jnp.bfloat16),
        (info, keys, values) + tuple(held[apart] for apart in range(0, chips, 2)),
        [VMEM((total, 2 * LANES), jnp.bfloat16)],
    )
    joined = call(
        merge_kernel,
        (array((2, rows, LANES), jnp.bfloat16),) * (half - 1),
        (info, staying, crossed),
        [],
    )
    back, blocks = [staying, crossed], [(0, 0, 0), (1, 0, 1)]
    apart_first = list(range(half // 2, half)) + list(range(1, half // 2))
    got = {apart: across(joined[apart - 1], 4 * apart, count) for apart in apart_first}
    for apart in range(1, half):
        blocks += [(len(back), side, 2 * apart + side) for side in range(2)]
        back.append(got[apart])
    return back, blocks


def per_device(
    hidden, latent, lengths, step_index, guidance, modulation, conv_kernel, w_qkv, w_out, w_mel
):
    copies, rows, width = hidden.shape
    count = lax.axis_size("seq")
    chips = count // 2
    index = lax.axis_index("seq").astype(jnp.int32)
    chip, core = index >> 1, index & 1
    chip_rows = 2 * rows
    info = jnp.stack([core, chip, lengths[0]])

    edges = lax.dynamic_slice(hidden, (0, core * (rows - HALO), 0), (copies, HALO, width))
    partner = lax.dynamic_slice(hidden, (1 - core, 0, 0), (1, rows, width))[0]
    near = lax.ppermute(edges, ("clip", "seq"), facing_pairs(lax.axis_size("clip"), count))
    far = across(near, 1, count)
    partner = across(partner, 1, count)
    own, taps, mods, is_first, live = call(
        stage_kernel,
        (
            array((rows, width), jnp.bfloat16),
            array(conv_kernel.shape),
            array(modulation.shape),
            array(latent.shape),
            array(latent.shape),
        ),
        (info, hidden, conv_kernel, modulation),
        [pltpu.SemaphoreType.DMA((3,))],
        hbm=(1, 2, 3),
    )
    tables = rotary_tables(chip * chip_rows + jnp.arange(chip_rows, dtype=jnp.int32))
    first_pair = send_order(chips)[0] if chips_hold_groups(count) else None
    group = array((3, chip_rows, LANES), jnp.bfloat16)
    residual, normed, weight, *made = call(
        functools.partial(front_kernel, first_pair),
        (
            array((chip_rows, width)),
            array((chip_rows, width), jnp.bfloat16),
            array(w_qkv.shape, jnp.bfloat16),
        )
        + (group,) * (0 if first_pair is None else 2),
        (info, own, partner, near, far, taps, mods) + tables + (w_qkv,),
        [
            VMEM((chip_rows + 2 * HALO, LANES), jnp.float32),
            pltpu.SemaphoreType.DMA((width // (2 * LANES),)),
        ],
        hbm=(9,),
    )
    if chips_hold_groups(count):
        back, blocks = attend_chips(made, normed, weight, tables, info, count)
    else:
        back = [attend_any(normed, weight, tables, info, lengths[0], count)]
        blocks = [(0, group, None) for group in range(back[0].shape[0])]
    mels = w_mel.shape[1]
    keep, send = call(
        functools.partial(back_kernel, tuple(blocks)),
        (array((rows, mels)),) * 2,
        (info, residual, w_mel.T, mods, w_out) + tuple(back),
        [
            VMEM((chip_rows, HEADS * HEAD_DIM), jnp.bfloat16),
            VMEM((chip_rows, width), jnp.float32),
            VMEM((chip_rows, mels), jnp.float32),
        ],
    )
    other = across(send, 1, count)
    first = jnp.where(is_first > 0.5, keep, other)
    second = jnp.where(is_first > 0.5, other, keep)
    guided = first + guidance[0] * (first - second)
    velocity = jnp.where(live > 0.5, guided, 0.0)
    progress = step_index[0].astype(jnp.float32) / STEPS
    time_now = 1.0 - jnp.cos(0.5 * jnp.pi * progress)
    return (velocity, latent + (1.0 - time_now) * velocity)


def solution(mesh):
    return jax.shard_map(
        per_device,
        mesh=mesh,
        in_specs=(
            P(None, ("clip", "seq"), None),
            P(("clip", "seq"), None),
            P("clip"),
            P(),
            P(),
            P(),
            P(),
            P(),
            P(),
            P(),
        ),
        out_specs=(P(("clip", "seq"), None), P(("clip", "seq"), None)),
        check_vma=False,
    )
```

```python
import functools

import jax
import jax.numpy as jnp
from jax import lax
from jax.experimental import pallas as pl
from jax.experimental.pallas import tpu as pltpu
from jax.sharding import PartitionSpec as P


HEADS = 16
HEAD_DIM = 64
KERNEL = 31
STEPS = 32
LANES = 128
HALO = 16


EPSILON = 1e-06
NEGATIVE = -1e30
CORE, CHIP, LENGTH = 0, 1, 2
VMEM = pltpu.VMEM
SMEM = pltpu.SMEM
GRANT = 12 << 20


def vmem_spec():
    return pl.BlockSpec(memory_space=VMEM)


def smem_spec():
    return pl.BlockSpec(memory_space=SMEM)


def rotary_tables(positions):
    half_dim = HEAD_DIM // 2
    lane = jnp.arange(LANES, dtype=jnp.int32)
    inverse = 10000.0 ** (-(lane % half_dim).astype(jnp.float32) / half_dim)
    angles = positions.astype(jnp.float32)[:, None] * inverse[None, :]
    sign = jnp.where(lane % HEAD_DIM < half_dim, -1.0, 1.0)
    return jnp.cos(angles), jnp.sin(angles) * sign[None, :]


def hbm_spec():
    return pl.BlockSpec(memory_space=pltpu.HBM)


def tile_lanes(tile):
    return pl.ds(pl.multiple_of(tile * LANES, LANES), LANES)


def row_norm(load, store, tiles, mod_ref, row, total):
    width = tiles * LANES
    mean = jnp.sum(total, axis=-1, keepdims=True) * (1.0 / width)

    def square(tile, acc):
        centered = load(tile) - mean
        return acc + centered * centered

    squares = lax.fori_loop(0, tiles, square, jnp.zeros(total.shape, jnp.float32), unroll=6)
    variance = jnp.sum(squares, axis=-1, keepdims=True) * (1.0 / width)
    factor = lax.rsqrt(variance + EPSILON)

    def write(tile, carry):
        lanes = tile_lanes(tile)
        scale = 1.0 + mod_ref[row + 1 : row + 2, lanes]
        shift = mod_ref[row : row + 1, lanes]
        store(lanes, (load(tile) - mean) * factor * scale + shift)
        return carry

    lax.fori_loop(0, tiles, write, 0, unroll=6)


def run_copies(pairs, sems):
    copies = [
        pltpu.make_async_copy(source, target, sems.at[at])
        for at, (source, target) in enumerate(pairs)
    ]
    for copy in copies:
        copy.start()
    for copy in copies:
        copy.wait()


def stage_kernel(
    info_ref, hidden_hbm, taps_hbm, mod_hbm, own_ref, taps_ref, mod_ref, first_ref, live_ref, sems
):
    rows = own_ref.shape[0]
    core = info_ref[CORE]
    first_ref[...] = jnp.zeros(first_ref.shape, jnp.float32) + (1 - core).astype(jnp.float32)
    row = lax.broadcasted_iota(jnp.int32, live_ref.shape, 0)
    frame = row + (2 * info_ref[CHIP] + core) * rows
    live_ref[...] = (frame < info_ref[LENGTH]).astype(jnp.float32)
    run_copies(
        [(hidden_hbm.at[core], own_ref), (taps_hbm, taps_ref), (mod_hbm, mod_ref)], sems
    )


def front_kernel(
    first_pair, info_ref, own_ref, partner_ref, near_ref, far_ref, taps_ref, mod_ref, cos_ref, sin_ref,
    weight_hbm, residual_ref, normed_ref, weight_ref, *refs,
):
    *out_refs, padded, sems = refs
    rows, width = own_ref.shape
    halo = near_ref.shape[1]
    total_rows = 2 * rows
    tiles = width // LANES
    parts = sems.shape[0]
    depth = width // parts
    loads = []
    for part in range(parts):
        here = pl.ds(part * depth, depth)
        loads.append(
            pltpu.make_async_copy(weight_hbm.at[here], weight_ref.at[here], sems.at[part])
        )
    for load in loads:
        load.start()
    length, core = info_ref[LENGTH], info_ref[CORE]
    offset = info_ref[CHIP] * total_rows
    span = total_rows + 2 * halo
    frame = offset - halo + lax.broadcasted_iota(jnp.int32, (span, LANES), 0)
    live = ((frame >= 0) & (frame < length)).astype(jnp.float32)
    first = halo - KERNEL // 2
    own_at = pl.ds(pl.multiple_of(halo + core * rows, 8), rows)
    partner_at = pl.ds(pl.multiple_of(halo + (1 - core) * rows, 8), rows)
    near_at = pl.ds(pl.multiple_of(core * (halo + total_rows), 8), halo)
    far_at = pl.ds(pl.multiple_of((1 - core) * (halo + total_rows), 8), halo)

    def convolve(tile, total):
        lanes = tile_lanes(tile)
        padded[near_at] = near_ref[core, :, lanes].astype(jnp.float32)
        padded[far_at] = far_ref[core, :, lanes].astype(jnp.float32)
        padded[own_at] = own_ref[:, lanes].astype(jnp.float32)
        padded[partner_at] = partner_ref[:, lanes].astype(jnp.float32)
        own = padded[halo : halo + total_rows]
        padded[...] = padded[...] * live
        acc = jnp.zeros((total_rows, LANES), jnp.float32)
        for tap in range(KERNEL):
            acc = acc + taps_ref[tap : tap + 1, lanes] * padded[
                first + tap : first + tap + total_rows
            ]
        grown = jnp.exp(jnp.minimum(acc, 20.0))
        product = grown * (grown + 2.0)
        value = own + acc * (product / (product + 2.0))
        residual_ref[:, lanes] = value
        return total + value

    total = lax.fori_loop(
        0, tiles, convolve, jnp.zeros((total_rows, LANES), jnp.float32), unroll=3
    )

    def store(lanes, value):
        normed_ref[:, lanes] = value.astype(jnp.bfloat16)

    row_norm(lambda tile: residual_ref[:, tile_lanes(tile)], store, tiles, mod_ref, 0, total)
    if first_pair is None:
        for load in loads:
            load.wait()
    else:
        project_landing(
            first_pair, info_ref[CHIP], loads, normed_ref, weight_ref, cos_ref, sin_ref, out_refs
        )


def pair_lanes(chip, apart, part, attn):
    wide = 2 * LANES
    start = part * attn + ((chip ^ apart) >> 1) * wide
    return pl.ds(pl.multiple_of(start, wide), wide)


def store_pair(products, chip, cos_ref, sin_ref, out_refs):
    rows = cos_ref.shape[0]
    half = HEAD_DIM // 2
    cosine, sine = cos_ref[...], sin_ref[...]
    lower = lax.broadcasted_iota(jnp.int32, (rows, LANES), 1) % HEAD_DIM < half
    swap = jnp.full((rows, LANES), chip & 1, jnp.int32) > 0
    for part, both in enumerate(products):
        sides = []
        for side in range(2):
            value = both[:, side * LANES : (side + 1) * LANES]
            if part < 2:
                swapped = jnp.where(
                    lower, pltpu.roll(value, LANES - half, 1), pltpu.roll(value, half, 1)
                )
                value = value * cosine + swapped * sine
            if part == 0:
                value = value * HEAD_DIM**-0.5
            sides.append(value)
        out_refs[0][part] = jnp.where(swap, sides[1], sides[0]).astype(jnp.bfloat16)
        out_refs[1][part] = jnp.where(swap, sides[0], sides[1]).astype(jnp.bfloat16)


def project_landing(apart, chip, loads, normed_ref, weight_ref, cos_ref, sin_ref, out_refs):
    depth = weight_ref.shape[0] // len(loads)
    attn = weight_ref.shape[1] // 3
    products = [jnp.zeros((normed_ref.shape[0], 2 * LANES), jnp.float32)] * 3
    for at, load in enumerate(loads):
        load.wait()
        here = slice(at * depth, (at + 1) * depth)
        for part in range(3):
            products[part] = products[part] + jnp.dot(
                normed_ref[:, here],
                weight_ref[here, pair_lanes(chip, apart, part, attn)],
                preferred_element_type=jnp.float32,
            )
    store_pair(products, chip, cos_ref, sin_ref, out_refs)


def project_kernel(firsts, origin, info_ref, normed_ref, weight_ref, cos_ref, sin_ref, *out_refs):
    chip = info_ref[CHIP] if origin is None else origin
    attn = weight_ref.shape[1] // 3
    for at, apart in enumerate(firsts):
        products = [
            jnp.dot(
                normed_ref[...],
                weight_ref[:, pair_lanes(chip, apart, part, attn)],
                preferred_element_type=jnp.float32,
            )
            for part in range(3)
        ]
        store_pair(products, chip, cos_ref, sin_ref, out_refs[2 * at : 2 * at + 2])


def place_keys(info_ref, apart, got_ref, keys, values, first):
    _, rows, _ = got_ref.shape
    chip = info_ref[CHIP] ^ apart
    lane = lax.broadcasted_iota(jnp.int32, (rows, LANES), 1)
    row = lax.broadcasted_iota(jnp.int32, (rows, LANES), 0)
    here = slice(first, first + rows)
    keys[here, :LANES] = got_ref[1]
    dead = (lane == 0) & (row + chip * rows >= info_ref[LENGTH])
    keys[here, LANES:] = jnp.where(dead, NEGATIVE, 0.0).astype(jnp.bfloat16)
    values[here, :] = got_ref[2]


def place_queries(query_refs, queries):
    _, rows, _ = query_refs[0].shape
    low = lax.broadcasted_iota(jnp.int32, (rows, LANES), 1) < HEAD_DIM
    zero = jnp.zeros((rows, LANES), jnp.bfloat16)
    queries[:, LANES:] = jnp.where(
        lax.broadcasted_iota(jnp.int32, (queries.shape[0], LANES), 1) == 0, 1.0, 0.0
    ).astype(jnp.bfloat16)
    for at, query_ref in enumerate(query_refs):
        query = query_ref[0]
        base = 2 * at * rows
        queries[base : base + rows, :LANES] = jnp.where(low, query, zero)
        queries[base + rows : base + 2 * rows, :LANES] = jnp.where(low, zero, query)


def score(queries, keys):
    return lax.dot_general(
        queries, keys, (((1,), (1,)), ((), ())), preferred_element_type=jnp.float32
    )


def mix(weights, values):
    return jnp.dot(weights.astype(jnp.bfloat16), values, preferred_element_type=jnp.float32)


def store_heads(mixed, out_ref, first):
    _, rows, _ = out_ref.shape
    low = lax.broadcasted_iota(jnp.int32, (rows, LANES), 1) < HEAD_DIM
    for at in range(mixed.shape[0] // (2 * rows)):
        base = 2 * at * rows
        out_ref[first + at] = jnp.where(
            low, mixed[base : base + rows], mixed[base + rows : base + 2 * rows]
        ).astype(jnp.bfloat16)


def attend_rows(keys, values, queries, out_ref, first):
    _, rows, _ = out_ref.shape
    total = queries.shape[0]
    for base in range(0, total, 4 * rows):
        block = slice(base, min(base + 4 * rows, total))
        scores = score(queries[block, :], keys[...])
        weights = jnp.exp(scores - jnp.max(scores, axis=1, keepdims=True))
        weight_sum = jnp.sum(weights, axis=1, keepdims=True)
        store_heads(mix(weights, values[...]) / weight_sum, out_ref, first + base // (2 * rows))


def attend_early_kernel(info_ref, *refs):
    chips = len(refs) - 6
    got_refs = refs[:chips]
    keys, values, queries, mixed_ref, peak_ref, sum_ref = refs[chips:]
    _, rows, _ = got_refs[0].shape
    for apart, got_ref in enumerate(got_refs):
        place_keys(info_ref, apart, got_ref, keys, values, apart * rows)
    place_queries(got_refs[1::2], queries)
    half = queries.shape[0] // 2
    for block in (slice(0, half), slice(half, 2 * half)):
        scores = score(queries[block, :], keys[...])
        peak = jnp.max(scores, axis=1, keepdims=True)
        weights = jnp.exp(scores - peak)
        peak_ref[block, :] = jnp.broadcast_to(peak, (half, LANES))
        weight_sum = jnp.sum(weights, axis=1, keepdims=True)
        sum_ref[block, :] = jnp.broadcast_to(weight_sum, (half, LANES))
        mixed_ref[block, :] = mix(weights, values[...])


def attend_last_kernel(
    info_ref, early_keys, early_values, early_queries, mixed_ref, peak_ref, sum_ref, last_ref,
    out_ref, keys, values, queries,
):
    held, _ = early_values.shape
    _, rows, _ = last_ref.shape
    keys[:held, :] = early_keys[...]
    values[:held, :] = early_values[...]
    place_keys(info_ref, held // rows, last_ref, keys, values, held)
    place_queries([last_ref], queries)
    attend_rows(keys, values, queries, out_ref, out_ref.shape[0] - 1)
    scores = score(early_queries[...], keys[held:, :])
    peak = peak_ref[...]
    joined = jnp.maximum(peak, jnp.max(scores, axis=1, keepdims=True))
    scale = jnp.exp(peak - joined)
    weights = jnp.exp(scores - joined[:, : scores.shape[1]])
    weight_sum = sum_ref[...] * scale + jnp.sum(weights, axis=1, keepdims=True)
    mixed = mixed_ref[...] * scale + mix(weights, values[held:, :])
    store_heads(mixed / weight_sum, out_ref, 0)


def attend_second_kernel(info_ref, keys, values, *refs):
    del info_ref
    out_ref, queries = refs[-2:]
    place_queries(refs[:-2], queries)
    attend_rows(keys, values, queries, out_ref, 0)


def merge_kernel(info_ref, own_ref, got_ref, *out_refs):
    del info_ref
    for at, out_ref in enumerate(out_refs):
        out_ref[0] = own_ref[at + 1]
        out_ref[1] = got_ref[at + 1]


def back_kernel(blocks, info_ref, residual, w_mel, mod_ref, w_out_ref, *refs):
    count = 1 + max(at for at, _, _ in blocks)
    got_refs = refs[:count]
    keep_ref, send_ref, attended, after, speed = refs[count:]
    rows, width = residual.shape
    tiles = width // LANES
    core, chip = info_ref[CORE], info_ref[CHIP]
    for at, place, apart in blocks:
        group = place if apart is None else chip ^ apart
        attended[:, tile_lanes(group)] = got_refs[at][place]
    wide = 2 * LANES
    total = jnp.zeros((rows, LANES), jnp.float32)
    for block in range(width // wide):
        lanes = slice(block * wide, (block + 1) * wide)
        branch = jnp.dot(attended[...], w_out_ref[:, lanes], preferred_element_type=jnp.float32)
        value = residual[:, lanes] + mod_ref[2:3, lanes] * branch
        after[:, lanes] = value
        total = total + value[:, :LANES] + value[:, LANES:]

    def store(lanes, value):
        after[:, lanes] = value

    row_norm(lambda tile: after[:, tile_lanes(tile)], store, tiles, mod_ref, 3, total)
    speed[...] = lax.dot_general(
        after[...].astype(jnp.bfloat16), w_mel[...], (((1,), (1,)), ((), ())),
        preferred_element_type=jnp.float32,
    )
    half = rows // 2
    keep_ref[...] = speed[pl.ds(pl.multiple_of(core * half, 8), half), :]
    send_ref[...] = speed[pl.ds(pl.multiple_of((1 - core) * half, 8), half), :]


def call(kernel, out_shape, inputs, scratch, hbm=()):
    single = not isinstance(out_shape, tuple)
    specs = [hbm_spec() if at in hbm else vmem_spec() for at in range(1, len(inputs))]
    inputs = list(inputs)
    for at in hbm:
        inputs[at] = pltpu.with_memory_space_constraint(inputs[at], pltpu.HBM)
    return pl.pallas_call(
        kernel,
        out_shape=out_shape,
        in_specs=[smem_spec()] + specs,
        out_specs=vmem_spec() if single else tuple(vmem_spec() for _ in out_shape),
        scratch_shapes=scratch,
        compiler_params=pltpu.CompilerParams(vmem_limit_bytes=GRANT),
    )(*inputs)


def array(shape, dtype=jnp.float32):
    return jax.ShapeDtypeStruct(shape, dtype)


def project(normed, w_qkv, tables, info, firsts, origin=None):
    shape = array((3, normed.shape[0], LANES), jnp.bfloat16)
    return call(
        functools.partial(project_kernel, tuple(firsts), origin),
        (shape,) * (2 * len(firsts)),
        (info, normed, w_qkv) + tables,
        [],
    )


def same_core(count):
    return [list(range(core, count, 2)) for core in range(2)]


def facing_pairs(clips, count):
    pairs = []
    for clip in range(clips):
        base = clip * count
        for at in range(1, count - 1, 2):
            pairs += [(base + at, base + at + 1), (base + at + 1, base + at)]
        if clip ^ 1 < clips:
            pairs += [(base + end, (clip ^ 1) * count + end) for end in (0, count - 1)]
    return pairs


def across(value, apart, count):
    return lax.ppermute(value, "seq", [(i, i ^ apart) for i in range(count)])


def to_groups(values, subs):
    rows, _ = values.shape
    grouped = values.reshape(subs, rows // subs, HEADS, HEAD_DIM).transpose(2, 0, 1, 3)
    return grouped.reshape(HEADS * subs, rows // subs, HEAD_DIM)


def from_groups(grouped, rows, subs):
    split = grouped.reshape(HEADS, subs, rows // subs, HEAD_DIM).transpose(1, 2, 0, 3)
    return split.reshape(rows, HEADS * HEAD_DIM)


def attend_blocks(queries, keys, values, live):
    groups, total, _ = queries.shape
    block = max(size for size in range(1, min(total, 1024) + 1) if total % size == 0)
    blocks = queries.reshape(groups, total // block, block, HEAD_DIM).transpose(1, 0, 2, 3)
    live = live[None, None, :]

    def one_block(query):
        scores = jnp.einsum("gqd,gkd->gqk", query, keys, preferred_element_type=jnp.float32)
        scores = jnp.where(live, scores, NEGATIVE)
        weights = jnp.exp(scores - jnp.max(scores, axis=-1, keepdims=True))
        weights = jnp.where(live, weights, 0.0)
        mixed = jnp.einsum(
            "gqk,gkd->gqd",
            weights.astype(jnp.bfloat16),
            values,
            preferred_element_type=jnp.float32,
        )
        return (mixed / jnp.sum(weights, axis=-1)[..., None]).astype(jnp.bfloat16)

    return lax.map(one_block, blocks).transpose(1, 0, 2, 3).reshape(groups, total, HEAD_DIM)


def attend_any(normed, w_qkv, tables, info, length, count):
    rows = normed.shape[0]
    chips = count // 2
    groups = HEADS * HEAD_DIM // LANES
    sent = project(normed, w_qkv, tables, info, range(0, groups, 2), 0)
    subs = max(1, chips // HEADS)
    chip = lax.axis_index("seq") >> 1
    part_rows = rows // subs

    def exchange(part):
        whole = jnp.concatenate([group[part] for group in sent], axis=1)
        return lax.all_to_all(
            to_groups(whole, subs), "seq", split_axis=0, concat_axis=1, tiled=True,
            axis_index_groups=same_core(count),
        )

    queries, keys, values = (exchange(part) for part in range(3))

    def frames_of(sub):
        start = jnp.arange(chips, dtype=jnp.int32)[:, None] * rows + sub * part_rows
        return (start + jnp.arange(part_rows, dtype=jnp.int32)[None, :]).reshape(-1)

    frames = [frames_of(chip % subs)]
    parts = [(keys, values)]
    for apart in range(1, subs):
        perm = []
        for i in range(count):
            at = i // 2
            target = at - at % subs + (at + apart) % subs
            perm.append((i, 2 * target + i % 2))
        parts.append(tuple(lax.ppermute(part, "seq", perm) for part in (keys, values)))
        frames.append(frames_of((chip - apart) % subs))
    keys = jnp.concatenate([part[0] for part in parts], axis=1)
    values = jnp.concatenate([part[1] for part in parts], axis=1)
    attended = attend_blocks(queries, keys, values, jnp.concatenate(frames) < length)
    back = lax.all_to_all(
        attended, "seq", split_axis=1, concat_axis=0, tiled=True,
        axis_index_groups=same_core(count),
    )
    return from_groups(back, rows, subs).reshape(rows, groups, LANES).transpose(1, 0, 2)


def chips_hold_groups(count):
    chips = count // 2
    return chips == HEADS * HEAD_DIM // LANES and chips >= 4 and chips & (chips - 1) == 0


def send_order(chips):
    far = list(range(chips // 2, chips, 2))
    return far[:1] + list(range(2, chips // 2, 2)) + far[1:] + [0]


def attend_chips(made, normed, w_qkv, tables, info, count):
    rows = normed.shape[0]
    chips = count // 2
    held = {}
    for first in send_order(chips):
        if held:
            made = project(normed, w_qkv, tables, info, [first])
        for side in range(2):
            apart = first + side
            held[apart] = across(made[side], 2 * apart, count) if apart else made[side]
    total, half = chips * rows, chips // 2
    early, early_rows = total - rows, 2 * (half - 1) * rows
    parts = call(
        attend_early_kernel,
        (
            array((early, 2 * LANES), jnp.bfloat16),
            array((early, LANES), jnp.bfloat16),
            array((early_rows, 2 * LANES), jnp.bfloat16),
        )
        + (array((early_rows, LANES)),) * 3,
        (info,) + tuple(held[apart] for apart in range(chips - 1)),
        [],
    )
    crossing, keys, values = call(
        attend_last_kernel,
        (
            array((half, rows, LANES), jnp.bfloat16),
            array((total, 2 * LANES), jnp.bfloat16),
            array((total, LANES), jnp.bfloat16),
        ),
        (info,) + tuple(parts) + (held[chips - 1],),
        [VMEM((2 * rows, 2 * LANES), jnp.bfloat16)],
    )
    crossed = across(crossing, 2, count)
    staying = call(
        attend_second_kernel,
        array((half, rows, LANES), jnp.bfloat16),
        (info, keys, values) + tuple(held[apart] for apart in range(0, chips, 2)),
        [VMEM((total, 2 * LANES), jnp.bfloat16)],
    )
    joined = call(
        merge_kernel,
        (array((2, rows, LANES), jnp.bfloat16),) * (half - 1),
        (info, staying, crossed),
        [],
    )
    back, blocks = [staying, crossed], [(0, 0, 0), (1, 0, 1)]
    got = {}
    for apart in range(1, half):
        got[apart] = across(joined[apart - 1], 4 * apart, count)
    for apart in range(1, half):
        blocks += [(len(back), side, 2 * apart + side) for side in range(2)]
        back.append(got[apart])
    return back, blocks


def per_device(
    hidden, latent, lengths, step_index, guidance, modulation, conv_kernel, w_qkv, w_out, w_mel
):
    copies, rows, width = hidden.shape
    count = lax.axis_size("seq")
    chips = count // 2
    index = lax.axis_index("seq").astype(jnp.int32)
    chip, core = index >> 1, index & 1
    chip_rows = 2 * rows
    info = jnp.stack([core, chip, lengths[0]])

    edges = lax.dynamic_slice(hidden, (0, core * (rows - HALO), 0), (copies, HALO, width))
    partner = lax.dynamic_slice(hidden, (1 - core, 0, 0), (1, rows, width))[0]
    near = lax.ppermute(edges, ("clip", "seq"), facing_pairs(lax.axis_size("clip"), count))
    far = across(near, 1, count)
    partner = across(partner, 1, count)
    own, taps, mods, is_first, live = call(
        stage_kernel,
        (
            array((rows, width), jnp.bfloat16),
            array(conv_kernel.shape),
            array(modulation.shape),
            array(latent.shape),
            array(latent.shape),
        ),
        (info, hidden, conv_kernel, modulation),
        [pltpu.SemaphoreType.DMA((3,))],
        hbm=(1, 2, 3),
    )
    tables = rotary_tables(chip * chip_rows + jnp.arange(chip_rows, dtype=jnp.int32))
    first_pair = send_order(chips)[0] if chips_hold_groups(count) else None
    group = array((3, chip_rows, LANES), jnp.bfloat16)
    residual, normed, weight, *made = call(
        functools.partial(front_kernel, first_pair),
        (
            array((chip_rows, width)),
            array((chip_rows, width), jnp.bfloat16),
            array(w_qkv.shape, jnp.bfloat16),
        )
        + (group,) * (0 if first_pair is None else 2),
        (info, own, partner, near, far, taps, mods) + tables + (w_qkv,),
        [
            VMEM((chip_rows + 2 * HALO, LANES), jnp.float32),
            pltpu.SemaphoreType.DMA((width // (2 * LANES),)),
        ],
        hbm=(9,),
    )
    if chips_hold_groups(count):
        back, blocks = attend_chips(made, normed, weight, tables, info, count)
    else:
        back = [attend_any(normed, weight, tables, info, lengths[0], count)]
        blocks = [(0, group, None) for group in range(back[0].shape[0])]
    mels = w_mel.shape[1]
    keep, send = call(
        functools.partial(back_kernel, tuple(blocks)),
        (array((rows, mels)),) * 2,
        (info, residual, w_mel.T, mods, w_out) + tuple(back),
        [
            VMEM((chip_rows, HEADS * HEAD_DIM), jnp.bfloat16),
            VMEM((chip_rows, width), jnp.float32),
            VMEM((chip_rows, mels), jnp.float32),
        ],
    )
    other = across(send, 1, count)
    first = jnp.where(is_first > 0.5, keep, other)
    second = jnp.where(is_first > 0.5, other, keep)
    guided = first + guidance[0] * (first - second)
    velocity = jnp.where(live > 0.5, guided, 0.0)
    progress = step_index[0].astype(jnp.float32) / STEPS
    time_now = 1.0 - jnp.cos(0.5 * jnp.pi * progress)
    return (velocity, latent + (1.0 - time_now) * velocity)


def solution(mesh):
    return jax.shard_map(
        per_device,
        mesh=mesh,
        in_specs=(
            P(None, ("clip", "seq"), None),
            P(("clip", "seq"), None),
            P("clip"),
            P(),
            P(),
            P(),
            P(),
            P(),
            P(),
            P(),
        ),
        out_specs=(P(("clip", "seq"), None), P(("clip", "seq"), None)),
        check_vma=False,
    )
```

```python
import functools

import jax
import jax.numpy as jnp
from jax import lax
from jax.experimental import pallas as pl
from jax.experimental.pallas import tpu as pltpu
from jax.sharding import PartitionSpec as P


HEADS = 16
HEAD_DIM = 64
KERNEL = 31
STEPS = 32
LANES = 128
HALO = 16


EPSILON = 1e-06
NEGATIVE = -1e30
CORE, CHIP, LENGTH = 0, 1, 2
VMEM = pltpu.VMEM
SMEM = pltpu.SMEM
GRANT = 12 << 20


def vmem_spec():
    return pl.BlockSpec(memory_space=VMEM)


def smem_spec():
    return pl.BlockSpec(memory_space=SMEM)


def rotary_tables(positions):
    half_dim = HEAD_DIM // 2
    lane = jnp.arange(LANES, dtype=jnp.int32)
    inverse = 10000.0 ** (-(lane % half_dim).astype(jnp.float32) / half_dim)
    angles = positions.astype(jnp.float32)[:, None] * inverse[None, :]
    sign = jnp.where(lane % HEAD_DIM < half_dim, -1.0, 1.0)
    return jnp.cos(angles), jnp.sin(angles) * sign[None, :]


def hbm_spec():
    return pl.BlockSpec(memory_space=pltpu.HBM)


def tile_lanes(tile):
    return pl.ds(pl.multiple_of(tile * LANES, LANES), LANES)


def row_norm(load, store, tiles, mod_ref, row, total):
    width = tiles * LANES
    mean = jnp.sum(total, axis=-1, keepdims=True) * (1.0 / width)

    def square(tile, acc):
        centered = load(tile) - mean
        return acc + centered * centered

    squares = lax.fori_loop(0, tiles, square, jnp.zeros(total.shape, jnp.float32), unroll=6)
    variance = jnp.sum(squares, axis=-1, keepdims=True) * (1.0 / width)
    factor = lax.rsqrt(variance + EPSILON)

    def write(tile, carry):
        lanes = tile_lanes(tile)
        scale = 1.0 + mod_ref[row + 1 : row + 2, lanes]
        shift = mod_ref[row : row + 1, lanes]
        store(lanes, (load(tile) - mean) * factor * scale + shift)
        return carry

    lax.fori_loop(0, tiles, write, 0, unroll=6)


def run_copies(pairs, sems):
    copies = [
        pltpu.make_async_copy(source, target, sems.at[at])
        for at, (source, target) in enumerate(pairs)
    ]
    for copy in copies:
        copy.start()
    for copy in copies:
        copy.wait()


def stage_kernel(
    info_ref, hidden_hbm, taps_hbm, mod_hbm, own_ref, taps_ref, mod_ref, first_ref, live_ref, sems
):
    rows = own_ref.shape[0]
    core = info_ref[CORE]
    first_ref[...] = jnp.zeros(first_ref.shape, jnp.float32) + (1 - core).astype(jnp.float32)
    row = lax.broadcasted_iota(jnp.int32, live_ref.shape, 0)
    frame = row + (2 * info_ref[CHIP] + core) * rows
    live_ref[...] = (frame < info_ref[LENGTH]).astype(jnp.float32)
    run_copies(
        [(hidden_hbm.at[core], own_ref), (taps_hbm, taps_ref), (mod_hbm, mod_ref)], sems
    )


def front_kernel(
    first_pair, info_ref, own_ref, partner_ref, near_ref, far_ref, taps_ref, mod_ref, cos_ref, sin_ref,
    weight_hbm, residual_ref, normed_ref, weight_ref, *refs,
):
    *out_refs, padded, sems = refs
    rows, width = own_ref.shape
    halo = near_ref.shape[1]
    total_rows = 2 * rows
    tiles = width // LANES
    parts = sems.shape[0]
    depth = width // parts
    loads = []
    for part in range(parts):
        here = pl.ds(part * depth, depth)
        loads.append(
            pltpu.make_async_copy(weight_hbm.at[here], weight_ref.at[here], sems.at[part])
        )
    for load in loads:
        load.start()
    length, core = info_ref[LENGTH], info_ref[CORE]
    offset = info_ref[CHIP] * total_rows
    span = total_rows + 2 * halo
    frame = offset - halo + lax.broadcasted_iota(jnp.int32, (span, LANES), 0)
    live = ((frame >= 0) & (frame < length)).astype(jnp.float32)
    first = halo - KERNEL // 2
    own_at = pl.ds(pl.multiple_of(halo + core * rows, 8), rows)
    partner_at = pl.ds(pl.multiple_of(halo + (1 - core) * rows, 8), rows)
    near_at = pl.ds(pl.multiple_of(core * (halo + total_rows), 8), halo)
    far_at = pl.ds(pl.multiple_of((1 - core) * (halo + total_rows), 8), halo)

    def convolve(tile, total):
        lanes = tile_lanes(tile)
        padded[near_at] = near_ref[core, :, lanes].astype(jnp.float32)
        padded[far_at] = far_ref[core, :, lanes].astype(jnp.float32)
        padded[own_at] = own_ref[:, lanes].astype(jnp.float32)
        padded[partner_at] = partner_ref[:, lanes].astype(jnp.float32)
        own = padded[halo : halo + total_rows]
        padded[...] = padded[...] * live
        acc = jnp.zeros((total_rows, LANES), jnp.float32)
        for tap in range(KERNEL):
            acc = acc + taps_ref[tap : tap + 1, lanes] * padded[
                first + tap : first + tap + total_rows
            ]
        grown = jnp.exp(jnp.minimum(acc, 20.0))
        product = grown * (grown + 2.0)
        value = own + acc * (product / (product + 2.0))
        residual_ref[:, lanes] = value
        return total + value

    total = lax.fori_loop(
        0, tiles, convolve, jnp.zeros((total_rows, LANES), jnp.float32), unroll=3
    )

    def store(lanes, value):
        normed_ref[:, lanes] = value.astype(jnp.bfloat16)

    row_norm(lambda tile: residual_ref[:, tile_lanes(tile)], store, tiles, mod_ref, 0, total)
    if first_pair is None:
        for load in loads:
            load.wait()
    else:
        project_landing(
            first_pair, info_ref[CHIP], loads, normed_ref, weight_ref, cos_ref, sin_ref, out_refs
        )


def pair_lanes(chip, apart, part, attn):
    wide = 2 * LANES
    start = part * attn + ((chip ^ apart) >> 1) * wide
    return pl.ds(pl.multiple_of(start, wide), wide)


def store_pair(products, chip, cos_ref, sin_ref, out_refs):
    rows = cos_ref.shape[0]
    half = HEAD_DIM // 2
    cosine, sine = cos_ref[...], sin_ref[...]
    lower = lax.broadcasted_iota(jnp.int32, (rows, LANES), 1) % HEAD_DIM < half
    swap = jnp.full((rows, LANES), chip & 1, jnp.int32) > 0
    for part, both in enumerate(products):
        sides = []
        for side in range(2):
            value = both[:, side * LANES : (side + 1) * LANES]
            if part < 2:
                swapped = jnp.where(
                    lower, pltpu.roll(value, LANES - half, 1), pltpu.roll(value, half, 1)
                )
                value = value * cosine + swapped * sine
            if part == 0:
                value = value * HEAD_DIM**-0.5
            sides.append(value)
        out_refs[0][part] = jnp.where(swap, sides[1], sides[0]).astype(jnp.bfloat16)
        out_refs[1][part] = jnp.where(swap, sides[0], sides[1]).astype(jnp.bfloat16)


def project_landing(apart, chip, loads, normed_ref, weight_ref, cos_ref, sin_ref, out_refs):
    depth = weight_ref.shape[0] // len(loads)
    attn = weight_ref.shape[1] // 3
    products = [jnp.zeros((normed_ref.shape[0], 2 * LANES), jnp.float32)] * 3
    for at, load in enumerate(loads):
        load.wait()
        here = slice(at * depth, (at + 1) * depth)
        for part in range(3):
            products[part] = products[part] + jnp.dot(
                normed_ref[:, here],
                weight_ref[here, pair_lanes(chip, apart, part, attn)],
                preferred_element_type=jnp.float32,
            )
    store_pair(products, chip, cos_ref, sin_ref, out_refs)


def project_kernel(firsts, origin, info_ref, normed_ref, weight_ref, cos_ref, sin_ref, *out_refs):
    chip = info_ref[CHIP] if origin is None else origin
    attn = weight_ref.shape[1] // 3
    for at, apart in enumerate(firsts):
        products = [
            jnp.dot(
                normed_ref[...],
                weight_ref[:, pair_lanes(chip, apart, part, attn)],
                preferred_element_type=jnp.float32,
            )
            for part in range(3)
        ]
        store_pair(products, chip, cos_ref, sin_ref, out_refs[2 * at : 2 * at + 2])


def place_keys(info_ref, apart, got_ref, keys, values, first):
    _, rows, _ = got_ref.shape
    chip = info_ref[CHIP] ^ apart
    lane = lax.broadcasted_iota(jnp.int32, (rows, LANES), 1)
    row = lax.broadcasted_iota(jnp.int32, (rows, LANES), 0)
    here = slice(first, first + rows)
    keys[here, :LANES] = got_ref[1]
    dead = (lane == 0) & (row + chip * rows >= info_ref[LENGTH])
    keys[here, LANES:] = jnp.where(dead, NEGATIVE, 0.0).astype(jnp.bfloat16)
    values[here, :] = got_ref[2]


def place_queries(query_refs, queries):
    _, rows, _ = query_refs[0].shape
    low = lax.broadcasted_iota(jnp.int32, (rows, LANES), 1) < HEAD_DIM
    zero = jnp.zeros((rows, LANES), jnp.bfloat16)
    queries[:, LANES:] = jnp.where(
        lax.broadcasted_iota(jnp.int32, (queries.shape[0], LANES), 1) == 0, 1.0, 0.0
    ).astype(jnp.bfloat16)
    for at, query_ref in enumerate(query_refs):
        query = query_ref[0]
        base = 2 * at * rows
        queries[base : base + rows, :LANES] = jnp.where(low, query, zero)
        queries[base + rows : base + 2 * rows, :LANES] = jnp.where(low, zero, query)


def score(queries, keys):
    return lax.dot_general(
        queries, keys, (((1,), (1,)), ((), ())), preferred_element_type=jnp.float32
    )


def mix(weights, values):
    return jnp.dot(weights.astype(jnp.bfloat16), values, preferred_element_type=jnp.float32)


def store_heads(mixed, out_ref, places):
    _, rows, _ = out_ref.shape
    low = lax.broadcasted_iota(jnp.int32, (rows, LANES), 1) < HEAD_DIM
    for at in range(mixed.shape[0] // (2 * rows)):
        base = 2 * at * rows
        out_ref[places[at]] = jnp.where(
            low, mixed[base : base + rows], mixed[base + rows : base + 2 * rows]
        ).astype(jnp.bfloat16)


def attend_rows(keys, values, queries, out_ref, places):
    _, rows, _ = out_ref.shape
    total = queries.shape[0]
    for base in range(0, total, 4 * rows):
        block = slice(base, min(base + 4 * rows, total))
        scores = score(queries[block, :], keys[...])
        weights = jnp.exp(scores - jnp.max(scores, axis=1, keepdims=True))
        weight_sum = jnp.sum(weights, axis=1, keepdims=True)
        mixed = mix(weights, values[...]) / weight_sum
        store_heads(mixed, out_ref, places[base // (2 * rows) :])


def attend_early_kernel(aparts, info_ref, *refs):
    chips = len(refs) - 6
    got_refs = refs[:chips]
    keys, values, queries, mixed_ref, peak_ref, sum_ref = refs[chips:]
    _, rows, _ = got_refs[0].shape
    for at, got_ref in enumerate(got_refs):
        place_keys(info_ref, aparts[at], got_ref, keys, values, at * rows)
    place_queries([ref for apart, ref in zip(aparts, got_refs) if apart % 2], queries)
    half = queries.shape[0] // 2
    for block in (slice(0, half), slice(half, 2 * half)):
        scores = score(queries[block, :], keys[...])
        peak = jnp.max(scores, axis=1, keepdims=True)
        weights = jnp.exp(scores - peak)
        peak_ref[block, :] = jnp.broadcast_to(peak, (half, LANES))
        weight_sum = jnp.sum(weights, axis=1, keepdims=True)
        sum_ref[block, :] = jnp.broadcast_to(weight_sum, (half, LANES))
        mixed_ref[block, :] = mix(weights, values[...])


def attend_last_kernel(
    late, places, info_ref, early_keys, early_values, early_queries, mixed_ref, peak_ref, sum_ref, last_ref,
    out_ref, keys, values, queries,
):
    held, _ = early_values.shape
    keys[:held, :] = early_keys[...]
    values[:held, :] = early_values[...]
    place_keys(info_ref, late, last_ref, keys, values, held)
    place_queries([last_ref], queries)
    attend_rows(keys, values, queries, out_ref, (late // 2,))
    scores = score(early_queries[...], keys[held:, :])
    peak = peak_ref[...]
    joined = jnp.maximum(peak, jnp.max(scores, axis=1, keepdims=True))
    scale = jnp.exp(peak - joined)
    weights = jnp.exp(scores - joined[:, : scores.shape[1]])
    weight_sum = sum_ref[...] * scale + jnp.sum(weights, axis=1, keepdims=True)
    mixed = mixed_ref[...] * scale + mix(weights, values[held:, :])
    store_heads(mixed / weight_sum, out_ref, places)


def attend_second_kernel(info_ref, keys, values, *refs):
    del info_ref
    out_ref, queries = refs[-2:]
    place_queries(refs[:-2], queries)
    attend_rows(keys, values, queries, out_ref, tuple(range(out_ref.shape[0])))


def merge_kernel(info_ref, own_ref, got_ref, *out_refs):
    del info_ref
    for at, out_ref in enumerate(out_refs):
        out_ref[0] = own_ref[at + 1]
        out_ref[1] = got_ref[at + 1]


def back_kernel(blocks, info_ref, residual, w_mel, mod_ref, w_out_ref, *refs):
    count = 1 + max(at for at, _, _ in blocks)
    got_refs = refs[:count]
    keep_ref, send_ref, attended, after, speed = refs[count:]
    rows, width = residual.shape
    tiles = width // LANES
    core, chip = info_ref[CORE], info_ref[CHIP]
    for at, place, apart in blocks:
        group = place if apart is None else chip ^ apart
        attended[:, tile_lanes(group)] = got_refs[at][place]
    wide = 2 * LANES
    total = jnp.zeros((rows, LANES), jnp.float32)
    for block in range(width // wide):
        lanes = slice(block * wide, (block + 1) * wide)
        branch = jnp.dot(attended[...], w_out_ref[:, lanes], preferred_element_type=jnp.float32)
        value = residual[:, lanes] + mod_ref[2:3, lanes] * branch
        after[:, lanes] = value
        total = total + value[:, :LANES] + value[:, LANES:]

    def store(lanes, value):
        after[:, lanes] = value

    row_norm(lambda tile: after[:, tile_lanes(tile)], store, tiles, mod_ref, 3, total)
    speed[...] = lax.dot_general(
        after[...].astype(jnp.bfloat16), w_mel[...], (((1,), (1,)), ((), ())),
        preferred_element_type=jnp.float32,
    )
    half = rows // 2
    keep_ref[...] = speed[pl.ds(pl.multiple_of(core * half, 8), half), :]
    send_ref[...] = speed[pl.ds(pl.multiple_of((1 - core) * half, 8), half), :]


def call(kernel, out_shape, inputs, scratch, hbm=()):
    single = not isinstance(out_shape, tuple)
    specs = [hbm_spec() if at in hbm else vmem_spec() for at in range(1, len(inputs))]
    inputs = list(inputs)
    for at in hbm:
        inputs[at] = pltpu.with_memory_space_constraint(inputs[at], pltpu.HBM)
    return pl.pallas_call(
        kernel,
        out_shape=out_shape,
        in_specs=[smem_spec()] + specs,
        out_specs=vmem_spec() if single else tuple(vmem_spec() for _ in out_shape),
        scratch_shapes=scratch,
        compiler_params=pltpu.CompilerParams(vmem_limit_bytes=GRANT),
    )(*inputs)


def array(shape, dtype=jnp.float32):
    return jax.ShapeDtypeStruct(shape, dtype)


def project(normed, w_qkv, tables, info, firsts, origin=None):
    shape = array((3, normed.shape[0], LANES), jnp.bfloat16)
    return call(
        functools.partial(project_kernel, tuple(firsts), origin),
        (shape,) * (2 * len(firsts)),
        (info, normed, w_qkv) + tables,
        [],
    )


def same_core(count):
    return [list(range(core, count, 2)) for core in range(2)]


def facing_pairs(clips, count):
    pairs = []
    for clip in range(clips):
        base = clip * count
        for at in range(1, count - 1, 2):
            pairs += [(base + at, base + at + 1), (base + at + 1, base + at)]
        if clip ^ 1 < clips:
            pairs += [(base + end, (clip ^ 1) * count + end) for end in (0, count - 1)]
    return pairs


def across(value, apart, count):
    return lax.ppermute(value, "seq", [(i, i ^ apart) for i in range(count)])


def to_groups(values, subs):
    rows, _ = values.shape
    grouped = values.reshape(subs, rows // subs, HEADS, HEAD_DIM).transpose(2, 0, 1, 3)
    return grouped.reshape(HEADS * subs, rows // subs, HEAD_DIM)


def from_groups(grouped, rows, subs):
    split = grouped.reshape(HEADS, subs, rows // subs, HEAD_DIM).transpose(1, 2, 0, 3)
    return split.reshape(rows, HEADS * HEAD_DIM)


def attend_blocks(queries, keys, values, live):
    groups, total, _ = queries.shape
    block = max(size for size in range(1, min(total, 1024) + 1) if total % size == 0)
    blocks = queries.reshape(groups, total // block, block, HEAD_DIM).transpose(1, 0, 2, 3)
    live = live[None, None, :]

    def one_block(query):
        scores = jnp.einsum("gqd,gkd->gqk", query, keys, preferred_element_type=jnp.float32)
        scores = jnp.where(live, scores, NEGATIVE)
        weights = jnp.exp(scores - jnp.max(scores, axis=-1, keepdims=True))
        weights = jnp.where(live, weights, 0.0)
        mixed = jnp.einsum(
            "gqk,gkd->gqd",
            weights.astype(jnp.bfloat16),
            values,
            preferred_element_type=jnp.float32,
        )
        return (mixed / jnp.sum(weights, axis=-1)[..., None]).astype(jnp.bfloat16)

    return lax.map(one_block, blocks).transpose(1, 0, 2, 3).reshape(groups, total, HEAD_DIM)


def attend_any(normed, w_qkv, tables, info, length, count):
    rows = normed.shape[0]
    chips = count // 2
    groups = HEADS * HEAD_DIM // LANES
    sent = project(normed, w_qkv, tables, info, range(0, groups, 2), 0)
    subs = max(1, chips // HEADS)
    chip = lax.axis_index("seq") >> 1
    part_rows = rows // subs

    def exchange(part):
        whole = jnp.concatenate([group[part] for group in sent], axis=1)
        return lax.all_to_all(
            to_groups(whole, subs), "seq", split_axis=0, concat_axis=1, tiled=True,
            axis_index_groups=same_core(count),
        )

    queries, keys, values = (exchange(part) for part in range(3))

    def frames_of(sub):
        start = jnp.arange(chips, dtype=jnp.int32)[:, None] * rows + sub * part_rows
        return (start + jnp.arange(part_rows, dtype=jnp.int32)[None, :]).reshape(-1)

    frames = [frames_of(chip % subs)]
    parts = [(keys, values)]
    for apart in range(1, subs):
        perm = []
        for i in range(count):
            at = i // 2
            target = at - at % subs + (at + apart) % subs
            perm.append((i, 2 * target + i % 2))
        parts.append(tuple(lax.ppermute(part, "seq", perm) for part in (keys, values)))
        frames.append(frames_of((chip - apart) % subs))
    keys = jnp.concatenate([part[0] for part in parts], axis=1)
    values = jnp.concatenate([part[1] for part in parts], axis=1)
    attended = attend_blocks(queries, keys, values, jnp.concatenate(frames) < length)
    back = lax.all_to_all(
        attended, "seq", split_axis=1, concat_axis=0, tiled=True,
        axis_index_groups=same_core(count),
    )
    return from_groups(back, rows, subs).reshape(rows, groups, LANES).transpose(1, 0, 2)


def chips_hold_groups(count):
    chips = count // 2
    return chips == HEADS * HEAD_DIM // LANES and chips >= 4 and chips & (chips - 1) == 0


def send_order(chips):
    far = list(range(chips // 2, chips, 2))[::-1]
    return far[:1] + list(range(2, chips // 2, 2)) + far[1:] + [0]


def late_send(chips):
    return chips // 2 + 1


def attend_chips(made, normed, w_qkv, tables, info, count):
    rows = normed.shape[0]
    chips = count // 2
    held = {}
    for first in send_order(chips):
        if held:
            made = project(normed, w_qkv, tables, info, [first])
        for side in range(2):
            apart = first + side
            held[apart] = across(made[side], 2 * apart, count) if apart else made[side]
    total, half = chips * rows, chips // 2
    late = late_send(chips)
    soon = tuple(apart for apart in range(chips) if apart != late)
    places = tuple(apart // 2 for apart in soon if apart % 2)
    early, early_rows = total - rows, 2 * (half - 1) * rows
    parts = call(
        functools.partial(attend_early_kernel, soon),
        (
            array((early, 2 * LANES), jnp.bfloat16),
            array((early, LANES), jnp.bfloat16),
            array((early_rows, 2 * LANES), jnp.bfloat16),
        )
        + (array((early_rows, LANES)),) * 3,
        (info,) + tuple(held[apart] for apart in soon),
        [],
    )
    crossing, keys, values = call(
        functools.partial(attend_last_kernel, late, places),
        (
            array((half, rows, LANES), jnp.bfloat16),
            array((total, 2 * LANES), jnp.bfloat16),
            array((total, LANES), jnp.bfloat16),
        ),
        (info,) + tuple(parts) + (held[late],),
        [VMEM((2 * rows, 2 * LANES), jnp.bfloat16)],
    )
    crossed = across(crossing, 2, count)
    staying = call(
        attend_second_kernel,
        array((half, rows, LANES), jnp.bfloat16),
        (info, keys, values) + tuple(held[apart] for apart in range(0, chips, 2)),
        [VMEM((total, 2 * LANES), jnp.bfloat16)],
    )
    joined = call(
        merge_kernel,
        (array((2, rows, LANES), jnp.bfloat16),) * (half - 1),
        (info, staying, crossed),
        [],
    )
    back, blocks = [staying, crossed], [(0, 0, 0), (1, 0, 1)]
    got = {}
    for apart in range(1, half):
        got[apart] = across(joined[apart - 1], 4 * apart, count)
    for apart in range(1, half):
        blocks += [(len(back), side, 2 * apart + side) for side in range(2)]
        back.append(got[apart])
    return back, blocks


def per_device(
    hidden, latent, lengths, step_index, guidance, modulation, conv_kernel, w_qkv, w_out, w_mel
):
    copies, rows, width = hidden.shape
    count = lax.axis_size("seq")
    chips = count // 2
    index = lax.axis_index("seq").astype(jnp.int32)
    chip, core = index >> 1, index & 1
    chip_rows = 2 * rows
    info = jnp.stack([core, chip, lengths[0]])

    edges = lax.dynamic_slice(hidden, (0, core * (rows - HALO), 0), (copies, HALO, width))
    partner = lax.dynamic_slice(hidden, (1 - core, 0, 0), (1, rows, width))[0]
    near = lax.ppermute(edges, ("clip", "seq"), facing_pairs(lax.axis_size("clip"), count))
    far = across(near, 1, count)
    partner = across(partner, 1, count)
    own, taps, mods, is_first, live = call(
        stage_kernel,
        (
            array((rows, width), jnp.bfloat16),
            array(conv_kernel.shape),
            array(modulation.shape),
            array(latent.shape),
            array(latent.shape),
        ),
        (info, hidden, conv_kernel, modulation),
        [pltpu.SemaphoreType.DMA((3,))],
        hbm=(1, 2, 3),
    )
    tables = rotary_tables(chip * chip_rows + jnp.arange(chip_rows, dtype=jnp.int32))
    first_pair = send_order(chips)[0] if chips_hold_groups(count) else None
    group = array((3, chip_rows, LANES), jnp.bfloat16)
    residual, normed, weight, *made = call(
        functools.partial(front_kernel, first_pair),
        (
            array((chip_rows, width)),
            array((chip_rows, width), jnp.bfloat16),
            array(w_qkv.shape, jnp.bfloat16),
        )
        + (group,) * (0 if first_pair is None else 2),
        (info, own, partner, near, far, taps, mods) + tables + (w_qkv,),
        [
            VMEM((chip_rows + 2 * HALO, LANES), jnp.float32),
            pltpu.SemaphoreType.DMA((width // (2 * LANES),)),
        ],
        hbm=(9,),
    )
    if chips_hold_groups(count):
        back, blocks = attend_chips(made, normed, weight, tables, info, count)
    else:
        back = [attend_any(normed, weight, tables, info, lengths[0], count)]
        blocks = [(0, group, None) for group in range(back[0].shape[0])]
    mels = w_mel.shape[1]
    keep, send = call(
        functools.partial(back_kernel, tuple(blocks)),
        (array((rows, mels)),) * 2,
        (info, residual, w_mel.T, mods, w_out) + tuple(back),
        [
            VMEM((chip_rows, HEADS * HEAD_DIM), jnp.bfloat16),
            VMEM((chip_rows, width), jnp.float32),
            VMEM((chip_rows, mels), jnp.float32),
        ],
    )
    other = across(send, 1, count)
    first = jnp.where(is_first > 0.5, keep, other)
    second = jnp.where(is_first > 0.5, other, keep)
    guided = first + guidance[0] * (first - second)
    velocity = jnp.where(live > 0.5, guided, 0.0)
    progress = step_index[0].astype(jnp.float32) / STEPS
    time_now = 1.0 - jnp.cos(0.5 * jnp.pi * progress)
    return (velocity, latent + (1.0 - time_now) * velocity)


def solution(mesh):
    return jax.shard_map(
        per_device,
        mesh=mesh,
        in_specs=(
            P(None, ("clip", "seq"), None),
            P(("clip", "seq"), None),
            P("clip"),
            P(),
            P(),
            P(),
            P(),
            P(),
            P(),
            P(),
        ),
        out_specs=(P(("clip", "seq"), None), P(("clip", "seq"), None)),
        check_vma=False,
    )
```
